32 devices in a mesh: fsdp: 8 (over y, x, core), ctx: 4 (over z).
Axes of the slice: x: 2, y: 2, z: 4, core: 2. Of those that a mesh axis runs over, the one named last changes fastest.
Arguments:
- inputs: bfloat16 [8, 4096, 1024], P('fsdp', 'ctx'), may hold values from -6 to 6
- cotangent: bfloat16 [8, 4096, 1024], P('fsdp', 'ctx'), may hold values from -6 to 6
- positions: int32 [8, 4096], P('fsdp', 'ctx'), may hold values from 0 to 2303, as said below
- segments: int32 [8, 4096], P('fsdp', 'ctx'), may hold values from 0 to 8, as said below
- ln1_gain: bfloat16 [1024], P('fsdp'), may hold values from 0.5 to 1.5
- ln1_bias: bfloat16 [1024], P('fsdp'), may hold values from -2.5 to 2.5
- w_qkv: bfloat16 [1024, 3072], P('fsdp'), may hold values from -0.1875 to 0.1875
- b_qkv: bfloat16 [3072], P('fsdp'), may hold values from -3 to 3
- w_attn_out: bfloat16 [1024, 1024], P('fsdp'), may hold values from -1.5 to 1.5
- b_out: bfloat16 [1024], P('fsdp'), may hold values from -2.5 to 2.5
- ln2_gain: bfloat16 [1024], P('fsdp'), may hold values from 0.5 to 1.5
- ln2_bias: bfloat16 [1024], P('fsdp'), may hold values from -2.5 to 2.5
- w_in: bfloat16 [1024, 4096], P('fsdp'), may hold values from -0.1875 to 0.1875
- b_in: bfloat16 [4096], P('fsdp'), may hold values from -2.5 to 2.5
- w_out: bfloat16 [4096, 1024], P('fsdp'), may hold values from -0.09375 to 0.09375
Outputs:
- output: bfloat16 [8, 4096, 1024], P('fsdp', 'ctx')
- grad_inputs: float32 [8, 4096, 1024], P('fsdp', 'ctx')
- grad_ln1_gain: float32 [1024], P(('fsdp', 'ctx'))
- grad_ln1_bias: float32 [1024], P(('fsdp', 'ctx'))
- grad_w_qkv: float32 [1024, 3072], P(('fsdp', 'ctx'))
- grad_b_qkv: float32 [3072], P(('fsdp', 'ctx'))
- grad_w_attn_out: float32 [1024, 1024], P(('fsdp', 'ctx'))
- grad_b_out: float32 [1024], P(('fsdp', 'ctx'))
- grad_ln2_gain: float32 [1024], P(('fsdp', 'ctx'))
- grad_ln2_bias: float32 [1024], P(('fsdp', 'ctx'))
- grad_w_in: float32 [1024, 4096], P(('fsdp', 'ctx'))
- grad_b_in: float32 [4096], P(('fsdp', 'ctx'))
- grad_w_out: float32 [4096, 1024], P(('fsdp', 'ctx'))
The draws below stay inside these ranges and needn't reach their ends.
Inputs may be any that keep to these rules, and one draw needn't show every extreme that they name: `positions`: in a group, token t of the natural order (the prompt, then the continuations one after another) has position t and segment 0 if t < 2048, else position 2048 + (t - 2048) % 256 and segment 1 + (t - 2048) // 256. The natural order is cut into 8 blocks of 512 tokens; index j of ctx holds block p_j followed by block 7 - p_j, where p is a permutation of 0 to 3 drawn for each group. `segments`: laid out with positions as stated there.
All inputs are finite; a program needn't handle non-finite values.
Results may differ from the reference program's by a relative error of at most 0.014.
Values may be sent and summed in bfloat16 or wider, within the bound.
No kernel may reach another device: no remote copies, remote signals or barrier semaphores. Data moves between devices by JAX's collectives and lax.ppermute only.
A program may use at most 256 MiB of HBM per device.

```python
import math
import jax
import jax.numpy as jnp
from jax import lax

D = 1024
HEADS = 16
HD = 64
FF = 4096
ROT = 16
PROMPT = 2048
CLEN = 256
NT = 4096
GROUPS = 8
NBLK = 8
BS = 512


def block_labels(key):
    base = jax.random.fold_in(key, 4711)
    group_keys = jax.random.split(base, GROUPS)
    slots = jnp.arange(NT, dtype=jnp.int32)
    holder = slots // (2 * BS)
    within = slots % (2 * BS)

    def one_group(group_key):
        order = jax.random.permutation(group_key, NBLK // 2)
        paired = order[holder]
        chosen = jnp.where(within < BS, paired, NBLK - 1 - paired)
        natural = chosen * BS + within % BS
        tail = natural - PROMPT
        segment = jnp.where(natural < PROMPT, 0, 1 + tail // CLEN)
        position = jnp.where(natural < PROMPT, natural, PROMPT + tail % CLEN)
        return (position.astype(jnp.int32), segment.astype(jnp.int32))
    return jax.vmap(one_group)(group_keys)


def draw_positions(key, part):
    return block_labels(key)[0]


def draw_segments(key, part):
    return block_labels(key)[1]


def steps_of(own_key, dims, cuts, low, largest):
    loudness = 1.0
    for axis_at, shards_of in cuts:
        heights = jax.random.uniform(jax.random.fold_in(jax.random.fold_in(own_key, 6), axis_at), (shards_of,), jnp.float32, low / len(cuts), largest / len(cuts))
        loudness = loudness * jnp.repeat(jnp.exp(heights), dims[axis_at] // shards_of).reshape((-1,) + (1,) * (len(dims) - 1 - axis_at))
    return loudness


def gaussian(own_key, dims, deviation, limit, cuts=(), kind=jnp.bfloat16):
    values = deviation * jax.random.normal(own_key, dims, jnp.float32)
    if cuts:
        values = values * steps_of(own_key, dims, cuts, -0.22, 0.18)
    return jnp.clip(values, -limit, limit).astype(kind)


def setup_inputs(seed: int = 0) -> dict:
    key_list = jax.random.split(jax.random.key(seed), 16)
    return {
        "inputs": gaussian(key_list[0], (GROUPS, NT, D), 1.0, 6.0, ((0, 8), (1, 4))),
        "cotangent": gaussian(key_list[1], (GROUPS, NT, D), 1.0, 6.0, ((0, 8), (1, 4))),
        "positions": draw_positions(jax.random.fold_in(key_list[15], 71), 0),
        "segments": draw_segments(jax.random.fold_in(key_list[15], 71), 0),
        "ln1_gain": jnp.clip(1.0 + 0.1 * jax.random.normal(key_list[4], (D,), jnp.float32), 0.5, 1.5).astype(jnp.bfloat16),
        "ln1_bias": gaussian(key_list[5], (D,), 0.3, 2.5, ((0, 8),)),
        "w_qkv": gaussian(key_list[6], (D, 3 * D), D ** -0.5, 0.1875, ((0, 8),)),
        "b_qkv": gaussian(key_list[7], (3 * D,), 0.5, 3.0, ((0, 8),)),
        "w_attn_out": gaussian(key_list[8], (D, D), (D // 64) ** -0.5, 1.5, ((0, 8),)),
        "b_out": gaussian(key_list[9], (D,), 0.3, 2.5, ((0, 8),)),
        "ln2_gain": jnp.clip(1.0 + 0.1 * jax.random.normal(key_list[10], (D,), jnp.float32), 0.5, 1.5).astype(jnp.bfloat16),
        "ln2_bias": gaussian(key_list[11], (D,), 0.3, 2.5, ((0, 8),)),
        "w_in": gaussian(key_list[12], (D, FF), D ** -0.5, 0.1875, ((0, 8),)),
        "b_in": gaussian(key_list[13], (FF,), 0.3, 2.5, ((0, 8),)),
        "w_out": gaussian(key_list[14], (FF, D), FF ** -0.5, 0.09375, ((0, 8),)),
    }


@jax.custom_vjp
def low(v):
    return lax.optimization_barrier(v.astype(jnp.bfloat16)).astype(jnp.float32)

@jax.custom_vjp
def low_back(v):
    return v

def low_keep(v):
    return (low(v), None)

def low_pass(kept, grad):
    return (grad,)

def back_keep(v):
    return (v, None)

def back_low(kept, grad):
    return (low(grad),)
low.defvjp(low_keep, low_pass)
low_back.defvjp(back_keep, back_low)
NORM_EPS = 1e-05
MASKED = -1e+30
HIGHEST = lax.Precision.HIGHEST

def layer_norm(values, scaling, offset):
    average = lax.optimization_barrier(jnp.mean(values, axis=-1, keepdims=True))
    centered = values - average
    variance = lax.optimization_barrier(jnp.mean(centered * centered, axis=-1, keepdims=True))
    return centered * lax.rsqrt(variance + NORM_EPS) * scaling + offset

def rotary_tables(positions):
    halfway = ROT // 2
    spacing = jnp.arange(halfway, dtype=jnp.float32) * (2.0 / ROT)
    inverse = jnp.exp(-math.log(10000.0) * spacing)
    angles = positions.astype(jnp.float32)[..., None] * inverse
    return (jnp.cos(angles), jnp.sin(angles))

def rotate(heads_in, cosine, sine):
    halfway = ROT // 2
    cosine = cosine[..., None, :]
    sine = sine[..., None, :]
    first = heads_in[..., :halfway]
    second = heads_in[..., halfway:ROT]
    return jnp.concatenate([first * cosine - second * sine, second * cosine + first * sine, heads_in[..., ROT:]], axis=-1)

def attention(queries, keys, values, positions, segments):
    length = queries.shape[0]
    width = math.gcd(length, 512)
    count = length // width

    def one_block(pieces):
        query_blk, pos_blk, seg_blk = pieces
        scores = low_back(jnp.einsum('qhd,khd->hqk', query_blk, keys, precision=HIGHEST))
        allowed = ((segments[None, :] == 0) | (segments[None, :] == seg_blk[:, None])) & (positions[None, :] <= pos_blk[:, None])
        scores = jnp.where(allowed[None], scores, MASKED)
        shifted = scores - lax.optimization_barrier(jnp.max(scores, axis=-1, keepdims=True))
        expon = jnp.exp(shifted)
        probs = expon / lax.optimization_barrier(jnp.sum(expon, axis=-1, keepdims=True))
        weights = low(probs)
        return jnp.einsum('hqk,khd->qhd', weights, values, precision=HIGHEST)
    blocks = lax.map(jax.checkpoint(one_block), (queries.reshape(count, width, HEADS, HD), positions.reshape(count, width), segments.reshape(count, width)))
    return blocks.reshape(length, HEADS * HD)

def group_forward(params, inputs, positions, segments):
    gain_attn, shift_attn, weight_qkv, bias_qkv, weight_attn, bias_out, gain_mlp, shift_mlp, weight_in, bias_in, weight_out = params
    length, width = inputs.shape
    normed_attn = low(layer_norm(inputs, gain_attn, shift_attn))
    normed_mlp = low(layer_norm(inputs, gain_mlp, shift_mlp))
    projected = low_back(jnp.dot(normed_attn, weight_qkv, precision=HIGHEST) + bias_qkv)
    cosine, sine = rotary_tables(positions)
    query_part = projected[:, :width].reshape(length, HEADS, HD)
    key_part = projected[:, width:2 * width].reshape(length, HEADS, HD)
    value_part = projected[:, 2 * width:].reshape(length, HEADS, HD)
    queries = low(rotate(query_part, cosine, sine) * HD ** (-0.5))
    keys = low(rotate(key_part, cosine, sine))
    values = low(value_part)
    attended = low(low_back(attention(queries, keys, values, positions, segments)))
    pre_act = low_back(jnp.dot(normed_mlp, weight_in, precision=HIGHEST) + bias_in)
    activated = low(jax.nn.gelu(pre_act, approximate=False))
    return inputs + jnp.dot(attended, weight_attn, precision=HIGHEST) + jnp.dot(activated, weight_out, precision=HIGHEST) + bias_out

def reference(inputs, cotangent, positions, segments, ln1_gain, ln1_bias, w_qkv, b_qkv, w_attn_out, b_out, ln2_gain, ln2_bias, w_in, b_in, w_out):
    params = tuple((array.astype(jnp.float32) for array in (ln1_gain, ln1_bias, w_qkv, b_qkv, w_attn_out, b_out, ln2_gain, ln2_bias, w_in, b_in, w_out)))

    def one_group(totals, pieces):
        group_inputs, group_cot, group_pos, group_seg = pieces

        def forward(weights, rows):
            return group_forward(weights, rows, group_pos, group_seg)
        outputs, pullback = jax.vjp(forward, params, group_inputs.astype(jnp.float32))
        grad_params, grad_rows = pullback(group_cot.astype(jnp.float32))
        totals = jax.tree.map(jnp.add, totals, grad_params)
        return (totals, (outputs.astype(jnp.bfloat16), grad_rows))
    zeros = jax.tree.map(jnp.zeros_like, params)
    totals, (outputs, grad_inputs) = lax.scan(one_group, zeros, (inputs, cotangent, positions, segments))
    return (outputs, grad_inputs, totals[0], totals[1], totals[2], totals[3], totals[4], totals[5], totals[6], totals[7], totals[8], totals[9], totals[10])
```

```python
from functools import partial
import math

import jax
import jax.numpy as jnp
from jax import lax
from jax.experimental import pallas as pl
from jax.experimental.pallas import tpu as pltpu
from jax.sharding import PartitionSpec as P

HEADS = 16
HD = 64
ROT = 16
CLEN = 256
QB = 256
PAIR = 2 * HD
bf16 = jnp.bfloat16
f32 = jnp.float32


NORM_EPS = 1e-05
MASKED = -1e30


def layer_norm(values, scaling, offset):
    average = jnp.mean(values, axis=-1, keepdims=True)
    centered = values - average
    variance = jnp.mean(centered * centered, axis=-1, keepdims=True)
    return centered * lax.rsqrt(variance + NORM_EPS) * scaling + offset


def rotary_tables(positions):
    halfway = ROT // 2
    spacing = jnp.arange(halfway, dtype=jnp.float32) * (2.0 / ROT)
    inverse = jnp.exp(-math.log(10000.0) * spacing)
    angles = positions.astype(jnp.float32)[..., None] * inverse
    return (jnp.cos(angles), jnp.sin(angles))


def rotate(heads_in, cosine, sine):
    halfway = ROT // 2
    cosine = cosine[..., None, :]
    sine = sine[..., None, :]
    first = heads_in[..., :halfway]
    second = heads_in[..., halfway:ROT]
    return jnp.concatenate(
        [first * cosine - second * sine, second * cosine + first * sine, heads_in[..., ROT:]],
        axis=-1,
    )


def unrotate(grads_in, cosine, sine):
    halfway = ROT // 2
    cosine = cosine[..., None, :]
    sine = sine[..., None, :]
    first = grads_in[..., :halfway]
    second = grads_in[..., halfway:ROT]
    return jnp.concatenate(
        [first * cosine + second * sine, second * cosine - first * sine, grads_in[..., ROT:]],
        axis=-1,
    )


def allowed_mask(query_pos, query_seg, key_pos, key_seg):
    same_doc = (key_seg[:, None, :] == 0) | (key_seg[:, None, :] == query_seg[:, :, None])
    causal = key_pos[:, None, :] <= query_pos[:, :, None]
    return (same_doc & causal)[:, None]


def scores_of(queries, keys_blk):
    return jnp.einsum("gqhd,gkhd->ghqk", queries, keys_blk, preferred_element_type=jnp.float32)


def block_grads(queries, grad_att, log_total, delta, mask, keys_blk, values_blk):
    probs = jnp.where(mask, jnp.exp(scores_of(queries, keys_blk) - log_total[..., None]), 0.0)
    dprobs = jnp.einsum("gqhd,gkhd->ghqk", grad_att, values_blk, preferred_element_type=jnp.float32)
    grad_scores = (probs * (dprobs - delta[..., None])).astype(jnp.bfloat16)
    return (probs.astype(jnp.bfloat16), grad_scores)


def attn_kernel(half, nctx, kind_ref, q_ref, do_ref, k_ref, v_ref, o_ref, dq_ref, dk_ref, dv_ref,
                kt_ref, vt_ref, s_ref, p_ref, ds_ref, dka_ref, dva_ref):
    qb = pl.program_id(1)
    nqb = pl.num_programs(1)
    keys = k_ref.shape[0]
    wide0 = half
    starts = [i for i in range(0, half, QB)] + [i for i in range(2*half, keys, QB)]
    nch = len(starts)
    @pl.when(qb == 0)
    def _():
        kt_ref[...] = k_ref[...].T
        vt_ref[...] = v_ref[...].T
        dka_ref[...] = jnp.zeros_like(dka_ref)
        dva_ref[...] = jnp.zeros_like(dva_ref)
    diag0 = pl.multiple_of(qb * QB, QB)
    lane = lax.broadcasted_iota(jnp.int32, (PAIR, QB), 0)
    qT = q_ref[...].T
    doT = do_ref[...].T.astype(f32)
    zero = jnp.zeros((), bf16)
    row = lax.broadcasted_iota(jnp.int32, (QB, QB), 0)
    col = lax.broadcasted_iota(jnp.int32, (QB, QB), 1)
    causal = row <= col
    lanes = lax.broadcasted_iota(jnp.int32, (QB, PAIR), 1)
    def red8(x, op):
        return op(x.reshape(x.shape[0] // 8, 8, x.shape[1]), axis=0)
    def kload(ref, c):
        return ref[pl.ds(diag0, QB), :] if c == nch else ref[starts[c]:starts[c]+QB, :]
    outs = []
    ots = []; dots_ = []; dqts = []
    ms = []
    for h in range(2):
        keep = (lane < HD) if h == 0 else (lane >= HD)
        qh = jnp.where(keep, qT, zero)
        mx = jnp.full((8, QB), MASKED, f32)
        for c in range(nch + 1):
            s = jnp.dot(kload(k_ref, c), qh, preferred_element_type=f32)
            if c == nch:
                s = jnp.where(causal, s, MASKED)
                mc = red8(s, jnp.max)
            else:
                mc = red8(s, jnp.max) + kind_ref[qb, c]
            s_ref[h, c] = s
            mx = jnp.maximum(mx, mc)
        m = jnp.max(mx, axis=0, keepdims=True)
        ms.append(m)
    for h in range(2):
        m = ms[h]
        l8 = jnp.zeros((8, QB), f32)
        ot = jnp.zeros((HD, QB), f32)
        for c in range(nch + 1):
            t = -m if c == nch else kind_ref[qb, c] - m
            e = jnp.exp2(s_ref[h, c] + t)
            l8 = l8 + red8(e, jnp.sum)
            p = e.astype(bf16)
            p_ref[h, c] = p
            if c == nch:
                vt = vt_ref[h*HD:(h+1)*HD, pl.ds(diag0, QB)]
            else:
                vt = vt_ref[h*HD:(h+1)*HD, starts[c]:starts[c]+QB]
            ot = ot + jnp.dot(vt, p, preferred_element_type=f32)
        l = jnp.sum(l8, axis=0, keepdims=True)
        r = 1.0 / l
        oth = ot * r
        ots.append(oth)
        doh = doT[h*HD:(h+1)*HD]
        delta = jnp.sum(oth * doh, axis=0, keepdims=True) * r
        dos = (doh * r).astype(bf16)
        z = jnp.zeros_like(dos)
        dop = jnp.concatenate([dos, z] if h == 0 else [z, dos], axis=0)
        dots_.append((dop, delta))
    for h in range(2):
        dop, delta = dots_[h]
        dqt = jnp.zeros((HD, QB), f32)
        for c in range(nch + 1):
            dp = jnp.dot(kload(v_ref, c), dop, preferred_element_type=f32)
            ds = (p_ref[h, c].astype(f32) * (dp - delta)).astype(bf16)
            ds_ref[h, c] = ds
            if c == nch:
                kt = kt_ref[h*HD:(h+1)*HD, pl.ds(diag0, QB)]
            else:
                kt = kt_ref[h*HD:(h+1)*HD, starts[c]:starts[c]+QB]
            dqt = dqt + jnp.dot(kt, ds, preferred_element_type=f32)
        dqts.append(dqt)
    qv = q_ref[...]
    qm = [jnp.where(lanes < HD, qv, zero), jnp.where(lanes >= HD, qv, zero)]
    dom = [dots_[h][0].T for h in range(2)]
    for c in range(nch + 1):
        dva = jnp.dot(p_ref[0, c], dom[0], preferred_element_type=f32) + jnp.dot(p_ref[1, c], dom[1], preferred_element_type=f32)
        dka = jnp.dot(ds_ref[0, c], qm[0], preferred_element_type=f32) + jnp.dot(ds_ref[1, c], qm[1], preferred_element_type=f32)
        if c == nch:
            sl = pl.ds(diag0, QB)
        else:
            sl = pl.ds(starts[c], QB)
        dva_ref[sl, :] += dva
        dka_ref[sl, :] += dka
    o_ref[...] = jnp.concatenate(ots, axis=0).T.astype(o_ref.dtype)
    dq_ref[...] = jnp.concatenate(dqts, axis=0).T.astype(dq_ref.dtype)
    @pl.when(qb == nqb - 1)
    def _():
        dk_ref[...] = (dka_ref[...] * math.log(2.0)).astype(dk_ref.dtype)
        dv_ref[...] = dva_ref[...].astype(dv_ref.dtype)

def attention(q, do, k, v, kind, half, nctx):
    rows, width = q.shape
    keys = k.shape[0]
    nqb = rows // QB
    nch = kind.shape[1]
    pairs = width // PAIR
    qspec = pl.BlockSpec((QB, PAIR), lambda p, b: (b, p))
    kspec = pl.BlockSpec((keys, PAIR), lambda p, b: (0, p))
    return pl.pallas_call(
        partial(attn_kernel, half, nctx),
        grid=(pairs, nqb),
        in_specs=[pl.BlockSpec(memory_space=pltpu.SMEM), qspec, qspec, kspec, kspec],
        out_specs=[qspec, qspec, kspec, kspec],
        out_shape=[jax.ShapeDtypeStruct((rows, width), bf16), jax.ShapeDtypeStruct((rows, width), f32),
                   jax.ShapeDtypeStruct((keys, width), bf16), jax.ShapeDtypeStruct((keys, width), bf16)],
        scratch_shapes=[pltpu.VMEM((PAIR, keys), bf16), pltpu.VMEM((PAIR, keys), bf16),
                        pltpu.VMEM((2, nch + 1, QB, QB), f32), pltpu.VMEM((2, nch + 1, QB, QB), bf16),
                        pltpu.VMEM((2, nch + 1, QB, QB), bf16),
                        pltpu.VMEM((keys, PAIR), f32), pltpu.VMEM((keys, PAIR), f32)],
        compiler_params=pltpu.CompilerParams(vmem_limit_bytes=60 << 20),
        name="attention",
    )(kind, q, do, k, v)


def turn_tables(positions):
    halfway = ROT // 2
    lane = jnp.arange(HEADS * HD) % HD
    inverse = jnp.exp(-math.log(10000.0) * (2.0 / ROT) * (lane % halfway).astype(f32))
    angles = positions.astype(f32)[:, None] * inverse[None, :]
    cosine = jnp.where(lane < ROT, jnp.cos(angles), 1.0)
    sine = jnp.sin(angles)
    return cosine, jnp.where(lane < halfway, sine, 0.0), jnp.where((lane >= halfway) & (lane < ROT), sine, 0.0)


def turn(u, tables):
    cosine, low, high = tables
    return u * cosine - jnp.roll(u, -(ROT // 2), 1) * low + jnp.roll(u, ROT // 2, 1) * high


def turn_back(g, tables):
    cosine, low, high = tables
    return g * cosine + jnp.roll(g, -(ROT // 2), 1) * low - jnp.roll(g, ROT // 2, 1) * high


def scatter_sum(terms):
    part = lax.psum_scatter(terms, "fsdp", scatter_dimension=0, tiled=True)
    return lax.psum_scatter(part, "ctx", scatter_dimension=0, tiled=True)


def fast(inputs, cotangent, positions, segments, ln1_gain, ln1_bias, w_qkv, b_qkv, w_attn_out, b_out,
         ln2_gain, ln2_bias, w_in, b_in, w_out):
    x, grad_out, pos = inputs[0], cotangent[0], positions[0]
    rows, width = x.shape
    half = rows // 2
    n = lax.axis_size("ctx")
    f = lax.axis_size("fsdp")
    ring = [(i, (i + 1) % n) for i in range(n)]
    back = [(i, (i - 1) % n) for i in range(n)]
    xs, poss = [x[:half]], [pos[:half]]
    for _ in range(n - 1):
        xs.append(lax.ppermute(xs[-1], "ctx", ring))
        poss.append(lax.ppermute(poss[-1], "ctx", ring))
    small = jnp.concatenate([ln1_gain, ln1_bias, b_qkv, b_out, ln2_gain, ln2_bias, b_in])
    small = lax.all_gather(small.reshape(1, -1), "fsdp", axis=0, tiled=True)
    sizes = [a.shape[0] for a in (ln1_gain, ln1_bias, b_qkv, b_out, ln2_gain, ln2_bias, b_in)]
    full, at = [], 0
    for size in sizes:
        full.append(small[:, at:at + size].reshape(-1).astype(f32))
        at += size
    gain_attn, shift_attn, bias_qkv, bias_out, gain_mlp, shift_mlp, bias_in = full
    weight_qkv = lax.all_gather(w_qkv, "fsdp", axis=0, tiled=True)
    weight_in = lax.all_gather(w_in, "fsdp", axis=0, tiled=True)
    weight_out = lax.all_gather(w_out, "fsdp", axis=0, tiled=True)
    weight_attn = lax.all_gather(w_attn_out, "fsdp", axis=0, tiled=True)

    x_all = jnp.concatenate([x] + xs[1:], axis=0)
    pos_all = jnp.concatenate([pos] + poss[1:], axis=0)
    normed_all = layer_norm(x_all.astype(f32), gain_attn, shift_attn).astype(bf16)
    normed_attn = normed_all[:rows]
    tables = turn_tables(pos_all)
    own = tuple(t[:rows] for t in tables)
    scale = HD ** (-0.5)
    q_part = jnp.dot(normed_attn, weight_qkv[:, :width], preferred_element_type=f32) + bias_qkv[:width]
    queries = (turn(q_part, own) * (scale / math.log(2.0))).astype(bf16)
    k_part = jnp.dot(normed_all, weight_qkv[:, width:2 * width], preferred_element_type=f32) + bias_qkv[width:2 * width]
    keys = turn(k_part, tables).astype(bf16)
    v_part = jnp.dot(normed_all, weight_qkv[:, 2 * width:], preferred_element_type=f32) + bias_qkv[2 * width:]
    values = v_part.astype(bf16)
    grad_att = jnp.einsum("rd,ad->ra", grad_out, weight_attn, preferred_element_type=f32).astype(bf16)

    flat_in = x.astype(f32)
    normed_mlp = layer_norm(flat_in, gain_mlp, shift_mlp).astype(bf16)
    pre_act = jnp.dot(normed_mlp, weight_in, preferred_element_type=f32) + bias_in
    activated = jax.nn.gelu(pre_act, approximate=False).astype(bf16)
    partial_out = jnp.dot(activated, weight_out, preferred_element_type=f32)
    grad_bias_out = jnp.sum(grad_out.astype(f32), axis=0)
    grad_weight_out = jnp.einsum("rf,rd->fd", activated, grad_out, preferred_element_type=f32).astype(bf16)
    grad_act = jnp.einsum("rd,fd->rf", grad_out, weight_out, preferred_element_type=f32)
    unused, gelu_back = jax.vjp(partial(jax.nn.gelu, approximate=False), pre_act)
    grad_pre = gelu_back(grad_act)[0].astype(bf16)
    grad_weight_in = jnp.einsum("rd,rf->df", normed_mlp, grad_pre, preferred_element_type=f32).astype(bf16)
    grad_bias_in = jnp.sum(grad_pre.astype(f32), axis=0)
    grad_normed_mlp = jnp.einsum("rf,df->rd", grad_pre, weight_in, preferred_element_type=f32)
    sum_out = scatter_sum(grad_weight_out)
    sum_in = scatter_sum(grad_weight_in)

    first = pos[0]
    free, shut = jnp.zeros((), f32), jnp.full((), MASKED, f32)
    per = half // QB
    table = []
    for qb in range(2 * per):
        line = [free if qb > c else shut for c in range(per)]
        for s in range(1, n):
            flag = free if qb >= per else jnp.where(poss[s][0] < first, free, shut)
            line += [flag] * per
        table.append(jnp.stack(line))
    kind = jnp.stack(table)
    attended, grad_q, grad_k, grad_v = attention(queries, grad_att, keys, values, kind, half, n)

    def piece(a, s):
        return a[:half] if s == 0 else a[(s + 1) * half:(s + 2) * half]

    run_k, run_v = piece(grad_k, n - 1), piece(grad_v, n - 1)
    for s in range(n - 2, -1, -1):
        run_k = lax.ppermute(run_k, "ctx", back).astype(f32) + piece(grad_k, s).astype(f32)
        run_v = lax.ppermute(run_v, "ctx", back).astype(f32) + piece(grad_v, s).astype(f32)
        if s:
            run_k, run_v = run_k.astype(bf16), run_v.astype(bf16)
    full_k = jnp.concatenate([run_k, grad_k[half:2 * half].astype(f32)], axis=0)
    full_v = jnp.concatenate([run_v, grad_v[half:2 * half].astype(f32)], axis=0)

    output = (flat_in + jnp.dot(attended, weight_attn, preferred_element_type=f32) + partial_out + bias_out).astype(bf16)
    grad_weight_attn = jnp.einsum("ra,rd->ad", attended, grad_out, preferred_element_type=f32).astype(bf16)
    sum_attn = scatter_sum(grad_weight_attn)
    grad_projected = jnp.concatenate(
        [turn_back(grad_q * scale, own), turn_back(full_k, own), full_v], axis=1).astype(bf16)
    grad_weight_qkv = jnp.einsum("rd,re->de", normed_attn, grad_projected, preferred_element_type=f32).astype(bf16)
    sum_qkv = scatter_sum(grad_weight_qkv)
    grad_bias_qkv = jnp.sum(grad_projected.astype(f32), axis=0)
    grad_normed_attn = jnp.einsum("re,de->rd", grad_projected, weight_qkv, preferred_element_type=f32)
    unused, norm_back_attn = jax.vjp(layer_norm, flat_in, gain_attn, shift_attn)
    grad_in_attn, grad_gain_attn, grad_shift_attn = norm_back_attn(grad_normed_attn)
    unused, norm_back_mlp = jax.vjp(layer_norm, flat_in, gain_mlp, shift_mlp)
    grad_in_mlp, grad_gain_mlp, grad_shift_mlp = norm_back_mlp(grad_normed_mlp)
    grad_inputs = grad_out.astype(f32) + grad_in_attn + grad_in_mlp
    parts = n * f
    smalls = (grad_gain_attn, grad_shift_attn, grad_bias_qkv, grad_bias_out, grad_gain_mlp, grad_shift_mlp, grad_bias_in)
    packed = jnp.concatenate([a.reshape(parts, -1) for a in smalls], axis=1)
    packed = lax.psum_scatter(packed, ("fsdp", "ctx"), scatter_dimension=0, tiled=True)[0]
    done, at = [], 0
    for a in smalls:
        size = a.shape[0] // parts
        done.append(packed[at:at + size])
        at += size
    return (output[None], grad_inputs[None], done[0], done[1], sum_qkv.astype(f32), done[2], sum_attn.astype(f32),
            done[3], done[4], done[5], sum_in.astype(f32), done[6], sum_out.astype(f32))


def local(*args):
    half = args[0].shape[1] // 2
    if args[0].shape[0] == 1 and half % CLEN == 0 and half % QB == 0:
        return fast(*args)
    return generic(*args)


def generic(
    inputs,
    cotangent,
    positions,
    segments,
    ln1_gain,
    ln1_bias,
    w_qkv,
    b_qkv,
    w_attn_out,
    b_out,
    ln2_gain,
    ln2_bias,
    w_in,
    b_in,
    w_out,
):
    shards = (
        ln1_gain,
        ln1_bias,
        w_qkv,
        b_qkv,
        w_attn_out,
        b_out,
        ln2_gain,
        ln2_bias,
        w_in,
        b_in,
        w_out,
    )
    params = (
        lax.all_gather(shards[0], "fsdp", axis=0, tiled=True),
        lax.all_gather(shards[1], "fsdp", axis=0, tiled=True),
        lax.all_gather(shards[2], "fsdp", axis=0, tiled=True),
        lax.all_gather(shards[3], "fsdp", axis=0, tiled=True),
        lax.all_gather(shards[4], "fsdp", axis=0, tiled=True),
        lax.all_gather(shards[5], "fsdp", axis=0, tiled=True),
        lax.all_gather(shards[6], "fsdp", axis=0, tiled=True),
        lax.all_gather(shards[7], "fsdp", axis=0, tiled=True),
        lax.all_gather(shards[8], "fsdp", axis=0, tiled=True),
        lax.all_gather(shards[9], "fsdp", axis=0, tiled=True),
        lax.all_gather(shards[10], "fsdp", axis=0, tiled=True),
    )
    groups, local_len, width = inputs.shape
    rows_total = groups * local_len
    block = math.gcd(local_len, 256)
    label_pos, label_seg = (
        lax.all_gather(positions, "ctx", axis=1, tiled=True),
        lax.all_gather(segments, "ctx", axis=1, tiled=True),
    )
    count = label_pos.shape[1] // block
    f32 = jnp.float32
    bf16 = jnp.bfloat16
    (
        gain_attn,
        shift_attn,
        weight_qkv,
        bias_qkv,
        weight_attn,
        bias_out,
        gain_mlp,
        shift_mlp,
        weight_in,
        bias_in,
        weight_out,
    ) = params
    flat_in = inputs.reshape(rows_total, width).astype(f32)
    normed_attn = layer_norm(flat_in, gain_attn.astype(f32), shift_attn.astype(f32)).astype(bf16)
    normed_mlp = layer_norm(flat_in, gain_mlp.astype(f32), shift_mlp.astype(f32)).astype(bf16)
    projected = jnp.dot(normed_attn, weight_qkv, preferred_element_type=f32) + bias_qkv.astype(f32)
    cosine, sine = rotary_tables(positions)

    def split_heads(columns):
        return columns.reshape(groups, local_len, HEADS, HD)

    scale = HD ** (-0.5)
    queries = (rotate(split_heads(projected[:, :width]), cosine, sine) * scale).astype(bf16)
    keys_own = rotate(split_heads(projected[:, width : 2 * width]), cosine, sine).astype(bf16)
    values_own = split_heads(projected[:, 2 * width :]).astype(bf16)
    keys_all, values_all = (
        lax.all_gather(keys_own, "ctx", axis=1, tiled=True),
        lax.all_gather(values_own, "ctx", axis=1, tiled=True),
    )

    def key_block(index):
        start = index * block
        keys_blk = lax.dynamic_slice_in_dim(keys_all, start, block, 1)
        values_blk = lax.dynamic_slice_in_dim(values_all, start, block, 1)
        mask = allowed_mask(
            positions,
            segments,
            lax.dynamic_slice_in_dim(label_pos, start, block, 1),
            lax.dynamic_slice_in_dim(label_seg, start, block, 1),
        )
        return (keys_blk, values_blk, mask)

    def total_step(carry, index):
        peak, total = carry
        keys_blk, values_blk, mask = key_block(index)
        scores = jnp.where(mask, scores_of(queries, keys_blk), MASKED)
        fresh = jnp.maximum(peak, jnp.max(scores, axis=-1))
        added = jnp.sum(jnp.where(mask, jnp.exp(scores - fresh[..., None]), 0.0), axis=-1)
        return ((fresh, total * jnp.exp(peak - fresh) + added), None)

    stat_shape = (groups, HEADS, local_len)
    (peak, total), unused = lax.scan(
        total_step,
        (jnp.full(stat_shape, MASKED, f32), jnp.zeros(stat_shape, f32)),
        jnp.arange(count),
    )
    log_total = peak + jnp.log(total)

    def attend_step(rounded_sum, index):
        keys_blk, values_blk, mask = key_block(index)
        probs = jnp.where(mask, jnp.exp(scores_of(queries, keys_blk) - log_total[..., None]), 0.0)
        rounded_sum = rounded_sum + jnp.einsum(
            "ghqk,gkhd->gqhd", probs.astype(bf16), values_blk, preferred_element_type=f32
        )
        return (rounded_sum, None)

    head_shape = (groups, local_len, HEADS, HD)
    rounded_sum, unused = lax.scan(attend_step, jnp.zeros(head_shape, f32), jnp.arange(count))
    attended = rounded_sum.reshape(rows_total, width).astype(bf16)
    pre_act = jnp.dot(normed_mlp, weight_in, preferred_element_type=f32) + bias_in.astype(f32)
    activated = jax.nn.gelu(pre_act, approximate=False).astype(bf16)
    output = (
        flat_in
        + jnp.dot(attended, weight_attn, preferred_element_type=f32)
        + jnp.dot(activated, weight_out, preferred_element_type=f32)
        + bias_out.astype(f32)
    )
    (
        gain_attn,
        shift_attn,
        weight_qkv,
        bias_qkv,
        weight_attn,
        bias_out,
        gain_mlp,
        shift_mlp,
        weight_in,
        bias_in,
        weight_out,
    ) = params
    grad_out = cotangent.reshape(rows_total, width)
    grad_bias_out = jnp.sum(grad_out.astype(f32), axis=0)
    grad_weight_out = jnp.einsum("rf,rd->fd", activated, grad_out, preferred_element_type=f32)
    grad_act = jnp.einsum("rd,fd->rf", grad_out, weight_out, preferred_element_type=f32)
    unused, gelu_back = jax.vjp(partial(jax.nn.gelu, approximate=False), pre_act)
    grad_pre = gelu_back(grad_act)[0].astype(bf16)
    grad_weight_in = jnp.einsum("rd,rf->df", normed_mlp, grad_pre, preferred_element_type=f32)
    grad_bias_in = jnp.sum(grad_pre.astype(f32), axis=0)
    grad_normed_mlp = jnp.einsum("rf,df->rd", grad_pre, weight_in, preferred_element_type=f32)
    grad_weight_attn = jnp.einsum("ra,rd->ad", attended, grad_out, preferred_element_type=f32)
    grad_att = (
        jnp.einsum("rd,ad->ra", grad_out, weight_attn, preferred_element_type=f32)
        .astype(bf16)
        .reshape(head_shape)
    )
    delta = jnp.einsum(
        "gqhd,gqhd->ghq", grad_att.astype(f32), rounded_sum, precision=lax.Precision.HIGHEST
    )

    def back_step(carry, index):
        keys_blk, values_blk, mask = key_block(index)
        rounded, grad_scores = block_grads(
            queries, grad_att, log_total, delta, mask, keys_blk, values_blk
        )
        carry = carry + jnp.einsum(
            "ghqk,gkhd->gqhd", grad_scores, keys_blk, preferred_element_type=f32
        )
        key_term = jnp.einsum("ghqk,gqhd->gkhd", grad_scores, queries, preferred_element_type=f32)
        value_term = jnp.einsum("ghqk,gqhd->gkhd", rounded, grad_att, preferred_element_type=f32)
        return (carry, (key_term, value_term))

    grad_queries, (key_terms, value_terms) = lax.scan(
        back_step, jnp.zeros(head_shape, f32), jnp.arange(count)
    )
    key_sums, value_sums = (
        lax.psum_scatter(
            key_terms.astype(jnp.bfloat16), "ctx", scatter_dimension=0, tiled=True
        ).astype(jnp.float32),
        lax.psum_scatter(
            value_terms.astype(jnp.bfloat16), "ctx", scatter_dimension=0, tiled=True
        ).astype(jnp.float32),
    )
    grad_keys = jnp.transpose(key_sums, (1, 0, 2, 3, 4)).reshape(head_shape)
    grad_values = jnp.transpose(value_sums, (1, 0, 2, 3, 4)).reshape(head_shape)
    grad_q_pre = unrotate(grad_queries * scale, cosine, sine).reshape(rows_total, width)
    grad_k_pre = unrotate(grad_keys, cosine, sine).reshape(rows_total, width)
    grad_projected = jnp.concatenate(
        [grad_q_pre, grad_k_pre, grad_values.reshape(rows_total, width)], axis=1
    ).astype(bf16)
    grad_weight_qkv = jnp.einsum(
        "rd,re->de", normed_attn, grad_projected, preferred_element_type=f32
    )
    grad_bias_qkv = jnp.sum(grad_projected.astype(f32), axis=0)
    grad_normed_attn = jnp.einsum(
        "re,de->rd", grad_projected, weight_qkv, preferred_element_type=f32
    )
    unused, norm_back_attn = jax.vjp(
        layer_norm, flat_in, gain_attn.astype(f32), shift_attn.astype(f32)
    )
    grad_in_attn, grad_gain_attn, grad_shift_attn = norm_back_attn(grad_normed_attn)
    unused, norm_back_mlp = jax.vjp(
        layer_norm, flat_in, gain_mlp.astype(f32), shift_mlp.astype(f32)
    )
    grad_in_mlp, grad_gain_mlp, grad_shift_mlp = norm_back_mlp(grad_normed_mlp)
    grad_inputs = (grad_out.astype(f32) + grad_in_attn + grad_in_mlp).reshape(
        groups, local_len, width
    )
    sums = (
        lax.psum_scatter(grad_gain_attn, ("fsdp", "ctx"), scatter_dimension=0, tiled=True),
        lax.psum_scatter(grad_shift_attn, ("fsdp", "ctx"), scatter_dimension=0, tiled=True),
        lax.psum_scatter(grad_weight_qkv, ("fsdp", "ctx"), scatter_dimension=0, tiled=True),
        lax.psum_scatter(grad_bias_qkv, ("fsdp", "ctx"), scatter_dimension=0, tiled=True),
        lax.psum_scatter(grad_weight_attn, ("fsdp", "ctx"), scatter_dimension=0, tiled=True),
        lax.psum_scatter(grad_bias_out, ("fsdp", "ctx"), scatter_dimension=0, tiled=True),
        lax.psum_scatter(grad_gain_mlp, ("fsdp", "ctx"), scatter_dimension=0, tiled=True),
        lax.psum_scatter(grad_shift_mlp, ("fsdp", "ctx"), scatter_dimension=0, tiled=True),
        lax.psum_scatter(grad_weight_in, ("fsdp", "ctx"), scatter_dimension=0, tiled=True),
        lax.psum_scatter(grad_bias_in, ("fsdp", "ctx"), scatter_dimension=0, tiled=True),
        lax.psum_scatter(grad_weight_out, ("fsdp", "ctx"), scatter_dimension=0, tiled=True),
    )
    result = output.reshape(groups, local_len, width).astype(bf16)
    return (
        result,
        grad_inputs,
        sums[0],
        sums[1],
        sums[2],
        sums[3],
        sums[4],
        sums[5],
        sums[6],
        sums[7],
        sums[8],
        sums[9],
        sums[10],
    )


def solution(mesh):
    in_specs = (
        P("fsdp", "ctx", None),
        P("fsdp", "ctx", None),
        P("fsdp", "ctx"),
        P("fsdp", "ctx"),
        P("fsdp"),
        P("fsdp"),
        P("fsdp", None),
        P("fsdp"),
        P("fsdp", None),
        P("fsdp"),
        P("fsdp"),
        P("fsdp"),
        P("fsdp", None),
        P("fsdp"),
        P("fsdp", None),
    )
    out_specs = (
        P("fsdp", "ctx", None),
        P("fsdp", "ctx", None),
        P(("fsdp", "ctx")),
        P(("fsdp", "ctx")),
        P(("fsdp", "ctx"), None),
        P(("fsdp", "ctx")),
        P(("fsdp", "ctx"), None),
        P(("fsdp", "ctx")),
        P(("fsdp", "ctx")),
        P(("fsdp", "ctx")),
        P(("fsdp", "ctx"), None),
        P(("fsdp", "ctx")),
        P(("fsdp", "ctx"), None),
    )
    return jax.shard_map(local, mesh=mesh, in_specs=in_specs, out_specs=out_specs, check_vma=False)
```

```python
from functools import partial
import math

import jax
import jax.numpy as jnp
from jax import lax
from jax.experimental import pallas as pl
from jax.experimental.pallas import tpu as pltpu
from jax.sharding import PartitionSpec as P

HEADS = 16
HD = 64
ROT = 16
CLEN = 256
QB = 256
RB = 256
PAIR = 2 * HD
bf16 = jnp.bfloat16
f32 = jnp.float32
NN = (((1,), (0,)), ((), ()))
NT = (((1,), (1,)), ((), ()))
TN = (((0,), (0,)), ((), ()))


NORM_EPS = 1e-05
MASKED = -1e30


def layer_norm(values, scaling, offset):
    average = jnp.mean(values, axis=-1, keepdims=True)
    centered = values - average
    variance = jnp.mean(centered * centered, axis=-1, keepdims=True)
    return centered * lax.rsqrt(variance + NORM_EPS) * scaling + offset


def rotary_tables(positions):
    halfway = ROT // 2
    spacing = jnp.arange(halfway, dtype=jnp.float32) * (2.0 / ROT)
    inverse = jnp.exp(-math.log(10000.0) * spacing)
    angles = positions.astype(jnp.float32)[..., None] * inverse
    return (jnp.cos(angles), jnp.sin(angles))


def rotate(heads_in, cosine, sine):
    halfway = ROT // 2
    cosine = cosine[..., None, :]
    sine = sine[..., None, :]
    first = heads_in[..., :halfway]
    second = heads_in[..., halfway:ROT]
    return jnp.concatenate(
        [first * cosine - second * sine, second * cosine + first * sine, heads_in[..., ROT:]],
        axis=-1,
    )


def unrotate(grads_in, cosine, sine):
    halfway = ROT // 2
    cosine = cosine[..., None, :]
    sine = sine[..., None, :]
    first = grads_in[..., :halfway]
    second = grads_in[..., halfway:ROT]
    return jnp.concatenate(
        [first * cosine + second * sine, second * cosine - first * sine, grads_in[..., ROT:]],
        axis=-1,
    )


def allowed_mask(query_pos, query_seg, key_pos, key_seg):
    same_doc = (key_seg[:, None, :] == 0) | (key_seg[:, None, :] == query_seg[:, :, None])
    causal = key_pos[:, None, :] <= query_pos[:, :, None]
    return (same_doc & causal)[:, None]


def scores_of(queries, keys_blk):
    return jnp.einsum("gqhd,gkhd->ghqk", queries, keys_blk, preferred_element_type=jnp.float32)


def block_grads(queries, grad_att, log_total, delta, mask, keys_blk, values_blk):
    probs = jnp.where(mask, jnp.exp(scores_of(queries, keys_blk) - log_total[..., None]), 0.0)
    dprobs = jnp.einsum("gqhd,gkhd->ghqk", grad_att, values_blk, preferred_element_type=jnp.float32)
    grad_scores = (probs * (dprobs - delta[..., None])).astype(jnp.bfloat16)
    return (probs.astype(jnp.bfloat16), grad_scores)


def mm(a, b, dims):
    return lax.dot_general(a, b, dims, preferred_element_type=f32)


def row_stats(x):
    average = jnp.mean(x, axis=1, keepdims=True)
    centered = x - average
    return centered, lax.rsqrt(jnp.mean(centered * centered, axis=1, keepdims=True) + NORM_EPS)


def norm_rows(x, scaling, offset):
    centered, inverse = row_stats(x)
    return (centered * inverse * scaling + offset).astype(bf16)


def norm_back(x, grad, scaling):
    centered, inverse = row_stats(x)
    unit = centered * inverse
    e = grad * scaling
    inner = e - jnp.mean(e, axis=1, keepdims=True) - unit * jnp.mean(e * unit, axis=1, keepdims=True)
    return inverse * inner, grad * unit


def col_sum(a):
    return jnp.sum(a, axis=0, keepdims=True)


def vmem(*shape, dtype=f32):
    return pltpu.VMEM(shape, dtype)


def params():
    return pltpu.CompilerParams(vmem_limit_bytes=60 << 20)


FC = 512
ROOT = math.sqrt(0.5)
DENS = 1.0 / math.sqrt(2.0 * math.pi)


def mlp_kernel(x_ref, c_ref, gain_ref, shift_ref, win_ref, bin_ref, wout_ref,
               out_ref, gin_ref, dwin_ref, dwout_ref, dbin_ref, dbout_ref, dgain_ref, dshift_ref,
               h_ref, act_ref, gp_ref, gh_ref):
    step = pl.program_id(0)
    rows = x_ref.shape[0]
    blocks = [slice(r, r + RB) for r in range(0, rows, RB)]

    @pl.when(step == 0)
    def _():
        for r in blocks:
            h_ref[r, :] = norm_rows(x_ref[r, :].astype(f32), gain_ref[...], shift_ref[...])
            out_ref[r, :] = jnp.zeros((RB, out_ref.shape[1]), f32)
            gh_ref[r, :] = jnp.zeros((RB, gh_ref.shape[1]), f32)

    dbin = jnp.zeros((1, FC), f32)
    for r in blocks:
        pre = mm(h_ref[r, :], win_ref[...], NN) + bin_ref[...]
        phi = 0.5 + 0.5 * lax.erf(pre * ROOT)
        act_ref[r, :] = (pre * phi).astype(bf16)
        gp = phi + pre * (DENS * jnp.exp(-0.5 * (pre * pre)))
        gact = mm(c_ref[r, :], wout_ref[...], NT)
        gpre = (gact * gp).astype(bf16)
        gp_ref[r, :] = gpre
        dbin = dbin + col_sum(gpre.astype(f32))
    for r in blocks:
        out_ref[r, :] += mm(act_ref[r, :], wout_ref[...], NN)
        gh_ref[r, :] += mm(gp_ref[r, :], win_ref[...], NT)
    dwout_ref[...] = mm(act_ref[...], c_ref[...], TN).astype(bf16)
    dwin_ref[...] = mm(h_ref[...], gp_ref[...], TN).astype(bf16)
    dbin_ref[...] = dbin

    @pl.when(step == pl.num_programs(0) - 1)
    def _():
        dgain = jnp.zeros(dgain_ref.shape, f32)
        dshift = jnp.zeros(dshift_ref.shape, f32)
        dbout = jnp.zeros(dbout_ref.shape, f32)
        for r in blocks:
            grad = gh_ref[r, :]
            back, scaled = norm_back(x_ref[r, :].astype(f32), grad, gain_ref[...])
            c = c_ref[r, :].astype(f32)
            gin_ref[r, :] = back + c
            dgain += col_sum(scaled)
            dshift += col_sum(grad)
            dbout += col_sum(c)
        dgain_ref[...] = dgain
        dshift_ref[...] = dshift
        dbout_ref[...] = dbout


def mlp(x, c, gain, shift, weight_in, bias_in, weight_out):
    rows, width = x.shape
    ff = weight_in.shape[1]
    whole = pl.BlockSpec((rows, width), lambda j: (0, 0))
    line = pl.BlockSpec((1, width), lambda j: (0, 0))
    s = jax.ShapeDtypeStruct
    return pl.pallas_call(
        mlp_kernel,
        grid=(ff // FC,),
        in_specs=[whole, whole, line, line, pl.BlockSpec((width, FC), lambda j: (0, j)),
                  pl.BlockSpec((1, FC), lambda j: (0, j)), pl.BlockSpec((FC, width), lambda j: (j, 0))],
        out_specs=[whole, whole, pl.BlockSpec((width, FC), lambda j: (0, j)), pl.BlockSpec((FC, width), lambda j: (j, 0)),
                   pl.BlockSpec((1, FC), lambda j: (0, j)), line, line, line],
        out_shape=[s((rows, width), f32), s((rows, width), f32), s((width, ff), bf16), s((ff, width), bf16),
                   s((1, ff), f32), s((1, width), f32), s((1, width), f32), s((1, width), f32)],
        scratch_shapes=[vmem(rows, width, dtype=bf16), vmem(rows, FC, dtype=bf16), vmem(rows, FC, dtype=bf16),
                        vmem(rows, width)],
        compiler_params=params(),
        cost_estimate=pl.CostEstimate(flops=12 * rows * width * ff, bytes_accessed=48 << 20, transcendentals=2 * rows * ff),
        name="mlp",
    )(x, c, gain.reshape(1, -1), shift.reshape(1, -1), weight_in, bias_in.reshape(1, -1), weight_out)


def turn_lanes(u, cosine, low, high, sign):
    half = ROT // 2
    parts = []
    for at in range(0, u.shape[1], PAIR):
        g = u[:, at:at + PAIR]
        parts.append(g * cosine + sign * (pltpu.roll(g, half, 1) * high - pltpu.roll(g, PAIR - half, 1) * low))
    return jnp.concatenate(parts, axis=1)


def qkv_kernel(with_q, spot_ref, x_ref, gain_ref, shift_ref, w_ref, b_ref, cos_ref, low_ref, high_ref, *outs):
    width = x_ref.shape[1]
    h = norm_rows(x_ref[...].astype(f32), gain_ref[...], shift_ref[...])
    tables = (cos_ref[...], low_ref[...], high_ref[...])
    if with_q:
        h_ref, q_ref, k_ref, v_ref = outs
        h_ref[...] = h
        q = mm(h, w_ref[:, :width], NN) + b_ref[:, :width]
        q_ref[...] = (turn_lanes(q, *tables, 1.0) * (HD ** (-0.5) / math.log(2.0))).astype(bf16)
    else:
        k_ref, v_ref = outs
    k = mm(h, w_ref[:, width:2 * width], NN) + b_ref[:, width:2 * width]
    k_ref[...] = turn_lanes(k, *tables, 1.0).astype(bf16)
    v_ref[...] = (mm(h, w_ref[:, 2 * width:], NN) + b_ref[:, 2 * width:]).astype(bf16)


def qkv(spots, x, gain, shift, weight, bias, tables, with_q):
    rows, width = x.shape
    s = jax.ShapeDtypeStruct((rows, width), bf16)
    block = pl.BlockSpec((RB, width), lambda j, spot: (j, 0))
    line = pl.BlockSpec((1, width), lambda j, spot: (0, 0))
    table = pl.BlockSpec((RB, PAIR), lambda j, spot: (spot[j], 0))
    count = 4 if with_q else 2
    return pl.pallas_call(
        partial(qkv_kernel, with_q),
        grid_spec=pltpu.PrefetchScalarGridSpec(
            num_scalar_prefetch=1,
            grid=(rows // RB,),
            in_specs=[block, line, line, pl.BlockSpec((width, 3 * width), lambda j, spot: (0, 0)),
                      pl.BlockSpec((1, 3 * width), lambda j, spot: (0, 0)), table, table, table],
            out_specs=[block] * count,
        ),
        out_shape=[s] * count,
        compiler_params=params(),
        cost_estimate=pl.CostEstimate(flops=2 * rows * width * width * (3 if with_q else 2), bytes_accessed=16 << 20,
                                      transcendentals=0),
        name="qkv_own" if with_q else "kv_remote",
    )(spots, x, gain.reshape(1, -1), shift.reshape(1, -1), weight, bias.reshape(1, -1), *tables)


def tail_kernel(groups, spot_ref, x_ref, h_ref, gain_ref, w_ref, cos_ref, low_ref, high_ref, gin_ref, *refs):
    dq_refs, own_refs, come_refs = refs[:groups], refs[groups:2 * groups], refs[2 * groups:3 * groups]
    grad_ref, dw_ref, db_ref, dgain_ref, dshift_ref, p_ref, gh_ref = refs[3 * groups:]
    step = pl.program_id(0)
    rows = x_ref.shape[0]
    half = rows // 2
    blocks = [slice(r, r + RB) for r in range(0, rows, RB)]
    part = dq_refs[0].shape[1]

    def put(shift):
        for r in blocks:
            spot = pl.ds(pl.multiple_of(spot_ref[r.start // RB] * RB, RB), RB)
            for g in range(groups):
                for at in range(0, part, PAIR):
                    if shift is None:
                        p_ref[r, g * part + at:g * part + at + PAIR] = dq_refs[g][r, at:at + PAIR]
                        continue
                    lanes = slice(2 * at + shift, 2 * at + shift + PAIR)
                    t = own_refs[g][r, lanes].astype(f32)
                    if r.start < half:
                        t = t + come_refs[g][r, lanes].astype(f32)
                    if shift == 0:
                        t = turn_lanes(t, cos_ref[spot, :], low_ref[spot, :], high_ref[spot, :], -1.0)
                    p_ref[r, g * part + at:g * part + at + PAIR] = t.astype(bf16)

    @pl.when(step == 0)
    def _():
        put(None)
        for r in blocks:
            gh_ref[r, :] = mm(p_ref[r, :], w_ref[...], NT)

    @pl.when(step == 1)
    def _():
        put(0)

    @pl.when(step == 2)
    def _():
        put(PAIR)

    @pl.when(step > 0)
    def _():
        for r in blocks:
            gh_ref[r, :] += mm(p_ref[r, :], w_ref[...], NT)

    dw_ref[...] = mm(h_ref[...], p_ref[...], TN).astype(bf16)
    db = jnp.zeros(db_ref.shape, f32)
    for r in blocks:
        db += col_sum(p_ref[r, :].astype(f32))
    db_ref[...] = db

    @pl.when(step == 2)
    def _():
        dgain = jnp.zeros(dgain_ref.shape, f32)
        dshift = jnp.zeros(dshift_ref.shape, f32)
        for r in blocks:
            grad = gh_ref[r, :]
            back, scaled = norm_back(x_ref[r, :].astype(f32), grad, gain_ref[...])
            grad_ref[r, :] = back + gin_ref[r, :]
            dgain += col_sum(scaled)
            dshift += col_sum(grad)
        dgain_ref[...] = dgain
        dshift_ref[...] = dshift


def tail(spots, x, h, gain, weight, tables, gin, dqs, owns, comes):
    rows, width = x.shape
    groups = len(dqs)
    s = jax.ShapeDtypeStruct

    def full(a):
        return pl.BlockSpec(a.shape, lambda j, spot: (0, 0))

    line = pl.BlockSpec((1, width), lambda j, spot: (0, 0))
    arrays = [*tables, gin, *dqs, *owns, *comes]
    return pl.pallas_call(
        partial(tail_kernel, groups),
        grid_spec=pltpu.PrefetchScalarGridSpec(
            num_scalar_prefetch=1,
            grid=(3,),
            in_specs=[full(x), full(h), line, pl.BlockSpec((width, width), lambda j, spot: (0, j))] + [full(a) for a in arrays],
            out_specs=[full(x), pl.BlockSpec((width, width), lambda j, spot: (0, j)),
                       pl.BlockSpec((1, width), lambda j, spot: (0, j)), line, line],
            scratch_shapes=[vmem(rows, width, dtype=bf16), vmem(rows, width)],
        ),
        out_shape=[s((rows, width), f32), s((width, 3 * width), bf16), s((1, 3 * width), f32), s((1, width), f32),
                   s((1, width), f32)],
        compiler_params=params(),
        cost_estimate=pl.CostEstimate(flops=12 * rows * width * width, bytes_accessed=32 << 20, transcendentals=0),
        name="tail",
    )(spots, x, h, gain.reshape(1, -1), weight, *arrays)


def join_kernel(x_ref, c_ref, att_ref, w_ref, mlp_ref, b_ref, out_ref, dw_ref, acc_ref):
    step = pl.program_id(0)
    out = x_ref[...].astype(f32) + mm(att_ref[...], w_ref[...], NN) + mlp_ref[...] + b_ref[...]
    out_ref[...] = out.astype(bf16)

    @pl.when(step == 0)
    def _():
        acc_ref[...] = mm(att_ref[...], c_ref[...], TN)

    @pl.when(step > 0)
    def _():
        acc_ref[...] += mm(att_ref[...], c_ref[...], TN)

    @pl.when(step == pl.num_programs(0) - 1)
    def _():
        dw_ref[...] = acc_ref[...].astype(bf16)


def join(x, c, attended, weight, mlp_out, bias):
    rows, width = x.shape
    s = jax.ShapeDtypeStruct
    block = pl.BlockSpec((RB, width), lambda j: (j, 0))
    square = pl.BlockSpec((width, width), lambda j: (0, 0))
    return pl.pallas_call(
        join_kernel,
        grid=(rows // RB,),
        in_specs=[block, block, block, square, block, pl.BlockSpec((1, width), lambda j: (0, 0))],
        out_specs=[block, square],
        out_shape=[s((rows, width), bf16), s((width, width), bf16)],
        scratch_shapes=[vmem(width, width)],
        compiler_params=params(),
        cost_estimate=pl.CostEstimate(flops=4 * rows * width * width, bytes_accessed=16 << 20, transcendentals=0),
        name="join",
    )(x, c, attended, weight, mlp_out, bias.reshape(1, -1))


def fold(x, op):
    return op(x.reshape(x.shape[0] // 8, 8, x.shape[1]), axis=0)


def eye(size):
    return (lax.broadcasted_iota(jnp.int32, (size, size), 0) == lax.broadcasted_iota(jnp.int32, (size, size), 1)).astype(bf16)


def attention_kernel(half, n, kind_ref, cos_ref, sin_ref, q_ref, do_ref, *refs):
    k_refs, v_refs = refs[:n], refs[n:2 * n]
    o_ref, dq_ref = refs[2 * n:2 * n + 2]
    g_refs = refs[2 * n + 2:3 * n + 2]
    kt_ref, vt_ref, s_ref, p_ref, ds_ref, dka_ref, dva_ref = refs[3 * n + 2:]
    per = half // QB
    wide = n * half
    count = wide // QB
    spots = [(0, c * QB) for c in range(per)] + [(s, c * QB) for s in range(1, n) for c in range(per)]

    ident = eye(PAIR)
    for refs_in, out in ((k_refs, kt_ref), (v_refs, vt_ref)):
        for c, (s, at) in enumerate(spots):
            out[:, c * QB:(c + 1) * QB] = refs_in[s][at:at + QB, :].T
        for c in range(per):
            out[:, wide + c * QB:wide + (c + 1) * QB] = refs_in[0][half + c * QB:half + (c + 1) * QB, :].T
    dka_ref[...] = jnp.zeros_like(dka_ref)
    dva_ref[...] = jnp.zeros_like(dva_ref)


    def block(qb, carry):
        own = pl.ds(pl.multiple_of(qb * QB, QB), QB)
        slot = pl.ds(pl.multiple_of(jnp.where(qb < per, qb * QB, wide + (qb - per) * QB), QB), QB)
        zero = jnp.zeros((), bf16)
        causal = lax.broadcasted_iota(jnp.int32, (QB, QB), 0) <= lax.broadcasted_iota(jnp.int32, (QB, QB), 1)
        left = lax.broadcasted_iota(jnp.int32, (QB, PAIR), 1) < HD

        def by_head(a):
            return jnp.where(left, a, zero), jnp.where(left, zero, a)

        def keys_of(some, c):
            if c == count:
                return some[0][own, :]
            s, at = spots[c]
            return some[s][at:at + QB, :]

        def cut(c):
            return slice(c * QB, (c + 1) * QB)

        ident = eye(QB)
        q_heads = by_head(q_ref[own, :])
        do_t = mm(eye(PAIR), do_ref[own, :], NT)
        upper = lax.broadcasted_iota(jnp.int32, (PAIR, QB), 0) < HD
        q_t = mm(eye(PAIR), q_ref[own, :], NT).astype(bf16)
        q_cols = jnp.where(upper, q_t, zero), jnp.where(upper, zero, q_t)
        peaks, norms, outs, deltas, scaled = [None, None], [None, None], [None, None], [None, None], [None, None]

        def scores(h):
            peak = jnp.full((8, QB), MASKED, f32)
            for c in range(count + 1):
                s = mm(keys_of(k_refs, c), q_cols[h], NN)
                if c == count:
                    s = jnp.where(causal, s, MASKED)
                    top = fold(s, jnp.max)
                else:
                    top = fold(s, jnp.max) + kind_ref[qb, c]
                s_ref[h, cut(c)] = s
                peak = jnp.maximum(peak, top)
            peaks[h] = jnp.max(peak, axis=0, keepdims=True)

        def weigh(h):
            total = jnp.zeros((8, QB), f32)
            for c in range(count + 1):
                bias = -peaks[h] if c == count else kind_ref[qb, c] - peaks[h]
                e = jnp.exp2(s_ref[h, cut(c)] + bias)
                total = total + fold(e, jnp.sum)
                p_ref[h, cut(c)] = e.astype(bf16)
            norms[h] = 1.0 / jnp.sum(total, axis=0, keepdims=True)

        def attend(h):
            lines = slice(h * HD, (h + 1) * HD)
            out = mm(vt_ref[lines, 0:wide], p_ref[h, 0:wide], NN) + mm(vt_ref[lines, slot], p_ref[h, wide:], NN)
            outs[h] = out * norms[h]
            deltas[h] = jnp.sum(outs[h] * do_t[lines], axis=0, keepdims=True) * norms[h]
            scaled[h] = do_t[lines] * norms[h]

        scores(0)
        scores(1)
        weigh(0)
        attend(0)
        weigh(1)
        attend(1)
        d_t = jnp.concatenate(scaled, axis=0).astype(bf16)
        d_cols = jnp.where(upper, d_t, zero), jnp.where(upper, zero, d_t)
        do_heads = by_head(mm(ident, d_t, NT).astype(bf16))
        grads = []
        for h in range(2):
            lines = slice(h * HD, (h + 1) * HD)
            for c in range(count + 1):
                dp = mm(keys_of(v_refs, c), d_cols[h], NN)
                ds_ref[h, cut(c)] = (p_ref[h, cut(c)].astype(f32) * (dp - deltas[h])).astype(bf16)
            dq = mm(kt_ref[lines, 0:wide], ds_ref[h, 0:wide], NN) + mm(kt_ref[lines, slot], ds_ref[h, wide:], NN)
            a, b = dq[:ROT // 2], dq[ROT // 2:ROT]
            cosine, sine = cos_ref[:, own], sin_ref[:, own]
            grads.append(jnp.concatenate([a * cosine + b * sine, b * cosine - a * sine, dq[ROT:]], axis=0))
        for c in range(count + 1):
            at = slot if c == count else cut(c)
            dva_ref[at, :] += mm(p_ref[0, cut(c)], do_heads[0], NN) + mm(p_ref[1, cut(c)], do_heads[1], NN)
            dka_ref[at, :] += mm(ds_ref[0, cut(c)], q_heads[0], NN) + mm(ds_ref[1, cut(c)], q_heads[1], NN)
        o_ref[own, :] = mm(ident, jnp.concatenate(outs, axis=0).astype(bf16), NT).astype(bf16)
        dq_ref[own, :] = mm(ident, (jnp.concatenate(grads, axis=0) * (HD ** (-0.5))).astype(bf16), NT).astype(bf16)

        return carry

    lax.fori_loop(0, 2 * per, block, 0)

    def flush(out, to, frm, size):
        out[to:to + size, :PAIR] = (dka_ref[frm:frm + size, :] * math.log(2.0)).astype(bf16)
        out[to:to + size, PAIR:] = dva_ref[frm:frm + size, :].astype(bf16)

    flush(g_refs[0], 0, 0, half)
    flush(g_refs[0], half, wide, half)
    for s in range(1, n):
        flush(g_refs[s], 0, s * half, half)


def attention(kind, cos_t, sin_t, q, do, ks, vs, first, pairs):
    rows = q.shape[0]
    half = rows // 2
    n = len(ks)
    wide = n * half
    keys = wide + half
    total = wide + QB
    qspec = pl.BlockSpec((rows, PAIR), lambda p: (0, p + first))
    ospec = pl.BlockSpec((rows, PAIR), lambda p: (0, p))
    table = pl.BlockSpec((ROT // 2, rows), lambda p: (0, 0))
    kspecs = [pl.BlockSpec((k.shape[0], PAIR), lambda p: (0, p + first)) for k in ks]
    gspecs = [pl.BlockSpec((k.shape[0], 2 * PAIR), lambda p: (0, p)) for k in ks]
    s = jax.ShapeDtypeStruct
    pieces = pairs * rows // QB
    return pl.pallas_call(
        partial(attention_kernel, half, n),
        grid=(pairs,),
        in_specs=[pl.BlockSpec(memory_space=pltpu.SMEM), table, table, qspec, qspec] + kspecs + kspecs,
        out_specs=[ospec, ospec] + gspecs,
        out_shape=[s((rows, pairs * PAIR), bf16), s((rows, pairs * PAIR), bf16)]
        + [s((k.shape[0], 2 * pairs * PAIR), bf16) for k in ks],
        scratch_shapes=[pltpu.VMEM((PAIR, keys), bf16), pltpu.VMEM((PAIR, keys), bf16),
                        pltpu.VMEM((2, total, QB), f32), pltpu.VMEM((2, total, QB), bf16),
                        pltpu.VMEM((2, total, QB), bf16),
                        pltpu.VMEM((keys, PAIR), f32), pltpu.VMEM((keys, PAIR), f32)],
        compiler_params=pltpu.CompilerParams(vmem_limit_bytes=60 << 20),
        cost_estimate=pl.CostEstimate(flops=pieces * 24 * total * QB * HD * 4, bytes_accessed=16 << 20,
                                      transcendentals=pieces * 2 * total * QB),
        name="attention",
    )(kind, cos_t, sin_t, q, do, *ks, *vs)


def pairs_of(bit, size):
    return [(a, a ^ bit) for a in range(size)]


def pick(a, axis, i):
    return lax.dynamic_index_in_dim(a, i, axis, keepdims=False)


def plus(a, b):
    return (a.astype(f32) + b.astype(f32)).astype(bf16)


def scatter_sum(terms):
    me = lax.axis_index("fsdp")
    y, x, core = me // 4, (me // 2) % 2, me % 2
    rows, cols = terms.shape
    t = terms.reshape(2, 2, 2, rows // 8, cols)
    t = plus(pick(t, 2, core), lax.ppermute(pick(t, 2, 1 - core), "fsdp", pairs_of(1, 8)))
    a, b = t[..., :cols // 2], t[..., cols // 2:]
    a = plus(pick(a, 1, x), lax.ppermute(pick(a, 1, 1 - x), "fsdp", pairs_of(2, 8)))
    b = plus(pick(b, 0, y), lax.ppermute(pick(b, 0, 1 - y), "fsdp", pairs_of(4, 8)))
    a = plus(pick(a, 0, y), lax.ppermute(pick(a, 0, 1 - y), "fsdp", pairs_of(4, 8)))
    b = plus(pick(b, 0, x), lax.ppermute(pick(b, 0, 1 - x), "fsdp", pairs_of(2, 8)))
    part = jnp.concatenate([a, b], axis=-1)
    return lax.psum_scatter(part, "ctx", scatter_dimension=0, tiled=True)


def after(value, *others):
    return lax.optimization_barrier((value, *others))[0]


def fast(inputs, cotangent, positions, segments, ln1_gain, ln1_bias, w_qkv, b_qkv, w_attn_out, b_out,
         ln2_gain, ln2_bias, w_in, b_in, w_out):
    x, grad_out, pos = inputs[0], cotangent[0], positions[0]
    rows, width = x.shape
    half = rows // 2
    n = lax.axis_size("ctx")
    ring = [(i, (i + 1) % n) for i in range(n)]
    back = [(i, (i - 1) % n) for i in range(n)]
    xs, spots = [x], [pos[::RB] // RB]
    run = x[:half]
    for s in range(1, n):
        run = lax.ppermute(run, "ctx", ring)
        xs.append(run)
        spots.append(lax.ppermute(spots[0][:half // RB], "ctx", [(i, (i + s) % n) for i in range(n)]))
    mine = (ln1_gain, ln1_bias, b_qkv, b_out, ln2_gain, ln2_bias, b_in)
    small = lax.all_gather(jnp.concatenate(mine).reshape(1, -1), "fsdp", axis=0, tiled=True)
    full, at = [], 0
    for a in mine:
        full.append(small[:, at:at + a.shape[0]].reshape(-1).astype(f32))
        at += a.shape[0]
    gain_attn, shift_attn, bias_qkv, bias_out, gain_mlp, shift_mlp, bias_in = full
    weight_qkv = lax.all_gather(w_qkv, "fsdp", axis=0, tiled=True)
    weight_attn = lax.all_gather(w_attn_out, "fsdp", axis=0, tiled=True)
    weight_in = lax.all_gather(w_in, "fsdp", axis=0, tiled=True)
    weight_out = lax.all_gather(w_out, "fsdp", axis=0, tiled=True)

    lane = jnp.arange(PAIR) % HD
    inverse = jnp.exp(-math.log(10000.0) * (2.0 / ROT) * (lane % (ROT // 2)).astype(f32))
    angles = jnp.arange(n * half + CLEN).astype(f32)[:, None] * inverse[None, :]
    sine = jnp.sin(angles)
    tables = (jnp.where(lane < ROT, jnp.cos(angles), 1.0), jnp.where(lane < ROT // 2, sine, 0.0),
              jnp.where((lane >= ROT // 2) & (lane < ROT), sine, 0.0))
    angles_t = pos.astype(f32)[None, :] * inverse[:ROT // 2, None]
    cos_t, sin_t = jnp.cos(angles_t), jnp.sin(angles_t)

    normed, queries, key, value = qkv(spots[0], x, gain_attn, shift_attn, weight_qkv, bias_qkv, tables, True)
    keys, values = [key], [value]
    for s in range(1, n):
        key, value = qkv(spots[s], xs[s], gain_attn, shift_attn, weight_qkv, bias_qkv, tables, False)
        keys.append(key)
        values.append(value)
    grad_att = mm(grad_out, weight_attn, NT).astype(bf16)

    per = half // QB
    earlier = jnp.stack([spots[s][0] < spots[0][0] for s in range(1, n)])
    local_row = jnp.arange(2 * per)[:, None]
    seen_own = local_row > jnp.arange(per)[None, :]
    seen_far = jnp.repeat(earlier[None, :] | (local_row >= per), per, axis=1)
    kind = jnp.where(jnp.concatenate([seen_own, seen_far], axis=1), 0.0, MASKED).astype(f32)

    groups = 2
    count = HEADS // 2 // groups
    attended, grad_q, own_kv, come_kv = [], [], [], []
    for g in range(groups):
        out = attention(kind, cos_t, sin_t, queries, grad_att, keys, values, g * count, count)
        attended.append(out[0])
        grad_q.append(out[1])
        own_kv.append(out[2])
        run = out[2 + n - 1]
        for s in range(n - 2, 0, -1):
            run = plus(lax.ppermute(run, "ctx", back), out[2 + s])
        come_kv.append(lax.ppermute(run, "ctx", back))
    attended = jnp.concatenate(attended, axis=1)

    x_late, attended = lax.optimization_barrier((x, attended))
    mlp_out, grad_mlp, dw_in, dw_out, db_in, db_out, dgain_mlp, dshift_mlp = mlp(
        x_late, grad_out, gain_mlp, shift_mlp, weight_in, bias_in, weight_out)
    output, dw_attn = join(x, grad_out, attended, weight_attn, mlp_out, bias_out)
    sum_out = scatter_sum(dw_out)
    sum_in = scatter_sum(dw_in)
    sum_attn = scatter_sum(dw_attn)
    grad_inputs, dw_qkv, db_qkv, dgain_attn, dshift_attn = tail(
        spots[0], x, normed, gain_attn, weight_qkv, tables, grad_mlp, grad_q, own_kv, come_kv)
    sum_qkv = scatter_sum(dw_qkv)
    smalls = [a.reshape(width, -1) for a in (dgain_attn, dshift_attn, db_qkv, db_out, dgain_mlp, dshift_mlp, db_in)]
    used = sum(a.shape[1] for a in smalls)
    packed = jnp.concatenate(smalls + [jnp.zeros((width, PAIR - used), f32)], axis=1).astype(bf16)
    packed = scatter_sum(packed).astype(f32)
    done, at = [], 0
    for a in smalls:
        done.append(packed[:, at:at + a.shape[1]].reshape(-1))
        at += a.shape[1]
    return (output[None], grad_inputs[None], done[0], done[1], sum_qkv.astype(f32), done[2], sum_attn.astype(f32),
            done[3], done[4], done[5], sum_in.astype(f32), done[6], sum_out.astype(f32))


def local(*args):
    half = args[0].shape[1] // 2
    if args[0].shape[0] == 1 and half % CLEN == 0 and lax.axis_size("fsdp") == 8:
        return fast(*args)
    return generic(*args)


def generic(
    inputs,
    cotangent,
    positions,
    segments,
    ln1_gain,
    ln1_bias,
    w_qkv,
    b_qkv,
    w_attn_out,
    b_out,
    ln2_gain,
    ln2_bias,
    w_in,
    b_in,
    w_out,
):
    shards = (
        ln1_gain,
        ln1_bias,
        w_qkv,
        b_qkv,
        w_attn_out,
        b_out,
        ln2_gain,
        ln2_bias,
        w_in,
        b_in,
        w_out,
    )
    params = (
        lax.all_gather(shards[0], "fsdp", axis=0, tiled=True),
        lax.all_gather(shards[1], "fsdp", axis=0, tiled=True),
        lax.all_gather(shards[2], "fsdp", axis=0, tiled=True),
        lax.all_gather(shards[3], "fsdp", axis=0, tiled=True),
        lax.all_gather(shards[4], "fsdp", axis=0, tiled=True),
        lax.all_gather(shards[5], "fsdp", axis=0, tiled=True),
        lax.all_gather(shards[6], "fsdp", axis=0, tiled=True),
        lax.all_gather(shards[7], "fsdp", axis=0, tiled=True),
        lax.all_gather(shards[8], "fsdp", axis=0, tiled=True),
        lax.all_gather(shards[9], "fsdp", axis=0, tiled=True),
        lax.all_gather(shards[10], "fsdp", axis=0, tiled=True),
    )
    groups, local_len, width = inputs.shape
    rows_total = groups * local_len
    block = math.gcd(local_len, 256)
    label_pos, label_seg = (
        lax.all_gather(positions, "ctx", axis=1, tiled=True),
        lax.all_gather(segments, "ctx", axis=1, tiled=True),
    )
    count = label_pos.shape[1] // block
    f32 = jnp.float32
    bf16 = jnp.bfloat16
    (
        gain_attn,
        shift_attn,
        weight_qkv,
        bias_qkv,
        weight_attn,
        bias_out,
        gain_mlp,
        shift_mlp,
        weight_in,
        bias_in,
        weight_out,
    ) = params
    flat_in = inputs.reshape(rows_total, width).astype(f32)
    normed_attn = layer_norm(flat_in, gain_attn.astype(f32), shift_attn.astype(f32)).astype(bf16)
    normed_mlp = layer_norm(flat_in, gain_mlp.astype(f32), shift_mlp.astype(f32)).astype(bf16)
    projected = jnp.dot(normed_attn, weight_qkv, preferred_element_type=f32) + bias_qkv.astype(f32)
    cosine, sine = rotary_tables(positions)

    def split_heads(columns):
        return columns.reshape(groups, local_len, HEADS, HD)

    scale = HD ** (-0.5)
    queries = (rotate(split_heads(projected[:, :width]), cosine, sine) * scale).astype(bf16)
    keys_own = rotate(split_heads(projected[:, width : 2 * width]), cosine, sine).astype(bf16)
    values_own = split_heads(projected[:, 2 * width :]).astype(bf16)
    keys_all, values_all = (
        lax.all_gather(keys_own, "ctx", axis=1, tiled=True),
        lax.all_gather(values_own, "ctx", axis=1, tiled=True),
    )

    def key_block(index):
        start = index * block
        keys_blk = lax.dynamic_slice_in_dim(keys_all, start, block, 1)
        values_blk = lax.dynamic_slice_in_dim(values_all, start, block, 1)
        mask = allowed_mask(
            positions,
            segments,
            lax.dynamic_slice_in_dim(label_pos, start, block, 1),
            lax.dynamic_slice_in_dim(label_seg, start, block, 1),
        )
        return (keys_blk, values_blk, mask)

    def total_step(carry, index):
        peak, total = carry
        keys_blk, values_blk, mask = key_block(index)
        scores = jnp.where(mask, scores_of(queries, keys_blk), MASKED)
        fresh = jnp.maximum(peak, jnp.max(scores, axis=-1))
        added = jnp.sum(jnp.where(mask, jnp.exp(scores - fresh[..., None]), 0.0), axis=-1)
        return ((fresh, total * jnp.exp(peak - fresh) + added), None)

    stat_shape = (groups, HEADS, local_len)
    (peak, total), unused = lax.scan(
        total_step,
        (jnp.full(stat_shape, MASKED, f32), jnp.zeros(stat_shape, f32)),
        jnp.arange(count),
    )
    log_total = peak + jnp.log(total)

    def attend_step(rounded_sum, index):
        keys_blk, values_blk, mask = key_block(index)
        probs = jnp.where(mask, jnp.exp(scores_of(queries, keys_blk) - log_total[..., None]), 0.0)
        rounded_sum = rounded_sum + jnp.einsum(
            "ghqk,gkhd->gqhd", probs.astype(bf16), values_blk, preferred_element_type=f32
        )
        return (rounded_sum, None)

    head_shape = (groups, local_len, HEADS, HD)
    rounded_sum, unused = lax.scan(attend_step, jnp.zeros(head_shape, f32), jnp.arange(count))
    attended = rounded_sum.reshape(rows_total, width).astype(bf16)
    pre_act = jnp.dot(normed_mlp, weight_in, preferred_element_type=f32) + bias_in.astype(f32)
    activated = jax.nn.gelu(pre_act, approximate=False).astype(bf16)
    output = (
        flat_in
        + jnp.dot(attended, weight_attn, preferred_element_type=f32)
        + jnp.dot(activated, weight_out, preferred_element_type=f32)
        + bias_out.astype(f32)
    )
    (
        gain_attn,
        shift_attn,
        weight_qkv,
        bias_qkv,
        weight_attn,
        bias_out,
        gain_mlp,
        shift_mlp,
        weight_in,
        bias_in,
        weight_out,
    ) = params
    grad_out = cotangent.reshape(rows_total, width)
    grad_bias_out = jnp.sum(grad_out.astype(f32), axis=0)
    grad_weight_out = jnp.einsum("rf,rd->fd", activated, grad_out, preferred_element_type=f32)
    grad_act = jnp.einsum("rd,fd->rf", grad_out, weight_out, preferred_element_type=f32)
    unused, gelu_back = jax.vjp(partial(jax.nn.gelu, approximate=False), pre_act)
    grad_pre = gelu_back(grad_act)[0].astype(bf16)
    grad_weight_in = jnp.einsum("rd,rf->df", normed_mlp, grad_pre, preferred_element_type=f32)
    grad_bias_in = jnp.sum(grad_pre.astype(f32), axis=0)
    grad_normed_mlp = jnp.einsum("rf,df->rd", grad_pre, weight_in, preferred_element_type=f32)
    grad_weight_attn = jnp.einsum("ra,rd->ad", attended, grad_out, preferred_element_type=f32)
    grad_att = (
        jnp.einsum("rd,ad->ra", grad_out, weight_attn, preferred_element_type=f32)
        .astype(bf16)
        .reshape(head_shape)
    )
    delta = jnp.einsum(
        "gqhd,gqhd->ghq", grad_att.astype(f32), rounded_sum, precision=lax.Precision.HIGHEST
    )

    def back_step(carry, index):
        keys_blk, values_blk, mask = key_block(index)
        rounded, grad_scores = block_grads(
            queries, grad_att, log_total, delta, mask, keys_blk, values_blk
        )
        carry = carry + jnp.einsum(
            "ghqk,gkhd->gqhd", grad_scores, keys_blk, preferred_element_type=f32
        )
        key_term = jnp.einsum("ghqk,gqhd->gkhd", grad_scores, queries, preferred_element_type=f32)
        value_term = jnp.einsum("ghqk,gqhd->gkhd", rounded, grad_att, preferred_element_type=f32)
        return (carry, (key_term, value_term))

    grad_queries, (key_terms, value_terms) = lax.scan(
        back_step, jnp.zeros(head_shape, f32), jnp.arange(count)
    )
    key_sums, value_sums = (
        lax.psum_scatter(
            key_terms.astype(jnp.bfloat16), "ctx", scatter_dimension=0, tiled=True
        ).astype(jnp.float32),
        lax.psum_scatter(
            value_terms.astype(jnp.bfloat16), "ctx", scatter_dimension=0, tiled=True
        ).astype(jnp.float32),
    )
    grad_keys = jnp.transpose(key_sums, (1, 0, 2, 3, 4)).reshape(head_shape)
    grad_values = jnp.transpose(value_sums, (1, 0, 2, 3, 4)).reshape(head_shape)
    grad_q_pre = unrotate(grad_queries * scale, cosine, sine).reshape(rows_total, width)
    grad_k_pre = unrotate(grad_keys, cosine, sine).reshape(rows_total, width)
    grad_projected = jnp.concatenate(
        [grad_q_pre, grad_k_pre, grad_values.reshape(rows_total, width)], axis=1
    ).astype(bf16)
    grad_weight_qkv = jnp.einsum(
        "rd,re->de", normed_attn, grad_projected, preferred_element_type=f32
    )
    grad_bias_qkv = jnp.sum(grad_projected.astype(f32), axis=0)
    grad_normed_attn = jnp.einsum(
        "re,de->rd", grad_projected, weight_qkv, preferred_element_type=f32
    )
    unused, norm_back_attn = jax.vjp(
        layer_norm, flat_in, gain_attn.astype(f32), shift_attn.astype(f32)
    )
    grad_in_attn, grad_gain_attn, grad_shift_attn = norm_back_attn(grad_normed_attn)
    unused, norm_back_mlp = jax.vjp(
        layer_norm, flat_in, gain_mlp.astype(f32), shift_mlp.astype(f32)
    )
    grad_in_mlp, grad_gain_mlp, grad_shift_mlp = norm_back_mlp(grad_normed_mlp)
    grad_inputs = (grad_out.astype(f32) + grad_in_attn + grad_in_mlp).reshape(
        groups, local_len, width
    )
    sums = (
        lax.psum_scatter(grad_gain_attn, ("fsdp", "ctx"), scatter_dimension=0, tiled=True),
        lax.psum_scatter(grad_shift_attn, ("fsdp", "ctx"), scatter_dimension=0, tiled=True),
        lax.psum_scatter(grad_weight_qkv, ("fsdp", "ctx"), scatter_dimension=0, tiled=True),
        lax.psum_scatter(grad_bias_qkv, ("fsdp", "ctx"), scatter_dimension=0, tiled=True),
        lax.psum_scatter(grad_weight_attn, ("fsdp", "ctx"), scatter_dimension=0, tiled=True),
        lax.psum_scatter(grad_bias_out, ("fsdp", "ctx"), scatter_dimension=0, tiled=True),
        lax.psum_scatter(grad_gain_mlp, ("fsdp", "ctx"), scatter_dimension=0, tiled=True),
        lax.psum_scatter(grad_shift_mlp, ("fsdp", "ctx"), scatter_dimension=0, tiled=True),
        lax.psum_scatter(grad_weight_in, ("fsdp", "ctx"), scatter_dimension=0, tiled=True),
        lax.psum_scatter(grad_bias_in, ("fsdp", "ctx"), scatter_dimension=0, tiled=True),
        lax.psum_scatter(grad_weight_out, ("fsdp", "ctx"), scatter_dimension=0, tiled=True),
    )
    result = output.reshape(groups, local_len, width).astype(bf16)
    return (
        result,
        grad_inputs,
        sums[0],
        sums[1],
        sums[2],
        sums[3],
        sums[4],
        sums[5],
        sums[6],
        sums[7],
        sums[8],
        sums[9],
        sums[10],
    )


def solution(mesh):
    in_specs = (
        P("fsdp", "ctx", None),
        P("fsdp", "ctx", None),
        P("fsdp", "ctx"),
        P("fsdp", "ctx"),
        P("fsdp"),
        P("fsdp"),
        P("fsdp", None),
        P("fsdp"),
        P("fsdp", None),
        P("fsdp"),
        P("fsdp"),
        P("fsdp"),
        P("fsdp", None),
        P("fsdp"),
        P("fsdp", None),
    )
    out_specs = (
        P("fsdp", "ctx", None),
        P("fsdp", "ctx", None),
        P(("fsdp", "ctx")),
        P(("fsdp", "ctx")),
        P(("fsdp", "ctx"), None),
        P(("fsdp", "ctx")),
        P(("fsdp", "ctx"), None),
        P(("fsdp", "ctx")),
        P(("fsdp", "ctx")),
        P(("fsdp", "ctx")),
        P(("fsdp", "ctx"), None),
        P(("fsdp", "ctx")),
        P(("fsdp", "ctx"), None),
    )
    return jax.shard_map(local, mesh=mesh, in_specs=in_specs, out_specs=out_specs, check_vma=False)
```

```python
from functools import partial
import math

import jax
import jax.numpy as jnp
from jax import lax
from jax.experimental import pallas as pl
from jax.experimental.pallas import tpu as pltpu
from jax.sharding import PartitionSpec as P

HEADS = 16
HD = 64
ROT = 16
CLEN = 256
QB = 256
RB = 256
PAIR = 2 * HD
bf16 = jnp.bfloat16
f32 = jnp.float32
NN = (((1,), (0,)), ((), ()))
NT = (((1,), (1,)), ((), ()))
TN = (((0,), (0,)), ((), ()))


NORM_EPS = 1e-05
MASKED = -1e30


def layer_norm(values, scaling, offset):
    average = jnp.mean(values, axis=-1, keepdims=True)
    centered = values - average
    variance = jnp.mean(centered * centered, axis=-1, keepdims=True)
    return centered * lax.rsqrt(variance + NORM_EPS) * scaling + offset


def rotary_tables(positions):
    halfway = ROT // 2
    spacing = jnp.arange(halfway, dtype=jnp.float32) * (2.0 / ROT)
    inverse = jnp.exp(-math.log(10000.0) * spacing)
    angles = positions.astype(jnp.float32)[..., None] * inverse
    return (jnp.cos(angles), jnp.sin(angles))


def rotate(heads_in, cosine, sine):
    halfway = ROT // 2
    cosine = cosine[..., None, :]
    sine = sine[..., None, :]
    first = heads_in[..., :halfway]
    second = heads_in[..., halfway:ROT]
    return jnp.concatenate(
        [first * cosine - second * sine, second * cosine + first * sine, heads_in[..., ROT:]],
        axis=-1,
    )


def unrotate(grads_in, cosine, sine):
    halfway = ROT // 2
    cosine = cosine[..., None, :]
    sine = sine[..., None, :]
    first = grads_in[..., :halfway]
    second = grads_in[..., halfway:ROT]
    return jnp.concatenate(
        [first * cosine + second * sine, second * cosine - first * sine, grads_in[..., ROT:]],
        axis=-1,
    )


def allowed_mask(query_pos, query_seg, key_pos, key_seg):
    same_doc = (key_seg[:, None, :] == 0) | (key_seg[:, None, :] == query_seg[:, :, None])
    causal = key_pos[:, None, :] <= query_pos[:, :, None]
    return (same_doc & causal)[:, None]


def scores_of(queries, keys_blk):
    return jnp.einsum("gqhd,gkhd->ghqk", queries, keys_blk, preferred_element_type=jnp.float32)


def block_grads(queries, grad_att, log_total, delta, mask, keys_blk, values_blk):
    probs = jnp.where(mask, jnp.exp(scores_of(queries, keys_blk) - log_total[..., None]), 0.0)
    dprobs = jnp.einsum("gqhd,gkhd->ghqk", grad_att, values_blk, preferred_element_type=jnp.float32)
    grad_scores = (probs * (dprobs - delta[..., None])).astype(jnp.bfloat16)
    return (probs.astype(jnp.bfloat16), grad_scores)


def mm(a, b, dims):
    return lax.dot_general(a, b, dims, preferred_element_type=f32)


def row_stats(x):
    average = jnp.mean(x, axis=1, keepdims=True)
    centered = x - average
    return centered, lax.rsqrt(jnp.mean(centered * centered, axis=1, keepdims=True) + NORM_EPS)


def norm_rows(x, scaling, offset):
    centered, inverse = row_stats(x)
    return (centered * inverse * scaling + offset).astype(bf16)


def norm_back(x, grad, scaling):
    centered, inverse = row_stats(x)
    unit = centered * inverse
    e = grad * scaling
    inner = e - jnp.mean(e, axis=1, keepdims=True) - unit * jnp.mean(e * unit, axis=1, keepdims=True)
    return inverse * inner, grad * unit


def col_sum(a):
    return jnp.sum(a, axis=0, keepdims=True)


def vmem(*shape, dtype=f32):
    return pltpu.VMEM(shape, dtype)


def params():
    return pltpu.CompilerParams(vmem_limit_bytes=60 << 20)


ROOT = math.sqrt(0.5)
DENS = 1.0 / math.sqrt(2.0 * math.pi)


def reorder(order_ref, source, target):
    size = source.shape[1] // order_ref.shape[0]
    for i in range(order_ref.shape[0]):
        at = pl.multiple_of(order_ref[i] * size, size)
        target[:, i * size:(i + 1) * size] = source[:, pl.ds(at, size)]


def mlp_kernel(order_ref, x_ref, c_ref, gain_ref, shift_ref, win_ref, bin_ref, wout_ref,
               out_ref, gin_ref, dwin_send, dwin_keep, dwout_send, dwout_keep, dbin_ref, dbout_ref, dgain_ref, dshift_ref,
               h_ref, turned_ref, act_ref, gp_ref, gh_ref):
    step = pl.program_id(0)
    rows = x_ref.shape[0]
    blocks = [slice(r, r + RB) for r in range(0, rows, RB)]

    @pl.when(step == 0)
    def _():
        for r in blocks:
            h_ref[r, :] = norm_rows(x_ref[r, :].astype(f32), gain_ref[...], shift_ref[...])
            out_ref[r, :] = jnp.zeros((RB, out_ref.shape[1]), f32)
            gh_ref[r, :] = jnp.zeros((RB, gh_ref.shape[1]), f32)
        reorder(order_ref, h_ref, turned_ref)

    dbin = jnp.zeros(dbin_ref.shape, f32)
    for r in blocks:
        pre = mm(h_ref[r, :], win_ref[...], NN) + bin_ref[...]
        phi = 0.5 + 0.5 * lax.erf(pre * ROOT)
        act_ref[r, :] = (pre * phi).astype(bf16)
        gp = phi + pre * (DENS * jnp.exp(-0.5 * (pre * pre)))
        gact = mm(c_ref[r, :], wout_ref[...], NT)
        gpre = (gact * gp).astype(bf16)
        gp_ref[r, :] = gpre
        dbin = dbin + col_sum(gpre.astype(f32))
    for r in blocks:
        out_ref[r, :] += mm(act_ref[r, :], wout_ref[...], NN)
        gh_ref[r, :] += mm(gp_ref[r, :], win_ref[...], NT)
    dwout = mm(act_ref[...], c_ref[...], TN).astype(bf16)
    middle = pl.num_programs(0) // 2

    @pl.when(step < middle)
    def _():
        dwout_send[...] = dwout

    @pl.when(step >= middle)
    def _():
        dwout_keep[...] = dwout

    dwin = mm(turned_ref[...], gp_ref[...], TN).astype(bf16)
    dwin_send[...] = dwin[:dwin_send.shape[0]]
    dwin_keep[...] = dwin[dwin_send.shape[0]:]
    dbin_ref[...] = dbin

    @pl.when(step == pl.num_programs(0) - 1)
    def _():
        dgain = jnp.zeros(dgain_ref.shape, f32)
        dshift = jnp.zeros(dshift_ref.shape, f32)
        dbout = jnp.zeros(dbout_ref.shape, f32)
        for r in blocks:
            grad = gh_ref[r, :]
            back, scaled = norm_back(x_ref[r, :].astype(f32), grad, gain_ref[...])
            c = c_ref[r, :].astype(f32)
            gin_ref[r, :] = back + c
            dgain += col_sum(scaled)
            dshift += col_sum(grad)
            dbout += col_sum(c)
        dgain_ref[...] = dgain
        dshift_ref[...] = dshift
        dbout_ref[...] = dbout


def mlp(order, x, c, gain, shift, weight_in, bias_in, weight_out):
    rows, width = x.shape
    ff = weight_in.shape[1]
    steps = order.shape[0]
    fc = ff // steps
    whole = pl.BlockSpec((rows, width), lambda j, o: (0, 0))
    line = pl.BlockSpec((1, width), lambda j, o: (0, 0))
    down = pl.BlockSpec((width // 2, fc), lambda j, o: (0, o[j]))
    s = jax.ShapeDtypeStruct
    return pl.pallas_call(
        mlp_kernel,
        grid_spec=pltpu.PrefetchScalarGridSpec(
            num_scalar_prefetch=1,
            grid=(steps,),
            in_specs=[whole, whole, line, line, pl.BlockSpec((width, fc), lambda j, o: (0, o[j])),
                      pl.BlockSpec((1, fc), lambda j, o: (0, o[j])), pl.BlockSpec((fc, width), lambda j, o: (o[j], 0))],
            out_specs=[whole, whole, down, down,
                       pl.BlockSpec((fc, width), lambda j, o: (jnp.minimum(j, steps // 2 - 1), 0)),
                       pl.BlockSpec((fc, width), lambda j, o: (jnp.maximum(j - steps // 2, 0), 0)),
                       pl.BlockSpec((1, fc), lambda j, o: (0, o[j])), line, line, line],
            scratch_shapes=[vmem(rows, width, dtype=bf16), vmem(rows, width, dtype=bf16), vmem(rows, fc, dtype=bf16),
                            vmem(rows, fc, dtype=bf16), vmem(rows, width)],
        ),
        out_shape=[s((rows, width), f32), s((rows, width), f32), s((width // 2, ff), bf16), s((width // 2, ff), bf16),
                   s((ff // 2, width), bf16), s((ff // 2, width), bf16), s((1, ff), f32), s((1, width), f32),
                   s((1, width), f32), s((1, width), f32)],
        compiler_params=params(),
        cost_estimate=pl.CostEstimate(flops=12 * rows * width * ff, bytes_accessed=48 << 20, transcendentals=2 * rows * ff),
        name="mlp",
    )(order, x, c, gain.reshape(1, -1), shift.reshape(1, -1), weight_in, bias_in.reshape(1, -1), weight_out)


def turn_lanes(u, cosine, low, high, sign):
    half = ROT // 2
    parts = []
    for at in range(0, u.shape[1], PAIR):
        g = u[:, at:at + PAIR]
        parts.append(g * cosine + sign * (pltpu.roll(g, half, 1) * high - pltpu.roll(g, PAIR - half, 1) * low))
    return jnp.concatenate(parts, axis=1)


def qkv_kernel(with_q, spot_ref, x_ref, gain_ref, shift_ref, w_ref, b_ref, cos_ref, low_ref, high_ref, *outs):
    width = x_ref.shape[1]
    h = norm_rows(x_ref[...].astype(f32), gain_ref[...], shift_ref[...])
    tables = (cos_ref[...], low_ref[...], high_ref[...])
    if with_q:
        h_ref, q_ref, k_ref, v_ref = outs
        h_ref[...] = h
        q = mm(h, w_ref[:, :width], NN) + b_ref[:, :width]
        q_ref[...] = (turn_lanes(q, *tables, 1.0) * (HD ** (-0.5) / math.log(2.0))).astype(bf16)
    else:
        k_ref, v_ref = outs
    k = mm(h, w_ref[:, width:2 * width], NN) + b_ref[:, width:2 * width]
    k_ref[...] = turn_lanes(k, *tables, 1.0).astype(bf16)
    v_ref[...] = (mm(h, w_ref[:, 2 * width:], NN) + b_ref[:, 2 * width:]).astype(bf16)


def qkv(spots, x, gain, shift, weight, bias, tables, with_q):
    rows, width = x.shape
    s = jax.ShapeDtypeStruct((rows, width), bf16)
    block = pl.BlockSpec((RB, width), lambda j, spot: (j, 0))
    line = pl.BlockSpec((1, width), lambda j, spot: (0, 0))
    table = pl.BlockSpec((RB, PAIR), lambda j, spot: (spot[j], 0))
    count = 4 if with_q else 2
    return pl.pallas_call(
        partial(qkv_kernel, with_q),
        grid_spec=pltpu.PrefetchScalarGridSpec(
            num_scalar_prefetch=1,
            grid=(rows // RB,),
            in_specs=[block, line, line, pl.BlockSpec((width, 3 * width), lambda j, spot: (0, 0)),
                      pl.BlockSpec((1, 3 * width), lambda j, spot: (0, 0)), table, table, table],
            out_specs=[block] * count,
        ),
        out_shape=[s] * count,
        compiler_params=params(),
        cost_estimate=pl.CostEstimate(flops=2 * rows * width * width * (3 if with_q else 2), bytes_accessed=16 << 20,
                                      transcendentals=0),
        name="qkv_own" if with_q else "kv_remote",
    )(spots, x, gain.reshape(1, -1), shift.reshape(1, -1), weight, bias.reshape(1, -1), *tables)


def tail_kernel(groups, spot_ref, order_ref, x_ref, h_ref, gain_ref, w_ref, cos_ref, low_ref, high_ref, gin_ref, *refs):
    dq_refs, own_refs, come_refs = refs[:groups], refs[groups:2 * groups], refs[2 * groups:3 * groups]
    grad_ref, send_ref, keep_ref, db_ref, dgain_ref, dshift_ref, p_ref, turned_ref, gh_ref = refs[3 * groups:]
    step = pl.program_id(0)
    rows = x_ref.shape[0]
    half = rows // 2
    blocks = [slice(r, r + RB) for r in range(0, rows, RB)]
    part = dq_refs[0].shape[1]

    def put(shift):
        for r in blocks:
            spot = pl.ds(pl.multiple_of(spot_ref[r.start // RB] * RB, RB), RB)
            for g in range(groups):
                for at in range(0, part, PAIR):
                    if shift is None:
                        p_ref[r, g * part + at:g * part + at + PAIR] = dq_refs[g][r, at:at + PAIR]
                        continue
                    lanes = slice(2 * at + shift, 2 * at + shift + PAIR)
                    if r.start < half:
                        t = come_refs[g][r, lanes].astype(f32)
                    else:
                        t = own_refs[g][r.start - half:r.stop - half, lanes].astype(f32)
                    if shift == 0:
                        t = turn_lanes(t, cos_ref[spot, :], low_ref[spot, :], high_ref[spot, :], -1.0)
                    p_ref[r, g * part + at:g * part + at + PAIR] = t.astype(bf16)

    @pl.when(step == 0)
    def _():
        reorder(order_ref, h_ref, turned_ref)
        put(None)
        for r in blocks:
            gh_ref[r, :] = mm(p_ref[r, :], w_ref[...], NT)

    @pl.when(step == 1)
    def _():
        put(0)

    @pl.when(step == 2)
    def _():
        put(PAIR)

    @pl.when(step > 0)
    def _():
        for r in blocks:
            gh_ref[r, :] += mm(p_ref[r, :], w_ref[...], NT)

    dw = mm(turned_ref[...], p_ref[...], TN).astype(bf16)
    send_ref[...] = dw[:send_ref.shape[0]]
    keep_ref[...] = dw[send_ref.shape[0]:]
    db = jnp.zeros(db_ref.shape, f32)
    for r in blocks:
        db += col_sum(p_ref[r, :].astype(f32))
    db_ref[...] = db

    @pl.when(step == 2)
    def _():
        dgain = jnp.zeros(dgain_ref.shape, f32)
        dshift = jnp.zeros(dshift_ref.shape, f32)
        for r in blocks:
            grad = gh_ref[r, :]
            back, scaled = norm_back(x_ref[r, :].astype(f32), grad, gain_ref[...])
            grad_ref[r, :] = back + gin_ref[r, :]
            dgain += col_sum(scaled)
            dshift += col_sum(grad)
        dgain_ref[...] = dgain
        dshift_ref[...] = dshift


def tail(spots, order, x, h, gain, weight, tables, gin, dqs, owns, comes):
    rows, width = x.shape
    groups = len(dqs)
    s = jax.ShapeDtypeStruct

    def full(a):
        return pl.BlockSpec(a.shape, lambda j, spot, o: (0, 0))

    line = pl.BlockSpec((1, width), lambda j, spot, o: (0, 0))
    down = pl.BlockSpec((width // 2, width), lambda j, spot, o: (0, j))
    arrays = [*tables, gin, *dqs, *owns, *comes]
    return pl.pallas_call(
        partial(tail_kernel, groups),
        grid_spec=pltpu.PrefetchScalarGridSpec(
            num_scalar_prefetch=2,
            grid=(3,),
            in_specs=[full(x), full(h), line, pl.BlockSpec((width, width), lambda j, spot, o: (0, j))] + [full(a) for a in arrays],
            out_specs=[full(x), down, down,
                       pl.BlockSpec((1, width), lambda j, spot, o: (0, j)), line, line],
            scratch_shapes=[vmem(rows, width, dtype=bf16), vmem(rows, width, dtype=bf16), vmem(rows, width)],
        ),
        out_shape=[s((rows, width), f32), s((width // 2, 3 * width), bf16), s((width // 2, 3 * width), bf16), s((1, 3 * width), f32), s((1, width), f32),
                   s((1, width), f32)],
        compiler_params=params(),
        cost_estimate=pl.CostEstimate(flops=12 * rows * width * width, bytes_accessed=32 << 20, transcendentals=0),
        name="tail",
    )(spots, order, x, h, gain.reshape(1, -1), weight, *arrays)


def join_kernel(groups, order_ref, x_ref, c_ref, w_ref, mlp_ref, b_ref, *refs):
    att_refs, (out_ref, send_ref, keep_ref, att_ref, turned_ref, acc_ref) = refs[:groups], refs[groups:]
    step = pl.program_id(0)
    part = att_refs[0].shape[1]
    for g in range(groups):
        att_ref[:, g * part:(g + 1) * part] = att_refs[g][...]
    out = x_ref[...].astype(f32) + mm(att_ref[...], w_ref[...], NN) + mlp_ref[...] + b_ref[...]
    out_ref[...] = out.astype(bf16)
    reorder(order_ref, att_ref, turned_ref)

    @pl.when(step == 0)
    def _():
        acc_ref[...] = mm(turned_ref[...], c_ref[...], TN)

    @pl.when(step > 0)
    def _():
        acc_ref[...] += mm(turned_ref[...], c_ref[...], TN)

    @pl.when(step == pl.num_programs(0) - 1)
    def _():
        half = send_ref.shape[0]
        send_ref[...] = acc_ref[:half, :].astype(bf16)
        keep_ref[...] = acc_ref[half:, :].astype(bf16)


def join(order, x, c, attended, weight, mlp_out, bias):
    rows, width = x.shape
    s = jax.ShapeDtypeStruct
    block = pl.BlockSpec((RB, width), lambda j, o: (j, 0))
    half = pl.BlockSpec((width // 2, width), lambda j, o: (0, 0))
    return pl.pallas_call(
        partial(join_kernel, len(attended)),
        grid_spec=pltpu.PrefetchScalarGridSpec(
            num_scalar_prefetch=1,
            grid=(rows // RB,),
            in_specs=[block, block, pl.BlockSpec((width, width), lambda j, o: (0, 0)), block,
                      pl.BlockSpec((1, width), lambda j, o: (0, 0))]
            + [pl.BlockSpec((RB, a.shape[1]), lambda j, o: (j, 0)) for a in attended],
            out_specs=[block, half, half],
            scratch_shapes=[vmem(RB, width, dtype=bf16), vmem(RB, width, dtype=bf16), vmem(width, width)],
        ),
        out_shape=[s((rows, width), bf16), s((width // 2, width), bf16), s((width // 2, width), bf16)],
        compiler_params=params(),
        cost_estimate=pl.CostEstimate(flops=4 * rows * width * width, bytes_accessed=16 << 20, transcendentals=0),
        name="join",
    )(order, x, c, weight, mlp_out, bias.reshape(1, -1), *attended)


def fold(x, op):
    return op(x.reshape(x.shape[0] // 8, 8, x.shape[1]), axis=0)


def eye(size):
    return (lax.broadcasted_iota(jnp.int32, (size, size), 0) == lax.broadcasted_iota(jnp.int32, (size, size), 1)).astype(bf16)


def attention_kernel(half, n, kind_ref, owner_ref, cos_ref, sin_ref, q_ref, do_ref, *refs):
    k_refs, v_refs = refs[:n], refs[n:2 * n]
    o_ref, dq_ref = refs[2 * n:2 * n + 2]
    all_ref, cont_ref = refs[2 * n + 2:2 * n + 4]
    kt_ref, vt_ref, s_ref, p_ref, ds_ref, dka_ref, dva_ref = refs[2 * n + 4:]
    per = half // QB
    wide = n * half
    count = wide // QB
    spots = [(0, c * QB) for c in range(per)] + [(s, c * QB) for s in range(1, n) for c in range(per)]

    ident = eye(PAIR)
    for refs_in, out in ((k_refs, kt_ref), (v_refs, vt_ref)):
        for c, (s, at) in enumerate(spots):
            out[:, c * QB:(c + 1) * QB] = refs_in[s][at:at + QB, :].T
        for c in range(per):
            out[:, wide + c * QB:wide + (c + 1) * QB] = refs_in[0][half + c * QB:half + (c + 1) * QB, :].T
    dka_ref[...] = jnp.zeros_like(dka_ref)
    dva_ref[...] = jnp.zeros_like(dva_ref)


    def block(qb, carry):
        own = pl.ds(pl.multiple_of(qb * QB, QB), QB)
        slot = pl.ds(pl.multiple_of(jnp.where(qb < per, qb * QB, wide + (qb - per) * QB), QB), QB)
        zero = jnp.zeros((), bf16)
        causal = lax.broadcasted_iota(jnp.int32, (QB, QB), 0) <= lax.broadcasted_iota(jnp.int32, (QB, QB), 1)
        left = lax.broadcasted_iota(jnp.int32, (QB, PAIR), 1) < HD

        def by_head(a):
            return jnp.where(left, a, zero), jnp.where(left, zero, a)

        def keys_of(some, c):
            if c == count:
                return some[0][own, :]
            s, at = spots[c]
            return some[s][at:at + QB, :]

        def cut(c):
            return slice(c * QB, (c + 1) * QB)

        ident = eye(QB)
        q_heads = by_head(q_ref[own, :])
        do_t = mm(eye(PAIR), do_ref[own, :], NT)
        upper = lax.broadcasted_iota(jnp.int32, (PAIR, QB), 0) < HD
        q_t = mm(eye(PAIR), q_ref[own, :], NT).astype(bf16)
        q_cols = jnp.where(upper, q_t, zero), jnp.where(upper, zero, q_t)
        peaks, norms, outs, deltas, scaled = [None, None], [None, None], [None, None], [None, None], [None, None]

        def scores(h):
            peak = jnp.full((8, QB), MASKED, f32)
            for c in range(count + 1):
                s = mm(keys_of(k_refs, c), q_cols[h], NN)
                if c == count:
                    s = jnp.where(causal, s, MASKED)
                    top = fold(s, jnp.max)
                else:
                    top = fold(s, jnp.max) + kind_ref[qb, c]
                s_ref[h, cut(c)] = s
                peak = jnp.maximum(peak, top)
            peaks[h] = jnp.max(peak, axis=0, keepdims=True)

        def weigh(h):
            total = jnp.zeros((8, QB), f32)
            for c in range(count + 1):
                bias = -peaks[h] if c == count else kind_ref[qb, c] - peaks[h]
                e = jnp.exp2(s_ref[h, cut(c)] + bias)
                total = total + fold(e, jnp.sum)
                p_ref[h, cut(c)] = e.astype(bf16)
            norms[h] = 1.0 / jnp.sum(total, axis=0, keepdims=True)

        def attend(h):
            lines = slice(h * HD, (h + 1) * HD)
            out = mm(vt_ref[lines, 0:wide], p_ref[h, 0:wide], NN) + mm(vt_ref[lines, slot], p_ref[h, wide:], NN)
            outs[h] = out * norms[h]
            deltas[h] = jnp.sum(outs[h] * do_t[lines], axis=0, keepdims=True) * norms[h]
            scaled[h] = do_t[lines] * norms[h]

        scores(0)
        scores(1)
        weigh(0)
        attend(0)
        weigh(1)
        attend(1)
        d_t = jnp.concatenate(scaled, axis=0).astype(bf16)
        d_cols = jnp.where(upper, d_t, zero), jnp.where(upper, zero, d_t)
        do_heads = by_head(mm(ident, d_t, NT).astype(bf16))
        grads = []
        for h in range(2):
            lines = slice(h * HD, (h + 1) * HD)
            for c in range(count + 1):
                dp = mm(keys_of(v_refs, c), d_cols[h], NN)
                ds_ref[h, cut(c)] = (p_ref[h, cut(c)].astype(f32) * (dp - deltas[h])).astype(bf16)
            dq = mm(kt_ref[lines, 0:wide], ds_ref[h, 0:wide], NN) + mm(kt_ref[lines, slot], ds_ref[h, wide:], NN)
            a, b = dq[:ROT // 2], dq[ROT // 2:ROT]
            cosine, sine = cos_ref[:, own], sin_ref[:, own]
            grads.append(jnp.concatenate([a * cosine + b * sine, b * cosine - a * sine, dq[ROT:]], axis=0))
        for c in range(count + 1):
            at = slot if c == count else cut(c)
            dva_ref[at, :] += mm(p_ref[0, cut(c)], do_heads[0], NN) + mm(p_ref[1, cut(c)], do_heads[1], NN)
            dka_ref[at, :] += mm(ds_ref[0, cut(c)], q_heads[0], NN) + mm(ds_ref[1, cut(c)], q_heads[1], NN)
        o_ref[own, :] = mm(ident, jnp.concatenate(outs, axis=0).astype(bf16), NT).astype(bf16)
        dq_ref[own, :] = mm(ident, (jnp.concatenate(grads, axis=0) * (HD ** (-0.5))).astype(bf16), NT).astype(bf16)

        return carry

    lax.fori_loop(0, 2 * per, block, 0)

    def flush(out, to, frm):
        rows = pl.ds(to, half)
        out[rows, :PAIR] = (dka_ref[frm:frm + half, :] * math.log(2.0)).astype(bf16)
        out[rows, PAIR:] = dva_ref[frm:frm + half, :].astype(bf16)

    flush(cont_ref, 0, wide)
    for s in range(n):
        flush(all_ref, pl.multiple_of(owner_ref[s] * half, half), s * half)


def attention(kind, owners, cos_t, sin_t, q, do, ks, vs, first, pairs):
    rows = q.shape[0]
    half = rows // 2
    n = len(ks)
    wide = n * half
    keys = wide + half
    total = wide + QB
    qspec = pl.BlockSpec((rows, PAIR), lambda p: (0, p + first))
    ospec = pl.BlockSpec((rows, PAIR), lambda p: (0, p))
    table = pl.BlockSpec((ROT // 2, rows), lambda p: (0, 0))
    kspecs = [pl.BlockSpec((k.shape[0], PAIR), lambda p: (0, p + first)) for k in ks]
    gspecs = [pl.BlockSpec((size, 2 * PAIR), lambda p: (0, p)) for size in (wide, half)]
    s = jax.ShapeDtypeStruct
    pieces = pairs * rows // QB
    return pl.pallas_call(
        partial(attention_kernel, half, n),
        grid=(pairs,),
        in_specs=[pl.BlockSpec(memory_space=pltpu.SMEM), pl.BlockSpec(memory_space=pltpu.SMEM), table, table, qspec, qspec] + kspecs + kspecs,
        out_specs=[ospec, ospec] + gspecs,
        out_shape=[s((rows, pairs * PAIR), bf16), s((rows, pairs * PAIR), bf16)]
        + [s((size, 2 * pairs * PAIR), bf16) for size in (wide, half)],
        scratch_shapes=[pltpu.VMEM((PAIR, keys), bf16), pltpu.VMEM((PAIR, keys), bf16),
                        pltpu.VMEM((2, total, QB), f32), pltpu.VMEM((2, total, QB), bf16),
                        pltpu.VMEM((2, total, QB), bf16),
                        pltpu.VMEM((keys, PAIR), f32), pltpu.VMEM((keys, PAIR), f32)],
        compiler_params=pltpu.CompilerParams(vmem_limit_bytes=60 << 20),
        cost_estimate=pl.CostEstimate(flops=pieces * 24 * total * QB * HD * 4, bytes_accessed=16 << 20,
                                      transcendentals=pieces * 2 * total * QB),
        name="attention",
    )(kind, owners, cos_t, sin_t, q, do, *ks, *vs)


def pairs_of(bit, size):
    return [(a, a ^ bit) for a in range(size)]


def pick(a, axis, i):
    return lax.dynamic_index_in_dim(a, i, axis, keepdims=False)


def plus(a, b):
    return (a.astype(f32) + b.astype(f32)).astype(bf16)


def core_step(send, keep):
    rows, cols = send.shape
    size = rows // 8
    got = lax.ppermute(send, "fsdp", pairs_of(1, 8)).reshape(2, 2, 2, size, cols)
    keep = keep.reshape(2, 2, 2, size, cols)

    def part(*at):
        return plus(keep[at], got[at])

    every = slice(None)
    return part(every, 1, 0), part(every, 0, 0), part(1, every, 1), part(0, every, 1)


def side_step(send_a, keep_a, send_b, keep_b):
    got_a = lax.ppermute(send_a, "fsdp", pairs_of(2, 8))
    got_b = lax.ppermute(send_b, "fsdp", pairs_of(4, 8))
    return plus(keep_a[1], got_a[1]), plus(keep_a[0], got_a[0]), plus(keep_b[1], got_b[1]), plus(keep_b[0], got_b[0])


def last_step(send_a, keep_a, send_b, keep_b):
    got_a = lax.ppermute(send_a, "fsdp", pairs_of(4, 8))
    got_b = lax.ppermute(send_b, "fsdp", pairs_of(2, 8))
    part = jnp.concatenate([plus(keep_a, got_a), plus(keep_b, got_b)], axis=0)
    return lax.psum_scatter(part, "ctx", scatter_dimension=0, tiled=True)


def scatter_sum(send, keep):
    return last_step(*side_step(*core_step(send, keep)))


def after(value, *others):
    return lax.optimization_barrier((value, *others))[0]


def fast(inputs, cotangent, positions, segments, ln1_gain, ln1_bias, w_qkv, b_qkv, w_attn_out, b_out,
         ln2_gain, ln2_bias, w_in, b_in, w_out):
    x, grad_out, pos = inputs[0], cotangent[0], positions[0]
    rows, width = x.shape
    half = rows // 2
    n = lax.axis_size("ctx")
    ring = [(i, (i + 1) % n) for i in range(n)]
    back = [(i, (i - 1) % n) for i in range(n)]
    xs, spots = [x], [pos[::RB] // RB]
    run = x[:half]
    for s in range(1, n):
        run = lax.ppermute(run, "ctx", ring)
        xs.append(run)
        spots.append(lax.ppermute(spots[0][:half // RB], "ctx", [(i, (i + s) % n) for i in range(n)]))
    mine = (ln1_gain, ln1_bias, b_qkv, b_out, ln2_gain, ln2_bias, b_in)
    small = lax.all_gather(jnp.concatenate(mine).reshape(1, -1), "fsdp", axis=0, tiled=True)
    full, at = [], 0
    for a in mine:
        full.append(small[:, at:at + a.shape[0]].reshape(-1).astype(f32))
        at += a.shape[0]
    gain_attn, shift_attn, bias_qkv, bias_out, gain_mlp, shift_mlp, bias_in = full
    weight_qkv = lax.all_gather(w_qkv, "fsdp", axis=0, tiled=True)
    weight_attn = lax.all_gather(after(w_attn_out, weight_qkv), "fsdp", axis=0, tiled=True)
    weight_in = lax.all_gather(after(w_in, weight_attn), "fsdp", axis=0, tiled=True)
    weight_out = lax.all_gather(after(w_out, weight_attn), "fsdp", axis=0, tiled=True)

    lane = jnp.arange(PAIR) % HD
    inverse = jnp.exp(-math.log(10000.0) * (2.0 / ROT) * (lane % (ROT // 2)).astype(f32))
    angles = jnp.arange(n * half + CLEN).astype(f32)[:, None] * inverse[None, :]
    sine = jnp.sin(angles)
    tables = (jnp.where(lane < ROT, jnp.cos(angles), 1.0), jnp.where(lane < ROT // 2, sine, 0.0),
              jnp.where((lane >= ROT // 2) & (lane < ROT), sine, 0.0))
    angles_t = pos.astype(f32)[None, :] * inverse[:ROT // 2, None]
    cos_t, sin_t = jnp.cos(angles_t), jnp.sin(angles_t)

    normed, queries, key, value = qkv(spots[0], x, gain_attn, shift_attn, weight_qkv, bias_qkv, tables, True)
    keys, values = [key], [value]
    for s in range(1, n):
        key, value = qkv(spots[s], xs[s], gain_attn, shift_attn, weight_qkv, bias_qkv, tables, False)
        keys.append(key)
        values.append(value)
    grad_att = mm(grad_out, weight_attn, NT).astype(bf16)

    per = half // QB
    earlier = jnp.stack([spots[s][0] < spots[0][0] for s in range(1, n)])
    local_row = jnp.arange(2 * per)[:, None]
    seen_own = local_row > jnp.arange(per)[None, :]
    seen_far = jnp.repeat(earlier[None, :] | (local_row >= per), per, axis=1)
    kind = jnp.where(jnp.concatenate([seen_own, seen_far], axis=1), 0.0, MASKED).astype(f32)

    me, place = lax.axis_index("fsdp"), lax.axis_index("ctx")
    relative = [4 * dy + 2 * dx + 1 - keep for keep in (0, 1) for dy in (0, 1) for dx in (0, 1)]
    order = jnp.bitwise_xor(me, jnp.array(relative, jnp.int32))
    owners = lax.rem(place + n - jnp.arange(n), n)
    groups = 2
    count = HEADS // 2 // groups
    attended, grad_q, own_kv, come_kv = [], [], [], []
    for g in range(groups):
        out = attention(kind, owners, cos_t, sin_t, queries, grad_att, keys, values, g * count, count)
        attended.append(out[0])
        grad_q.append(out[1])
        come_kv.append(lax.psum_scatter(out[2], "ctx", scatter_dimension=0, tiled=True))
        own_kv.append(out[3])

    x_late, attended = lax.optimization_barrier((x, attended))
    mlp_out, grad_mlp, in_send, in_keep, out_send, out_keep, db_in, db_out, dgain_mlp, dshift_mlp = mlp(
        order, x_late, grad_out, gain_mlp, shift_mlp, weight_in, bias_in, weight_out)
    output, attn_send, attn_keep = join(order, x, grad_out, attended, weight_attn, mlp_out, bias_out)
    sum_out = scatter_sum(out_send, out_keep)
    sum_in = scatter_sum(in_send, in_keep)
    sum_attn = scatter_sum(attn_send, attn_keep)
    grad_inputs, qkv_send, qkv_keep, db_qkv, dgain_attn, dshift_attn = tail(
        spots[0], order, after(x, output), normed, gain_attn, weight_qkv, tables, grad_mlp, grad_q, own_kv, come_kv)
    sum_qkv = scatter_sum(qkv_send, qkv_keep)
    smalls = [a.reshape(width, -1) for a in (dgain_attn, dshift_attn, db_qkv, db_out, dgain_mlp, dshift_mlp, db_in)]
    used = sum(a.shape[1] for a in smalls)
    packed = jnp.concatenate(smalls + [jnp.zeros((width, PAIR - used), f32)], axis=1).astype(bf16)
    packed = packed.reshape(8, width // 8, PAIR)[order].reshape(2, width // 2, PAIR)
    packed = scatter_sum(packed[0], packed[1]).astype(f32)
    done, at = [], 0
    for a in smalls:
        done.append(packed[:, at:at + a.shape[1]].reshape(-1))
        at += a.shape[1]
    return (output[None], grad_inputs[None], done[0], done[1], sum_qkv.astype(f32), done[2], sum_attn.astype(f32),
            done[3], done[4], done[5], sum_in.astype(f32), done[6], sum_out.astype(f32))


def local(*args):
    half = args[0].shape[1] // 2
    if args[0].shape[0] == 1 and half % CLEN == 0 and lax.axis_size("fsdp") == 8:
        return fast(*args)
    return generic(*args)


def generic(
    inputs,
    cotangent,
    positions,
    segments,
    ln1_gain,
    ln1_bias,
    w_qkv,
    b_qkv,
    w_attn_out,
    b_out,
    ln2_gain,
    ln2_bias,
    w_in,
    b_in,
    w_out,
):
    shards = (
        ln1_gain,
        ln1_bias,
        w_qkv,
        b_qkv,
        w_attn_out,
        b_out,
        ln2_gain,
        ln2_bias,
        w_in,
        b_in,
        w_out,
    )
    params = (
        lax.all_gather(shards[0], "fsdp", axis=0, tiled=True),
        lax.all_gather(shards[1], "fsdp", axis=0, tiled=True),
        lax.all_gather(shards[2], "fsdp", axis=0, tiled=True),
        lax.all_gather(shards[3], "fsdp", axis=0, tiled=True),
        lax.all_gather(shards[4], "fsdp", axis=0, tiled=True),
        lax.all_gather(shards[5], "fsdp", axis=0, tiled=True),
        lax.all_gather(shards[6], "fsdp", axis=0, tiled=True),
        lax.all_gather(shards[7], "fsdp", axis=0, tiled=True),
        lax.all_gather(shards[8], "fsdp", axis=0, tiled=True),
        lax.all_gather(shards[9], "fsdp", axis=0, tiled=True),
        lax.all_gather(shards[10], "fsdp", axis=0, tiled=True),
    )
    groups, local_len, width = inputs.shape
    rows_total = groups * local_len
    block = math.gcd(local_len, 256)
    label_pos, label_seg = (
        lax.all_gather(positions, "ctx", axis=1, tiled=True),
        lax.all_gather(segments, "ctx", axis=1, tiled=True),
    )
    count = label_pos.shape[1] // block
    f32 = jnp.float32
    bf16 = jnp.bfloat16
    (
        gain_attn,
        shift_attn,
        weight_qkv,
        bias_qkv,
        weight_attn,
        bias_out,
        gain_mlp,
        shift_mlp,
        weight_in,
        bias_in,
        weight_out,
    ) = params
    flat_in = inputs.reshape(rows_total, width).astype(f32)
    normed_attn = layer_norm(flat_in, gain_attn.astype(f32), shift_attn.astype(f32)).astype(bf16)
    normed_mlp = layer_norm(flat_in, gain_mlp.astype(f32), shift_mlp.astype(f32)).astype(bf16)
    projected = jnp.dot(normed_attn, weight_qkv, preferred_element_type=f32) + bias_qkv.astype(f32)
    cosine, sine = rotary_tables(positions)

    def split_heads(columns):
        return columns.reshape(groups, local_len, HEADS, HD)

    scale = HD ** (-0.5)
    queries = (rotate(split_heads(projected[:, :width]), cosine, sine) * scale).astype(bf16)
    keys_own = rotate(split_heads(projected[:, width : 2 * width]), cosine, sine).astype(bf16)
    values_own = split_heads(projected[:, 2 * width :]).astype(bf16)
    keys_all, values_all = (
        lax.all_gather(keys_own, "ctx", axis=1, tiled=True),
        lax.all_gather(values_own, "ctx", axis=1, tiled=True),
    )

    def key_block(index):
        start = index * block
        keys_blk = lax.dynamic_slice_in_dim(keys_all, start, block, 1)
        values_blk = lax.dynamic_slice_in_dim(values_all, start, block, 1)
        mask = allowed_mask(
            positions,
            segments,
            lax.dynamic_slice_in_dim(label_pos, start, block, 1),
            lax.dynamic_slice_in_dim(label_seg, start, block, 1),
        )
        return (keys_blk, values_blk, mask)

    def total_step(carry, index):
        peak, total = carry
        keys_blk, values_blk, mask = key_block(index)
        scores = jnp.where(mask, scores_of(queries, keys_blk), MASKED)
        fresh = jnp.maximum(peak, jnp.max(scores, axis=-1))
        added = jnp.sum(jnp.where(mask, jnp.exp(scores - fresh[..., None]), 0.0), axis=-1)
        return ((fresh, total * jnp.exp(peak - fresh) + added), None)

    stat_shape = (groups, HEADS, local_len)
    (peak, total), unused = lax.scan(
        total_step,
        (jnp.full(stat_shape, MASKED, f32), jnp.zeros(stat_shape, f32)),
        jnp.arange(count),
    )
    log_total = peak + jnp.log(total)

    def attend_step(rounded_sum, index):
        keys_blk, values_blk, mask = key_block(index)
        probs = jnp.where(mask, jnp.exp(scores_of(queries, keys_blk) - log_total[..., None]), 0.0)
        rounded_sum = rounded_sum + jnp.einsum(
            "ghqk,gkhd->gqhd", probs.astype(bf16), values_blk, preferred_element_type=f32
        )
        return (rounded_sum, None)

    head_shape = (groups, local_len, HEADS, HD)
    rounded_sum, unused = lax.scan(attend_step, jnp.zeros(head_shape, f32), jnp.arange(count))
    attended = rounded_sum.reshape(rows_total, width).astype(bf16)
    pre_act = jnp.dot(normed_mlp, weight_in, preferred_element_type=f32) + bias_in.astype(f32)
    activated = jax.nn.gelu(pre_act, approximate=False).astype(bf16)
    output = (
        flat_in
        + jnp.dot(attended, weight_attn, preferred_element_type=f32)
        + jnp.dot(activated, weight_out, preferred_element_type=f32)
        + bias_out.astype(f32)
    )
    (
        gain_attn,
        shift_attn,
        weight_qkv,
        bias_qkv,
        weight_attn,
        bias_out,
        gain_mlp,
        shift_mlp,
        weight_in,
        bias_in,
        weight_out,
    ) = params
    grad_out = cotangent.reshape(rows_total, width)
    grad_bias_out = jnp.sum(grad_out.astype(f32), axis=0)
    grad_weight_out = jnp.einsum("rf,rd->fd", activated, grad_out, preferred_element_type=f32)
    grad_act = jnp.einsum("rd,fd->rf", grad_out, weight_out, preferred_element_type=f32)
    unused, gelu_back = jax.vjp(partial(jax.nn.gelu, approximate=False), pre_act)
    grad_pre = gelu_back(grad_act)[0].astype(bf16)
    grad_weight_in = jnp.einsum("rd,rf->df", normed_mlp, grad_pre, preferred_element_type=f32)
    grad_bias_in = jnp.sum(grad_pre.astype(f32), axis=0)
    grad_normed_mlp = jnp.einsum("rf,df->rd", grad_pre, weight_in, preferred_element_type=f32)
    grad_weight_attn = jnp.einsum("ra,rd->ad", attended, grad_out, preferred_element_type=f32)
    grad_att = (
        jnp.einsum("rd,ad->ra", grad_out, weight_attn, preferred_element_type=f32)
        .astype(bf16)
        .reshape(head_shape)
    )
    delta = jnp.einsum(
        "gqhd,gqhd->ghq", grad_att.astype(f32), rounded_sum, precision=lax.Precision.HIGHEST
    )

    def back_step(carry, index):
        keys_blk, values_blk, mask = key_block(index)
        rounded, grad_scores = block_grads(
            queries, grad_att, log_total, delta, mask, keys_blk, values_blk
        )
        carry = carry + jnp.einsum(
            "ghqk,gkhd->gqhd", grad_scores, keys_blk, preferred_element_type=f32
        )
        key_term = jnp.einsum("ghqk,gqhd->gkhd", grad_scores, queries, preferred_element_type=f32)
        value_term = jnp.einsum("ghqk,gqhd->gkhd", rounded, grad_att, preferred_element_type=f32)
        return (carry, (key_term, value_term))

    grad_queries, (key_terms, value_terms) = lax.scan(
        back_step, jnp.zeros(head_shape, f32), jnp.arange(count)
    )
    key_sums, value_sums = (
        lax.psum_scatter(
            key_terms.astype(jnp.bfloat16), "ctx", scatter_dimension=0, tiled=True
        ).astype(jnp.float32),
        lax.psum_scatter(
            value_terms.astype(jnp.bfloat16), "ctx", scatter_dimension=0, tiled=True
        ).astype(jnp.float32),
    )
    grad_keys = jnp.transpose(key_sums, (1, 0, 2, 3, 4)).reshape(head_shape)
    grad_values = jnp.transpose(value_sums, (1, 0, 2, 3, 4)).reshape(head_shape)
    grad_q_pre = unrotate(grad_queries * scale, cosine, sine).reshape(rows_total, width)
    grad_k_pre = unrotate(grad_keys, cosine, sine).reshape(rows_total, width)
    grad_projected = jnp.concatenate(
        [grad_q_pre, grad_k_pre, grad_values.reshape(rows_total, width)], axis=1
    ).astype(bf16)
    grad_weight_qkv = jnp.einsum(
        "rd,re->de", normed_attn, grad_projected, preferred_element_type=f32
    )
    grad_bias_qkv = jnp.sum(grad_projected.astype(f32), axis=0)
    grad_normed_attn = jnp.einsum(
        "re,de->rd", grad_projected, weight_qkv, preferred_element_type=f32
    )
    unused, norm_back_attn = jax.vjp(
        layer_norm, flat_in, gain_attn.astype(f32), shift_attn.astype(f32)
    )
    grad_in_attn, grad_gain_attn, grad_shift_attn = norm_back_attn(grad_normed_attn)
    unused, norm_back_mlp = jax.vjp(
        layer_norm, flat_in, gain_mlp.astype(f32), shift_mlp.astype(f32)
    )
    grad_in_mlp, grad_gain_mlp, grad_shift_mlp = norm_back_mlp(grad_normed_mlp)
    grad_inputs = (grad_out.astype(f32) + grad_in_attn + grad_in_mlp).reshape(
        groups, local_len, width
    )
    sums = (
        lax.psum_scatter(grad_gain_attn, ("fsdp", "ctx"), scatter_dimension=0, tiled=True),
        lax.psum_scatter(grad_shift_attn, ("fsdp", "ctx"), scatter_dimension=0, tiled=True),
        lax.psum_scatter(grad_weight_qkv, ("fsdp", "ctx"), scatter_dimension=0, tiled=True),
        lax.psum_scatter(grad_bias_qkv, ("fsdp", "ctx"), scatter_dimension=0, tiled=True),
        lax.psum_scatter(grad_weight_attn, ("fsdp", "ctx"), scatter_dimension=0, tiled=True),
        lax.psum_scatter(grad_bias_out, ("fsdp", "ctx"), scatter_dimension=0, tiled=True),
        lax.psum_scatter(grad_gain_mlp, ("fsdp", "ctx"), scatter_dimension=0, tiled=True),
        lax.psum_scatter(grad_shift_mlp, ("fsdp", "ctx"), scatter_dimension=0, tiled=True),
        lax.psum_scatter(grad_weight_in, ("fsdp", "ctx"), scatter_dimension=0, tiled=True),
        lax.psum_scatter(grad_bias_in, ("fsdp", "ctx"), scatter_dimension=0, tiled=True),
        lax.psum_scatter(grad_weight_out, ("fsdp", "ctx"), scatter_dimension=0, tiled=True),
    )
    result = output.reshape(groups, local_len, width).astype(bf16)
    return (
        result,
        grad_inputs,
        sums[0],
        sums[1],
        sums[2],
        sums[3],
        sums[4],
        sums[5],
        sums[6],
        sums[7],
        sums[8],
        sums[9],
        sums[10],
    )


def solution(mesh):
    in_specs = (
        P("fsdp", "ctx", None),
        P("fsdp", "ctx", None),
        P("fsdp", "ctx"),
        P("fsdp", "ctx"),
        P("fsdp"),
        P("fsdp"),
        P("fsdp", None),
        P("fsdp"),
        P("fsdp", None),
        P("fsdp"),
        P("fsdp"),
        P("fsdp"),
        P("fsdp", None),
        P("fsdp"),
        P("fsdp", None),
    )
    out_specs = (
        P("fsdp", "ctx", None),
        P("fsdp", "ctx", None),
        P(("fsdp", "ctx")),
        P(("fsdp", "ctx")),
        P(("fsdp", "ctx"), None),
        P(("fsdp", "ctx")),
        P(("fsdp", "ctx"), None),
        P(("fsdp", "ctx")),
        P(("fsdp", "ctx")),
        P(("fsdp", "ctx")),
        P(("fsdp", "ctx"), None),
        P(("fsdp", "ctx")),
        P(("fsdp", "ctx"), None),
    )
    return jax.shard_map(local, mesh=mesh, in_specs=in_specs, out_specs=out_specs, check_vma=False)
```

```python
from functools import partial
import math

import jax
import jax.numpy as jnp
from jax import lax
from jax.experimental import pallas as pl
from jax.experimental.pallas import tpu as pltpu
from jax.sharding import PartitionSpec as P

HEADS = 16
HD = 64
ROT = 16
CLEN = 256
QB = 256
RB = 256
PAIR = 2 * HD
bf16 = jnp.bfloat16
f32 = jnp.float32
NN = (((1,), (0,)), ((), ()))
NT = (((1,), (1,)), ((), ()))
TN = (((0,), (0,)), ((), ()))


NORM_EPS = 1e-05
MASKED = -1e30


def layer_norm(values, scaling, offset):
    average = jnp.mean(values, axis=-1, keepdims=True)
    centered = values - average
    variance = jnp.mean(centered * centered, axis=-1, keepdims=True)
    return centered * lax.rsqrt(variance + NORM_EPS) * scaling + offset


def rotary_tables(positions):
    halfway = ROT // 2
    spacing = jnp.arange(halfway, dtype=jnp.float32) * (2.0 / ROT)
    inverse = jnp.exp(-math.log(10000.0) * spacing)
    angles = positions.astype(jnp.float32)[..., None] * inverse
    return (jnp.cos(angles), jnp.sin(angles))


def rotate(heads_in, cosine, sine):
    halfway = ROT // 2
    cosine = cosine[..., None, :]
    sine = sine[..., None, :]
    first = heads_in[..., :halfway]
    second = heads_in[..., halfway:ROT]
    return jnp.concatenate(
        [first * cosine - second * sine, second * cosine + first * sine, heads_in[..., ROT:]],
        axis=-1,
    )


def unrotate(grads_in, cosine, sine):
    halfway = ROT // 2
    cosine = cosine[..., None, :]
    sine = sine[..., None, :]
    first = grads_in[..., :halfway]
    second = grads_in[..., halfway:ROT]
    return jnp.concatenate(
        [first * cosine + second * sine, second * cosine - first * sine, grads_in[..., ROT:]],
        axis=-1,
    )


def allowed_mask(query_pos, query_seg, key_pos, key_seg):
    same_doc = (key_seg[:, None, :] == 0) | (key_seg[:, None, :] == query_seg[:, :, None])
    causal = key_pos[:, None, :] <= query_pos[:, :, None]
    return (same_doc & causal)[:, None]


def scores_of(queries, keys_blk):
    return jnp.einsum("gqhd,gkhd->ghqk", queries, keys_blk, preferred_element_type=jnp.float32)


def block_grads(queries, grad_att, log_total, delta, mask, keys_blk, values_blk):
    probs = jnp.where(mask, jnp.exp(scores_of(queries, keys_blk) - log_total[..., None]), 0.0)
    dprobs = jnp.einsum("gqhd,gkhd->ghqk", grad_att, values_blk, preferred_element_type=jnp.float32)
    grad_scores = (probs * (dprobs - delta[..., None])).astype(jnp.bfloat16)
    return (probs.astype(jnp.bfloat16), grad_scores)


def mm(a, b, dims):
    return lax.dot_general(a, b, dims, preferred_element_type=f32)


def row_stats(x):
    average = jnp.mean(x, axis=1, keepdims=True)
    centered = x - average
    return centered, lax.rsqrt(jnp.mean(centered * centered, axis=1, keepdims=True) + NORM_EPS)


def norm_rows(x, scaling, offset):
    centered, inverse = row_stats(x)
    return (centered * inverse * scaling + offset).astype(bf16)


def norm_back(x, grad, scaling):
    centered, inverse = row_stats(x)
    unit = centered * inverse
    e = grad * scaling
    inner = e - jnp.mean(e, axis=1, keepdims=True) - unit * jnp.mean(e * unit, axis=1, keepdims=True)
    return inverse * inner, grad * unit


def col_sum(a):
    return jnp.sum(a, axis=0, keepdims=True)


def vmem(*shape, dtype=f32):
    return pltpu.VMEM(shape, dtype)


def params():
    return pltpu.CompilerParams(vmem_limit_bytes=60 << 20)


ROOT = math.sqrt(0.5)
DENS = 1.0 / math.sqrt(2.0 * math.pi)


def reorder(order_ref, source, target):
    size = source.shape[1] // order_ref.shape[0]
    for i in range(order_ref.shape[0]):
        at = pl.multiple_of(order_ref[i] * size, size)
        target[:, i * size:(i + 1) * size] = source[:, pl.ds(at, size)]


def mlp_kernel(order_ref, x_ref, c_ref, gain_ref, shift_ref, win_ref, bin_ref, wout_ref,
               out_ref, gin_ref, dwin_send, dwin_keep, dwout_send, dwout_keep, dbin_ref, dbout_ref, dgain_ref, dshift_ref,
               h_ref, turned_ref, act_ref, gp_ref, gh_ref):
    step = pl.program_id(0)
    rows = x_ref.shape[0]
    blocks = [slice(r, r + RB) for r in range(0, rows, RB)]

    @pl.when(step == 0)
    def _():
        for r in blocks:
            h_ref[r, :] = norm_rows(x_ref[r, :].astype(f32), gain_ref[...], shift_ref[...])
            out_ref[r, :] = jnp.zeros((RB, out_ref.shape[1]), f32)
            gh_ref[r, :] = jnp.zeros((RB, gh_ref.shape[1]), f32)
        reorder(order_ref, h_ref, turned_ref)

    dbin = jnp.zeros(dbin_ref.shape, f32)
    for r in blocks:
        pre = mm(h_ref[r, :], win_ref[...], NN) + bin_ref[...]
        phi = 0.5 + 0.5 * lax.erf(pre * ROOT)
        act_ref[r, :] = (pre * phi).astype(bf16)
        gp = phi + pre * (DENS * jnp.exp(-0.5 * (pre * pre)))
        gact = mm(c_ref[r, :], wout_ref[...], NT)
        gpre = (gact * gp).astype(bf16)
        gp_ref[r, :] = gpre
        dbin = dbin + col_sum(gpre.astype(f32))
    for r in blocks:
        out_ref[r, :] += mm(act_ref[r, :], wout_ref[...], NN)
        gh_ref[r, :] += mm(gp_ref[r, :], win_ref[...], NT)
    dwout = mm(act_ref[...], c_ref[...], TN).astype(bf16)
    middle = pl.num_programs(0) // 2

    @pl.when(step < middle)
    def _():
        dwout_send[...] = dwout

    @pl.when(step >= middle)
    def _():
        dwout_keep[...] = dwout

    dwin = mm(turned_ref[...], gp_ref[...], TN).astype(bf16)
    dwin_send[...] = dwin[:dwin_send.shape[0]]
    dwin_keep[...] = dwin[dwin_send.shape[0]:]
    dbin_ref[...] = dbin

    @pl.when(step == pl.num_programs(0) - 1)
    def _():
        dgain = jnp.zeros(dgain_ref.shape, f32)
        dshift = jnp.zeros(dshift_ref.shape, f32)
        dbout = jnp.zeros(dbout_ref.shape, f32)
        for r in blocks:
            grad = gh_ref[r, :]
            back, scaled = norm_back(x_ref[r, :].astype(f32), grad, gain_ref[...])
            c = c_ref[r, :].astype(f32)
            gin_ref[r, :] = back + c
            dgain += col_sum(scaled)
            dshift += col_sum(grad)
            dbout += col_sum(c)
        dgain_ref[...] = dgain
        dshift_ref[...] = dshift
        dbout_ref[...] = dbout


def mlp(order, x, c, gain, shift, weight_in, bias_in, weight_out):
    rows, width = x.shape
    ff = weight_in.shape[1]
    steps = order.shape[0]
    fc = ff // steps
    whole = pl.BlockSpec((rows, width), lambda j, o: (0, 0))
    line = pl.BlockSpec((1, width), lambda j, o: (0, 0))
    down = pl.BlockSpec((width // 2, fc), lambda j, o: (0, o[j]))
    s = jax.ShapeDtypeStruct
    return pl.pallas_call(
        mlp_kernel,
        grid_spec=pltpu.PrefetchScalarGridSpec(
            num_scalar_prefetch=1,
            grid=(steps,),
            in_specs=[whole, whole, line, line, pl.BlockSpec((width, fc), lambda j, o: (0, o[j])),
                      pl.BlockSpec((1, fc), lambda j, o: (0, o[j])), pl.BlockSpec((fc, width), lambda j, o: (o[j], 0))],
            out_specs=[whole, whole, down, down,
                       pl.BlockSpec((fc, width), lambda j, o: (jnp.minimum(j, steps // 2 - 1), 0)),
                       pl.BlockSpec((fc, width), lambda j, o: (jnp.maximum(j - steps // 2, 0), 0)),
                       pl.BlockSpec((1, fc), lambda j, o: (0, o[j])), line, line, line],
            scratch_shapes=[vmem(rows, width, dtype=bf16), vmem(rows, width, dtype=bf16), vmem(rows, fc, dtype=bf16),
                            vmem(rows, fc, dtype=bf16), vmem(rows, width)],
        ),
        out_shape=[s((rows, width), f32), s((rows, width), f32), s((width // 2, ff), bf16), s((width // 2, ff), bf16),
                   s((ff // 2, width), bf16), s((ff // 2, width), bf16), s((1, ff), f32), s((1, width), f32),
                   s((1, width), f32), s((1, width), f32)],
        compiler_params=params(),
        cost_estimate=pl.CostEstimate(flops=12 * rows * width * ff, bytes_accessed=48 << 20, transcendentals=2 * rows * ff),
        name="mlp",
    )(order, x, c, gain.reshape(1, -1), shift.reshape(1, -1), weight_in, bias_in.reshape(1, -1), weight_out)


def turn_lanes(u, cosine, low, high, sign):
    half = ROT // 2
    parts = []
    for at in range(0, u.shape[1], PAIR):
        g = u[:, at:at + PAIR]
        parts.append(g * cosine + sign * (pltpu.roll(g, half, 1) * high - pltpu.roll(g, PAIR - half, 1) * low))
    return jnp.concatenate(parts, axis=1)


def qkv_kernel(with_q, spot_ref, x_ref, gain_ref, shift_ref, w_ref, b_ref, cos_ref, low_ref, high_ref, *outs):
    width = x_ref.shape[1]
    h = norm_rows(x_ref[...].astype(f32), gain_ref[...], shift_ref[...])
    tables = (cos_ref[...], low_ref[...], high_ref[...])
    if with_q:
        h_ref, q_ref, k_ref, v_ref = outs
        h_ref[...] = h
        q = mm(h, w_ref[:, :width], NN) + b_ref[:, :width]
        q_ref[...] = (turn_lanes(q, *tables, 1.0) * (HD ** (-0.5) / math.log(2.0))).astype(bf16)
    else:
        k_ref, v_ref = outs
    k = mm(h, w_ref[:, width:2 * width], NN) + b_ref[:, width:2 * width]
    k_ref[...] = turn_lanes(k, *tables, 1.0).astype(bf16)
    v_ref[...] = (mm(h, w_ref[:, 2 * width:], NN) + b_ref[:, 2 * width:]).astype(bf16)


def qkv(spots, x, gain, shift, weight, bias, tables, with_q):
    rows, width = x.shape
    s = jax.ShapeDtypeStruct((rows, width), bf16)
    block = pl.BlockSpec((RB, width), lambda j, spot: (j, 0))
    line = pl.BlockSpec((1, width), lambda j, spot: (0, 0))
    table = pl.BlockSpec((RB, PAIR), lambda j, spot: (spot[j], 0))
    count = 4 if with_q else 2
    return pl.pallas_call(
        partial(qkv_kernel, with_q),
        grid_spec=pltpu.PrefetchScalarGridSpec(
            num_scalar_prefetch=1,
            grid=(rows // RB,),
            in_specs=[block, line, line, pl.BlockSpec((width, 3 * width), lambda j, spot: (0, 0)),
                      pl.BlockSpec((1, 3 * width), lambda j, spot: (0, 0)), table, table, table],
            out_specs=[block] * count,
        ),
        out_shape=[s] * count,
        compiler_params=params(),
        cost_estimate=pl.CostEstimate(flops=2 * rows * width * width * (3 if with_q else 2), bytes_accessed=16 << 20,
                                      transcendentals=0),
        name="qkv_own" if with_q else "kv_remote",
    )(spots, x, gain.reshape(1, -1), shift.reshape(1, -1), weight, bias.reshape(1, -1), *tables)


def tail_kernel(groups, spot_ref, order_ref, x_ref, c_ref, h_ref, gain_ref, w_ref, cos_ref, low_ref, high_ref, gin_ref, *refs):
    att_refs, dq_refs, own_refs, come_refs = (refs[i * groups:(i + 1) * groups] for i in range(4))
    grad_ref, send_ref, keep_ref, db_ref, dgain_ref, dshift_ref, p_ref, turned_ref, gh_ref = refs[4 * groups:]
    step = pl.program_id(0)
    rows = x_ref.shape[0]
    half = rows // 2
    blocks = [slice(r, r + RB) for r in range(0, rows, RB)]
    columns = []
    for g in range(groups):
        columns += [(g, at) for at in range(0, dq_refs[g].shape[1], PAIR)]

    def put(shift):
        for r in blocks:
            spot = pl.ds(pl.multiple_of(spot_ref[r.start // RB] * RB, RB), RB)
            for to, (g, at) in enumerate(columns):
                lanes = slice(2 * at + shift, 2 * at + shift + PAIR)
                if r.start < half:
                    t = come_refs[g][r, lanes].astype(f32)
                else:
                    t = own_refs[g][r.start - half:r.stop - half, lanes].astype(f32)
                if shift == 0:
                    t = turn_lanes(t, cos_ref[spot, :], low_ref[spot, :], high_ref[spot, :], -1.0)
                p_ref[r, to * PAIR:(to + 1) * PAIR] = t.astype(bf16)

    def lay(some):
        for to, (g, at) in enumerate(columns):
            p_ref[:, to * PAIR:(to + 1) * PAIR] = some[g][:, at:at + PAIR]

    def give(dw):
        send_ref[...] = dw[:send_ref.shape[0]]
        keep_ref[...] = dw[send_ref.shape[0]:]

    @pl.when(step == 0)
    def _():
        lay(att_refs)
        reorder(order_ref, p_ref, turned_ref)
        give(mm(turned_ref[...], c_ref[...], TN).astype(bf16))

    @pl.when(step == 1)
    def _():
        reorder(order_ref, h_ref, turned_ref)
        lay(dq_refs)

    @pl.when(step == 2)
    def _():
        put(0)

    @pl.when(step == 3)
    def _():
        put(PAIR)

    @pl.when(step == 1)
    def _():
        for r in blocks:
            gh_ref[r, :] = mm(p_ref[r, :], w_ref[...], NT)

    @pl.when(step > 1)
    def _():
        for r in blocks:
            gh_ref[r, :] += mm(p_ref[r, :], w_ref[...], NT)

    @pl.when(step > 0)
    def _():
        give(mm(turned_ref[...], p_ref[...], TN).astype(bf16))
        db = jnp.zeros(db_ref.shape, f32)
        for r in blocks:
            db += col_sum(p_ref[r, :].astype(f32))
        db_ref[...] = db

    @pl.when(step == 3)
    def _():
        dgain = jnp.zeros(dgain_ref.shape, f32)
        dshift = jnp.zeros(dshift_ref.shape, f32)
        for r in blocks:
            grad = gh_ref[r, :]
            back, scaled = norm_back(x_ref[r, :].astype(f32), grad, gain_ref[...])
            grad_ref[r, :] = back + gin_ref[r, :]
            dgain += col_sum(scaled)
            dshift += col_sum(grad)
        dgain_ref[...] = dgain
        dshift_ref[...] = dshift


def tail(spots, order, x, c, h, gain, weights, tables, gin, attended, dqs, owns, comes):
    rows, width = x.shape
    groups = len(dqs)
    s = jax.ShapeDtypeStruct

    def full(a):
        return pl.BlockSpec(a.shape, lambda j, spot, o: (0, 0))

    def behind(j):
        return jnp.maximum(j - 1, 0)

    line = pl.BlockSpec((1, width), lambda j, spot, o: (0, 0))
    down = pl.BlockSpec((width // 2, width), lambda j, spot, o: (0, lax.rem(j + 3, 4)))
    arrays = [*tables, gin, *attended, *dqs, *owns, *comes]
    return pl.pallas_call(
        partial(tail_kernel, groups),
        grid_spec=pltpu.PrefetchScalarGridSpec(
            num_scalar_prefetch=2,
            grid=(4,),
            in_specs=[full(x), full(c), full(h), line, pl.BlockSpec((width, width), lambda j, spot, o: (0, behind(j)))]
            + [full(a) for a in arrays],
            out_specs=[full(x), down, down, pl.BlockSpec((1, width), lambda j, spot, o: (0, behind(j))), line, line],
            scratch_shapes=[vmem(rows, width, dtype=bf16), vmem(rows, width, dtype=bf16), vmem(rows, width)],
        ),
        out_shape=[s((rows, width), f32), s((width // 2, 4 * width), bf16), s((width // 2, 4 * width), bf16),
                   s((1, 3 * width), f32), s((1, width), f32), s((1, width), f32)],
        compiler_params=params(),
        cost_estimate=pl.CostEstimate(flops=14 * rows * width * width, bytes_accessed=32 << 20, transcendentals=0),
        name="tail",
    )(spots, order, x, c, h, gain.reshape(1, -1), weights, *arrays)


def join_kernel(groups, x_ref, w_ref, mlp_ref, b_ref, *refs):
    att_refs, (out_ref, att_ref) = refs[:groups], refs[groups:]
    at = 0
    for ref in att_refs:
        att_ref[:, at:at + ref.shape[1]] = ref[...]
        at += ref.shape[1]
    out = x_ref[...].astype(f32) + mm(att_ref[...], w_ref[...], NN) + mlp_ref[...] + b_ref[...]
    out_ref[...] = out.astype(bf16)


def join(x, attended, weights, mlp_out, bias):
    rows, width = x.shape
    s = jax.ShapeDtypeStruct
    block = pl.BlockSpec((RB, width), lambda j: (j, 0))
    return pl.pallas_call(
        partial(join_kernel, len(attended)),
        grid=(rows // RB,),
        in_specs=[block, pl.BlockSpec((width, width), lambda j: (0, 3)), block, pl.BlockSpec((1, width), lambda j: (0, 0))]
        + [pl.BlockSpec((RB, a.shape[1]), lambda j: (j, 0)) for a in attended],
        out_specs=block,
        out_shape=s((rows, width), bf16),
        scratch_shapes=[vmem(RB, width, dtype=bf16)],
        compiler_params=params(),
        cost_estimate=pl.CostEstimate(flops=2 * rows * width * width, bytes_accessed=12 << 20, transcendentals=0),
        name="join",
    )(x, weights, mlp_out, bias.reshape(1, -1), *attended)


def spread_kernel(c_ref, w_ref, out_ref):
    out_ref[...] = mm(c_ref[...], w_ref[...], NT).astype(bf16)


def spread(c, weights):
    rows, width = c.shape
    block = pl.BlockSpec((RB, width), lambda j: (j, 0))
    return pl.pallas_call(
        spread_kernel,
        grid=(rows // RB,),
        in_specs=[block, pl.BlockSpec((width, width), lambda j: (0, 3))],
        out_specs=block,
        out_shape=jax.ShapeDtypeStruct((rows, width), bf16),
        compiler_params=params(),
        cost_estimate=pl.CostEstimate(flops=2 * rows * width * width, bytes_accessed=8 << 20, transcendentals=0),
        name="spread",
    )(c, weights)


def fold(x, op):
    return op(x.reshape(x.shape[0] // 8, 8, x.shape[1]), axis=0)


def eye(size):
    return (lax.broadcasted_iota(jnp.int32, (size, size), 0) == lax.broadcasted_iota(jnp.int32, (size, size), 1)).astype(bf16)


def attention_kernel(half, n, kind_ref, owner_ref, cos_ref, sin_ref, q_ref, do_ref, *refs):
    k_refs, v_refs = refs[:n], refs[n:2 * n]
    o_ref, dq_ref = refs[2 * n:2 * n + 2]
    all_ref, cont_ref = refs[2 * n + 2:2 * n + 4]
    kt_ref, vt_ref, s_ref, p_ref, ds_ref, dka_ref, dva_ref = refs[2 * n + 4:]
    per = half // QB
    wide = n * half
    count = wide // QB
    spots = [(0, c * QB) for c in range(per)] + [(s, c * QB) for s in range(1, n) for c in range(per)]

    ident = eye(PAIR)
    for refs_in, out in ((k_refs, kt_ref), (v_refs, vt_ref)):
        for c, (s, at) in enumerate(spots):
            out[:, c * QB:(c + 1) * QB] = refs_in[s][at:at + QB, :].T
        for c in range(per):
            out[:, wide + c * QB:wide + (c + 1) * QB] = refs_in[0][half + c * QB:half + (c + 1) * QB, :].T
    dka_ref[...] = jnp.zeros_like(dka_ref)
    dva_ref[...] = jnp.zeros_like(dva_ref)


    def block(qb, carry):
        own = pl.ds(pl.multiple_of(qb * QB, QB), QB)
        slot = pl.ds(pl.multiple_of(jnp.where(qb < per, qb * QB, wide + (qb - per) * QB), QB), QB)
        zero = jnp.zeros((), bf16)
        causal = lax.broadcasted_iota(jnp.int32, (QB, QB), 0) <= lax.broadcasted_iota(jnp.int32, (QB, QB), 1)
        left = lax.broadcasted_iota(jnp.int32, (QB, PAIR), 1) < HD

        def by_head(a):
            return jnp.where(left, a, zero), jnp.where(left, zero, a)

        def keys_of(some, c):
            if c == count:
                return some[0][own, :]
            s, at = spots[c]
            return some[s][at:at + QB, :]

        def cut(c):
            return slice(c * QB, (c + 1) * QB)

        ident = eye(QB)
        q_heads = by_head(q_ref[own, :])
        do_t = mm(eye(PAIR), do_ref[own, :], NT)
        upper = lax.broadcasted_iota(jnp.int32, (PAIR, QB), 0) < HD
        q_t = mm(eye(PAIR), q_ref[own, :], NT).astype(bf16)
        q_cols = jnp.where(upper, q_t, zero), jnp.where(upper, zero, q_t)
        peaks, norms, outs, deltas, scaled = [None, None], [None, None], [None, None], [None, None], [None, None]

        def scores(h):
            peak = jnp.full((8, QB), MASKED, f32)
            for c in range(count + 1):
                s = mm(keys_of(k_refs, c), q_cols[h], NN)
                if c == count:
                    s = jnp.where(causal, s, MASKED)
                    top = fold(s, jnp.max)
                else:
                    top = fold(s, jnp.max) + kind_ref[qb, c]
                s_ref[h, cut(c)] = s
                peak = jnp.maximum(peak, top)
            peaks[h] = jnp.max(peak, axis=0, keepdims=True)

        def weigh(h):
            total = jnp.zeros((8, QB), f32)
            for c in range(count + 1):
                bias = -peaks[h] if c == count else kind_ref[qb, c] - peaks[h]
                e = jnp.exp2(s_ref[h, cut(c)] + bias)
                total = total + fold(e, jnp.sum)
                p_ref[h, cut(c)] = e.astype(bf16)
            norms[h] = 1.0 / jnp.sum(total, axis=0, keepdims=True)

        def attend(h):
            lines = slice(h * HD, (h + 1) * HD)
            out = mm(vt_ref[lines, 0:wide], p_ref[h, 0:wide], NN) + mm(vt_ref[lines, slot], p_ref[h, wide:], NN)
            outs[h] = out * norms[h]
            deltas[h] = jnp.sum(outs[h] * do_t[lines], axis=0, keepdims=True) * norms[h]
            scaled[h] = do_t[lines] * norms[h]

        scores(0)
        scores(1)
        weigh(0)
        attend(0)
        weigh(1)
        attend(1)
        d_t = jnp.concatenate(scaled, axis=0).astype(bf16)
        d_cols = jnp.where(upper, d_t, zero), jnp.where(upper, zero, d_t)
        do_heads = by_head(mm(ident, d_t, NT).astype(bf16))
        grads = []
        for h in range(2):
            lines = slice(h * HD, (h + 1) * HD)
            for c in range(count + 1):
                dp = mm(keys_of(v_refs, c), d_cols[h], NN)
                ds_ref[h, cut(c)] = (p_ref[h, cut(c)].astype(f32) * (dp - deltas[h])).astype(bf16)
            dq = mm(kt_ref[lines, 0:wide], ds_ref[h, 0:wide], NN) + mm(kt_ref[lines, slot], ds_ref[h, wide:], NN)
            a, b = dq[:ROT // 2], dq[ROT // 2:ROT]
            cosine, sine = cos_ref[:, own], sin_ref[:, own]
            grads.append(jnp.concatenate([a * cosine + b * sine, b * cosine - a * sine, dq[ROT:]], axis=0))
        for c in range(count + 1):
            at = slot if c == count else cut(c)
            dva_ref[at, :] += mm(p_ref[0, cut(c)], do_heads[0], NN) + mm(p_ref[1, cut(c)], do_heads[1], NN)
            dka_ref[at, :] += mm(ds_ref[0, cut(c)], q_heads[0], NN) + mm(ds_ref[1, cut(c)], q_heads[1], NN)
        o_ref[own, :] = mm(ident, jnp.concatenate(outs, axis=0).astype(bf16), NT).astype(bf16)
        dq_ref[own, :] = mm(ident, (jnp.concatenate(grads, axis=0) * (HD ** (-0.5))).astype(bf16), NT).astype(bf16)

        return carry

    lax.fori_loop(0, 2 * per, block, 0)

    def flush(out, to, frm):
        rows = pl.ds(to, half)
        out[rows, :PAIR] = (dka_ref[frm:frm + half, :] * math.log(2.0)).astype(bf16)
        out[rows, PAIR:] = dva_ref[frm:frm + half, :].astype(bf16)

    flush(cont_ref, 0, wide)
    for s in range(n):
        flush(all_ref, pl.multiple_of(owner_ref[s] * half, half), s * half)


def attention(kind, owners, cos_t, sin_t, q, do, ks, vs, first, pairs):
    rows = q.shape[0]
    half = rows // 2
    n = len(ks)
    wide = n * half
    keys = wide + half
    total = wide + QB
    qspec = pl.BlockSpec((rows, PAIR), lambda p: (0, p + first))
    ospec = pl.BlockSpec((rows, PAIR), lambda p: (0, p))
    table = pl.BlockSpec((ROT // 2, rows), lambda p: (0, 0))
    kspecs = [pl.BlockSpec((k.shape[0], PAIR), lambda p: (0, p + first)) for k in ks]
    gspecs = [pl.BlockSpec((size, 2 * PAIR), lambda p: (0, p)) for size in (wide, half)]
    s = jax.ShapeDtypeStruct
    pieces = pairs * rows // QB
    return pl.pallas_call(
        partial(attention_kernel, half, n),
        grid=(pairs,),
        in_specs=[pl.BlockSpec(memory_space=pltpu.SMEM), pl.BlockSpec(memory_space=pltpu.SMEM), table, table, qspec, qspec] + kspecs + kspecs,
        out_specs=[ospec, ospec] + gspecs,
        out_shape=[s((rows, pairs * PAIR), bf16), s((rows, pairs * PAIR), bf16)]
        + [s((size, 2 * pairs * PAIR), bf16) for size in (wide, half)],
        scratch_shapes=[pltpu.VMEM((PAIR, keys), bf16), pltpu.VMEM((PAIR, keys), bf16),
                        pltpu.VMEM((2, total, QB), f32), pltpu.VMEM((2, total, QB), bf16),
                        pltpu.VMEM((2, total, QB), bf16),
                        pltpu.VMEM((keys, PAIR), f32), pltpu.VMEM((keys, PAIR), f32)],
        compiler_params=pltpu.CompilerParams(vmem_limit_bytes=60 << 20),
        cost_estimate=pl.CostEstimate(flops=pieces * 24 * total * QB * HD * 4, bytes_accessed=16 << 20,
                                      transcendentals=pieces * 2 * total * QB),
        name="attention",
    )(kind, owners, cos_t, sin_t, q, do, *ks, *vs)


def pairs_of(bit, size):
    return [(a, a ^ bit) for a in range(size)]


def pick(a, axis, i):
    return lax.dynamic_index_in_dim(a, i, axis, keepdims=False)


def plus(a, b):
    return (a.astype(f32) + b.astype(f32)).astype(bf16)


def core_step(send, keep):
    rows, cols = send.shape
    size = rows // 8
    got = lax.ppermute(send, "fsdp", pairs_of(1, 8)).reshape(2, 2, 2, size, cols)
    keep = keep.reshape(2, 2, 2, size, cols)

    def part(*at):
        return plus(keep[at], got[at])

    every = slice(None)
    return part(every, 1, 0), part(every, 0, 0), part(1, every, 1), part(0, every, 1)


def side_step(send_a, keep_a, send_b, keep_b):
    got_a = lax.ppermute(send_a, "fsdp", pairs_of(2, 8))
    got_b = lax.ppermute(send_b, "fsdp", pairs_of(4, 8))
    return plus(keep_a[1], got_a[1]), plus(keep_a[0], got_a[0]), plus(keep_b[1], got_b[1]), plus(keep_b[0], got_b[0])


def last_step(send_a, keep_a, send_b, keep_b):
    got_a = lax.ppermute(send_a, "fsdp", pairs_of(4, 8))
    got_b = lax.ppermute(send_b, "fsdp", pairs_of(2, 8))
    part = jnp.concatenate([plus(keep_a, got_a), plus(keep_b, got_b)], axis=0)
    return lax.psum_scatter(part, "ctx", scatter_dimension=0, tiled=True)


def scatter_sum(send, keep):
    return last_step(*side_step(*core_step(send, keep)))


def after(value, *others):
    return lax.optimization_barrier((value, *others))[0]


def fast(inputs, cotangent, positions, segments, ln1_gain, ln1_bias, w_qkv, b_qkv, w_attn_out, b_out,
         ln2_gain, ln2_bias, w_in, b_in, w_out):
    x, grad_out, pos = inputs[0], cotangent[0], positions[0]
    rows, width = x.shape
    half = rows // 2
    n = lax.axis_size("ctx")
    ring = [(i, (i + 1) % n) for i in range(n)]
    back = [(i, (i - 1) % n) for i in range(n)]
    xs, spots = [x], [pos[::RB] // RB]
    run = x[:half]
    for s in range(1, n):
        run = lax.ppermute(run, "ctx", ring)
        xs.append(run)
        spots.append(lax.ppermute(spots[0][:half // RB], "ctx", [(i, (i + s) % n) for i in range(n)]))
    mine = (ln1_gain, ln1_bias, b_qkv, b_out, ln2_gain, ln2_bias, b_in)
    small = lax.all_gather(jnp.concatenate(mine).reshape(1, -1), "fsdp", axis=0, tiled=True)
    full, at = [], 0
    for a in mine:
        full.append(small[:, at:at + a.shape[0]].reshape(-1).astype(f32))
        at += a.shape[0]
    gain_attn, shift_attn, bias_qkv, bias_out, gain_mlp, shift_mlp, bias_in = full
    weights = lax.all_gather(jnp.concatenate([w_qkv, w_attn_out], axis=1), "fsdp", axis=0, tiled=True)

    lane = jnp.arange(PAIR) % HD
    inverse = jnp.exp(-math.log(10000.0) * (2.0 / ROT) * (lane % (ROT // 2)).astype(f32))
    angles = jnp.arange(n * half + CLEN).astype(f32)[:, None] * inverse[None, :]
    sine = jnp.sin(angles)
    tables = (jnp.where(lane < ROT, jnp.cos(angles), 1.0), jnp.where(lane < ROT // 2, sine, 0.0),
              jnp.where((lane >= ROT // 2) & (lane < ROT), sine, 0.0))
    angles_t = pos.astype(f32)[None, :] * inverse[:ROT // 2, None]
    cos_t, sin_t = jnp.cos(angles_t), jnp.sin(angles_t)

    normed, queries, key, value = qkv(spots[0], x, gain_attn, shift_attn, weights, bias_qkv, tables, True)
    keys, values = [key], [value]
    for s in range(1, n):
        key, value = qkv(spots[s], xs[s], gain_attn, shift_attn, weights, bias_qkv, tables, False)
        keys.append(key)
        values.append(value)
    grad_att = spread(grad_out, weights)
    weight_in = lax.all_gather(after(w_in, queries), "fsdp", axis=0, tiled=True)
    weight_out = lax.all_gather(after(w_out, queries), "fsdp", axis=0, tiled=True)

    per = half // QB
    earlier = jnp.stack([spots[s][0] < spots[0][0] for s in range(1, n)])
    local_row = jnp.arange(2 * per)[:, None]
    seen_own = local_row > jnp.arange(per)[None, :]
    seen_far = jnp.repeat(earlier[None, :] | (local_row >= per), per, axis=1)
    kind = jnp.where(jnp.concatenate([seen_own, seen_far], axis=1), 0.0, MASKED).astype(f32)

    me, place = lax.axis_index("fsdp"), lax.axis_index("ctx")
    relative = [4 * dy + 2 * dx + 1 - keep for keep in (0, 1) for dy in (0, 1) for dx in (0, 1)]
    order = jnp.bitwise_xor(me, jnp.array(relative, jnp.int32))
    owners = lax.rem(place + n - jnp.arange(n), n)
    attended, grad_q, own_kv, come_kv = [], [], [], []

    def attend(first, count, wait):
        out = attention(kind, owners, cos_t, sin_t, after(queries, *wait), grad_att, keys, values, first, count)
        attended.append(out[0])
        grad_q.append(out[1])
        come_kv.append(lax.psum_scatter(out[2], "ctx", scatter_dimension=0, tiled=True))
        own_kv.append(out[3])

    attend(0, 5, ())
    mlp_out, grad_mlp, in_send, in_keep, out_send, out_keep, db_in, db_out, dgain_mlp, dshift_mlp = mlp(
        order, after(x, *attended), grad_out, gain_mlp, shift_mlp, weight_in, bias_in, weight_out)
    attend(5, 2, (mlp_out,))
    steps_out = core_step(out_send, out_keep)
    steps_in = core_step(in_send, in_keep)
    attend(7, 1, (*attended, *steps_out, *steps_in))
    output = join(x, attended, weights, mlp_out, bias_out)
    steps_out = side_step(*steps_out)
    steps_in = side_step(*steps_in)
    grad_inputs, qkv_send, qkv_keep, db_qkv, dgain_attn, dshift_attn = tail(
        spots[0], order, after(x, output, *steps_out, *steps_in), grad_out, normed, gain_attn, weights, tables, grad_mlp,
        attended, grad_q, own_kv, come_kv)
    sum_out = last_step(*steps_out)
    sum_in = last_step(*steps_in)
    both = scatter_sum(qkv_send, qkv_keep)
    sum_qkv, sum_attn = both[:, :3 * width], both[:, 3 * width:]
    smalls = [a.reshape(width, -1) for a in (dgain_attn, dshift_attn, db_qkv, db_out, dgain_mlp, dshift_mlp, db_in)]
    used = sum(a.shape[1] for a in smalls)
    packed = jnp.concatenate(smalls + [jnp.zeros((width, PAIR - used), f32)], axis=1).astype(bf16)
    packed = packed.reshape(8, width // 8, PAIR)[order].reshape(2, width // 2, PAIR)
    packed = scatter_sum(packed[0], packed[1]).astype(f32)
    done, at = [], 0
    for a in smalls:
        done.append(packed[:, at:at + a.shape[1]].reshape(-1))
        at += a.shape[1]
    return (output[None], grad_inputs[None], done[0], done[1], sum_qkv.astype(f32), done[2], sum_attn.astype(f32),
            done[3], done[4], done[5], sum_in.astype(f32), done[6], sum_out.astype(f32))


def local(*args):
    half = args[0].shape[1] // 2
    if args[0].shape[0] == 1 and half % CLEN == 0 and lax.axis_size("fsdp") == 8:
        return fast(*args)
    return generic(*args)


def generic(
    inputs,
    cotangent,
    positions,
    segments,
    ln1_gain,
    ln1_bias,
    w_qkv,
    b_qkv,
    w_attn_out,
    b_out,
    ln2_gain,
    ln2_bias,
    w_in,
    b_in,
    w_out,
):
    shards = (
        ln1_gain,
        ln1_bias,
        w_qkv,
        b_qkv,
        w_attn_out,
        b_out,
        ln2_gain,
        ln2_bias,
        w_in,
        b_in,
        w_out,
    )
    params = (
        lax.all_gather(shards[0], "fsdp", axis=0, tiled=True),
        lax.all_gather(shards[1], "fsdp", axis=0, tiled=True),
        lax.all_gather(shards[2], "fsdp", axis=0, tiled=True),
        lax.all_gather(shards[3], "fsdp", axis=0, tiled=True),
        lax.all_gather(shards[4], "fsdp", axis=0, tiled=True),
        lax.all_gather(shards[5], "fsdp", axis=0, tiled=True),
        lax.all_gather(shards[6], "fsdp", axis=0, tiled=True),
        lax.all_gather(shards[7], "fsdp", axis=0, tiled=True),
        lax.all_gather(shards[8], "fsdp", axis=0, tiled=True),
        lax.all_gather(shards[9], "fsdp", axis=0, tiled=True),
        lax.all_gather(shards[10], "fsdp", axis=0, tiled=True),
    )
    groups, local_len, width = inputs.shape
    rows_total = groups * local_len
    block = math.gcd(local_len, 256)
    label_pos, label_seg = (
        lax.all_gather(positions, "ctx", axis=1, tiled=True),
        lax.all_gather(segments, "ctx", axis=1, tiled=True),
    )
    count = label_pos.shape[1] // block
    f32 = jnp.float32
    bf16 = jnp.bfloat16
    (
        gain_attn,
        shift_attn,
        weight_qkv,
        bias_qkv,
        weight_attn,
        bias_out,
        gain_mlp,
        shift_mlp,
        weight_in,
        bias_in,
        weight_out,
    ) = params
    flat_in = inputs.reshape(rows_total, width).astype(f32)
    normed_attn = layer_norm(flat_in, gain_attn.astype(f32), shift_attn.astype(f32)).astype(bf16)
    normed_mlp = layer_norm(flat_in, gain_mlp.astype(f32), shift_mlp.astype(f32)).astype(bf16)
    projected = jnp.dot(normed_attn, weight_qkv, preferred_element_type=f32) + bias_qkv.astype(f32)
    cosine, sine = rotary_tables(positions)

    def split_heads(columns):
        return columns.reshape(groups, local_len, HEADS, HD)

    scale = HD ** (-0.5)
    queries = (rotate(split_heads(projected[:, :width]), cosine, sine) * scale).astype(bf16)
    keys_own = rotate(split_heads(projected[:, width : 2 * width]), cosine, sine).astype(bf16)
    values_own = split_heads(projected[:, 2 * width :]).astype(bf16)
    keys_all, values_all = (
        lax.all_gather(keys_own, "ctx", axis=1, tiled=True),
        lax.all_gather(values_own, "ctx", axis=1, tiled=True),
    )

    def key_block(index):
        start = index * block
        keys_blk = lax.dynamic_slice_in_dim(keys_all, start, block, 1)
        values_blk = lax.dynamic_slice_in_dim(values_all, start, block, 1)
        mask = allowed_mask(
            positions,
            segments,
            lax.dynamic_slice_in_dim(label_pos, start, block, 1),
            lax.dynamic_slice_in_dim(label_seg, start, block, 1),
        )
        return (keys_blk, values_blk, mask)

    def total_step(carry, index):
        peak, total = carry
        keys_blk, values_blk, mask = key_block(index)
        scores = jnp.where(mask, scores_of(queries, keys_blk), MASKED)
        fresh = jnp.maximum(peak, jnp.max(scores, axis=-1))
        added = jnp.sum(jnp.where(mask, jnp.exp(scores - fresh[..., None]), 0.0), axis=-1)
        return ((fresh, total * jnp.exp(peak - fresh) + added), None)

    stat_shape = (groups, HEADS, local_len)
    (peak, total), unused = lax.scan(
        total_step,
        (jnp.full(stat_shape, MASKED, f32), jnp.zeros(stat_shape, f32)),
        jnp.arange(count),
    )
    log_total = peak + jnp.log(total)

    def attend_step(rounded_sum, index):
        keys_blk, values_blk, mask = key_block(index)
        probs = jnp.where(mask, jnp.exp(scores_of(queries, keys_blk) - log_total[..., None]), 0.0)
        rounded_sum = rounded_sum + jnp.einsum(
            "ghqk,gkhd->gqhd", probs.astype(bf16), values_blk, preferred_element_type=f32
        )
        return (rounded_sum, None)

    head_shape = (groups, local_len, HEADS, HD)
    rounded_sum, unused = lax.scan(attend_step, jnp.zeros(head_shape, f32), jnp.arange(count))
    attended = rounded_sum.reshape(rows_total, width).astype(bf16)
    pre_act = jnp.dot(normed_mlp, weight_in, preferred_element_type=f32) + bias_in.astype(f32)
    activated = jax.nn.gelu(pre_act, approximate=False).astype(bf16)
    output = (
        flat_in
        + jnp.dot(attended, weight_attn, preferred_element_type=f32)
        + jnp.dot(activated, weight_out, preferred_element_type=f32)
        + bias_out.astype(f32)
    )
    (
        gain_attn,
        shift_attn,
        weight_qkv,
        bias_qkv,
        weight_attn,
        bias_out,
        gain_mlp,
        shift_mlp,
        weight_in,
        bias_in,
        weight_out,
    ) = params
    grad_out = cotangent.reshape(rows_total, width)
    grad_bias_out = jnp.sum(grad_out.astype(f32), axis=0)
    grad_weight_out = jnp.einsum("rf,rd->fd", activated, grad_out, preferred_element_type=f32)
    grad_act = jnp.einsum("rd,fd->rf", grad_out, weight_out, preferred_element_type=f32)
    unused, gelu_back = jax.vjp(partial(jax.nn.gelu, approximate=False), pre_act)
    grad_pre = gelu_back(grad_act)[0].astype(bf16)
    grad_weight_in = jnp.einsum("rd,rf->df", normed_mlp, grad_pre, preferred_element_type=f32)
    grad_bias_in = jnp.sum(grad_pre.astype(f32), axis=0)
    grad_normed_mlp = jnp.einsum("rf,df->rd", grad_pre, weight_in, preferred_element_type=f32)
    grad_weight_attn = jnp.einsum("ra,rd->ad", attended, grad_out, preferred_element_type=f32)
    grad_att = (
        jnp.einsum("rd,ad->ra", grad_out, weight_attn, preferred_element_type=f32)
        .astype(bf16)
        .reshape(head_shape)
    )
    delta = jnp.einsum(
        "gqhd,gqhd->ghq", grad_att.astype(f32), rounded_sum, precision=lax.Precision.HIGHEST
    )

    def back_step(carry, index):
        keys_blk, values_blk, mask = key_block(index)
        rounded, grad_scores = block_grads(
            queries, grad_att, log_total, delta, mask, keys_blk, values_blk
        )
        carry = carry + jnp.einsum(
            "ghqk,gkhd->gqhd", grad_scores, keys_blk, preferred_element_type=f32
        )
        key_term = jnp.einsum("ghqk,gqhd->gkhd", grad_scores, queries, preferred_element_type=f32)
        value_term = jnp.einsum("ghqk,gqhd->gkhd", rounded, grad_att, preferred_element_type=f32)
        return (carry, (key_term, value_term))

    grad_queries, (key_terms, value_terms) = lax.scan(
        back_step, jnp.zeros(head_shape, f32), jnp.arange(count)
    )
    key_sums, value_sums = (
        lax.psum_scatter(
            key_terms.astype(jnp.bfloat16), "ctx", scatter_dimension=0, tiled=True
        ).astype(jnp.float32),
        lax.psum_scatter(
            value_terms.astype(jnp.bfloat16), "ctx", scatter_dimension=0, tiled=True
        ).astype(jnp.float32),
    )
    grad_keys = jnp.transpose(key_sums, (1, 0, 2, 3, 4)).reshape(head_shape)
    grad_values = jnp.transpose(value_sums, (1, 0, 2, 3, 4)).reshape(head_shape)
    grad_q_pre = unrotate(grad_queries * scale, cosine, sine).reshape(rows_total, width)
    grad_k_pre = unrotate(grad_keys, cosine, sine).reshape(rows_total, width)
    grad_projected = jnp.concatenate(
        [grad_q_pre, grad_k_pre, grad_values.reshape(rows_total, width)], axis=1
    ).astype(bf16)
    grad_weight_qkv = jnp.einsum(
        "rd,re->de", normed_attn, grad_projected, preferred_element_type=f32
    )
    grad_bias_qkv = jnp.sum(grad_projected.astype(f32), axis=0)
    grad_normed_attn = jnp.einsum(
        "re,de->rd", grad_projected, weight_qkv, preferred_element_type=f32
    )
    unused, norm_back_attn = jax.vjp(
        layer_norm, flat_in, gain_attn.astype(f32), shift_attn.astype(f32)
    )
    grad_in_attn, grad_gain_attn, grad_shift_attn = norm_back_attn(grad_normed_attn)
    unused, norm_back_mlp = jax.vjp(
        layer_norm, flat_in, gain_mlp.astype(f32), shift_mlp.astype(f32)
    )
    grad_in_mlp, grad_gain_mlp, grad_shift_mlp = norm_back_mlp(grad_normed_mlp)
    grad_inputs = (grad_out.astype(f32) + grad_in_attn + grad_in_mlp).reshape(
        groups, local_len, width
    )
    sums = (
        lax.psum_scatter(grad_gain_attn, ("fsdp", "ctx"), scatter_dimension=0, tiled=True),
        lax.psum_scatter(grad_shift_attn, ("fsdp", "ctx"), scatter_dimension=0, tiled=True),
        lax.psum_scatter(grad_weight_qkv, ("fsdp", "ctx"), scatter_dimension=0, tiled=True),
        lax.psum_scatter(grad_bias_qkv, ("fsdp", "ctx"), scatter_dimension=0, tiled=True),
        lax.psum_scatter(grad_weight_attn, ("fsdp", "ctx"), scatter_dimension=0, tiled=True),
        lax.psum_scatter(grad_bias_out, ("fsdp", "ctx"), scatter_dimension=0, tiled=True),
        lax.psum_scatter(grad_gain_mlp, ("fsdp", "ctx"), scatter_dimension=0, tiled=True),
        lax.psum_scatter(grad_shift_mlp, ("fsdp", "ctx"), scatter_dimension=0, tiled=True),
        lax.psum_scatter(grad_weight_in, ("fsdp", "ctx"), scatter_dimension=0, tiled=True),
        lax.psum_scatter(grad_bias_in, ("fsdp", "ctx"), scatter_dimension=0, tiled=True),
        lax.psum_scatter(grad_weight_out, ("fsdp", "ctx"), scatter_dimension=0, tiled=True),
    )
    result = output.reshape(groups, local_len, width).astype(bf16)
    return (
        result,
        grad_inputs,
        sums[0],
        sums[1],
        sums[2],
        sums[3],
        sums[4],
        sums[5],
        sums[6],
        sums[7],
        sums[8],
        sums[9],
        sums[10],
    )


def solution(mesh):
    in_specs = (
        P("fsdp", "ctx", None),
        P("fsdp", "ctx", None),
        P("fsdp", "ctx"),
        P("fsdp", "ctx"),
        P("fsdp"),
        P("fsdp"),
        P("fsdp", None),
        P("fsdp"),
        P("fsdp", None),
        P("fsdp"),
        P("fsdp"),
        P("fsdp"),
        P("fsdp", None),
        P("fsdp"),
        P("fsdp", None),
    )
    out_specs = (
        P("fsdp", "ctx", None),
        P("fsdp", "ctx", None),
        P(("fsdp", "ctx")),
        P(("fsdp", "ctx")),
        P(("fsdp", "ctx"), None),
        P(("fsdp", "ctx")),
        P(("fsdp", "ctx"), None),
        P(("fsdp", "ctx")),
        P(("fsdp", "ctx")),
        P(("fsdp", "ctx")),
        P(("fsdp", "ctx"), None),
        P(("fsdp", "ctx")),
        P(("fsdp", "ctx"), None),
    )
    return jax.shard_map(local, mesh=mesh, in_specs=in_specs, out_specs=out_specs, check_vma=False)
```

```python
from functools import partial
import math

import jax
import jax.numpy as jnp
from jax import lax
from jax.experimental import pallas as pl
from jax.experimental.pallas import tpu as pltpu
from jax.sharding import PartitionSpec as P

HEADS = 16
HD = 64
ROT = 16
CLEN = 256
QB = 256
RB = 256
PAIR = 2 * HD
bf16 = jnp.bfloat16
f32 = jnp.float32
NN = (((1,), (0,)), ((), ()))
NT = (((1,), (1,)), ((), ()))
TN = (((0,), (0,)), ((), ()))


NORM_EPS = 1e-05
MASKED = -1e30


def layer_norm(values, scaling, offset):
    average = jnp.mean(values, axis=-1, keepdims=True)
    centered = values - average
    variance = jnp.mean(centered * centered, axis=-1, keepdims=True)
    return centered * lax.rsqrt(variance + NORM_EPS) * scaling + offset


def rotary_tables(positions):
    halfway = ROT // 2
    spacing = jnp.arange(halfway, dtype=jnp.float32) * (2.0 / ROT)
    inverse = jnp.exp(-math.log(10000.0) * spacing)
    angles = positions.astype(jnp.float32)[..., None] * inverse
    return (jnp.cos(angles), jnp.sin(angles))


def rotate(heads_in, cosine, sine):
    halfway = ROT // 2
    cosine = cosine[..., None, :]
    sine = sine[..., None, :]
    first = heads_in[..., :halfway]
    second = heads_in[..., halfway:ROT]
    return jnp.concatenate(
        [first * cosine - second * sine, second * cosine + first * sine, heads_in[..., ROT:]],
        axis=-1,
    )


def unrotate(grads_in, cosine, sine):
    halfway = ROT // 2
    cosine = cosine[..., None, :]
    sine = sine[..., None, :]
    first = grads_in[..., :halfway]
    second = grads_in[..., halfway:ROT]
    return jnp.concatenate(
        [first * cosine + second * sine, second * cosine - first * sine, grads_in[..., ROT:]],
        axis=-1,
    )


def allowed_mask(query_pos, query_seg, key_pos, key_seg):
    same_doc = (key_seg[:, None, :] == 0) | (key_seg[:, None, :] == query_seg[:, :, None])
    causal = key_pos[:, None, :] <= query_pos[:, :, None]
    return (same_doc & causal)[:, None]


def scores_of(queries, keys_blk):
    return jnp.einsum("gqhd,gkhd->ghqk", queries, keys_blk, preferred_element_type=jnp.float32)


def block_grads(queries, grad_att, log_total, delta, mask, keys_blk, values_blk):
    probs = jnp.where(mask, jnp.exp(scores_of(queries, keys_blk) - log_total[..., None]), 0.0)
    dprobs = jnp.einsum("gqhd,gkhd->ghqk", grad_att, values_blk, preferred_element_type=jnp.float32)
    grad_scores = (probs * (dprobs - delta[..., None])).astype(jnp.bfloat16)
    return (probs.astype(jnp.bfloat16), grad_scores)


def mm(a, b, dims):
    return lax.dot_general(a, b, dims, preferred_element_type=f32)


def row_stats(x):
    average = jnp.mean(x, axis=1, keepdims=True)
    centered = x - average
    return centered, lax.rsqrt(jnp.mean(centered * centered, axis=1, keepdims=True) + NORM_EPS)


def norm_rows(x, scaling, offset):
    centered, inverse = row_stats(x)
    return (centered * inverse * scaling + offset).astype(bf16)


def norm_back(x, grad, scaling):
    centered, inverse = row_stats(x)
    unit = centered * inverse
    e = grad * scaling
    inner = e - jnp.mean(e, axis=1, keepdims=True) - unit * jnp.mean(e * unit, axis=1, keepdims=True)
    return inverse * inner, grad * unit


def col_sum(a):
    return jnp.sum(a, axis=0, keepdims=True)


def vmem(*shape, dtype=f32):
    return pltpu.VMEM(shape, dtype)


def params():
    return pltpu.CompilerParams(vmem_limit_bytes=60 << 20)


ROOT = math.sqrt(0.5)
DENS = 1.0 / math.sqrt(2.0 * math.pi)


def reorder(order_ref, source, target):
    size = source.shape[1] // order_ref.shape[0]
    for i in range(order_ref.shape[0]):
        at = pl.multiple_of(order_ref[i] * size, size)
        target[:, i * size:(i + 1) * size] = source[:, pl.ds(at, size)]


def mlp_kernel(order_ref, x_ref, c_ref, gain_ref, shift_ref, win_ref, bin_ref, wout_ref,
               out_ref, gin_ref, dwin_send, dwin_keep, dwout_send, dwout_keep, dbin_ref, dbout_ref, dgain_ref, dshift_ref,
               h_ref, turned_ref, act_ref, gp_ref, gh_ref):
    step = pl.program_id(0)
    rows = x_ref.shape[0]
    blocks = [slice(r, r + RB) for r in range(0, rows, RB)]

    @pl.when(step == 0)
    def _():
        for r in blocks:
            h_ref[r, :] = norm_rows(x_ref[r, :].astype(f32), gain_ref[...], shift_ref[...])
            out_ref[r, :] = jnp.zeros((RB, out_ref.shape[1]), f32)
            gh_ref[r, :] = jnp.zeros((RB, gh_ref.shape[1]), f32)
        reorder(order_ref, h_ref, turned_ref)

    dbin = jnp.zeros(dbin_ref.shape, f32)
    for r in blocks:
        pre = mm(h_ref[r, :], win_ref[...], NN) + bin_ref[...]
        phi = 0.5 + 0.5 * lax.erf(pre * ROOT)
        act_ref[r, :] = (pre * phi).astype(bf16)
        gp = phi + pre * (DENS * jnp.exp(-0.5 * (pre * pre)))
        gact = mm(c_ref[r, :], wout_ref[...], NT)
        gpre = (gact * gp).astype(bf16)
        gp_ref[r, :] = gpre
        dbin = dbin + col_sum(gpre.astype(f32))
    for r in blocks:
        out_ref[r, :] += mm(act_ref[r, :], wout_ref[...], NN)
        gh_ref[r, :] += mm(gp_ref[r, :], win_ref[...], NT)
    dwout = mm(act_ref[...], c_ref[...], TN).astype(bf16)
    middle = pl.num_programs(0) // 2

    @pl.when(step < middle)
    def _():
        dwout_send[...] = dwout

    @pl.when(step >= middle)
    def _():
        dwout_keep[...] = dwout

    dwin = mm(turned_ref[...], gp_ref[...], TN).astype(bf16)
    dwin_send[...] = dwin[:dwin_send.shape[0]]
    dwin_keep[...] = dwin[dwin_send.shape[0]:]
    dbin_ref[...] = dbin

    @pl.when(step == pl.num_programs(0) - 1)
    def _():
        dgain = jnp.zeros(dgain_ref.shape, f32)
        dshift = jnp.zeros(dshift_ref.shape, f32)
        dbout = jnp.zeros(dbout_ref.shape, f32)
        for r in blocks:
            grad = gh_ref[r, :]
            back, scaled = norm_back(x_ref[r, :].astype(f32), grad, gain_ref[...])
            c = c_ref[r, :].astype(f32)
            gin_ref[r, :] = back + c
            dgain += col_sum(scaled)
            dshift += col_sum(grad)
            dbout += col_sum(c)
        dgain_ref[...] = dgain
        dshift_ref[...] = dshift
        dbout_ref[...] = dbout


def mlp(order, x, c, gain, shift, weight_in, bias_in, weight_out):
    rows, width = x.shape
    ff = weight_in.shape[1]
    steps = order.shape[0]
    fc = ff // steps
    whole = pl.BlockSpec((rows, width), lambda j, o: (0, 0))
    line = pl.BlockSpec((1, width), lambda j, o: (0, 0))
    down = pl.BlockSpec((width // 2, fc), lambda j, o: (0, o[j]))
    s = jax.ShapeDtypeStruct
    return pl.pallas_call(
        mlp_kernel,
        grid_spec=pltpu.PrefetchScalarGridSpec(
            num_scalar_prefetch=1,
            grid=(steps,),
            in_specs=[whole, whole, line, line, pl.BlockSpec((width, fc), lambda j, o: (0, o[j])),
                      pl.BlockSpec((1, fc), lambda j, o: (0, o[j])), pl.BlockSpec((fc, width), lambda j, o: (o[j], 0))],
            out_specs=[whole, whole, down, down,
                       pl.BlockSpec((fc, width), lambda j, o: (jnp.minimum(j, steps // 2 - 1), 0)),
                       pl.BlockSpec((fc, width), lambda j, o: (jnp.maximum(j - steps // 2, 0), 0)),
                       pl.BlockSpec((1, fc), lambda j, o: (0, o[j])), line, line, line],
            scratch_shapes=[vmem(rows, width, dtype=bf16), vmem(rows, width, dtype=bf16), vmem(rows, fc, dtype=bf16),
                            vmem(rows, fc, dtype=bf16), vmem(rows, width)],
        ),
        out_shape=[s((rows, width), f32), s((rows, width), f32), s((width // 2, ff), bf16), s((width // 2, ff), bf16),
                   s((ff // 2, width), bf16), s((ff // 2, width), bf16), s((1, ff), f32), s((1, width), f32),
                   s((1, width), f32), s((1, width), f32)],
        compiler_params=params(),
        cost_estimate=pl.CostEstimate(flops=12 * rows * width * ff, bytes_accessed=48 << 20, transcendentals=2 * rows * ff),
        name="mlp",
    )(order, x, c, gain.reshape(1, -1), shift.reshape(1, -1), weight_in, bias_in.reshape(1, -1), weight_out)


def turn_lanes(u, cosine, low, high, sign):
    half = ROT // 2
    parts = []
    for at in range(0, u.shape[1], PAIR):
        g = u[:, at:at + PAIR]
        parts.append(g * cosine + sign * (pltpu.roll(g, half, 1) * high - pltpu.roll(g, PAIR - half, 1) * low))
    return jnp.concatenate(parts, axis=1)


def qkv_kernel(with_q, spot_ref, order_ref, x_ref, gain_ref, shift_ref, w_ref, b_ref, cos_ref, low_ref, high_ref, *outs):
    width = x_ref.shape[1]
    h = norm_rows(x_ref[...].astype(f32), gain_ref[...], shift_ref[...])
    tables = (cos_ref[...], low_ref[...], high_ref[...])
    if with_q:
        h_ref, q_ref, k_ref, v_ref, plain_ref = outs
        plain_ref[...] = h
        reorder(order_ref, plain_ref, h_ref)
        q = mm(h, w_ref[:, :width], NN) + b_ref[:, :width]
        q_ref[...] = (turn_lanes(q, *tables, 1.0) * (HD ** (-0.5) / math.log(2.0))).astype(bf16)
    else:
        k_ref, v_ref = outs
    k = mm(h, w_ref[:, width:2 * width], NN) + b_ref[:, width:2 * width]
    k_ref[...] = turn_lanes(k, *tables, 1.0).astype(bf16)
    v_ref[...] = (mm(h, w_ref[:, 2 * width:], NN) + b_ref[:, 2 * width:]).astype(bf16)


def qkv(spots, order, x, gain, shift, weight, bias, tables, with_q):
    rows, width = x.shape
    s = jax.ShapeDtypeStruct((rows, width), bf16)
    block = pl.BlockSpec((RB, width), lambda j, spot, o: (j, 0))
    line = pl.BlockSpec((1, width), lambda j, spot, o: (0, 0))
    table = pl.BlockSpec((RB, PAIR), lambda j, spot, o: (spot[j], 0))
    count = 4 if with_q else 2
    return pl.pallas_call(
        partial(qkv_kernel, with_q),
        grid_spec=pltpu.PrefetchScalarGridSpec(
            num_scalar_prefetch=2,
            grid=(rows // RB,),
            in_specs=[block, line, line, pl.BlockSpec((width, 3 * width), lambda j, spot, o: (0, 0)),
                      pl.BlockSpec((1, 3 * width), lambda j, spot, o: (0, 0)), table, table, table],
            out_specs=[block] * count,
            scratch_shapes=[vmem(RB, width, dtype=bf16)] if with_q else [],
        ),
        out_shape=[s] * count,
        compiler_params=params(),
        cost_estimate=pl.CostEstimate(flops=1 << 20, bytes_accessed=1 << 16, transcendentals=0),
        name="qkv_own" if with_q else "kv_remote",
    )(spots, order, x, gain.reshape(1, -1), shift.reshape(1, -1), weight, bias.reshape(1, -1), *tables)


def first_kernel(groups, order_ref, c_ref, h_ref, w_ref, *refs):
    att_refs, dq_refs = refs[:groups], refs[groups:2 * groups]
    send_ref, keep_ref, gh_ref, db_ref, p_ref, turned_ref = refs[2 * groups:]
    step = pl.program_id(0)
    blocks = [slice(r, r + RB) for r in range(0, c_ref.shape[0], RB)]

    def lay(some):
        at = 0
        for ref in some:
            p_ref[:, at:at + ref.shape[1]] = ref[...]
            at += ref.shape[1]

    def give(dw):
        send_ref[...] = dw[:send_ref.shape[0]]
        keep_ref[...] = dw[send_ref.shape[0]:]

    @pl.when(step == 0)
    def _():
        lay(att_refs)
        reorder(order_ref, p_ref, turned_ref)
        give(mm(turned_ref[...], c_ref[...], TN).astype(bf16))

    @pl.when(step == 1)
    def _():
        lay(dq_refs)
        db = jnp.zeros(db_ref.shape, f32)
        for r in blocks:
            gh_ref[r, :] = mm(p_ref[r, :], w_ref[...], NT)
            db += col_sum(p_ref[r, :].astype(f32))
        db_ref[...] = db
        give(mm(h_ref[...], p_ref[...], TN).astype(bf16))


def first_tail(order, c, h, weights, attended, dqs):
    rows, width = c.shape
    s = jax.ShapeDtypeStruct

    def full(a):
        return pl.BlockSpec(a.shape, lambda j, o: (0, 0))

    down = pl.BlockSpec((width // 2, width), lambda j, o: (0, j))
    arrays = [*attended, *dqs]
    return pl.pallas_call(
        partial(first_kernel, len(dqs)),
        grid_spec=pltpu.PrefetchScalarGridSpec(
            num_scalar_prefetch=1,
            grid=(2,),
            in_specs=[full(c), full(h), pl.BlockSpec((width, width), lambda j, o: (0, 0))] + [full(a) for a in arrays],
            out_specs=[down, down, full(c), pl.BlockSpec((1, width), lambda j, o: (0, 0))],
            scratch_shapes=[vmem(rows, width, dtype=bf16), vmem(rows, width, dtype=bf16)],
        ),
        out_shape=[s((width // 2, 2 * width), bf16), s((width // 2, 2 * width), bf16), s((rows, width), f32), s((1, width), f32)],
        compiler_params=params(),
        cost_estimate=pl.CostEstimate(flops=6 * rows * width * width, bytes_accessed=24 << 20, transcendentals=0),
        name="first_tail",
    )(order, c, h, weights, *arrays)


def last_kernel(groups, spot_ref, x_ref, h_ref, gain_ref, w_ref, cos_ref, low_ref, high_ref, gin_ref, ghq_ref, *refs):
    own_refs, come_refs = refs[:groups], refs[groups:2 * groups]
    grad_ref, send_ref, keep_ref, db_ref, dgain_ref, dshift_ref, p_ref, gh_ref = refs[2 * groups:]
    step = pl.program_id(0)
    rows = x_ref.shape[0]
    half = rows // 2
    blocks = [slice(r, r + RB) for r in range(0, rows, RB)]
    columns = []
    for g in range(groups):
        columns += [(g, at) for at in range(0, own_refs[g].shape[1], 2 * PAIR)]

    def put(shift):
        db = jnp.zeros(db_ref.shape, f32)
        for r in blocks:
            spot = pl.ds(pl.multiple_of(spot_ref[r.start // RB] * RB, RB), RB)
            for to, (g, at) in enumerate(columns):
                lanes = slice(at + shift, at + shift + PAIR)
                if r.start < half:
                    t = come_refs[g][r, lanes]
                else:
                    t = own_refs[g][r.start - half:r.stop - half, lanes]
                if shift == 0:
                    t = turn_lanes(t.astype(f32), cos_ref[spot, :], low_ref[spot, :], high_ref[spot, :], -1.0).astype(bf16)
                p_ref[r, to * PAIR:(to + 1) * PAIR] = t
            db += col_sum(p_ref[r, :].astype(f32))
        db_ref[...] = db
        dw = mm(h_ref[...], p_ref[...], TN).astype(bf16)
        send_ref[...] = dw[:send_ref.shape[0]]
        keep_ref[...] = dw[send_ref.shape[0]:]

    @pl.when(step == 0)
    def _():
        put(0)
        for r in blocks:
            gh_ref[r, :] = ghq_ref[r, :] + mm(p_ref[r, :], w_ref[...], NT)

    @pl.when(step == 1)
    def _():
        put(PAIR)
        dgain = jnp.zeros(dgain_ref.shape, f32)
        dshift = jnp.zeros(dshift_ref.shape, f32)
        for r in blocks:
            grad = gh_ref[r, :] + mm(p_ref[r, :], w_ref[...], NT)
            back, scaled = norm_back(x_ref[r, :].astype(f32), grad, gain_ref[...])
            grad_ref[r, :] = back + gin_ref[r, :]
            dgain += col_sum(scaled)
            dshift += col_sum(grad)
        dgain_ref[...] = dgain
        dshift_ref[...] = dshift


def last_tail(spots, x, h, gain, weights, tables, gin, ghq, owns, comes):
    rows, width = x.shape
    s = jax.ShapeDtypeStruct

    def full(a):
        return pl.BlockSpec(a.shape, lambda j, spot: (0, 0))

    line = pl.BlockSpec((1, width), lambda j, spot: (0, 0))
    down = pl.BlockSpec((width // 2, width), lambda j, spot: (0, j))
    arrays = [*tables, gin, ghq, *owns, *comes]
    return pl.pallas_call(
        partial(last_kernel, len(owns)),
        grid_spec=pltpu.PrefetchScalarGridSpec(
            num_scalar_prefetch=1,
            grid=(2,),
            in_specs=[full(x), full(h), line, pl.BlockSpec((width, width), lambda j, spot: (0, j + 1))] + [full(a) for a in arrays],
            out_specs=[full(x), down, down, pl.BlockSpec((1, width), lambda j, spot: (0, j)), line, line],
            scratch_shapes=[vmem(rows, width, dtype=bf16), vmem(rows, width)],
        ),
        out_shape=[s((rows, width), f32), s((width // 2, 2 * width), bf16), s((width // 2, 2 * width), bf16),
                   s((1, 2 * width), f32), s((1, width), f32), s((1, width), f32)],
        compiler_params=params(),
        cost_estimate=pl.CostEstimate(flops=8 * rows * width * width, bytes_accessed=32 << 20, transcendentals=0),
        name="last_tail",
    )(spots, x, h, gain.reshape(1, -1), weights, *arrays)


def join_kernel(groups, x_ref, w_ref, mlp_ref, b_ref, *refs):
    att_refs, (out_ref, att_ref) = refs[:groups], refs[groups:]
    at = 0
    for ref in att_refs:
        att_ref[:, at:at + ref.shape[1]] = ref[...]
        at += ref.shape[1]
    out = x_ref[...].astype(f32) + mm(att_ref[...], w_ref[...], NN) + mlp_ref[...] + b_ref[...]
    out_ref[...] = out.astype(bf16)


def join(x, attended, weights, mlp_out, bias):
    rows, width = x.shape
    s = jax.ShapeDtypeStruct
    block = pl.BlockSpec((RB, width), lambda j: (j, 0))
    return pl.pallas_call(
        partial(join_kernel, len(attended)),
        grid=(rows // RB,),
        in_specs=[block, pl.BlockSpec((width, width), lambda j: (0, 3)), block, pl.BlockSpec((1, width), lambda j: (0, 0))]
        + [pl.BlockSpec((RB, a.shape[1]), lambda j: (j, 0)) for a in attended],
        out_specs=block,
        out_shape=s((rows, width), bf16),
        scratch_shapes=[vmem(RB, width, dtype=bf16)],
        compiler_params=params(),
        cost_estimate=pl.CostEstimate(flops=2 * rows * width * width, bytes_accessed=12 << 20, transcendentals=0),
        name="join",
    )(x, weights, mlp_out, bias.reshape(1, -1), *attended)


def spread_kernel(c_ref, w_ref, out_ref):
    out_ref[...] = mm(c_ref[...], w_ref[...], NT).astype(bf16)


def spread(c, weights):
    rows, width = c.shape
    block = pl.BlockSpec((RB, width), lambda j: (j, 0))
    return pl.pallas_call(
        spread_kernel,
        grid=(rows // RB,),
        in_specs=[block, pl.BlockSpec((width, width), lambda j: (0, 3))],
        out_specs=block,
        out_shape=jax.ShapeDtypeStruct((rows, width), bf16),
        compiler_params=params(),
        cost_estimate=pl.CostEstimate(flops=1 << 20, bytes_accessed=1 << 16, transcendentals=0),
        name="spread",
    )(c, weights)


def fold(x, op):
    return op(x.reshape(x.shape[0] // 8, 8, x.shape[1]), axis=0)


def eye(size):
    return (lax.broadcasted_iota(jnp.int32, (size, size), 0) == lax.broadcasted_iota(jnp.int32, (size, size), 1)).astype(bf16)


def attention_kernel(half, n, kind_ref, owner_ref, cos_ref, sin_ref, q_ref, do_ref, *refs):
    k_refs, v_refs = refs[:n], refs[n:2 * n]
    o_ref, dq_ref = refs[2 * n:2 * n + 2]
    all_ref, cont_ref = refs[2 * n + 2:2 * n + 4]
    kt_ref, vt_ref, s_ref, p_ref, ds_ref, dka_ref, dva_ref = refs[2 * n + 4:]
    per = half // QB
    wide = n * half
    count = wide // QB
    spots = [(0, c * QB) for c in range(per)] + [(s, c * QB) for s in range(1, n) for c in range(per)]

    ident = eye(PAIR)
    for refs_in, out in ((k_refs, kt_ref), (v_refs, vt_ref)):
        for c, (s, at) in enumerate(spots):
            out[:, c * QB:(c + 1) * QB] = refs_in[s][at:at + QB, :].T
        for c in range(per):
            out[:, wide + c * QB:wide + (c + 1) * QB] = refs_in[0][half + c * QB:half + (c + 1) * QB, :].T
    dka_ref[...] = jnp.zeros_like(dka_ref)
    dva_ref[...] = jnp.zeros_like(dva_ref)


    def block(qb, carry):
        own = pl.ds(pl.multiple_of(qb * QB, QB), QB)
        slot = pl.ds(pl.multiple_of(jnp.where(qb < per, qb * QB, wide + (qb - per) * QB), QB), QB)
        zero = jnp.zeros((), bf16)
        causal = lax.broadcasted_iota(jnp.int32, (QB, QB), 0) <= lax.broadcasted_iota(jnp.int32, (QB, QB), 1)
        left = lax.broadcasted_iota(jnp.int32, (QB, PAIR), 1) < HD

        def by_head(a):
            return jnp.where(left, a, zero), jnp.where(left, zero, a)

        def keys_of(some, c):
            if c == count:
                return some[0][own, :]
            s, at = spots[c]
            return some[s][at:at + QB, :]

        def cut(c):
            return slice(c * QB, (c + 1) * QB)

        ident = eye(QB)
        q_heads = by_head(q_ref[own, :])
        do_t = mm(eye(PAIR), do_ref[own, :], NT)
        upper = lax.broadcasted_iota(jnp.int32, (PAIR, QB), 0) < HD
        q_t = mm(eye(PAIR), q_ref[own, :], NT).astype(bf16)
        q_cols = jnp.where(upper, q_t, zero), jnp.where(upper, zero, q_t)
        peaks, norms, outs, deltas, scaled = [None, None], [None, None], [None, None], [None, None], [None, None]

        def scores(h):
            peak = jnp.full((8, QB), MASKED, f32)
            for c in range(count + 1):
                s = mm(keys_of(k_refs, c), q_cols[h], NN)
                if c == count:
                    s = jnp.where(causal, s, MASKED)
                    top = fold(s, jnp.max)
                else:
                    top = fold(s, jnp.max) + kind_ref[qb, c]
                s_ref[h, cut(c)] = s
                peak = jnp.maximum(peak, top)
            peaks[h] = jnp.max(peak, axis=0, keepdims=True)

        def weigh(h):
            total = jnp.zeros((8, QB), f32)
            for c in range(count + 1):
                bias = -peaks[h] if c == count else kind_ref[qb, c] - peaks[h]
                e = jnp.exp2(s_ref[h, cut(c)] + bias)
                total = total + fold(e, jnp.sum)
                p_ref[h, cut(c)] = e.astype(bf16)
            norms[h] = 1.0 / jnp.sum(total, axis=0, keepdims=True)

        def attend(h):
            lines = slice(h * HD, (h + 1) * HD)
            out = mm(vt_ref[lines, 0:wide], p_ref[h, 0:wide], NN) + mm(vt_ref[lines, slot], p_ref[h, wide:], NN)
            outs[h] = out * norms[h]
            deltas[h] = jnp.sum(outs[h] * do_t[lines], axis=0, keepdims=True) * norms[h]
            scaled[h] = do_t[lines] * norms[h]

        scores(0)
        scores(1)
        weigh(0)
        attend(0)
        weigh(1)
        attend(1)
        d_t = jnp.concatenate(scaled, axis=0).astype(bf16)
        d_cols = jnp.where(upper, d_t, zero), jnp.where(upper, zero, d_t)
        do_heads = by_head(mm(ident, d_t, NT).astype(bf16))
        grads = []
        for h in range(2):
            lines = slice(h * HD, (h + 1) * HD)
            for c in range(count + 1):
                dp = mm(keys_of(v_refs, c), d_cols[h], NN)
                ds_ref[h, cut(c)] = (p_ref[h, cut(c)].astype(f32) * (dp - deltas[h])).astype(bf16)
            dq = mm(kt_ref[lines, 0:wide], ds_ref[h, 0:wide], NN) + mm(kt_ref[lines, slot], ds_ref[h, wide:], NN)
            a, b = dq[:ROT // 2], dq[ROT // 2:ROT]
            cosine, sine = cos_ref[:, own], sin_ref[:, own]
            grads.append(jnp.concatenate([a * cosine + b * sine, b * cosine - a * sine, dq[ROT:]], axis=0))
        for c in range(count + 1):
            at = slot if c == count else cut(c)
            dva_ref[at, :] += mm(p_ref[0, cut(c)], do_heads[0], NN) + mm(p_ref[1, cut(c)], do_heads[1], NN)
            dka_ref[at, :] += mm(ds_ref[0, cut(c)], q_heads[0], NN) + mm(ds_ref[1, cut(c)], q_heads[1], NN)
        o_ref[own, :] = mm(ident, jnp.concatenate(outs, axis=0).astype(bf16), NT).astype(bf16)
        dq_ref[own, :] = mm(ident, (jnp.concatenate(grads, axis=0) * (HD ** (-0.5))).astype(bf16), NT).astype(bf16)

        return carry

    lax.fori_loop(0, 2 * per, block, 0)

    def flush(out, to, frm):
        rows = pl.ds(to, half)
        out[rows, :PAIR] = (dka_ref[frm:frm + half, :] * math.log(2.0)).astype(bf16)
        out[rows, PAIR:] = dva_ref[frm:frm + half, :].astype(bf16)

    flush(cont_ref, 0, wide)
    for s in range(n):
        flush(all_ref, pl.multiple_of(owner_ref[s] * half, half), s * half)


def attention(kind, owners, cos_t, sin_t, q, do, ks, vs, first, pairs):
    rows = q.shape[0]
    half = rows // 2
    n = len(ks)
    wide = n * half
    keys = wide + half
    total = wide + QB
    qspec = pl.BlockSpec((rows, PAIR), lambda p: (0, p + first))
    ospec = pl.BlockSpec((rows, PAIR), lambda p: (0, p))
    table = pl.BlockSpec((ROT // 2, rows), lambda p: (0, 0))
    kspecs = [pl.BlockSpec((k.shape[0], PAIR), lambda p: (0, p + first)) for k in ks]
    gspecs = [pl.BlockSpec((size, 2 * PAIR), lambda p: (0, p)) for size in (wide, half)]
    s = jax.ShapeDtypeStruct
    pieces = pairs * rows // QB
    return pl.pallas_call(
        partial(attention_kernel, half, n),
        grid=(pairs,),
        in_specs=[pl.BlockSpec(memory_space=pltpu.SMEM), pl.BlockSpec(memory_space=pltpu.SMEM), table, table, qspec, qspec] + kspecs + kspecs,
        out_specs=[ospec, ospec] + gspecs,
        out_shape=[s((rows, pairs * PAIR), bf16), s((rows, pairs * PAIR), bf16)]
        + [s((size, 2 * pairs * PAIR), bf16) for size in (wide, half)],
        scratch_shapes=[pltpu.VMEM((PAIR, keys), bf16), pltpu.VMEM((PAIR, keys), bf16),
                        pltpu.VMEM((2, total, QB), f32), pltpu.VMEM((2, total, QB), bf16),
                        pltpu.VMEM((2, total, QB), bf16),
                        pltpu.VMEM((keys, PAIR), f32), pltpu.VMEM((keys, PAIR), f32)],
        compiler_params=pltpu.CompilerParams(vmem_limit_bytes=60 << 20),
        cost_estimate=pl.CostEstimate(flops=pieces * 24 * total * QB * HD * 4, bytes_accessed=16 << 20,
                                      transcendentals=pieces * 2 * total * QB),
        name="attention",
    )(kind, owners, cos_t, sin_t, q, do, *ks, *vs)


def pairs_of(bit, size):
    return [(a, a ^ bit) for a in range(size)]


def pick(a, axis, i):
    return lax.dynamic_index_in_dim(a, i, axis, keepdims=False)


def plus(a, b):
    return (a.astype(f32) + b.astype(f32)).astype(bf16)


def core_step(send, keep):
    rows, cols = send.shape
    size = rows // 8
    got = lax.ppermute(send, "fsdp", pairs_of(1, 8)).reshape(2, 2, 2, size, cols)
    keep = keep.reshape(2, 2, 2, size, cols)

    def part(*at):
        return plus(keep[at], got[at])

    every = slice(None)
    return part(every, 1, 0), part(every, 0, 0), part(1, every, 1), part(0, every, 1)


def side_step(send_a, keep_a, send_b, keep_b):
    got_a = lax.ppermute(send_a, "fsdp", pairs_of(2, 8))
    got_b = lax.ppermute(send_b, "fsdp", pairs_of(4, 8))
    return plus(keep_a[1], got_a[1]), plus(keep_a[0], got_a[0]), plus(keep_b[1], got_b[1]), plus(keep_b[0], got_b[0])


def last_step(send_a, keep_a, send_b, keep_b):
    got_a = lax.ppermute(send_a, "fsdp", pairs_of(4, 8))
    got_b = lax.ppermute(send_b, "fsdp", pairs_of(2, 8))
    return jnp.concatenate([plus(keep_a, got_a), plus(keep_b, got_b)], axis=0)


def along(part):
    return lax.psum_scatter(part, "ctx", scatter_dimension=0, tiled=True)


def after(value, *others):
    return lax.optimization_barrier((value, *others))[0]


def fast(inputs, cotangent, positions, segments, ln1_gain, ln1_bias, w_qkv, b_qkv, w_attn_out, b_out,
         ln2_gain, ln2_bias, w_in, b_in, w_out):
    x, grad_out, pos = inputs[0], cotangent[0], positions[0]
    rows, width = x.shape
    half = rows // 2
    n = lax.axis_size("ctx")
    ring = [(i, (i + 1) % n) for i in range(n)]
    back = [(i, (i - 1) % n) for i in range(n)]
    me, place = lax.axis_index("fsdp"), lax.axis_index("ctx")
    relative = [4 * dy + 2 * dx + 1 - keep for keep in (0, 1) for dy in (0, 1) for dx in (0, 1)]
    order = jnp.bitwise_xor(me, jnp.array(relative, jnp.int32))
    owners = lax.rem(place + n - jnp.arange(n), n)
    xs, spots = [x], [pos[::RB] // RB]
    run = x[:half]
    for s in range(1, n):
        run = lax.ppermute(run, "ctx", ring)
        xs.append(run)
        spots.append(lax.ppermute(spots[0][:half // RB], "ctx", [(i, (i + s) % n) for i in range(n)]))
    mine = (ln1_gain, ln1_bias, b_qkv, b_out, ln2_gain, ln2_bias, b_in)
    small = lax.all_gather(jnp.concatenate(mine).reshape(1, -1), "fsdp", axis=0, tiled=True)
    full, at = [], 0
    for a in mine:
        full.append(small[:, at:at + a.shape[0]].reshape(-1).astype(f32))
        at += a.shape[0]
    gain_attn, shift_attn, bias_qkv, bias_out, gain_mlp, shift_mlp, bias_in = full
    weights = lax.all_gather(jnp.concatenate([w_qkv, w_attn_out], axis=1), "fsdp", axis=0, tiled=True)

    lane = jnp.arange(PAIR) % HD
    inverse = jnp.exp(-math.log(10000.0) * (2.0 / ROT) * (lane % (ROT // 2)).astype(f32))
    angles = jnp.arange(n * half + CLEN).astype(f32)[:, None] * inverse[None, :]
    sine = jnp.sin(angles)
    tables = (jnp.where(lane < ROT, jnp.cos(angles), 1.0), jnp.where(lane < ROT // 2, sine, 0.0),
              jnp.where((lane >= ROT // 2) & (lane < ROT), sine, 0.0))
    angles_t = pos.astype(f32)[None, :] * inverse[:ROT // 2, None]
    cos_t, sin_t = jnp.cos(angles_t), jnp.sin(angles_t)

    normed, queries, key, value = qkv(spots[0], order, after(x, xs[2], *spots[1:]), gain_attn, shift_attn, weights, bias_qkv, tables, True)
    keys, values = [key], [value]
    for s in range(1, n):
        key, value = qkv(spots[s], order, xs[s], gain_attn, shift_attn, weights, bias_qkv, tables, False)
        keys.append(key)
        values.append(value)
    grad_att = spread(grad_out, weights)
    weight_in = lax.all_gather(after(w_in, queries), "fsdp", axis=0, tiled=True)
    weight_out = lax.all_gather(after(w_out, queries), "fsdp", axis=0, tiled=True)

    per = half // QB
    earlier = jnp.stack([spots[s][0] < spots[0][0] for s in range(1, n)])
    local_row = jnp.arange(2 * per)[:, None]
    seen_own = local_row > jnp.arange(per)[None, :]
    seen_far = jnp.repeat(earlier[None, :] | (local_row >= per), per, axis=1)
    kind = jnp.where(jnp.concatenate([seen_own, seen_far], axis=1), 0.0, MASKED).astype(f32)

    attended, grad_q, own_kv, come_kv = [], [], [], []

    def attend(first, count, wait):
        out = attention(kind, owners, cos_t, sin_t, after(queries, *wait), grad_att, keys, values, first, count)
        attended.append(out[0])
        grad_q.append(out[1])
        come_kv.append(lax.psum_scatter(out[2], "ctx", scatter_dimension=0, tiled=True))
        own_kv.append(out[3])

    attend(0, 5, ())
    mlp_out, grad_mlp, in_send, in_keep, out_send, out_keep, db_in, db_out, dgain_mlp, dshift_mlp = mlp(
        order, after(x, *attended), grad_out, gain_mlp, shift_mlp, weight_in, bias_in, weight_out)
    attend(5, 2, (mlp_out,))
    steps_out = core_step(out_send, out_keep)
    steps_in = core_step(in_send, in_keep)
    attend(7, 1, (*attended, *steps_out, *steps_in))
    output = join(x, attended, weights, mlp_out, bias_out)
    steps_out = side_step(*steps_out)
    steps_in = side_step(*steps_in)
    first_send, first_keep, grad_heads, db_q = first_tail(
        order, after(grad_out, output), normed, weights, attended, grad_q)
    steps_first = core_step(first_send, first_keep)
    grad_inputs, last_send, last_keep, db_kv, dgain_attn, dshift_attn = last_tail(
        spots[0], after(x, *steps_out, *steps_in, *steps_first), normed, gain_attn, weights, tables, grad_mlp, grad_heads,
        own_kv, come_kv)
    sum_out = along(last_step(*steps_out))
    sum_in = along(last_step(*steps_in))
    steps_first = side_step(*steps_first)
    sum_first = along(last_step(*steps_first))
    steps_last = core_step(after(last_send, *steps_first), last_keep)
    smalls = [a.reshape(width, -1) for a in
              (dgain_attn, dshift_attn, jnp.concatenate([db_q, db_kv], axis=1), db_out, dgain_mlp, dshift_mlp, db_in)]
    used = sum(a.shape[1] for a in smalls)
    packed = jnp.concatenate(smalls + [jnp.zeros((width, PAIR - used), f32)], axis=1).astype(bf16)
    packed = packed.reshape(8, width // 8, PAIR)[order].reshape(2, width // 2, PAIR)
    part = last_step(*side_step(*core_step(packed[0], packed[1])))
    joined = along(jnp.concatenate([last_step(*side_step(*steps_last)), part], axis=1))
    packed = joined[:, 2 * width:].astype(f32)
    sum_qkv = jnp.concatenate([sum_first[:, width:], joined[:, :2 * width]], axis=1)
    sum_attn = sum_first[:, :width]
    done, at = [], 0
    for a in smalls:
        done.append(packed[:, at:at + a.shape[1]].reshape(-1))
        at += a.shape[1]
    return (output[None], grad_inputs[None], done[0], done[1], sum_qkv.astype(f32), done[2], sum_attn.astype(f32),
            done[3], done[4], done[5], sum_in.astype(f32), done[6], sum_out.astype(f32))


def local(*args):
    half = args[0].shape[1] // 2
    if args[0].shape[0] == 1 and half % CLEN == 0 and lax.axis_size("fsdp") == 8:
        return fast(*args)
    return generic(*args)


def generic(
    inputs,
    cotangent,
    positions,
    segments,
    ln1_gain,
    ln1_bias,
    w_qkv,
    b_qkv,
    w_attn_out,
    b_out,
    ln2_gain,
    ln2_bias,
    w_in,
    b_in,
    w_out,
):
    shards = (
        ln1_gain,
        ln1_bias,
        w_qkv,
        b_qkv,
        w_attn_out,
        b_out,
        ln2_gain,
        ln2_bias,
        w_in,
        b_in,
        w_out,
    )
    params = (
        lax.all_gather(shards[0], "fsdp", axis=0, tiled=True),
        lax.all_gather(shards[1], "fsdp", axis=0, tiled=True),
        lax.all_gather(shards[2], "fsdp", axis=0, tiled=True),
        lax.all_gather(shards[3], "fsdp", axis=0, tiled=True),
        lax.all_gather(shards[4], "fsdp", axis=0, tiled=True),
        lax.all_gather(shards[5], "fsdp", axis=0, tiled=True),
        lax.all_gather(shards[6], "fsdp", axis=0, tiled=True),
        lax.all_gather(shards[7], "fsdp", axis=0, tiled=True),
        lax.all_gather(shards[8], "fsdp", axis=0, tiled=True),
        lax.all_gather(shards[9], "fsdp", axis=0, tiled=True),
        lax.all_gather(shards[10], "fsdp", axis=0, tiled=True),
    )
    groups, local_len, width = inputs.shape
    rows_total = groups * local_len
    block = math.gcd(local_len, 256)
    label_pos, label_seg = (
        lax.all_gather(positions, "ctx", axis=1, tiled=True),
        lax.all_gather(segments, "ctx", axis=1, tiled=True),
    )
    count = label_pos.shape[1] // block
    f32 = jnp.float32
    bf16 = jnp.bfloat16
    (
        gain_attn,
        shift_attn,
        weight_qkv,
        bias_qkv,
        weight_attn,
        bias_out,
        gain_mlp,
        shift_mlp,
        weight_in,
        bias_in,
        weight_out,
    ) = params
    flat_in = inputs.reshape(rows_total, width).astype(f32)
    normed_attn = layer_norm(flat_in, gain_attn.astype(f32), shift_attn.astype(f32)).astype(bf16)
    normed_mlp = layer_norm(flat_in, gain_mlp.astype(f32), shift_mlp.astype(f32)).astype(bf16)
    projected = jnp.dot(normed_attn, weight_qkv, preferred_element_type=f32) + bias_qkv.astype(f32)
    cosine, sine = rotary_tables(positions)

    def split_heads(columns):
        return columns.reshape(groups, local_len, HEADS, HD)

    scale = HD ** (-0.5)
    queries = (rotate(split_heads(projected[:, :width]), cosine, sine) * scale).astype(bf16)
    keys_own = rotate(split_heads(projected[:, width : 2 * width]), cosine, sine).astype(bf16)
    values_own = split_heads(projected[:, 2 * width :]).astype(bf16)
    keys_all, values_all = (
        lax.all_gather(keys_own, "ctx", axis=1, tiled=True),
        lax.all_gather(values_own, "ctx", axis=1, tiled=True),
    )

    def key_block(index):
        start = index * block
        keys_blk = lax.dynamic_slice_in_dim(keys_all, start, block, 1)
        values_blk = lax.dynamic_slice_in_dim(values_all, start, block, 1)
        mask = allowed_mask(
            positions,
            segments,
            lax.dynamic_slice_in_dim(label_pos, start, block, 1),
            lax.dynamic_slice_in_dim(label_seg, start, block, 1),
        )
        return (keys_blk, values_blk, mask)

    def total_step(carry, index):
        peak, total = carry
        keys_blk, values_blk, mask = key_block(index)
        scores = jnp.where(mask, scores_of(queries, keys_blk), MASKED)
        fresh = jnp.maximum(peak, jnp.max(scores, axis=-1))
        added = jnp.sum(jnp.where(mask, jnp.exp(scores - fresh[..., None]), 0.0), axis=-1)
        return ((fresh, total * jnp.exp(peak - fresh) + added), None)

    stat_shape = (groups, HEADS, local_len)
    (peak, total), unused = lax.scan(
        total_step,
        (jnp.full(stat_shape, MASKED, f32), jnp.zeros(stat_shape, f32)),
        jnp.arange(count),
    )
    log_total = peak + jnp.log(total)

    def attend_step(rounded_sum, index):
        keys_blk, values_blk, mask = key_block(index)
        probs = jnp.where(mask, jnp.exp(scores_of(queries, keys_blk) - log_total[..., None]), 0.0)
        rounded_sum = rounded_sum + jnp.einsum(
            "ghqk,gkhd->gqhd", probs.astype(bf16), values_blk, preferred_element_type=f32
        )
        return (rounded_sum, None)

    head_shape = (groups, local_len, HEADS, HD)
    rounded_sum, unused = lax.scan(attend_step, jnp.zeros(head_shape, f32), jnp.arange(count))
    attended = rounded_sum.reshape(rows_total, width).astype(bf16)
    pre_act = jnp.dot(normed_mlp, weight_in, preferred_element_type=f32) + bias_in.astype(f32)
    activated = jax.nn.gelu(pre_act, approximate=False).astype(bf16)
    output = (
        flat_in
        + jnp.dot(attended, weight_attn, preferred_element_type=f32)
        + jnp.dot(activated, weight_out, preferred_element_type=f32)
        + bias_out.astype(f32)
    )
    (
        gain_attn,
        shift_attn,
        weight_qkv,
        bias_qkv,
        weight_attn,
        bias_out,
        gain_mlp,
        shift_mlp,
        weight_in,
        bias_in,
        weight_out,
    ) = params
    grad_out = cotangent.reshape(rows_total, width)
    grad_bias_out = jnp.sum(grad_out.astype(f32), axis=0)
    grad_weight_out = jnp.einsum("rf,rd->fd", activated, grad_out, preferred_element_type=f32)
    grad_act = jnp.einsum("rd,fd->rf", grad_out, weight_out, preferred_element_type=f32)
    unused, gelu_back = jax.vjp(partial(jax.nn.gelu, approximate=False), pre_act)
    grad_pre = gelu_back(grad_act)[0].astype(bf16)
    grad_weight_in = jnp.einsum("rd,rf->df", normed_mlp, grad_pre, preferred_element_type=f32)
    grad_bias_in = jnp.sum(grad_pre.astype(f32), axis=0)
    grad_normed_mlp = jnp.einsum("rf,df->rd", grad_pre, weight_in, preferred_element_type=f32)
    grad_weight_attn = jnp.einsum("ra,rd->ad", attended, grad_out, preferred_element_type=f32)
    grad_att = (
        jnp.einsum("rd,ad->ra", grad_out, weight_attn, preferred_element_type=f32)
        .astype(bf16)
        .reshape(head_shape)
    )
    delta = jnp.einsum(
        "gqhd,gqhd->ghq", grad_att.astype(f32), rounded_sum, precision=lax.Precision.HIGHEST
    )

    def back_step(carry, index):
        keys_blk, values_blk, mask = key_block(index)
        rounded, grad_scores = block_grads(
            queries, grad_att, log_total, delta, mask, keys_blk, values_blk
        )
        carry = carry + jnp.einsum(
            "ghqk,gkhd->gqhd", grad_scores, keys_blk, preferred_element_type=f32
        )
        key_term = jnp.einsum("ghqk,gqhd->gkhd", grad_scores, queries, preferred_element_type=f32)
        value_term = jnp.einsum("ghqk,gqhd->gkhd", rounded, grad_att, preferred_element_type=f32)
        return (carry, (key_term, value_term))

    grad_queries, (key_terms, value_terms) = lax.scan(
        back_step, jnp.zeros(head_shape, f32), jnp.arange(count)
    )
    key_sums, value_sums = (
        lax.psum_scatter(
            key_terms.astype(jnp.bfloat16), "ctx", scatter_dimension=0, tiled=True
        ).astype(jnp.float32),
        lax.psum_scatter(
            value_terms.astype(jnp.bfloat16), "ctx", scatter_dimension=0, tiled=True
        ).astype(jnp.float32),
    )
    grad_keys = jnp.transpose(key_sums, (1, 0, 2, 3, 4)).reshape(head_shape)
    grad_values = jnp.transpose(value_sums, (1, 0, 2, 3, 4)).reshape(head_shape)
    grad_q_pre = unrotate(grad_queries * scale, cosine, sine).reshape(rows_total, width)
    grad_k_pre = unrotate(grad_keys, cosine, sine).reshape(rows_total, width)
    grad_projected = jnp.concatenate(
        [grad_q_pre, grad_k_pre, grad_values.reshape(rows_total, width)], axis=1
    ).astype(bf16)
    grad_weight_qkv = jnp.einsum(
        "rd,re->de", normed_attn, grad_projected, preferred_element_type=f32
    )
    grad_bias_qkv = jnp.sum(grad_projected.astype(f32), axis=0)
    grad_normed_attn = jnp.einsum(
        "re,de->rd", grad_projected, weight_qkv, preferred_element_type=f32
    )
    unused, norm_back_attn = jax.vjp(
        layer_norm, flat_in, gain_attn.astype(f32), shift_attn.astype(f32)
    )
    grad_in_attn, grad_gain_attn, grad_shift_attn = norm_back_attn(grad_normed_attn)
    unused, norm_back_mlp = jax.vjp(
        layer_norm, flat_in, gain_mlp.astype(f32), shift_mlp.astype(f32)
    )
    grad_in_mlp, grad_gain_mlp, grad_shift_mlp = norm_back_mlp(grad_normed_mlp)
    grad_inputs = (grad_out.astype(f32) + grad_in_attn + grad_in_mlp).reshape(
        groups, local_len, width
    )
    sums = (
        lax.psum_scatter(grad_gain_attn, ("fsdp", "ctx"), scatter_dimension=0, tiled=True),
        lax.psum_scatter(grad_shift_attn, ("fsdp", "ctx"), scatter_dimension=0, tiled=True),
        lax.psum_scatter(grad_weight_qkv, ("fsdp", "ctx"), scatter_dimension=0, tiled=True),
        lax.psum_scatter(grad_bias_qkv, ("fsdp", "ctx"), scatter_dimension=0, tiled=True),
        lax.psum_scatter(grad_weight_attn, ("fsdp", "ctx"), scatter_dimension=0, tiled=True),
        lax.psum_scatter(grad_bias_out, ("fsdp", "ctx"), scatter_dimension=0, tiled=True),
        lax.psum_scatter(grad_gain_mlp, ("fsdp", "ctx"), scatter_dimension=0, tiled=True),
        lax.psum_scatter(grad_shift_mlp, ("fsdp", "ctx"), scatter_dimension=0, tiled=True),
        lax.psum_scatter(grad_weight_in, ("fsdp", "ctx"), scatter_dimension=0, tiled=True),
        lax.psum_scatter(grad_bias_in, ("fsdp", "ctx"), scatter_dimension=0, tiled=True),
        lax.psum_scatter(grad_weight_out, ("fsdp", "ctx"), scatter_dimension=0, tiled=True),
    )
    result = output.reshape(groups, local_len, width).astype(bf16)
    return (
        result,
        grad_inputs,
        sums[0],
        sums[1],
        sums[2],
        sums[3],
        sums[4],
        sums[5],
        sums[6],
        sums[7],
        sums[8],
        sums[9],
        sums[10],
    )


def solution(mesh):
    in_specs = (
        P("fsdp", "ctx", None),
        P("fsdp", "ctx", None),
        P("fsdp", "ctx"),
        P("fsdp", "ctx"),
        P("fsdp"),
        P("fsdp"),
        P("fsdp", None),
        P("fsdp"),
        P("fsdp", None),
        P("fsdp"),
        P("fsdp"),
        P("fsdp"),
        P("fsdp", None),
        P("fsdp"),
        P("fsdp", None),
    )
    out_specs = (
        P("fsdp", "ctx", None),
        P("fsdp", "ctx", None),
        P(("fsdp", "ctx")),
        P(("fsdp", "ctx")),
        P(("fsdp", "ctx"), None),
        P(("fsdp", "ctx")),
        P(("fsdp", "ctx"), None),
        P(("fsdp", "ctx")),
        P(("fsdp", "ctx")),
        P(("fsdp", "ctx")),
        P(("fsdp", "ctx"), None),
        P(("fsdp", "ctx")),
        P(("fsdp", "ctx"), None),
    )
    return jax.shard_map(local, mesh=mesh, in_specs=in_specs, out_specs=out_specs, check_vma=False)
```

```python
from functools import partial
import math

import jax
import jax.numpy as jnp
from jax import lax
from jax.experimental import pallas as pl
from jax.experimental.pallas import tpu as pltpu
from jax.sharding import PartitionSpec as P

HEADS = 16
HD = 64
ROT = 16
CLEN = 256
QB = 256
RB = 256
PAIR = 2 * HD
bf16 = jnp.bfloat16
f32 = jnp.float32
NN = (((1,), (0,)), ((), ()))
NT = (((1,), (1,)), ((), ()))
TN = (((0,), (0,)), ((), ()))


NORM_EPS = 1e-05
MASKED = -1e30


def layer_norm(values, scaling, offset):
    average = jnp.mean(values, axis=-1, keepdims=True)
    centered = values - average
    variance = jnp.mean(centered * centered, axis=-1, keepdims=True)
    return centered * lax.rsqrt(variance + NORM_EPS) * scaling + offset


def rotary_tables(positions):
    halfway = ROT // 2
    spacing = jnp.arange(halfway, dtype=jnp.float32) * (2.0 / ROT)
    inverse = jnp.exp(-math.log(10000.0) * spacing)
    angles = positions.astype(jnp.float32)[..., None] * inverse
    return (jnp.cos(angles), jnp.sin(angles))


def rotate(heads_in, cosine, sine):
    halfway = ROT // 2
    cosine = cosine[..., None, :]
    sine = sine[..., None, :]
    first = heads_in[..., :halfway]
    second = heads_in[..., halfway:ROT]
    return jnp.concatenate(
        [first * cosine - second * sine, second * cosine + first * sine, heads_in[..., ROT:]],
        axis=-1,
    )


def unrotate(grads_in, cosine, sine):
    halfway = ROT // 2
    cosine = cosine[..., None, :]
    sine = sine[..., None, :]
    first = grads_in[..., :halfway]
    second = grads_in[..., halfway:ROT]
    return jnp.concatenate(
        [first * cosine + second * sine, second * cosine - first * sine, grads_in[..., ROT:]],
        axis=-1,
    )


def allowed_mask(query_pos, query_seg, key_pos, key_seg):
    same_doc = (key_seg[:, None, :] == 0) | (key_seg[:, None, :] == query_seg[:, :, None])
    causal = key_pos[:, None, :] <= query_pos[:, :, None]
    return (same_doc & causal)[:, None]


def scores_of(queries, keys_blk):
    return jnp.einsum("gqhd,gkhd->ghqk", queries, keys_blk, preferred_element_type=jnp.float32)


def block_grads(queries, grad_att, log_total, delta, mask, keys_blk, values_blk):
    probs = jnp.where(mask, jnp.exp(scores_of(queries, keys_blk) - log_total[..., None]), 0.0)
    dprobs = jnp.einsum("gqhd,gkhd->ghqk", grad_att, values_blk, preferred_element_type=jnp.float32)
    grad_scores = (probs * (dprobs - delta[..., None])).astype(jnp.bfloat16)
    return (probs.astype(jnp.bfloat16), grad_scores)


def mm(a, b, dims):
    return lax.dot_general(a, b, dims, preferred_element_type=f32)


def row_stats(x):
    average = jnp.mean(x, axis=1, keepdims=True)
    centered = x - average
    return centered, lax.rsqrt(jnp.mean(centered * centered, axis=1, keepdims=True) + NORM_EPS)


def norm_rows(x, scaling, offset):
    centered, inverse = row_stats(x)
    return (centered * inverse * scaling + offset).astype(bf16)


def norm_back(x, grad, scaling):
    centered, inverse = row_stats(x)
    unit = centered * inverse
    e = grad * scaling
    inner = e - jnp.mean(e, axis=1, keepdims=True) - unit * jnp.mean(e * unit, axis=1, keepdims=True)
    return inverse * inner, grad * unit


def col_sum(a):
    return jnp.sum(a, axis=0, keepdims=True)


def vmem(*shape, dtype=f32):
    return pltpu.VMEM(shape, dtype)


def params():
    return pltpu.CompilerParams(vmem_limit_bytes=60 << 20)


ROOT = math.sqrt(0.5)
DENS = 1.0 / math.sqrt(2.0 * math.pi)


def reorder(order_ref, source, target):
    size = source.shape[1] // order_ref.shape[0]
    for i in range(order_ref.shape[0]):
        at = pl.multiple_of(order_ref[i] * size, size)
        target[:, i * size:(i + 1) * size] = source[:, pl.ds(at, size)]


def mlp_kernel(order_ref, x_ref, c_ref, gain_ref, shift_ref, win_ref, bin_ref, wout_ref,
               out_ref, gin_ref, dwin_send, dwin_keep, dwout_send, dwout_keep, dbin_ref, dbout_ref, dgain_ref, dshift_ref,
               h_ref, turned_ref, act_ref, gp_ref, gh_ref):
    step = pl.program_id(0)
    rows = x_ref.shape[0]
    blocks = [slice(r, r + RB) for r in range(0, rows, RB)]

    @pl.when(step == 0)
    def _():
        for r in blocks:
            h_ref[r, :] = norm_rows(x_ref[r, :].astype(f32), gain_ref[...], shift_ref[...])
            out_ref[r, :] = jnp.zeros((RB, out_ref.shape[1]), f32)
            gh_ref[r, :] = jnp.zeros((RB, gh_ref.shape[1]), f32)
        reorder(order_ref, h_ref, turned_ref)

    dbin = jnp.zeros(dbin_ref.shape, f32)
    for r in blocks:
        pre = mm(h_ref[r, :], win_ref[...], NN) + bin_ref[...]
        phi = 0.5 + 0.5 * lax.erf(pre * ROOT)
        act_ref[r, :] = (pre * phi).astype(bf16)
        gp = phi + pre * (DENS * jnp.exp(-0.5 * (pre * pre)))
        gact = mm(c_ref[r, :], wout_ref[...], NT)
        gpre = (gact * gp).astype(bf16)
        gp_ref[r, :] = gpre
        dbin = dbin + col_sum(gpre.astype(f32))
    for r in blocks:
        out_ref[r, :] += mm(act_ref[r, :], wout_ref[...], NN)
        gh_ref[r, :] += mm(gp_ref[r, :], win_ref[...], NT)
    dwout = mm(act_ref[...], c_ref[...], TN).astype(bf16)
    middle = pl.num_programs(0) // 2

    @pl.when(step < middle)
    def _():
        dwout_send[...] = dwout

    @pl.when(step >= middle)
    def _():
        dwout_keep[...] = dwout

    dwin = mm(turned_ref[...], gp_ref[...], TN).astype(bf16)
    dwin_send[...] = dwin[:dwin_send.shape[0]]
    dwin_keep[...] = dwin[dwin_send.shape[0]:]
    dbin_ref[...] = dbin

    @pl.when(step == pl.num_programs(0) - 1)
    def _():
        dgain = jnp.zeros(dgain_ref.shape, f32)
        dshift = jnp.zeros(dshift_ref.shape, f32)
        dbout = jnp.zeros(dbout_ref.shape, f32)
        for r in blocks:
            grad = gh_ref[r, :]
            back, scaled = norm_back(x_ref[r, :].astype(f32), grad, gain_ref[...])
            c = c_ref[r, :].astype(f32)
            gin_ref[r, :] = back + c
            dgain += col_sum(scaled)
            dshift += col_sum(grad)
            dbout += col_sum(c)
        dgain_ref[...] = dgain
        dshift_ref[...] = dshift
        dbout_ref[...] = dbout


def mlp(order, x, c, gain, shift, weight_in, bias_in, weight_out):
    rows, width = x.shape
    ff = weight_in.shape[1]
    steps = order.shape[0]
    fc = ff // steps
    whole = pl.BlockSpec((rows, width), lambda j, o: (0, 0))
    line = pl.BlockSpec((1, width), lambda j, o: (0, 0))
    down = pl.BlockSpec((width // 2, fc), lambda j, o: (0, o[j]))
    s = jax.ShapeDtypeStruct
    return pl.pallas_call(
        mlp_kernel,
        grid_spec=pltpu.PrefetchScalarGridSpec(
            num_scalar_prefetch=1,
            grid=(steps,),
            in_specs=[whole, whole, line, line, pl.BlockSpec((width, fc), lambda j, o: (0, o[j])),
                      pl.BlockSpec((1, fc), lambda j, o: (0, o[j])), pl.BlockSpec((fc, width), lambda j, o: (o[j], 0))],
            out_specs=[whole, whole, down, down,
                       pl.BlockSpec((fc, width), lambda j, o: (jnp.minimum(j, steps // 2 - 1), 0)),
                       pl.BlockSpec((fc, width), lambda j, o: (jnp.maximum(j - steps // 2, 0), 0)),
                       pl.BlockSpec((1, fc), lambda j, o: (0, o[j])), line, line, line],
            scratch_shapes=[vmem(rows, width, dtype=bf16), vmem(rows, width, dtype=bf16), vmem(rows, fc, dtype=bf16),
                            vmem(rows, fc, dtype=bf16), vmem(rows, width)],
        ),
        out_shape=[s((rows, width), f32), s((rows, width), f32), s((width // 2, ff), bf16), s((width // 2, ff), bf16),
                   s((ff // 2, width), bf16), s((ff // 2, width), bf16), s((1, ff), f32), s((1, width), f32),
                   s((1, width), f32), s((1, width), f32)],
        compiler_params=params(),
        cost_estimate=pl.CostEstimate(flops=1 << 20, bytes_accessed=1 << 16, transcendentals=0),
        name="mlp",
    )(order, x, c, gain.reshape(1, -1), shift.reshape(1, -1), weight_in, bias_in.reshape(1, -1), weight_out)


def turn_lanes(u, cosine, low, high, sign):
    half = ROT // 2
    parts = []
    for at in range(0, u.shape[1], PAIR):
        g = u[:, at:at + PAIR]
        parts.append(g * cosine + sign * (pltpu.roll(g, half, 1) * high - pltpu.roll(g, PAIR - half, 1) * low))
    return jnp.concatenate(parts, axis=1)


def qkv_kernel(far, spot_ref, order_ref, gain_ref, shift_ref, w_ref, b_ref, cos_ref, low_ref, high_ref, *refs):
    with_q = far == 0
    if with_q:
        x_ref, outs = refs[0], refs[1:]
    else:
        x_refs, outs, x_ref = refs[:far], refs[far:-1], refs[-1]
        step = pl.program_id(0)
        per = pl.num_programs(0) // far
        for s in range(far):
            @pl.when(step // per == s)
            def _(s=s):
                x_ref[...] = x_refs[s][...]
    width = x_ref.shape[1]
    h = norm_rows(x_ref[...].astype(f32), gain_ref[...], shift_ref[...])
    tables = (cos_ref[...], low_ref[...], high_ref[...])
    if with_q:
        h_ref, q_ref, k_ref, v_ref, plain_ref = outs
        plain_ref[...] = h
        reorder(order_ref, plain_ref, h_ref)
        q = mm(h, w_ref[:, :width], NN) + b_ref[:, :width]
        q_ref[...] = (turn_lanes(q, *tables, 1.0) * (HD ** (-0.5) / math.log(2.0))).astype(bf16)
    else:
        k_ref, v_ref = outs
    k = mm(h, w_ref[:, width:2 * width], NN) + b_ref[:, width:2 * width]
    k_ref[...] = turn_lanes(k, *tables, 1.0).astype(bf16)
    v_ref[...] = (mm(h, w_ref[:, 2 * width:], NN) + b_ref[:, 2 * width:]).astype(bf16)


def qkv(spots, order, xs, gain, shift, weight, bias, tables):
    far = len(xs) if len(xs) > 1 else 0
    rows, width = xs[0].shape
    per = rows // RB
    total = len(xs) * rows
    s = jax.ShapeDtypeStruct((total, width), bf16)
    block = pl.BlockSpec((RB, width), lambda j, spot, o: (j, 0))
    line = pl.BlockSpec((1, width), lambda j, spot, o: (0, 0))
    table = pl.BlockSpec((RB, PAIR), lambda j, spot, o: (spot[j], 0))
    count = 2 if far else 4

    def window(i):
        return pl.BlockSpec((RB, width), lambda j, spot, o: (jnp.clip(j - i * per, 0, per - 1), 0))

    return pl.pallas_call(
        partial(qkv_kernel, far),
        grid_spec=pltpu.PrefetchScalarGridSpec(
            num_scalar_prefetch=2,
            grid=(total // RB,),
            in_specs=[line, line, pl.BlockSpec((width, 3 * width), lambda j, spot, o: (0, 0)),
                      pl.BlockSpec((1, 3 * width), lambda j, spot, o: (0, 0)), table, table, table]
            + [window(i) for i in range(len(xs))],
            out_specs=[block] * count,
            scratch_shapes=[vmem(RB, width, dtype=bf16)],
        ),
        out_shape=[s] * count,
        compiler_params=params(),
        cost_estimate=pl.CostEstimate(flops=1 << 20, bytes_accessed=1 << 16, transcendentals=0),
        name="kv_remote" if far else "qkv_own",
    )(spots, order, gain.reshape(1, -1), shift.reshape(1, -1), weight, bias.reshape(1, -1), *tables, *xs)


def first_kernel(groups, order_ref, c_ref, h_ref, w_ref, *refs):
    att_refs, dq_refs = refs[:groups], refs[groups:2 * groups]
    send_ref, keep_ref, gh_ref, db_ref, p_ref, turned_ref = refs[2 * groups:]
    step = pl.program_id(0)
    blocks = [slice(r, r + RB) for r in range(0, c_ref.shape[0], RB)]

    def lay(some):
        at = 0
        for ref in some:
            p_ref[:, at:at + ref.shape[1]] = ref[...]
            at += ref.shape[1]

    def give(dw):
        send_ref[...] = dw[:send_ref.shape[0]]
        keep_ref[...] = dw[send_ref.shape[0]:]

    @pl.when(step == 0)
    def _():
        lay(att_refs)
        reorder(order_ref, p_ref, turned_ref)
        give(mm(turned_ref[...], c_ref[...], TN).astype(bf16))

    @pl.when(step == 1)
    def _():
        lay(dq_refs)
        db = jnp.zeros(db_ref.shape, f32)
        for r in blocks:
            gh_ref[r, :] = mm(p_ref[r, :], w_ref[...], NT)
            db += col_sum(p_ref[r, :].astype(f32))
        db_ref[...] = db
        give(mm(h_ref[...], p_ref[...], TN).astype(bf16))


def first_tail(order, c, h, weights, attended, dqs):
    rows, width = c.shape
    s = jax.ShapeDtypeStruct

    def full(a):
        return pl.BlockSpec(a.shape, lambda j, o: (0, 0))

    down = pl.BlockSpec((width // 2, width), lambda j, o: (0, j))
    arrays = [*attended, *dqs]
    return pl.pallas_call(
        partial(first_kernel, len(dqs)),
        grid_spec=pltpu.PrefetchScalarGridSpec(
            num_scalar_prefetch=1,
            grid=(2,),
            in_specs=[full(c), full(h), pl.BlockSpec((width, width), lambda j, o: (0, 0))] + [full(a) for a in arrays],
            out_specs=[down, down, full(c), pl.BlockSpec((1, width), lambda j, o: (0, 0))],
            scratch_shapes=[vmem(rows, width, dtype=bf16), vmem(rows, width, dtype=bf16)],
        ),
        out_shape=[s((width // 2, 2 * width), bf16), s((width // 2, 2 * width), bf16), s((rows, width), f32), s((1, width), f32)],
        compiler_params=params(),
        cost_estimate=pl.CostEstimate(flops=12884901888, bytes_accessed=1048576, transcendentals=0),
        name="first_tail",
    )(order, c, h, weights, *arrays)


def kv_kernel(groups, final, first, spot_ref, x_ref, h_ref, gain_ref, wk_ref, wv_ref, cos_ref, low_ref, high_ref, gin_ref,
              gh_ref, *refs):
    count = len(groups)
    own_refs, come_refs = refs[:count], refs[count:2 * count]
    send_ref, keep_ref, db_ref, grad_ref = refs[2 * count:2 * count + 4]
    p_ref, w_ref, acc_ref = refs[-3:]
    step = pl.program_id(0)
    rows = x_ref.shape[0]
    half = rows // 2
    blocks = [slice(r, r + RB) for r in range(0, rows, RB)]

    def put(own_ref, come_ref):
        for r in blocks:
            spot = pl.ds(pl.multiple_of(spot_ref[r.start // RB] * RB, RB), RB)
            t = come_ref[r, :] if r.start < half else own_ref[r.start - half:r.stop - half, :]
            p_ref[r, :PAIR] = turn_lanes(t[:, :PAIR].astype(f32), cos_ref[spot, :], low_ref[spot, :], high_ref[spot, :],
                                         -1.0).astype(bf16)
            p_ref[r, PAIR:] = t[:, PAIR:]

    at = 0
    for g, size in enumerate(groups):
        @pl.when((step >= at) & (step < at + size))
        def _(g=g):
            put(own_refs[g], come_refs[g])
        at += size
    w_ref[:, :PAIR] = wk_ref[...]
    w_ref[:, PAIR:] = wv_ref[...]

    @pl.when(step == 0)
    def _():
        acc_ref[...] = gh_ref[...]

    db = jnp.zeros(db_ref.shape, f32)
    for r in blocks:
        acc_ref[r, :] += mm(p_ref[r, :], w_ref[...], NT)
        db += col_sum(p_ref[r, :].astype(f32))
    db_ref[...] = db
    dw = mm(h_ref[...], p_ref[...], TN).astype(bf16)
    send_ref[...] = dw[:send_ref.shape[0]]
    keep_ref[...] = dw[send_ref.shape[0]:]

    @pl.when(step == pl.num_programs(0) - 1)
    def _():
        if not final:
            grad_ref[...] = acc_ref[...]
            return
        dgain_ref, dshift_ref = refs[2 * count + 4:2 * count + 6]
        dgain = jnp.zeros(dgain_ref.shape, f32)
        dshift = jnp.zeros(dshift_ref.shape, f32)
        for r in blocks:
            grad = acc_ref[r, :]
            back, scaled = norm_back(x_ref[r, :].astype(f32), grad, gain_ref[...])
            grad_ref[r, :] = back + gin_ref[r, :]
            dgain += col_sum(scaled)
            dshift += col_sum(grad)
        dgain_ref[...] = dgain
        dshift_ref[...] = dshift


def kv_tail(final, first, spots, x, h, gain, weights, tables, gin, gh, owns, comes):
    rows, width = x.shape
    groups = [a.shape[1] // (2 * PAIR) for a in owns]
    pairs = sum(groups)
    s = jax.ShapeDtypeStruct

    def full(a):
        return pl.BlockSpec(a.shape, lambda j, spot: (0, 0), pipeline_mode=pl.Buffered(1))

    def windows(arrays):
        specs, at = [], 0
        for a, size in zip(arrays, groups):
            specs.append(pl.BlockSpec((a.shape[0], 2 * PAIR), lambda j, spot, at=at, size=size: (0, jnp.clip(j - at, 0, size - 1))))
            at += size
        return specs

    line = pl.BlockSpec((1, width), lambda j, spot: (0, 0))
    down = pl.BlockSpec((width // 2, 2 * PAIR), lambda j, spot: (0, j))
    column = width // PAIR
    more = [line, line] if final else []
    return pl.pallas_call(
        partial(kv_kernel, groups, final, first),
        grid_spec=pltpu.PrefetchScalarGridSpec(
            num_scalar_prefetch=1,
            grid=(pairs,),
            in_specs=[full(x), full(h), line, pl.BlockSpec((width, PAIR), lambda j, spot: (0, column + first + j)),
                      pl.BlockSpec((width, PAIR), lambda j, spot: (0, 2 * column + first + j))]
            + [full(a) for a in (*tables, gin, gh)] + windows(owns) + windows(comes),
            out_specs=[down, down, pl.BlockSpec((1, 2 * PAIR), lambda j, spot: (0, j)),
                       pl.BlockSpec((rows, width), lambda j, spot: (0, 0))] + more,
            scratch_shapes=[vmem(rows, 2 * PAIR, dtype=bf16), vmem(width, 2 * PAIR, dtype=bf16), vmem(rows, width)],
        ),
        out_shape=[s((width // 2, 2 * PAIR * pairs), bf16), s((width // 2, 2 * PAIR * pairs), bf16),
                   s((1, 2 * PAIR * pairs), f32), s((rows, width), f32)] + [s((1, width), f32)] * len(more),
        compiler_params=params(),
        cost_estimate=pl.CostEstimate(flops=12884901888, bytes_accessed=1 << 20, transcendentals=0),
        name="kv_last" if final else "kv_first",
    )(spots, x, h, gain.reshape(1, -1), weights, weights, *tables, gin, gh, *owns, *comes)


def join_kernel(groups, x_ref, w_ref, mlp_ref, b_ref, *refs):
    att_refs, (out_ref, att_ref) = refs[:groups], refs[groups:]
    at = 0
    for ref in att_refs:
        att_ref[:, at:at + ref.shape[1]] = ref[...]
        at += ref.shape[1]
    out = x_ref[...].astype(f32) + mm(att_ref[...], w_ref[...], NN) + mlp_ref[...] + b_ref[...]
    out_ref[...] = out.astype(bf16)


def join(x, attended, weights, mlp_out, bias):
    rows, width = x.shape
    s = jax.ShapeDtypeStruct
    block = pl.BlockSpec((RB, width), lambda j: (j, 0))
    return pl.pallas_call(
        partial(join_kernel, len(attended)),
        grid=(rows // RB,),
        in_specs=[block, pl.BlockSpec((width, width), lambda j: (0, 3)), block, pl.BlockSpec((1, width), lambda j: (0, 0))]
        + [pl.BlockSpec((RB, a.shape[1]), lambda j: (j, 0)) for a in attended],
        out_specs=block,
        out_shape=s((rows, width), bf16),
        scratch_shapes=[vmem(RB, width, dtype=bf16)],
        compiler_params=params(),
        cost_estimate=pl.CostEstimate(flops=12884901888, bytes_accessed=1048576, transcendentals=0),
        name="join",
    )(x, weights, mlp_out, bias.reshape(1, -1), *attended)


def spread_kernel(c_ref, w_ref, out_ref):
    out_ref[...] = mm(c_ref[...], w_ref[...], NT).astype(bf16)


def spread(c, weights):
    rows, width = c.shape
    block = pl.BlockSpec((RB, width), lambda j: (j, 0))
    return pl.pallas_call(
        spread_kernel,
        grid=(rows // RB,),
        in_specs=[block, pl.BlockSpec((width, width), lambda j: (0, 3))],
        out_specs=block,
        out_shape=jax.ShapeDtypeStruct((rows, width), bf16),
        compiler_params=params(),
        cost_estimate=pl.CostEstimate(flops=1 << 20, bytes_accessed=1 << 16, transcendentals=0),
        name="spread",
    )(c, weights)


def fold(x, op):
    return op(x.reshape(x.shape[0] // 8, 8, x.shape[1]), axis=0)


def eye(size):
    return (lax.broadcasted_iota(jnp.int32, (size, size), 0) == lax.broadcasted_iota(jnp.int32, (size, size), 1)).astype(bf16)


def attention_kernel(half, n, kind_ref, owner_ref, cos_ref, sin_ref, q_ref, do_ref, *refs):
    k_refs, v_refs = refs[:2], refs[2:4]
    o_ref, dq_ref, all_ref, cont_ref, kt_ref, vt_ref, s_ref, p_ref, ds_ref, dka_ref, dva_ref = refs[4:]
    per = half // QB
    wide = n * half
    count = wide // QB
    spots = [(0, c * QB) for c in range(per)] + [(1, c * QB) for c in range((n - 1) * per)]

    ident = eye(PAIR)
    for refs_in, out in ((k_refs, kt_ref), (v_refs, vt_ref)):
        for c, (s, at) in enumerate(spots):
            out[:, c * QB:(c + 1) * QB] = refs_in[s][at:at + QB, :].T
        for c in range(per):
            out[:, wide + c * QB:wide + (c + 1) * QB] = refs_in[0][half + c * QB:half + (c + 1) * QB, :].T
    dka_ref[...] = jnp.zeros_like(dka_ref)
    dva_ref[...] = jnp.zeros_like(dva_ref)


    def block(qb, carry):
        own = pl.ds(pl.multiple_of(qb * QB, QB), QB)
        slot = pl.ds(pl.multiple_of(jnp.where(qb < per, qb * QB, wide + (qb - per) * QB), QB), QB)
        zero = jnp.zeros((), bf16)
        causal = lax.broadcasted_iota(jnp.int32, (QB, QB), 0) <= lax.broadcasted_iota(jnp.int32, (QB, QB), 1)
        left = lax.broadcasted_iota(jnp.int32, (QB, PAIR), 1) < HD

        def by_head(a):
            return jnp.where(left, a, zero), jnp.where(left, zero, a)

        def keys_of(some, c):
            if c == count:
                return some[0][own, :]
            s, at = spots[c]
            return some[s][at:at + QB, :]

        def cut(c):
            return slice(c * QB, (c + 1) * QB)

        ident = eye(QB)
        q_heads = by_head(q_ref[own, :])
        do_t = mm(eye(PAIR), do_ref[own, :], NT)
        upper = lax.broadcasted_iota(jnp.int32, (PAIR, QB), 0) < HD
        q_t = mm(eye(PAIR), q_ref[own, :], NT).astype(bf16)
        q_cols = jnp.where(upper, q_t, zero), jnp.where(upper, zero, q_t)
        peaks, norms, outs, deltas, scaled = [None, None], [None, None], [None, None], [None, None], [None, None]

        def scores(h):
            peak = jnp.full((8, QB), MASKED, f32)
            for c in range(count + 1):
                s = mm(keys_of(k_refs, c), q_cols[h], NN)
                if c == count:
                    s = jnp.where(causal, s, MASKED)
                    top = fold(s, jnp.max)
                else:
                    top = fold(s, jnp.max) + kind_ref[qb, c]
                s_ref[h, cut(c)] = s
                peak = jnp.maximum(peak, top)
            peaks[h] = jnp.max(peak, axis=0, keepdims=True)

        def weigh(h):
            total = jnp.zeros((8, QB), f32)
            for c in range(count + 1):
                bias = -peaks[h] if c == count else kind_ref[qb, c] - peaks[h]
                e = jnp.exp2(s_ref[h, cut(c)] + bias)
                total = total + fold(e, jnp.sum)
                p_ref[h, cut(c)] = e.astype(bf16)
            norms[h] = 1.0 / jnp.sum(total, axis=0, keepdims=True)

        def attend(h):
            lines = slice(h * HD, (h + 1) * HD)
            out = mm(vt_ref[lines, 0:wide], p_ref[h, 0:wide], NN) + mm(vt_ref[lines, slot], p_ref[h, wide:], NN)
            outs[h] = out * norms[h]
            deltas[h] = jnp.sum(outs[h] * do_t[lines], axis=0, keepdims=True) * norms[h]
            scaled[h] = do_t[lines] * norms[h]

        scores(0)
        scores(1)
        weigh(0)
        attend(0)
        weigh(1)
        attend(1)
        d_t = jnp.concatenate(scaled, axis=0).astype(bf16)
        d_cols = jnp.where(upper, d_t, zero), jnp.where(upper, zero, d_t)
        do_heads = by_head(mm(ident, d_t, NT).astype(bf16))
        grads = []
        for h in range(2):
            lines = slice(h * HD, (h + 1) * HD)
            for c in range(count + 1):
                dp = mm(keys_of(v_refs, c), d_cols[h], NN)
                ds_ref[h, cut(c)] = (p_ref[h, cut(c)].astype(f32) * (dp - deltas[h])).astype(bf16)
            dq = mm(kt_ref[lines, 0:wide], ds_ref[h, 0:wide], NN) + mm(kt_ref[lines, slot], ds_ref[h, wide:], NN)
            a, b = dq[:ROT // 2], dq[ROT // 2:ROT]
            cosine, sine = cos_ref[:, own], sin_ref[:, own]
            grads.append(jnp.concatenate([a * cosine + b * sine, b * cosine - a * sine, dq[ROT:]], axis=0))
        for c in range(count + 1):
            at = slot if c == count else cut(c)
            dva_ref[at, :] += mm(p_ref[0, cut(c)], do_heads[0], NN) + mm(p_ref[1, cut(c)], do_heads[1], NN)
            dka_ref[at, :] += mm(ds_ref[0, cut(c)], q_heads[0], NN) + mm(ds_ref[1, cut(c)], q_heads[1], NN)
        o_ref[own, :] = mm(ident, jnp.concatenate(outs, axis=0).astype(bf16), NT).astype(bf16)
        dq_ref[own, :] = mm(ident, (jnp.concatenate(grads, axis=0) * (HD ** (-0.5))).astype(bf16), NT).astype(bf16)

        return carry

    lax.fori_loop(0, 2 * per, block, 0)

    def flush(out, to, frm):
        rows = pl.ds(to, half)
        out[rows, :PAIR] = (dka_ref[frm:frm + half, :] * math.log(2.0)).astype(bf16)
        out[rows, PAIR:] = dva_ref[frm:frm + half, :].astype(bf16)

    flush(cont_ref, 0, wide)
    for s in range(n):
        flush(all_ref, pl.multiple_of(owner_ref[s] * half, half), s * half)


def attention(kind, owners, cos_t, sin_t, q, do, ks, vs, first, pairs):
    rows = q.shape[0]
    half = rows // 2
    n = 1 + ks[1].shape[0] // half
    wide = n * half
    keys = wide + half
    total = wide + QB
    qspec = pl.BlockSpec((rows, PAIR), lambda p: (0, p + first))
    ospec = pl.BlockSpec((rows, PAIR), lambda p: (0, p))
    table = pl.BlockSpec((ROT // 2, rows), lambda p: (0, 0))
    kspecs = [pl.BlockSpec((k.shape[0], PAIR), lambda p: (0, p + first)) for k in ks]
    gspecs = [pl.BlockSpec((size, 2 * PAIR), lambda p: (0, p)) for size in (wide, half)]
    s = jax.ShapeDtypeStruct
    pieces = pairs * rows // QB
    return pl.pallas_call(
        partial(attention_kernel, half, n),
        grid=(pairs,),
        in_specs=[pl.BlockSpec(memory_space=pltpu.SMEM), pl.BlockSpec(memory_space=pltpu.SMEM), table, table, qspec, qspec] + kspecs + kspecs,
        out_specs=[ospec, ospec] + gspecs,
        out_shape=[s((rows, pairs * PAIR), bf16), s((rows, pairs * PAIR), bf16)]
        + [s((size, 2 * pairs * PAIR), bf16) for size in (wide, half)],
        scratch_shapes=[pltpu.VMEM((PAIR, keys), bf16), pltpu.VMEM((PAIR, keys), bf16),
                        pltpu.VMEM((2, total, QB), f32), pltpu.VMEM((2, total, QB), bf16),
                        pltpu.VMEM((2, total, QB), bf16),
                        pltpu.VMEM((keys, PAIR), f32), pltpu.VMEM((keys, PAIR), f32)],
        compiler_params=pltpu.CompilerParams(vmem_limit_bytes=60 << 20),
        cost_estimate=pl.CostEstimate(flops=1 << 20, bytes_accessed=1 << 16, transcendentals=0),
        name="attention",
    )(kind, owners, cos_t, sin_t, q, do, *ks, *vs)


def pairs_of(bit, size):
    return [(a, a ^ bit) for a in range(size)]


def add_kernel(plan, *refs):
    for a, b, moves in plan:
        for source, to, target in moves:
            refs[to][target] = (refs[a][source].astype(f32) + refs[b][source].astype(f32)).astype(bf16)


def add_parts(arrays, plan, shapes, steps):
    def spec(shape):
        block = (*shape[:-1], shape[-1] // steps)
        return pl.BlockSpec(block, lambda j: (0,) * (len(shape) - 1) + (j,))

    return pl.pallas_call(
        partial(add_kernel, plan),
        grid=(steps,),
        in_specs=[spec(a.shape) for a in arrays],
        out_specs=[spec(shape) for shape in shapes],
        out_shape=[jax.ShapeDtypeStruct(shape, bf16) for shape in shapes],
        compiler_params=params(),
        cost_estimate=pl.CostEstimate(flops=1 << 20, bytes_accessed=1 << 16, transcendentals=0),
        name="add_parts",
    )(*arrays)


EVERY = slice(None)


def swap(a, bit):
    return lax.ppermute(a, "fsdp", pairs_of(bit, 8))


def steps_for(arrays):
    smallest = min(a.shape[-1] for a in arrays)
    return 4 if smallest % (4 * PAIR) == 0 else 1


def core_step(sends, keeps):
    count = len(sends)
    arrays, plan, shapes = [], [], []
    for send, keep in zip(sends, keeps):
        rows, cols = send.shape
        cut = (2, 2, 2, rows // 8, cols)
        to = 2 * count + len(shapes)
        moves = [((EVERY, 1, 0), to, (EVERY,)), ((EVERY, 0, 0), to + 1, (EVERY,)),
                 ((1, EVERY, 1), to + 2, (EVERY,)), ((0, EVERY, 1), to + 3, (EVERY,))]
        plan.append((len(arrays), len(arrays) + 1, moves))
        arrays += [keep.reshape(cut), swap(send, 1).reshape(cut)]
        shapes += [(2, rows // 8, cols)] * 4
    return add_parts(arrays, plan, shapes, steps_for(arrays))


def side_step(items):
    arrays, plan, shapes = [], [], []
    for i in range(0, len(items), 4):
        for send, keep, bit in ((items[i], items[i + 1], 2), (items[i + 2], items[i + 3], 4)):
            to = len(items) + len(shapes)
            plan.append((len(arrays), len(arrays) + 1, [((1,), to, (EVERY,)), ((0,), to + 1, (EVERY,))]))
            arrays += [keep, swap(send, bit)]
            shapes += [keep.shape[1:]] * 2
    return add_parts(arrays, plan, shapes, steps_for(arrays))


def last_step(items):
    arrays, plan, shapes = [], [], []
    for i in range(0, len(items), 4):
        to = len(items) + len(shapes)
        for at, (send, keep, bit) in enumerate(((items[i], items[i + 1], 4), (items[i + 2], items[i + 3], 2))):
            plan.append((len(arrays), len(arrays) + 1, [((EVERY,), to, (at,))]))
            arrays += [keep, swap(send, bit)]
        shapes.append((2, *keep.shape))
    parts = add_parts(arrays, plan, shapes, steps_for(arrays))
    return [part.reshape(-1, part.shape[-1]) for part in parts]


def along(part):
    return lax.psum_scatter(part, "ctx", scatter_dimension=0, tiled=True)


def after(value, *others):
    return lax.optimization_barrier((value, *others))[0]


def kept_after(items, *others):
    return [after(a, *others) if i % 2 else a for i, a in enumerate(items)]


def fast(inputs, cotangent, positions, segments, ln1_gain, ln1_bias, w_qkv, b_qkv, w_attn_out, b_out,
         ln2_gain, ln2_bias, w_in, b_in, w_out):
    x, grad_out, pos = inputs[0], cotangent[0], positions[0]
    rows, width = x.shape
    half = rows // 2
    n = lax.axis_size("ctx")
    ring = [(i, (i + 1) % n) for i in range(n)]
    back = [(i, (i - 1) % n) for i in range(n)]
    me, place = lax.axis_index("fsdp"), lax.axis_index("ctx")
    relative = [4 * dy + 2 * dx + 1 - keep for keep in (0, 1) for dy in (0, 1) for dx in (0, 1)]
    order = jnp.bitwise_xor(me, jnp.array(relative, jnp.int32))
    owners = lax.rem(place + n - jnp.arange(n), n)
    far = [None] * n
    toward, away = x[:half], x[:half]
    for s in range(1, n // 2 + 1):
        toward = lax.ppermute(toward, "ctx", ring)
        far[s] = toward
        if n - s > n // 2:
            away = lax.ppermute(away, "ctx", back)
            far[n - s] = away
    spots = [pos[::RB] // RB]
    for s in range(1, n):
        spots.append(lax.ppermute(spots[0][:half // RB], "ctx", [(i, (i + s) % n) for i in range(n)]))
    mine = (ln1_gain, ln1_bias, b_qkv, b_out, ln2_gain, ln2_bias, b_in)
    small = lax.all_gather(jnp.concatenate(mine).reshape(1, -1), "fsdp", axis=0, tiled=True)
    full, at = [], 0
    for a in mine:
        full.append(small[:, at:at + a.shape[0]].reshape(-1).astype(f32))
        at += a.shape[0]
    gain_attn, shift_attn, bias_qkv, bias_out, gain_mlp, shift_mlp, bias_in = full
    weights = lax.all_gather(jnp.concatenate([w_qkv, w_attn_out], axis=1), "fsdp", axis=0, tiled=True)

    lane = jnp.arange(PAIR) % HD
    inverse = jnp.exp(-math.log(10000.0) * (2.0 / ROT) * (lane % (ROT // 2)).astype(f32))
    angles = jnp.arange(n * half + CLEN).astype(f32)[:, None] * inverse[None, :]
    sine = jnp.sin(angles)
    tables = (jnp.where(lane < ROT, jnp.cos(angles), 1.0), jnp.where(lane < ROT // 2, sine, 0.0),
              jnp.where((lane >= ROT // 2) & (lane < ROT), sine, 0.0))
    angles_t = pos.astype(f32)[None, :] * inverse[:ROT // 2, None]
    cos_t, sin_t = jnp.cos(angles_t), jnp.sin(angles_t)

    normed, queries, own_keys, own_values = qkv(
        spots[0], order, [after(x, far[1], far[n - 1], *spots[1:])], gain_attn, shift_attn, weights, bias_qkv, tables)
    far_keys, far_values = qkv(
        jnp.concatenate(spots[1:]), order, far[1:], gain_attn, shift_attn, weights, bias_qkv, tables)
    keys, values = (own_keys, far_keys), (own_values, far_values)
    grad_att = spread(grad_out, weights)
    weight_in = lax.all_gather(after(w_in, queries), "fsdp", axis=0, tiled=True)
    weight_out = lax.all_gather(after(w_out, queries), "fsdp", axis=0, tiled=True)

    per = half // QB
    earlier = jnp.stack([spots[s][0] < spots[0][0] for s in range(1, n)])
    local_row = jnp.arange(2 * per)[:, None]
    seen_own = local_row > jnp.arange(per)[None, :]
    seen_far = jnp.repeat(earlier[None, :] | (local_row >= per), per, axis=1)
    kind = jnp.where(jnp.concatenate([seen_own, seen_far], axis=1), 0.0, MASKED).astype(f32)

    attended, grad_q, own_kv, come_kv = [], [], [], []

    def attend(first, count, wait):
        out = attention(kind, owners, cos_t, sin_t, after(queries, *wait), grad_att, keys, values, first, count)
        attended.append(out[0])
        grad_q.append(out[1])
        come_kv.append(lax.psum_scatter(out[2], "ctx", scatter_dimension=0, tiled=True))
        own_kv.append(out[3])

    attend(0, 5, ())
    mlp_out, grad_mlp, in_send, in_keep, out_send, out_keep, db_in, db_out, dgain_mlp, dshift_mlp = mlp(
        order, after(x, *attended), grad_out, gain_mlp, shift_mlp, weight_in, bias_in, weight_out)
    attend(5, 1, (mlp_out,))
    steps_mlp = core_step([out_send, in_send], [out_keep, in_keep])
    attend(6, 2, (*attended, *steps_mlp))
    steps_mlp = side_step(kept_after(steps_mlp, *attended))
    output = join(after(x, *steps_mlp), attended, weights, mlp_out, bias_out)
    first_send, first_keep, grad_heads, db_q = first_tail(
        order, after(grad_out, output), normed, weights, attended, grad_q)
    next_send, next_keep, db_next, grad_heads = kv_tail(
        False, 0, spots[0], x, normed, gain_attn, weights, tables, grad_mlp, grad_heads, own_kv[:1], come_kv[:1])
    part_out, part_in = last_step(kept_after(steps_mlp, grad_heads))
    steps_first = core_step([first_send, next_send], [first_keep, next_keep])
    last_send, last_keep, db_last, grad_inputs, dgain_attn, dshift_attn = kv_tail(
        True, 5, spots[0], after(x, part_out, part_in, *steps_first), normed, gain_attn, weights, tables, grad_mlp, grad_heads,
        own_kv[1:], come_kv[1:])
    sum_out, sum_in = along(part_out), along(part_in)
    steps_first = side_step(kept_after(steps_first, last_send))

    def halves(a, i):
        return a.reshape(a.shape[0], -1, 2, PAIR)[:, :, i].reshape(a.shape[0], -1)

    db_kv = [halves(jnp.concatenate([db_next, db_last], axis=1), i) for i in range(2)]
    smalls = [a.reshape(width, -1) for a in
              (dgain_attn, dshift_attn, jnp.concatenate([db_q, *db_kv], axis=1), db_out, dgain_mlp, dshift_mlp, db_in)]
    used = sum(a.shape[1] for a in smalls)
    packed = jnp.concatenate(smalls + [jnp.zeros((width, PAIR - used), f32)], axis=1).astype(bf16)
    packed = packed.reshape(8, width // 8, PAIR)[order].reshape(2, width // 2, PAIR)
    steps_last = core_step([after(last_send, *steps_first), packed[0]], [last_keep, packed[1]])
    part_first = jnp.concatenate(last_step(steps_first), axis=1)
    sum_first = along(part_first)
    sum_last = along(jnp.concatenate(last_step(side_step(kept_after(steps_last, part_first))), axis=1))
    packed = sum_last[:, -PAIR:].astype(f32)
    sum_attn, sum_q = sum_first[:, :width], sum_first[:, width:2 * width]
    rest = jnp.concatenate([sum_first[:, 2 * width:], sum_last[:, :-PAIR]], axis=1)
    sum_qkv = jnp.concatenate([sum_q, halves(rest, 0), halves(rest, 1)], axis=1)
    done, at = [], 0
    for a in smalls:
        done.append(packed[:, at:at + a.shape[1]].reshape(-1))
        at += a.shape[1]
    return (output[None], grad_inputs[None], done[0], done[1], sum_qkv.astype(f32), done[2], sum_attn.astype(f32),
            done[3], done[4], done[5], sum_in.astype(f32), done[6], sum_out.astype(f32))


def local(*args):
    half = args[0].shape[1] // 2
    if args[0].shape[0] == 1 and half % CLEN == 0 and lax.axis_size("fsdp") == 8:
        return fast(*args)
    return generic(*args)


def generic(
    inputs,
    cotangent,
    positions,
    segments,
    ln1_gain,
    ln1_bias,
    w_qkv,
    b_qkv,
    w_attn_out,
    b_out,
    ln2_gain,
    ln2_bias,
    w_in,
    b_in,
    w_out,
):
    shards = (
        ln1_gain,
        ln1_bias,
        w_qkv,
        b_qkv,
        w_attn_out,
        b_out,
        ln2_gain,
        ln2_bias,
        w_in,
        b_in,
        w_out,
    )
    params = (
        lax.all_gather(shards[0], "fsdp", axis=0, tiled=True),
        lax.all_gather(shards[1], "fsdp", axis=0, tiled=True),
        lax.all_gather(shards[2], "fsdp", axis=0, tiled=True),
        lax.all_gather(shards[3], "fsdp", axis=0, tiled=True),
        lax.all_gather(shards[4], "fsdp", axis=0, tiled=True),
        lax.all_gather(shards[5], "fsdp", axis=0, tiled=True),
        lax.all_gather(shards[6], "fsdp", axis=0, tiled=True),
        lax.all_gather(shards[7], "fsdp", axis=0, tiled=True),
        lax.all_gather(shards[8], "fsdp", axis=0, tiled=True),
        lax.all_gather(shards[9], "fsdp", axis=0, tiled=True),
        lax.all_gather(shards[10], "fsdp", axis=0, tiled=True),
    )
    groups, local_len, width = inputs.shape
    rows_total = groups * local_len
    block = math.gcd(local_len, 256)
    label_pos, label_seg = (
        lax.all_gather(positions, "ctx", axis=1, tiled=True),
        lax.all_gather(segments, "ctx", axis=1, tiled=True),
    )
    count = label_pos.shape[1] // block
    f32 = jnp.float32
    bf16 = jnp.bfloat16
    (
        gain_attn,
        shift_attn,
        weight_qkv,
        bias_qkv,
        weight_attn,
        bias_out,
        gain_mlp,
        shift_mlp,
        weight_in,
        bias_in,
        weight_out,
    ) = params
    flat_in = inputs.reshape(rows_total, width).astype(f32)
    normed_attn = layer_norm(flat_in, gain_attn.astype(f32), shift_attn.astype(f32)).astype(bf16)
    normed_mlp = layer_norm(flat_in, gain_mlp.astype(f32), shift_mlp.astype(f32)).astype(bf16)
    projected = jnp.dot(normed_attn, weight_qkv, preferred_element_type=f32) + bias_qkv.astype(f32)
    cosine, sine = rotary_tables(positions)

    def split_heads(columns):
        return columns.reshape(groups, local_len, HEADS, HD)

    scale = HD ** (-0.5)
    queries = (rotate(split_heads(projected[:, :width]), cosine, sine) * scale).astype(bf16)
    keys_own = rotate(split_heads(projected[:, width : 2 * width]), cosine, sine).astype(bf16)
    values_own = split_heads(projected[:, 2 * width :]).astype(bf16)
    keys_all, values_all = (
        lax.all_gather(keys_own, "ctx", axis=1, tiled=True),
        lax.all_gather(values_own, "ctx", axis=1, tiled=True),
    )

    def key_block(index):
        start = index * block
        keys_blk = lax.dynamic_slice_in_dim(keys_all, start, block, 1)
        values_blk = lax.dynamic_slice_in_dim(values_all, start, block, 1)
        mask = allowed_mask(
            positions,
            segments,
            lax.dynamic_slice_in_dim(label_pos, start, block, 1),
            lax.dynamic_slice_in_dim(label_seg, start, block, 1),
        )
        return (keys_blk, values_blk, mask)

    def total_step(carry, index):
        peak, total = carry
        keys_blk, values_blk, mask = key_block(index)
        scores = jnp.where(mask, scores_of(queries, keys_blk), MASKED)
        fresh = jnp.maximum(peak, jnp.max(scores, axis=-1))
        added = jnp.sum(jnp.where(mask, jnp.exp(scores - fresh[..., None]), 0.0), axis=-1)
        return ((fresh, total * jnp.exp(peak - fresh) + added), None)

    stat_shape = (groups, HEADS, local_len)
    (peak, total), unused = lax.scan(
        total_step,
        (jnp.full(stat_shape, MASKED, f32), jnp.zeros(stat_shape, f32)),
        jnp.arange(count),
    )
    log_total = peak + jnp.log(total)

    def attend_step(rounded_sum, index):
        keys_blk, values_blk, mask = key_block(index)
        probs = jnp.where(mask, jnp.exp(scores_of(queries, keys_blk) - log_total[..., None]), 0.0)
        rounded_sum = rounded_sum + jnp.einsum(
            "ghqk,gkhd->gqhd", probs.astype(bf16), values_blk, preferred_element_type=f32
        )
        return (rounded_sum, None)

    head_shape = (groups, local_len, HEADS, HD)
    rounded_sum, unused = lax.scan(attend_step, jnp.zeros(head_shape, f32), jnp.arange(count))
    attended = rounded_sum.reshape(rows_total, width).astype(bf16)
    pre_act = jnp.dot(normed_mlp, weight_in, preferred_element_type=f32) + bias_in.astype(f32)
    activated = jax.nn.gelu(pre_act, approximate=False).astype(bf16)
    output = (
        flat_in
        + jnp.dot(attended, weight_attn, preferred_element_type=f32)
        + jnp.dot(activated, weight_out, preferred_element_type=f32)
        + bias_out.astype(f32)
    )
    (
        gain_attn,
        shift_attn,
        weight_qkv,
        bias_qkv,
        weight_attn,
        bias_out,
        gain_mlp,
        shift_mlp,
        weight_in,
        bias_in,
        weight_out,
    ) = params
    grad_out = cotangent.reshape(rows_total, width)
    grad_bias_out = jnp.sum(grad_out.astype(f32), axis=0)
    grad_weight_out = jnp.einsum("rf,rd->fd", activated, grad_out, preferred_element_type=f32)
    grad_act = jnp.einsum("rd,fd->rf", grad_out, weight_out, preferred_element_type=f32)
    unused, gelu_back = jax.vjp(partial(jax.nn.gelu, approximate=False), pre_act)
    grad_pre = gelu_back(grad_act)[0].astype(bf16)
    grad_weight_in = jnp.einsum("rd,rf->df", normed_mlp, grad_pre, preferred_element_type=f32)
    grad_bias_in = jnp.sum(grad_pre.astype(f32), axis=0)
    grad_normed_mlp = jnp.einsum("rf,df->rd", grad_pre, weight_in, preferred_element_type=f32)
    grad_weight_attn = jnp.einsum("ra,rd->ad", attended, grad_out, preferred_element_type=f32)
    grad_att = (
        jnp.einsum("rd,ad->ra", grad_out, weight_attn, preferred_element_type=f32)
        .astype(bf16)
        .reshape(head_shape)
    )
    delta = jnp.einsum(
        "gqhd,gqhd->ghq", grad_att.astype(f32), rounded_sum, precision=lax.Precision.HIGHEST
    )

    def back_step(carry, index):
        keys_blk, values_blk, mask = key_block(index)
        rounded, grad_scores = block_grads(
            queries, grad_att, log_total, delta, mask, keys_blk, values_blk
        )
        carry = carry + jnp.einsum(
            "ghqk,gkhd->gqhd", grad_scores, keys_blk, preferred_element_type=f32
        )
        key_term = jnp.einsum("ghqk,gqhd->gkhd", grad_scores, queries, preferred_element_type=f32)
        value_term = jnp.einsum("ghqk,gqhd->gkhd", rounded, grad_att, preferred_element_type=f32)
        return (carry, (key_term, value_term))

    grad_queries, (key_terms, value_terms) = lax.scan(
        back_step, jnp.zeros(head_shape, f32), jnp.arange(count)
    )
    key_sums, value_sums = (
        lax.psum_scatter(
            key_terms.astype(jnp.bfloat16), "ctx", scatter_dimension=0, tiled=True
        ).astype(jnp.float32),
        lax.psum_scatter(
            value_terms.astype(jnp.bfloat16), "ctx", scatter_dimension=0, tiled=True
        ).astype(jnp.float32),
    )
    grad_keys = jnp.transpose(key_sums, (1, 0, 2, 3, 4)).reshape(head_shape)
    grad_values = jnp.transpose(value_sums, (1, 0, 2, 3, 4)).reshape(head_shape)
    grad_q_pre = unrotate(grad_queries * scale, cosine, sine).reshape(rows_total, width)
    grad_k_pre = unrotate(grad_keys, cosine, sine).reshape(rows_total, width)
    grad_projected = jnp.concatenate(
        [grad_q_pre, grad_k_pre, grad_values.reshape(rows_total, width)], axis=1
    ).astype(bf16)
    grad_weight_qkv = jnp.einsum(
        "rd,re->de", normed_attn, grad_projected, preferred_element_type=f32
    )
    grad_bias_qkv = jnp.sum(grad_projected.astype(f32), axis=0)
    grad_normed_attn = jnp.einsum(
        "re,de->rd", grad_projected, weight_qkv, preferred_element_type=f32
    )
    unused, norm_back_attn = jax.vjp(
        layer_norm, flat_in, gain_attn.astype(f32), shift_attn.astype(f32)
    )
    grad_in_attn, grad_gain_attn, grad_shift_attn = norm_back_attn(grad_normed_attn)
    unused, norm_back_mlp = jax.vjp(
        layer_norm, flat_in, gain_mlp.astype(f32), shift_mlp.astype(f32)
    )
    grad_in_mlp, grad_gain_mlp, grad_shift_mlp = norm_back_mlp(grad_normed_mlp)
    grad_inputs = (grad_out.astype(f32) + grad_in_attn + grad_in_mlp).reshape(
        groups, local_len, width
    )
    sums = (
        lax.psum_scatter(grad_gain_attn, ("fsdp", "ctx"), scatter_dimension=0, tiled=True),
        lax.psum_scatter(grad_shift_attn, ("fsdp", "ctx"), scatter_dimension=0, tiled=True),
        lax.psum_scatter(grad_weight_qkv, ("fsdp", "ctx"), scatter_dimension=0, tiled=True),
        lax.psum_scatter(grad_bias_qkv, ("fsdp", "ctx"), scatter_dimension=0, tiled=True),
        lax.psum_scatter(grad_weight_attn, ("fsdp", "ctx"), scatter_dimension=0, tiled=True),
        lax.psum_scatter(grad_bias_out, ("fsdp", "ctx"), scatter_dimension=0, tiled=True),
        lax.psum_scatter(grad_gain_mlp, ("fsdp", "ctx"), scatter_dimension=0, tiled=True),
        lax.psum_scatter(grad_shift_mlp, ("fsdp", "ctx"), scatter_dimension=0, tiled=True),
        lax.psum_scatter(grad_weight_in, ("fsdp", "ctx"), scatter_dimension=0, tiled=True),
        lax.psum_scatter(grad_bias_in, ("fsdp", "ctx"), scatter_dimension=0, tiled=True),
        lax.psum_scatter(grad_weight_out, ("fsdp", "ctx"), scatter_dimension=0, tiled=True),
    )
    result = output.reshape(groups, local_len, width).astype(bf16)
    return (
        result,
        grad_inputs,
        sums[0],
        sums[1],
        sums[2],
        sums[3],
        sums[4],
        sums[5],
        sums[6],
        sums[7],
        sums[8],
        sums[9],
        sums[10],
    )


def solution(mesh):
    in_specs = (
        P("fsdp", "ctx", None),
        P("fsdp", "ctx", None),
        P("fsdp", "ctx"),
        P("fsdp", "ctx"),
        P("fsdp"),
        P("fsdp"),
        P("fsdp", None),
        P("fsdp"),
        P("fsdp", None),
        P("fsdp"),
        P("fsdp"),
        P("fsdp"),
        P("fsdp", None),
        P("fsdp"),
        P("fsdp", None),
    )
    out_specs = (
        P("fsdp", "ctx", None),
        P("fsdp", "ctx", None),
        P(("fsdp", "ctx")),
        P(("fsdp", "ctx")),
        P(("fsdp", "ctx"), None),
        P(("fsdp", "ctx")),
        P(("fsdp", "ctx"), None),
        P(("fsdp", "ctx")),
        P(("fsdp", "ctx")),
        P(("fsdp", "ctx")),
        P(("fsdp", "ctx"), None),
        P(("fsdp", "ctx")),
        P(("fsdp", "ctx"), None),
    )
    return jax.shard_map(local, mesh=mesh, in_specs=in_specs, out_specs=out_specs, check_vma=False)
```

```python
from functools import partial
import math

import jax
import jax.numpy as jnp
from jax import lax
from jax.experimental import pallas as pl
from jax.experimental.pallas import tpu as pltpu
from jax.sharding import PartitionSpec as P

HEADS = 16
HD = 64
ROT = 16
CLEN = 256
QB = 256
RB = 256
PAIR = 2 * HD
bf16 = jnp.bfloat16
f32 = jnp.float32
NN = (((1,), (0,)), ((), ()))
NT = (((1,), (1,)), ((), ()))
TN = (((0,), (0,)), ((), ()))


NORM_EPS = 1e-05
MASKED = -1e30


def layer_norm(values, scaling, offset):
    average = jnp.mean(values, axis=-1, keepdims=True)
    centered = values - average
    variance = jnp.mean(centered * centered, axis=-1, keepdims=True)
    return centered * lax.rsqrt(variance + NORM_EPS) * scaling + offset


def rotary_tables(positions):
    halfway = ROT // 2
    spacing = jnp.arange(halfway, dtype=jnp.float32) * (2.0 / ROT)
    inverse = jnp.exp(-math.log(10000.0) * spacing)
    angles = positions.astype(jnp.float32)[..., None] * inverse
    return (jnp.cos(angles), jnp.sin(angles))


def rotate(heads_in, cosine, sine):
    halfway = ROT // 2
    cosine = cosine[..., None, :]
    sine = sine[..., None, :]
    first = heads_in[..., :halfway]
    second = heads_in[..., halfway:ROT]
    return jnp.concatenate(
        [first * cosine - second * sine, second * cosine + first * sine, heads_in[..., ROT:]],
        axis=-1,
    )


def unrotate(grads_in, cosine, sine):
    halfway = ROT // 2
    cosine = cosine[..., None, :]
    sine = sine[..., None, :]
    first = grads_in[..., :halfway]
    second = grads_in[..., halfway:ROT]
    return jnp.concatenate(
        [first * cosine + second * sine, second * cosine - first * sine, grads_in[..., ROT:]],
        axis=-1,
    )


def allowed_mask(query_pos, query_seg, key_pos, key_seg):
    same_doc = (key_seg[:, None, :] == 0) | (key_seg[:, None, :] == query_seg[:, :, None])
    causal = key_pos[:, None, :] <= query_pos[:, :, None]
    return (same_doc & causal)[:, None]


def scores_of(queries, keys_blk):
    return jnp.einsum("gqhd,gkhd->ghqk", queries, keys_blk, preferred_element_type=jnp.float32)


def block_grads(queries, grad_att, log_total, delta, mask, keys_blk, values_blk):
    probs = jnp.where(mask, jnp.exp(scores_of(queries, keys_blk) - log_total[..., None]), 0.0)
    dprobs = jnp.einsum("gqhd,gkhd->ghqk", grad_att, values_blk, preferred_element_type=jnp.float32)
    grad_scores = (probs * (dprobs - delta[..., None])).astype(jnp.bfloat16)
    return (probs.astype(jnp.bfloat16), grad_scores)


def mm(a, b, dims):
    return lax.dot_general(a, b, dims, preferred_element_type=f32)


def row_stats(x):
    average = jnp.mean(x, axis=1, keepdims=True)
    centered = x - average
    return centered, lax.rsqrt(jnp.mean(centered * centered, axis=1, keepdims=True) + NORM_EPS)


def norm_rows(x, scaling, offset):
    centered, inverse = row_stats(x)
    return (centered * inverse * scaling + offset).astype(bf16)


def norm_back(x, grad, scaling):
    centered, inverse = row_stats(x)
    unit = centered * inverse
    e = grad * scaling
    inner = e - jnp.mean(e, axis=1, keepdims=True) - unit * jnp.mean(e * unit, axis=1, keepdims=True)
    return inverse * inner, grad * unit


def col_sum(a):
    return jnp.sum(a, axis=0, keepdims=True)


def vmem(*shape, dtype=f32):
    return pltpu.VMEM(shape, dtype)


def params():
    return pltpu.CompilerParams(vmem_limit_bytes=60 << 20)


ROOT = math.sqrt(0.5)
DENS = 1.0 / math.sqrt(2.0 * math.pi)


def reorder(order_ref, source, target):
    size = source.shape[1] // order_ref.shape[0]
    for i in range(order_ref.shape[0]):
        at = pl.multiple_of(order_ref[i] * size, size)
        target[:, i * size:(i + 1) * size] = source[:, pl.ds(at, size)]


def mlp_kernel(order_ref, x_ref, c_ref, gain_ref, shift_ref, win_ref, bin_ref, wout_ref,
               out_ref, gin_ref, dwin_send, dwin_keep, dwout_send, dwout_keep, dbin_ref, dbout_ref, dgain_ref, dshift_ref,
               h_ref, turned_ref, act_ref, gp_ref, gh_ref):
    step = pl.program_id(0)
    rows = x_ref.shape[0]
    blocks = [slice(r, r + RB) for r in range(0, rows, RB)]

    @pl.when(step == 0)
    def _():
        for r in blocks:
            h_ref[r, :] = norm_rows(x_ref[r, :].astype(f32), gain_ref[...], shift_ref[...])
            out_ref[r, :] = jnp.zeros((RB, out_ref.shape[1]), f32)
            gh_ref[r, :] = jnp.zeros((RB, gh_ref.shape[1]), f32)
        reorder(order_ref, h_ref, turned_ref)

    dbin = jnp.zeros(dbin_ref.shape, f32)
    for r in blocks:
        pre = mm(h_ref[r, :], win_ref[...], NN) + bin_ref[...]
        phi = 0.5 + 0.5 * lax.erf(pre * ROOT)
        act_ref[r, :] = (pre * phi).astype(bf16)
        gp = phi + pre * (DENS * jnp.exp(-0.5 * (pre * pre)))
        gact = mm(c_ref[r, :], wout_ref[...], NT)
        gpre = (gact * gp).astype(bf16)
        gp_ref[r, :] = gpre
        dbin = dbin + col_sum(gpre.astype(f32))
    for r in blocks:
        out_ref[r, :] += mm(act_ref[r, :], wout_ref[...], NN)
        gh_ref[r, :] += mm(gp_ref[r, :], win_ref[...], NT)
    dwout = mm(act_ref[...], c_ref[...], TN).astype(bf16)
    middle = pl.num_programs(0) // 2

    @pl.when(step < middle)
    def _():
        dwout_send[...] = dwout

    @pl.when(step >= middle)
    def _():
        dwout_keep[...] = dwout

    dwin = mm(turned_ref[...], gp_ref[...], TN).astype(bf16)
    dwin_send[...] = dwin[:dwin_send.shape[0]]
    dwin_keep[...] = dwin[dwin_send.shape[0]:]
    dbin_ref[...] = dbin

    @pl.when(step == pl.num_programs(0) - 1)
    def _():
        dgain = jnp.zeros(dgain_ref.shape, f32)
        dshift = jnp.zeros(dshift_ref.shape, f32)
        dbout = jnp.zeros(dbout_ref.shape, f32)
        for r in blocks:
            grad = gh_ref[r, :]
            back, scaled = norm_back(x_ref[r, :].astype(f32), grad, gain_ref[...])
            c = c_ref[r, :].astype(f32)
            gin_ref[r, :] = back + c
            dgain += col_sum(scaled)
            dshift += col_sum(grad)
            dbout += col_sum(c)
        dgain_ref[...] = dgain
        dshift_ref[...] = dshift
        dbout_ref[...] = dbout


def mlp(order, x, c, gain, shift, weight_in, bias_in, weight_out):
    rows, width = x.shape
    ff = weight_in.shape[1]
    steps = order.shape[0]
    fc = ff // steps
    whole = pl.BlockSpec((rows, width), lambda j, o: (0, 0))
    line = pl.BlockSpec((1, width), lambda j, o: (0, 0))
    down = pl.BlockSpec((width // 2, fc), lambda j, o: (0, o[j]))
    s = jax.ShapeDtypeStruct
    return pl.pallas_call(
        mlp_kernel,
        grid_spec=pltpu.PrefetchScalarGridSpec(
            num_scalar_prefetch=1,
            grid=(steps,),
            in_specs=[whole, whole, line, line, pl.BlockSpec((width, fc), lambda j, o: (0, o[j])),
                      pl.BlockSpec((1, fc), lambda j, o: (0, o[j])), pl.BlockSpec((fc, width), lambda j, o: (o[j], 0))],
            out_specs=[whole, whole, down, down,
                       pl.BlockSpec((fc, width), lambda j, o: (jnp.minimum(j, steps // 2 - 1), 0)),
                       pl.BlockSpec((fc, width), lambda j, o: (jnp.maximum(j - steps // 2, 0), 0)),
                       pl.BlockSpec((1, fc), lambda j, o: (0, o[j])), line, line, line],
            scratch_shapes=[vmem(rows, width, dtype=bf16), vmem(rows, width, dtype=bf16), vmem(rows, fc, dtype=bf16),
                            vmem(rows, fc, dtype=bf16), vmem(rows, width)],
        ),
        out_shape=[s((rows, width), f32), s((rows, width), f32), s((width // 2, ff), bf16), s((width // 2, ff), bf16),
                   s((ff // 2, width), bf16), s((ff // 2, width), bf16), s((1, ff), f32), s((1, width), f32),
                   s((1, width), f32), s((1, width), f32)],
        compiler_params=params(),
        cost_estimate=pl.CostEstimate(flops=1 << 20, bytes_accessed=1 << 16, transcendentals=0),
        name="mlp",
    )(order, x, c, gain.reshape(1, -1), shift.reshape(1, -1), weight_in, bias_in.reshape(1, -1), weight_out)


def turn_lanes(u, cosine, low, high, sign):
    half = ROT // 2
    parts = []
    for at in range(0, u.shape[1], PAIR):
        g = u[:, at:at + PAIR]
        parts.append(g * cosine + sign * (pltpu.roll(g, half, 1) * high - pltpu.roll(g, PAIR - half, 1) * low))
    return jnp.concatenate(parts, axis=1)


def qkv_kernel(far, spot_ref, order_ref, gain_ref, shift_ref, w_ref, b_ref, cos_ref, low_ref, high_ref, *refs):
    with_q = far == 0
    if with_q:
        x_ref, outs = refs[0], refs[1:]
    else:
        x_refs, outs, x_ref = refs[:far], refs[far:-1], refs[-1]
        step = pl.program_id(0)
        per = pl.num_programs(0) // far
        for s in range(far):
            @pl.when(step // per == s)
            def _(s=s):
                x_ref[...] = x_refs[s][...]
    width = x_ref.shape[1]
    h = norm_rows(x_ref[...].astype(f32), gain_ref[...], shift_ref[...])
    tables = (cos_ref[...], low_ref[...], high_ref[...])
    if with_q:
        h_ref, q_ref, k_ref, v_ref, plain_ref = outs
        plain_ref[...] = h
        reorder(order_ref, plain_ref, h_ref)
        q = mm(h, w_ref[:, :width], NN) + b_ref[:, :width]
        q_ref[...] = (turn_lanes(q, *tables, 1.0) * (HD ** (-0.5) / math.log(2.0))).astype(bf16)
    else:
        k_ref, v_ref = outs
    k = mm(h, w_ref[:, width:2 * width], NN) + b_ref[:, width:2 * width]
    k_ref[...] = turn_lanes(k, *tables, 1.0).astype(bf16)
    v_ref[...] = (mm(h, w_ref[:, 2 * width:], NN) + b_ref[:, 2 * width:]).astype(bf16)


def qkv(spots, order, xs, gain, shift, weight, bias, tables):
    far = len(xs) if len(xs) > 1 else 0
    rows, width = xs[0].shape
    per = rows // RB
    total = len(xs) * rows
    s = jax.ShapeDtypeStruct((total, width), bf16)
    block = pl.BlockSpec((RB, width), lambda j, spot, o: (j, 0))
    line = pl.BlockSpec((1, width), lambda j, spot, o: (0, 0))
    table = pl.BlockSpec((RB, PAIR), lambda j, spot, o: (spot[j], 0))
    count = 2 if far else 4

    def window(i):
        return pl.BlockSpec((RB, width), lambda j, spot, o: (jnp.clip(j - i * per, 0, per - 1), 0))

    return pl.pallas_call(
        partial(qkv_kernel, far),
        grid_spec=pltpu.PrefetchScalarGridSpec(
            num_scalar_prefetch=2,
            grid=(total // RB,),
            in_specs=[line, line, pl.BlockSpec((width, 3 * width), lambda j, spot, o: (0, 0)),
                      pl.BlockSpec((1, 3 * width), lambda j, spot, o: (0, 0)), table, table, table]
            + [window(i) for i in range(len(xs))],
            out_specs=[block] * count,
            scratch_shapes=[vmem(RB, width, dtype=bf16)],
        ),
        out_shape=[s] * count,
        compiler_params=params(),
        cost_estimate=pl.CostEstimate(flops=1 << 20, bytes_accessed=1 << 16, transcendentals=0),
        name="kv_remote" if far else "qkv_own",
    )(spots, order, gain.reshape(1, -1), shift.reshape(1, -1), weight, bias.reshape(1, -1), *tables, *xs)


def gather_rows(step, spot, tables, own_refs, come_refs, p_ref, k_at, v_at):
    half = pl.num_programs(0) // 2
    columns = [(g, at) for g in range(len(own_refs)) for at in range(0, own_refs[g].shape[1], 2 * PAIR)]

    def put(refs):
        for to, (g, at) in enumerate(columns):
            turned = turn_lanes(refs[g][:, at:at + PAIR].astype(f32), *tables, -1.0).astype(bf16)
            p_ref[spot, k_at + to * PAIR:k_at + (to + 1) * PAIR] = turned
            p_ref[spot, v_at + to * PAIR:v_at + (to + 1) * PAIR] = refs[g][:, at + PAIR:at + 2 * PAIR]

    @pl.when(step < half)
    def _():
        put(come_refs)

    @pl.when(step >= half)
    def _():
        put(own_refs)


def half_windows(arrays, count):
    half = count // 2
    come = [pl.BlockSpec((RB, a.shape[1]), lambda j, *o: (jnp.clip(j, 0, half - 1), 0)) for a in arrays]
    own = [pl.BlockSpec((RB, a.shape[1]), lambda j, *o: (jnp.clip(j - half, 0, half - 1), 0)) for a in arrays]
    return own, come


def first_kernel(groups, spot_ref, order_ref, c_ref, h_ref, wq_ref, wk_ref, wv_ref, cos_ref, low_ref, high_ref, own_ref,
                 come_ref, *refs):
    att_refs, dq_refs = refs[:groups], refs[groups:2 * groups]
    send_ref, keep_ref, gh_ref, db_ref, p_ref, att_ref, turned_ref = refs[2 * groups:]
    step = pl.program_id(0)
    width = c_ref.shape[1]
    spot = pl.ds(pl.multiple_of(step * RB, RB), RB)
    at = 0
    for g in range(groups):
        size = att_refs[g].shape[1]
        att_ref[:, at:at + size] = att_refs[g][...]
        p_ref[spot, at:at + size] = dq_refs[g][...]
        at += size
    for i in range(order_ref.shape[0]):
        size = width // order_ref.shape[0]
        lanes = pl.ds(pl.multiple_of(order_ref[i] * size, size), size)
        turned_ref[spot, i * size:(i + 1) * size] = att_ref[:, lanes]
    count = wk_ref.shape[1]
    gather_rows(step, spot, (cos_ref[...], low_ref[...], high_ref[...]), [own_ref], [come_ref], p_ref, width, width + count)
    gh_ref[...] = (mm(p_ref[spot, :width], wq_ref[...], NT) + mm(p_ref[spot, width:width + count], wk_ref[...], NT)
                   + mm(p_ref[spot, width + count:], wv_ref[...], NT))
    db = col_sum(p_ref[spot, :].astype(f32))

    @pl.when(step == 0)
    def _():
        db_ref[...] = db

    @pl.when(step > 0)
    def _():
        db_ref[...] += db

    @pl.when(step == pl.num_programs(0) - 1)
    def _():
        half = send_ref.shape[0]
        for to in range(0, send_ref.shape[1], 512):
            if to < width:
                dw = mm(turned_ref[...], c_ref[:, to:to + 512], TN)
            else:
                dw = mm(h_ref[...], p_ref[:, to - width:to - width + 512], TN)
            dw = dw.astype(bf16)
            send_ref[:, to:to + 512] = dw[:half]
            keep_ref[:, to:to + 512] = dw[half:]


def first_tail(spots, order, c, h, weights, tables, attended, dqs, own, come):
    rows, width = c.shape
    cols = own.shape[1] // 2
    steps = rows // RB
    total = 2 * width + 2 * cols
    s = jax.ShapeDtypeStruct

    def full(shape):
        return pl.BlockSpec(shape, lambda j, spot, o: (0, 0), pipeline_mode=pl.Buffered(1))

    def weight(size, at):
        return pl.BlockSpec((width, size), lambda j, spot, o: (0, at // size), pipeline_mode=pl.Buffered(1))

    def window(a):
        return pl.BlockSpec((RB, a.shape[1]), lambda j, spot, o: (j, 0))

    table = pl.BlockSpec((RB, PAIR), lambda j, spot, o: (spot[j], 0))
    owns, comes = half_windows([own], steps)
    return pl.pallas_call(
        partial(first_kernel, len(dqs)),
        grid_spec=pltpu.PrefetchScalarGridSpec(
            num_scalar_prefetch=2,
            grid=(steps,),
            in_specs=[full(c.shape), full(h.shape), weight(width, 0), weight(cols, width), weight(cols, 2 * width)] + [table] * 3
            + owns + comes + [window(a) for a in (*attended, *dqs)],
            out_specs=[full((width // 2, total)), full((width // 2, total)), window(c), full((1, total - width))],
            scratch_shapes=[vmem(rows, total - width, dtype=bf16), vmem(RB, width, dtype=bf16), vmem(rows, width, dtype=bf16)],
        ),
        out_shape=[s((width // 2, total), bf16), s((width // 2, total), bf16), s((rows, width), f32), s((1, total - width), f32)],
        compiler_params=params(),
        cost_estimate=pl.CostEstimate(flops=24 << 30, bytes_accessed=1 << 20, transcendentals=0),
        name="first_tail",
    )(spots, order, c, h, weights, weights, weights, *tables, own, come, *attended, *dqs)


def last_kernel(groups, spot_ref, h_ref, gain_ref, wk_ref, wv_ref, x_ref, cos_ref, low_ref, high_ref, gin_ref, ghin_ref, *refs):
    own_refs, come_refs = refs[:groups], refs[groups:2 * groups]
    grad_ref, send_ref, keep_ref, db_ref, dgain_ref, dshift_ref, p_ref = refs[2 * groups:]
    step = pl.program_id(0)
    spot = pl.ds(pl.multiple_of(step * RB, RB), RB)
    count = wk_ref.shape[1]
    gather_rows(step, spot, (cos_ref[...], low_ref[...], high_ref[...]), own_refs, come_refs, p_ref, 0, count)
    grad = (ghin_ref[...] + mm(p_ref[spot, :count], wk_ref[...], NT) + mm(p_ref[spot, count:], wv_ref[...], NT))
    back, scaled = norm_back(x_ref[...].astype(f32), grad, gain_ref[...])
    grad_ref[...] = back + gin_ref[...]
    sums = col_sum(p_ref[spot, :].astype(f32)), col_sum(scaled), col_sum(grad)

    @pl.when(step == 0)
    def _():
        for ref, value in zip((db_ref, dgain_ref, dshift_ref), sums):
            ref[...] = value

    @pl.when(step > 0)
    def _():
        for ref, value in zip((db_ref, dgain_ref, dshift_ref), sums):
            ref[...] += value

    @pl.when(step == pl.num_programs(0) - 1)
    def _():
        half = send_ref.shape[0]
        for to in range(0, send_ref.shape[1], 512):
            dw = mm(h_ref[...], p_ref[:, to:to + 512], TN).astype(bf16)
            send_ref[:, to:to + 512] = dw[:half]
            keep_ref[:, to:to + 512] = dw[half:]


def last_tail(spots, x, h, gain, weights, tables, gin, gh, owns, comes):
    rows, width = x.shape
    cols = sum(a.shape[1] for a in owns) // 2
    steps = rows // RB
    s = jax.ShapeDtypeStruct

    def full(shape):
        return pl.BlockSpec(shape, lambda j, spot: (0, 0), pipeline_mode=pl.Buffered(1))

    def weight(at):
        return pl.BlockSpec((width, cols), lambda j, spot: (0, at // cols), pipeline_mode=pl.Buffered(1))

    block = pl.BlockSpec((RB, width), lambda j, spot: (j, 0))
    table = pl.BlockSpec((RB, PAIR), lambda j, spot: (spot[j], 0))
    own_windows, come_windows = half_windows(owns, steps)
    return pl.pallas_call(
        partial(last_kernel, len(owns)),
        grid_spec=pltpu.PrefetchScalarGridSpec(
            num_scalar_prefetch=1,
            grid=(steps,),
            in_specs=[full(h.shape), full((1, width)), weight(2 * width - cols), weight(3 * width - cols), block] + [table] * 3
            + [block, block] + own_windows + come_windows,
            out_specs=[block, full((width // 2, 2 * cols)), full((width // 2, 2 * cols)), full((1, 2 * cols)), full((1, width)),
                       full((1, width))],
            scratch_shapes=[vmem(rows, 2 * cols, dtype=bf16)],
        ),
        out_shape=[s((rows, width), f32), s((width // 2, 2 * cols), bf16), s((width // 2, 2 * cols), bf16), s((1, 2 * cols), f32),
                   s((1, width), f32), s((1, width), f32)],
        compiler_params=params(),
        cost_estimate=pl.CostEstimate(flops=12 << 30, bytes_accessed=1 << 20, transcendentals=0),
        name="last_tail",
    )(spots, h, gain.reshape(1, -1), weights, weights, x, *tables, gin, gh, *owns, *comes)


def join_kernel(groups, x_ref, w_ref, mlp_ref, b_ref, *refs):
    att_refs, (out_ref, att_ref) = refs[:groups], refs[groups:]
    at = 0
    for ref in att_refs:
        att_ref[:, at:at + ref.shape[1]] = ref[...]
        at += ref.shape[1]
    out = x_ref[...].astype(f32) + mm(att_ref[...], w_ref[...], NN) + mlp_ref[...] + b_ref[...]
    out_ref[...] = out.astype(bf16)


def join(x, attended, weights, mlp_out, bias):
    rows, width = x.shape
    s = jax.ShapeDtypeStruct
    block = pl.BlockSpec((RB, width), lambda j: (j, 0))
    return pl.pallas_call(
        partial(join_kernel, len(attended)),
        grid=(rows // RB,),
        in_specs=[block, pl.BlockSpec((width, width), lambda j: (0, 3)), block, pl.BlockSpec((1, width), lambda j: (0, 0))]
        + [pl.BlockSpec((RB, a.shape[1]), lambda j: (j, 0)) for a in attended],
        out_specs=block,
        out_shape=s((rows, width), bf16),
        scratch_shapes=[vmem(RB, width, dtype=bf16)],
        compiler_params=params(),
        cost_estimate=pl.CostEstimate(flops=12 << 30, bytes_accessed=1 << 20, transcendentals=0),
        name="join",
    )(x, weights, mlp_out, bias.reshape(1, -1), *attended)


def spread_kernel(c_ref, w_ref, out_ref):
    out_ref[...] = mm(c_ref[...], w_ref[...], NT).astype(bf16)


def spread(c, weights):
    rows, width = c.shape
    block = pl.BlockSpec((RB, width), lambda j: (j, 0))
    return pl.pallas_call(
        spread_kernel,
        grid=(rows // RB,),
        in_specs=[block, pl.BlockSpec((width, width), lambda j: (0, 3))],
        out_specs=block,
        out_shape=jax.ShapeDtypeStruct((rows, width), bf16),
        compiler_params=params(),
        cost_estimate=pl.CostEstimate(flops=1 << 20, bytes_accessed=1 << 16, transcendentals=0),
        name="spread",
    )(c, weights)


def fold(x, op):
    return op(x.reshape(x.shape[0] // 8, 8, x.shape[1]), axis=0)


def eye(size):
    return (lax.broadcasted_iota(jnp.int32, (size, size), 0) == lax.broadcasted_iota(jnp.int32, (size, size), 1)).astype(bf16)


def attention_kernel(half, n, kind_ref, owner_ref, cos_ref, sin_ref, q_ref, do_ref, *refs):
    k_refs, v_refs = refs[:2], refs[2:4]
    o_ref, dq_ref, all_ref, cont_ref, kt_ref, vt_ref, s_ref, p_ref, ds_ref, dka_ref, dva_ref = refs[4:]
    per = half // QB
    wide = n * half
    count = wide // QB
    spots = [(0, c * QB) for c in range(per)] + [(1, c * QB) for c in range((n - 1) * per)]

    ident = eye(PAIR)
    for refs_in, out in ((k_refs, kt_ref), (v_refs, vt_ref)):
        for c, (s, at) in enumerate(spots):
            out[:, c * QB:(c + 1) * QB] = refs_in[s][at:at + QB, :].T
        for c in range(per):
            out[:, wide + c * QB:wide + (c + 1) * QB] = refs_in[0][half + c * QB:half + (c + 1) * QB, :].T
    dka_ref[...] = jnp.zeros_like(dka_ref)
    dva_ref[...] = jnp.zeros_like(dva_ref)


    def block(qb, carry):
        own = pl.ds(pl.multiple_of(qb * QB, QB), QB)
        slot = pl.ds(pl.multiple_of(jnp.where(qb < per, qb * QB, wide + (qb - per) * QB), QB), QB)
        zero = jnp.zeros((), bf16)
        causal = lax.broadcasted_iota(jnp.int32, (QB, QB), 0) <= lax.broadcasted_iota(jnp.int32, (QB, QB), 1)
        left = lax.broadcasted_iota(jnp.int32, (QB, PAIR), 1) < HD

        def by_head(a):
            return jnp.where(left, a, zero), jnp.where(left, zero, a)

        def keys_of(some, c):
            if c == count:
                return some[0][own, :]
            s, at = spots[c]
            return some[s][at:at + QB, :]

        def cut(c):
            return slice(c * QB, (c + 1) * QB)

        ident = eye(QB)
        q_heads = by_head(q_ref[own, :])
        do_t = mm(eye(PAIR), do_ref[own, :], NT)
        upper = lax.broadcasted_iota(jnp.int32, (PAIR, QB), 0) < HD
        q_t = mm(eye(PAIR), q_ref[own, :], NT).astype(bf16)
        q_cols = jnp.where(upper, q_t, zero), jnp.where(upper, zero, q_t)
        peaks, norms, outs, deltas, scaled = [None, None], [None, None], [None, None], [None, None], [None, None]

        def scores(h):
            peak = jnp.full((8, QB), MASKED, f32)
            for c in range(count + 1):
                s = mm(keys_of(k_refs, c), q_cols[h], NN)
                if c == count:
                    s = jnp.where(causal, s, MASKED)
                    top = fold(s, jnp.max)
                else:
                    top = fold(s, jnp.max) + kind_ref[qb, c]
                s_ref[h, cut(c)] = s
                peak = jnp.maximum(peak, top)
            peaks[h] = jnp.max(peak, axis=0, keepdims=True)

        def weigh(h):
            total = jnp.zeros((8, QB), f32)
            for c in range(count + 1):
                bias = -peaks[h] if c == count else kind_ref[qb, c] - peaks[h]
                e = jnp.exp2(s_ref[h, cut(c)] + bias)
                total = total + fold(e, jnp.sum)
                p_ref[h, cut(c)] = e.astype(bf16)
            norms[h] = 1.0 / jnp.sum(total, axis=0, keepdims=True)

        def attend(h):
            lines = slice(h * HD, (h + 1) * HD)
            out = mm(vt_ref[lines, 0:wide], p_ref[h, 0:wide], NN) + mm(vt_ref[lines, slot], p_ref[h, wide:], NN)
            outs[h] = out * norms[h]
            deltas[h] = jnp.sum(outs[h] * do_t[lines], axis=0, keepdims=True) * norms[h]
            scaled[h] = do_t[lines] * norms[h]

        scores(0)
        scores(1)
        weigh(0)
        attend(0)
        weigh(1)
        attend(1)
        d_t = jnp.concatenate(scaled, axis=0).astype(bf16)
        d_cols = jnp.where(upper, d_t, zero), jnp.where(upper, zero, d_t)
        do_heads = by_head(mm(ident, d_t, NT).astype(bf16))
        grads = []
        for h in range(2):
            lines = slice(h * HD, (h + 1) * HD)
            for c in range(count + 1):
                dp = mm(keys_of(v_refs, c), d_cols[h], NN)
                ds_ref[h, cut(c)] = (p_ref[h, cut(c)].astype(f32) * (dp - deltas[h])).astype(bf16)
            dq = mm(kt_ref[lines, 0:wide], ds_ref[h, 0:wide], NN) + mm(kt_ref[lines, slot], ds_ref[h, wide:], NN)
            a, b = dq[:ROT // 2], dq[ROT // 2:ROT]
            cosine, sine = cos_ref[:, own], sin_ref[:, own]
            grads.append(jnp.concatenate([a * cosine + b * sine, b * cosine - a * sine, dq[ROT:]], axis=0))
        for c in range(count + 1):
            at = slot if c == count else cut(c)
            dva_ref[at, :] += mm(p_ref[0, cut(c)], do_heads[0], NN) + mm(p_ref[1, cut(c)], do_heads[1], NN)
            dka_ref[at, :] += mm(ds_ref[0, cut(c)], q_heads[0], NN) + mm(ds_ref[1, cut(c)], q_heads[1], NN)
        o_ref[own, :] = mm(ident, jnp.concatenate(outs, axis=0).astype(bf16), NT).astype(bf16)
        dq_ref[own, :] = mm(ident, (jnp.concatenate(grads, axis=0) * (HD ** (-0.5))).astype(bf16), NT).astype(bf16)

        return carry

    lax.fori_loop(0, 2 * per, block, 0)

    def flush(out, to, frm):
        rows = pl.ds(to, half)
        out[rows, :PAIR] = (dka_ref[frm:frm + half, :] * math.log(2.0)).astype(bf16)
        out[rows, PAIR:] = dva_ref[frm:frm + half, :].astype(bf16)

    flush(cont_ref, 0, wide)
    for s in range(n):
        flush(all_ref, pl.multiple_of(owner_ref[s] * half, half), s * half)


def attention(kind, owners, cos_t, sin_t, q, do, ks, vs, first, pairs):
    rows = q.shape[0]
    half = rows // 2
    n = 1 + ks[1].shape[0] // half
    wide = n * half
    keys = wide + half
    total = wide + QB
    qspec = pl.BlockSpec((rows, PAIR), lambda p: (0, p + first))
    ospec = pl.BlockSpec((rows, PAIR), lambda p: (0, p))
    table = pl.BlockSpec((ROT // 2, rows), lambda p: (0, 0))
    kspecs = [pl.BlockSpec((k.shape[0], PAIR), lambda p: (0, p + first)) for k in ks]
    gspecs = [pl.BlockSpec((size, 2 * PAIR), lambda p: (0, p)) for size in (wide, half)]
    s = jax.ShapeDtypeStruct
    pieces = pairs * rows // QB
    return pl.pallas_call(
        partial(attention_kernel, half, n),
        grid=(pairs,),
        in_specs=[pl.BlockSpec(memory_space=pltpu.SMEM), pl.BlockSpec(memory_space=pltpu.SMEM), table, table, qspec, qspec] + kspecs + kspecs,
        out_specs=[ospec, ospec] + gspecs,
        out_shape=[s((rows, pairs * PAIR), bf16), s((rows, pairs * PAIR), bf16)]
        + [s((size, 2 * pairs * PAIR), bf16) for size in (wide, half)],
        scratch_shapes=[pltpu.VMEM((PAIR, keys), bf16), pltpu.VMEM((PAIR, keys), bf16),
                        pltpu.VMEM((2, total, QB), f32), pltpu.VMEM((2, total, QB), bf16),
                        pltpu.VMEM((2, total, QB), bf16),
                        pltpu.VMEM((keys, PAIR), f32), pltpu.VMEM((keys, PAIR), f32)],
        compiler_params=pltpu.CompilerParams(vmem_limit_bytes=60 << 20),
        cost_estimate=pl.CostEstimate(flops=1 << 20, bytes_accessed=1 << 16, transcendentals=0),
        name="attention",
    )(kind, owners, cos_t, sin_t, q, do, *ks, *vs)


def pairs_of(bit, size):
    return [(a, a ^ bit) for a in range(size)]


def add_kernel(plan, *refs):
    for a, b, moves in plan:
        for source, to, target in moves:
            refs[to][target] = (refs[a][source].astype(f32) + refs[b][source].astype(f32)).astype(bf16)


def add_parts(arrays, plan, shapes, steps, load=0):
    def spec(shape):
        block = (*shape[:-1], shape[-1] // steps)
        return pl.BlockSpec(block, lambda j: (0,) * (len(shape) - 1) + (j,))

    return pl.pallas_call(
        partial(add_kernel, plan),
        grid=(steps,),
        in_specs=[spec(a.shape) for a in arrays],
        out_specs=[spec(shape) for shape in shapes],
        out_shape=[jax.ShapeDtypeStruct(shape, bf16) for shape in shapes],
        compiler_params=params(),
        cost_estimate=pl.CostEstimate(flops=(load << 30) + 1, bytes_accessed=1 << 16, transcendentals=0),
        name="add_parts",
    )(*arrays)


EVERY = slice(None)


def swap(a, bit):
    return lax.ppermute(a, "fsdp", pairs_of(bit, 8))


def steps_for(arrays):
    smallest = min(a.shape[-1] for a in arrays)
    return 4 if smallest % (4 * PAIR) == 0 else 1


def core_step(sends, keeps):
    count = len(sends)
    arrays, plan, shapes = [], [], []
    for send, keep in zip(sends, keeps):
        rows, cols = send.shape
        cut = (2, 2, 2, rows // 8, cols)
        to = 2 * count + len(shapes)
        moves = [((EVERY, 1, 0), to, (EVERY,)), ((EVERY, 0, 0), to + 1, (EVERY,)),
                 ((1, EVERY, 1), to + 2, (EVERY,)), ((0, EVERY, 1), to + 3, (EVERY,))]
        plan.append((len(arrays), len(arrays) + 1, moves))
        arrays += [keep.reshape(cut), swap(send, 1).reshape(cut)]
        shapes += [(2, rows // 8, cols)] * 4
    return add_parts(arrays, plan, shapes, steps_for(arrays))


def side_step(items):
    arrays, plan, shapes = [], [], []
    for i in range(0, len(items), 4):
        for send, keep, bit in ((items[i], items[i + 1], 2), (items[i + 2], items[i + 3], 4)):
            to = len(items) + len(shapes)
            plan.append((len(arrays), len(arrays) + 1, [((1,), to, (EVERY,)), ((0,), to + 1, (EVERY,))]))
            arrays += [keep, swap(send, bit)]
            shapes += [keep.shape[1:]] * 2
    return add_parts(arrays, plan, shapes, steps_for(arrays))


def last_step(items, load=0):
    arrays, plan, shapes = [], [], []
    for i in range(0, len(items), 4):
        to = len(items) + len(shapes)
        for at, (send, keep, bit) in enumerate(((items[i], items[i + 1], 4), (items[i + 2], items[i + 3], 2))):
            plan.append((len(arrays), len(arrays) + 1, [((EVERY,), to, (at,))]))
            arrays += [keep, swap(send, bit)]
        shapes.append((2, *keep.shape))
    parts = add_parts(arrays, plan, shapes, steps_for(arrays), load)
    return [part.reshape(-1, part.shape[-1]) for part in parts]


def along(part):
    return lax.psum_scatter(part, "ctx", scatter_dimension=0, tiled=True)


def after(value, *others):
    return lax.optimization_barrier((value, *others))[0]


def kept_after(items, *others):
    return [after(a, *others) if i % 2 else a for i, a in enumerate(items)]


def fast(inputs, cotangent, positions, segments, ln1_gain, ln1_bias, w_qkv, b_qkv, w_attn_out, b_out,
         ln2_gain, ln2_bias, w_in, b_in, w_out):
    x, grad_out, pos = inputs[0], cotangent[0], positions[0]
    rows, width = x.shape
    half = rows // 2
    n = lax.axis_size("ctx")
    ring = [(i, (i + 1) % n) for i in range(n)]
    back = [(i, (i - 1) % n) for i in range(n)]
    me, place = lax.axis_index("fsdp"), lax.axis_index("ctx")
    relative = [4 * dy + 2 * dx + 1 - keep for keep in (0, 1) for dy in (0, 1) for dx in (0, 1)]
    order = jnp.bitwise_xor(me, jnp.array(relative, jnp.int32))
    owners = lax.rem(place + n - jnp.arange(n), n)
    far = [None] * n
    toward, away = x[:half], x[:half]
    for s in range(1, n // 2 + 1):
        toward = lax.ppermute(toward, "ctx", ring)
        far[s] = toward
        if n - s > n // 2:
            away = lax.ppermute(away, "ctx", back)
            far[n - s] = away
    spots = [pos[::RB] // RB]
    for s in range(1, n):
        spots.append(lax.ppermute(spots[0][:half // RB], "ctx", [(i, (i + s) % n) for i in range(n)]))
    mine = (ln1_gain, ln1_bias, b_qkv, b_out, ln2_gain, ln2_bias, b_in)
    small = lax.all_gather(jnp.concatenate(mine).reshape(1, -1), "fsdp", axis=0, tiled=True)
    full, at = [], 0
    for a in mine:
        full.append(small[:, at:at + a.shape[0]].reshape(-1).astype(f32))
        at += a.shape[0]
    gain_attn, shift_attn, bias_qkv, bias_out, gain_mlp, shift_mlp, bias_in = full
    weights = lax.all_gather(jnp.concatenate([w_qkv, w_attn_out], axis=1), "fsdp", axis=0, tiled=True)

    lane = jnp.arange(PAIR) % HD
    inverse = jnp.exp(-math.log(10000.0) * (2.0 / ROT) * (lane % (ROT // 2)).astype(f32))
    angles = jnp.arange(n * half + CLEN).astype(f32)[:, None] * inverse[None, :]
    sine = jnp.sin(angles)
    tables = (jnp.where(lane < ROT, jnp.cos(angles), 1.0), jnp.where(lane < ROT // 2, sine, 0.0),
              jnp.where((lane >= ROT // 2) & (lane < ROT), sine, 0.0))
    angles_t = pos.astype(f32)[None, :] * inverse[:ROT // 2, None]
    cos_t, sin_t = jnp.cos(angles_t), jnp.sin(angles_t)

    normed, queries, own_keys, own_values = qkv(
        spots[0], order, [after(x, far[1], far[n - 1], *spots[1:])], gain_attn, shift_attn, weights, bias_qkv, tables)
    far_keys, far_values = qkv(
        jnp.concatenate(spots[1:]), order, far[1:], gain_attn, shift_attn, weights, bias_qkv, tables)
    keys, values = (own_keys, far_keys), (own_values, far_values)
    grad_att = spread(after(grad_out, far[n // 2]), weights)
    weight_in = lax.all_gather(after(w_in, queries), "fsdp", axis=0, tiled=True)
    weight_out = lax.all_gather(after(w_out, queries), "fsdp", axis=0, tiled=True)

    per = half // QB
    earlier = jnp.stack([spots[s][0] < spots[0][0] for s in range(1, n)])
    local_row = jnp.arange(2 * per)[:, None]
    seen_own = local_row > jnp.arange(per)[None, :]
    seen_far = jnp.repeat(earlier[None, :] | (local_row >= per), per, axis=1)
    kind = jnp.where(jnp.concatenate([seen_own, seen_far], axis=1), 0.0, MASKED).astype(f32)

    attended, grad_q, own_kv, come_kv = [], [], [], []

    def attend(first, count, wait):
        out = attention(kind, owners, cos_t, sin_t, after(queries, *wait), grad_att, keys, values, first, count)
        attended.append(out[0])
        grad_q.append(out[1])
        come_kv.append(lax.psum_scatter(out[2], "ctx", scatter_dimension=0, tiled=True))
        own_kv.append(out[3])

    attend(0, 4, ())
    mlp_out, grad_mlp, in_send, in_keep, out_send, out_keep, db_in, db_out, dgain_mlp, dshift_mlp = mlp(
        order, after(x, *attended), grad_out, gain_mlp, shift_mlp, weight_in, bias_in, weight_out)
    attend(4, 2, (mlp_out,))
    steps_mlp = core_step([out_send, in_send], [out_keep, in_keep])
    attend(6, 2, (*attended, *steps_mlp))
    steps_mlp = side_step(kept_after(steps_mlp, *attended))
    output = join(after(x, *steps_mlp), attended, weights, mlp_out, bias_out)
    first_send, first_keep, grad_heads, db_first = first_tail(
        spots[0], order, after(grad_out, output), normed, weights, tables, attended, grad_q, own_kv[0], come_kv[0])
    part_out, part_in = last_step(kept_after(steps_mlp, grad_heads), 48)
    steps_first = core_step([first_send], [first_keep])
    grad_inputs, last_send, last_keep, db_last, dgain_attn, dshift_attn = last_tail(
        spots[0], after(x, part_out, part_in, *steps_first), normed, gain_attn, weights, tables, grad_mlp, grad_heads,
        own_kv[1:], come_kv[1:])
    sum_out, sum_in = along(part_out), along(part_in)
    steps_first = side_step(kept_after(steps_first, last_send))
    cols = db_last.shape[1] // 2
    split = [width, width + (db_first.shape[1] - width) // 2]
    db_q, db_k, db_v = jnp.split(db_first, split, axis=1)
    db_qkv = jnp.concatenate([db_q, db_k, db_last[:, :cols], db_v, db_last[:, cols:]], axis=1)
    smalls = [a.reshape(width, -1) for a in
              (dgain_attn, dshift_attn, db_qkv, db_out, dgain_mlp, dshift_mlp, db_in)]
    used = sum(a.shape[1] for a in smalls)
    packed = jnp.concatenate(smalls + [jnp.zeros((width, PAIR - used), f32)], axis=1).astype(bf16)
    packed = packed.reshape(8, width // 8, PAIR)[order].reshape(2, width // 2, PAIR)
    steps_last = core_step([after(last_send, *steps_first), packed[0]], [last_keep, packed[1]])
    part_first = last_step(steps_first)
    part_last = last_step(side_step(kept_after(steps_last, *part_first)))
    total = along(jnp.concatenate([*part_first, *part_last], axis=1))
    ends = [width, 2 * width, split[1] + width, db_first.shape[1] + width]
    ends += [ends[-1] + cols, ends[-1] + 2 * cols]
    sum_attn, sum_q, sum_k, sum_v, end_k, end_v, packed = jnp.split(total, ends, axis=1)
    sum_qkv = jnp.concatenate([sum_q, sum_k, end_k, sum_v, end_v], axis=1)
    packed = packed.astype(f32)
    done, at = [], 0
    for a in smalls:
        done.append(packed[:, at:at + a.shape[1]].reshape(-1))
        at += a.shape[1]
    return (output[None], grad_inputs[None], done[0], done[1], sum_qkv.astype(f32), done[2], sum_attn.astype(f32),
            done[3], done[4], done[5], sum_in.astype(f32), done[6], sum_out.astype(f32))


def local(*args):
    half = args[0].shape[1] // 2
    if args[0].shape[0] == 1 and half % CLEN == 0 and lax.axis_size("fsdp") == 8:
        return fast(*args)
    return generic(*args)


def generic(
    inputs,
    cotangent,
    positions,
    segments,
    ln1_gain,
    ln1_bias,
    w_qkv,
    b_qkv,
    w_attn_out,
    b_out,
    ln2_gain,
    ln2_bias,
    w_in,
    b_in,
    w_out,
):
    shards = (
        ln1_gain,
        ln1_bias,
        w_qkv,
        b_qkv,
        w_attn_out,
        b_out,
        ln2_gain,
        ln2_bias,
        w_in,
        b_in,
        w_out,
    )
    params = (
        lax.all_gather(shards[0], "fsdp", axis=0, tiled=True),
        lax.all_gather(shards[1], "fsdp", axis=0, tiled=True),
        lax.all_gather(shards[2], "fsdp", axis=0, tiled=True),
        lax.all_gather(shards[3], "fsdp", axis=0, tiled=True),
        lax.all_gather(shards[4], "fsdp", axis=0, tiled=True),
        lax.all_gather(shards[5], "fsdp", axis=0, tiled=True),
        lax.all_gather(shards[6], "fsdp", axis=0, tiled=True),
        lax.all_gather(shards[7], "fsdp", axis=0, tiled=True),
        lax.all_gather(shards[8], "fsdp", axis=0, tiled=True),
        lax.all_gather(shards[9], "fsdp", axis=0, tiled=True),
        lax.all_gather(shards[10], "fsdp", axis=0, tiled=True),
    )
    groups, local_len, width = inputs.shape
    rows_total = groups * local_len
    block = math.gcd(local_len, 256)
    label_pos, label_seg = (
        lax.all_gather(positions, "ctx", axis=1, tiled=True),
        lax.all_gather(segments, "ctx", axis=1, tiled=True),
    )
    count = label_pos.shape[1] // block
    f32 = jnp.float32
    bf16 = jnp.bfloat16
    (
        gain_attn,
        shift_attn,
        weight_qkv,
        bias_qkv,
        weight_attn,
        bias_out,
        gain_mlp,
        shift_mlp,
        weight_in,
        bias_in,
        weight_out,
    ) = params
    flat_in = inputs.reshape(rows_total, width).astype(f32)
    normed_attn = layer_norm(flat_in, gain_attn.astype(f32), shift_attn.astype(f32)).astype(bf16)
    normed_mlp = layer_norm(flat_in, gain_mlp.astype(f32), shift_mlp.astype(f32)).astype(bf16)
    projected = jnp.dot(normed_attn, weight_qkv, preferred_element_type=f32) + bias_qkv.astype(f32)
    cosine, sine = rotary_tables(positions)

    def split_heads(columns):
        return columns.reshape(groups, local_len, HEADS, HD)

    scale = HD ** (-0.5)
    queries = (rotate(split_heads(projected[:, :width]), cosine, sine) * scale).astype(bf16)
    keys_own = rotate(split_heads(projected[:, width : 2 * width]), cosine, sine).astype(bf16)
    values_own = split_heads(projected[:, 2 * width :]).astype(bf16)
    keys_all, values_all = (
        lax.all_gather(keys_own, "ctx", axis=1, tiled=True),
        lax.all_gather(values_own, "ctx", axis=1, tiled=True),
    )

    def key_block(index):
        start = index * block
        keys_blk = lax.dynamic_slice_in_dim(keys_all, start, block, 1)
        values_blk = lax.dynamic_slice_in_dim(values_all, start, block, 1)
        mask = allowed_mask(
            positions,
            segments,
            lax.dynamic_slice_in_dim(label_pos, start, block, 1),
            lax.dynamic_slice_in_dim(label_seg, start, block, 1),
        )
        return (keys_blk, values_blk, mask)

    def total_step(carry, index):
        peak, total = carry
        keys_blk, values_blk, mask = key_block(index)
        scores = jnp.where(mask, scores_of(queries, keys_blk), MASKED)
        fresh = jnp.maximum(peak, jnp.max(scores, axis=-1))
        added = jnp.sum(jnp.where(mask, jnp.exp(scores - fresh[..., None]), 0.0), axis=-1)
        return ((fresh, total * jnp.exp(peak - fresh) + added), None)

    stat_shape = (groups, HEADS, local_len)
    (peak, total), unused = lax.scan(
        total_step,
        (jnp.full(stat_shape, MASKED, f32), jnp.zeros(stat_shape, f32)),
        jnp.arange(count),
    )
    log_total = peak + jnp.log(total)

    def attend_step(rounded_sum, index):
        keys_blk, values_blk, mask = key_block(index)
        probs = jnp.where(mask, jnp.exp(scores_of(queries, keys_blk) - log_total[..., None]), 0.0)
        rounded_sum = rounded_sum + jnp.einsum(
            "ghqk,gkhd->gqhd", probs.astype(bf16), values_blk, preferred_element_type=f32
        )
        return (rounded_sum, None)

    head_shape = (groups, local_len, HEADS, HD)
    rounded_sum, unused = lax.scan(attend_step, jnp.zeros(head_shape, f32), jnp.arange(count))
    attended = rounded_sum.reshape(rows_total, width).astype(bf16)
    pre_act = jnp.dot(normed_mlp, weight_in, preferred_element_type=f32) + bias_in.astype(f32)
    activated = jax.nn.gelu(pre_act, approximate=False).astype(bf16)
    output = (
        flat_in
        + jnp.dot(attended, weight_attn, preferred_element_type=f32)
        + jnp.dot(activated, weight_out, preferred_element_type=f32)
        + bias_out.astype(f32)
    )
    (
        gain_attn,
        shift_attn,
        weight_qkv,
        bias_qkv,
        weight_attn,
        bias_out,
        gain_mlp,
        shift_mlp,
        weight_in,
        bias_in,
        weight_out,
    ) = params
    grad_out = cotangent.reshape(rows_total, width)
    grad_bias_out = jnp.sum(grad_out.astype(f32), axis=0)
    grad_weight_out = jnp.einsum("rf,rd->fd", activated, grad_out, preferred_element_type=f32)
    grad_act = jnp.einsum("rd,fd->rf", grad_out, weight_out, preferred_element_type=f32)
    unused, gelu_back = jax.vjp(partial(jax.nn.gelu, approximate=False), pre_act)
    grad_pre = gelu_back(grad_act)[0].astype(bf16)
    grad_weight_in = jnp.einsum("rd,rf->df", normed_mlp, grad_pre, preferred_element_type=f32)
    grad_bias_in = jnp.sum(grad_pre.astype(f32), axis=0)
    grad_normed_mlp = jnp.einsum("rf,df->rd", grad_pre, weight_in, preferred_element_type=f32)
    grad_weight_attn = jnp.einsum("ra,rd->ad", attended, grad_out, preferred_element_type=f32)
    grad_att = (
        jnp.einsum("rd,ad->ra", grad_out, weight_attn, preferred_element_type=f32)
        .astype(bf16)
        .reshape(head_shape)
    )
    delta = jnp.einsum(
        "gqhd,gqhd->ghq", grad_att.astype(f32), rounded_sum, precision=lax.Precision.HIGHEST
    )

    def back_step(carry, index):
        keys_blk, values_blk, mask = key_block(index)
        rounded, grad_scores = block_grads(
            queries, grad_att, log_total, delta, mask, keys_blk, values_blk
        )
        carry = carry + jnp.einsum(
            "ghqk,gkhd->gqhd", grad_scores, keys_blk, preferred_element_type=f32
        )
        key_term = jnp.einsum("ghqk,gqhd->gkhd", grad_scores, queries, preferred_element_type=f32)
        value_term = jnp.einsum("ghqk,gqhd->gkhd", rounded, grad_att, preferred_element_type=f32)
        return (carry, (key_term, value_term))

    grad_queries, (key_terms, value_terms) = lax.scan(
        back_step, jnp.zeros(head_shape, f32), jnp.arange(count)
    )
    key_sums, value_sums = (
        lax.psum_scatter(
            key_terms.astype(jnp.bfloat16), "ctx", scatter_dimension=0, tiled=True
        ).astype(jnp.float32),
        lax.psum_scatter(
            value_terms.astype(jnp.bfloat16), "ctx", scatter_dimension=0, tiled=True
        ).astype(jnp.float32),
    )
    grad_keys = jnp.transpose(key_sums, (1, 0, 2, 3, 4)).reshape(head_shape)
    grad_values = jnp.transpose(value_sums, (1, 0, 2, 3, 4)).reshape(head_shape)
    grad_q_pre = unrotate(grad_queries * scale, cosine, sine).reshape(rows_total, width)
    grad_k_pre = unrotate(grad_keys, cosine, sine).reshape(rows_total, width)
    grad_projected = jnp.concatenate(
        [grad_q_pre, grad_k_pre, grad_values.reshape(rows_total, width)], axis=1
    ).astype(bf16)
    grad_weight_qkv = jnp.einsum(
        "rd,re->de", normed_attn, grad_projected, preferred_element_type=f32
    )
    grad_bias_qkv = jnp.sum(grad_projected.astype(f32), axis=0)
    grad_normed_attn = jnp.einsum(
        "re,de->rd", grad_projected, weight_qkv, preferred_element_type=f32
    )
    unused, norm_back_attn = jax.vjp(
        layer_norm, flat_in, gain_attn.astype(f32), shift_attn.astype(f32)
    )
    grad_in_attn, grad_gain_attn, grad_shift_attn = norm_back_attn(grad_normed_attn)
    unused, norm_back_mlp = jax.vjp(
        layer_norm, flat_in, gain_mlp.astype(f32), shift_mlp.astype(f32)
    )
    grad_in_mlp, grad_gain_mlp, grad_shift_mlp = norm_back_mlp(grad_normed_mlp)
    grad_inputs = (grad_out.astype(f32) + grad_in_attn + grad_in_mlp).reshape(
        groups, local_len, width
    )
    sums = (
        lax.psum_scatter(grad_gain_attn, ("fsdp", "ctx"), scatter_dimension=0, tiled=True),
        lax.psum_scatter(grad_shift_attn, ("fsdp", "ctx"), scatter_dimension=0, tiled=True),
        lax.psum_scatter(grad_weight_qkv, ("fsdp", "ctx"), scatter_dimension=0, tiled=True),
        lax.psum_scatter(grad_bias_qkv, ("fsdp", "ctx"), scatter_dimension=0, tiled=True),
        lax.psum_scatter(grad_weight_attn, ("fsdp", "ctx"), scatter_dimension=0, tiled=True),
        lax.psum_scatter(grad_bias_out, ("fsdp", "ctx"), scatter_dimension=0, tiled=True),
        lax.psum_scatter(grad_gain_mlp, ("fsdp", "ctx"), scatter_dimension=0, tiled=True),
        lax.psum_scatter(grad_shift_mlp, ("fsdp", "ctx"), scatter_dimension=0, tiled=True),
        lax.psum_scatter(grad_weight_in, ("fsdp", "ctx"), scatter_dimension=0, tiled=True),
        lax.psum_scatter(grad_bias_in, ("fsdp", "ctx"), scatter_dimension=0, tiled=True),
        lax.psum_scatter(grad_weight_out, ("fsdp", "ctx"), scatter_dimension=0, tiled=True),
    )
    result = output.reshape(groups, local_len, width).astype(bf16)
    return (
        result,
        grad_inputs,
        sums[0],
        sums[1],
        sums[2],
        sums[3],
        sums[4],
        sums[5],
        sums[6],
        sums[7],
        sums[8],
        sums[9],
        sums[10],
    )


def solution(mesh):
    in_specs = (
        P("fsdp", "ctx", None),
        P("fsdp", "ctx", None),
        P("fsdp", "ctx"),
        P("fsdp", "ctx"),
        P("fsdp"),
        P("fsdp"),
        P("fsdp", None),
        P("fsdp"),
        P("fsdp", None),
        P("fsdp"),
        P("fsdp"),
        P("fsdp"),
        P("fsdp", None),
        P("fsdp"),
        P("fsdp", None),
    )
    out_specs = (
        P("fsdp", "ctx", None),
        P("fsdp", "ctx", None),
        P(("fsdp", "ctx")),
        P(("fsdp", "ctx")),
        P(("fsdp", "ctx"), None),
        P(("fsdp", "ctx")),
        P(("fsdp", "ctx"), None),
        P(("fsdp", "ctx")),
        P(("fsdp", "ctx")),
        P(("fsdp", "ctx")),
        P(("fsdp", "ctx"), None),
        P(("fsdp", "ctx")),
        P(("fsdp", "ctx"), None),
    )
    return jax.shard_map(local, mesh=mesh, in_specs=in_specs, out_specs=out_specs, check_vma=False)
```

```python
from functools import partial
import math

import jax
import jax.numpy as jnp
from jax import lax
from jax.experimental import pallas as pl
from jax.experimental.pallas import tpu as pltpu
from jax.sharding import PartitionSpec as P

HEADS = 16
HD = 64
ROT = 16
CLEN = 256
QB = 256
RB = 256
PAIR = 2 * HD
bf16 = jnp.bfloat16
f32 = jnp.float32
NN = (((1,), (0,)), ((), ()))
NT = (((1,), (1,)), ((), ()))
TN = (((0,), (0,)), ((), ()))


NORM_EPS = 1e-05
MASKED = -1e30


def layer_norm(values, scaling, offset):
    average = jnp.mean(values, axis=-1, keepdims=True)
    centered = values - average
    variance = jnp.mean(centered * centered, axis=-1, keepdims=True)
    return centered * lax.rsqrt(variance + NORM_EPS) * scaling + offset


def rotary_tables(positions):
    halfway = ROT // 2
    spacing = jnp.arange(halfway, dtype=jnp.float32) * (2.0 / ROT)
    inverse = jnp.exp(-math.log(10000.0) * spacing)
    angles = positions.astype(jnp.float32)[..., None] * inverse
    return (jnp.cos(angles), jnp.sin(angles))


def rotate(heads_in, cosine, sine):
    halfway = ROT // 2
    cosine = cosine[..., None, :]
    sine = sine[..., None, :]
    first = heads_in[..., :halfway]
    second = heads_in[..., halfway:ROT]
    return jnp.concatenate(
        [first * cosine - second * sine, second * cosine + first * sine, heads_in[..., ROT:]],
        axis=-1,
    )


def unrotate(grads_in, cosine, sine):
    halfway = ROT // 2
    cosine = cosine[..., None, :]
    sine = sine[..., None, :]
    first = grads_in[..., :halfway]
    second = grads_in[..., halfway:ROT]
    return jnp.concatenate(
        [first * cosine + second * sine, second * cosine - first * sine, grads_in[..., ROT:]],
        axis=-1,
    )


def allowed_mask(query_pos, query_seg, key_pos, key_seg):
    same_doc = (key_seg[:, None, :] == 0) | (key_seg[:, None, :] == query_seg[:, :, None])
    causal = key_pos[:, None, :] <= query_pos[:, :, None]
    return (same_doc & causal)[:, None]


def scores_of(queries, keys_blk):
    return jnp.einsum("gqhd,gkhd->ghqk", queries, keys_blk, preferred_element_type=jnp.float32)


def block_grads(queries, grad_att, log_total, delta, mask, keys_blk, values_blk):
    probs = jnp.where(mask, jnp.exp(scores_of(queries, keys_blk) - log_total[..., None]), 0.0)
    dprobs = jnp.einsum("gqhd,gkhd->ghqk", grad_att, values_blk, preferred_element_type=jnp.float32)
    grad_scores = (probs * (dprobs - delta[..., None])).astype(jnp.bfloat16)
    return (probs.astype(jnp.bfloat16), grad_scores)


def mm(a, b, dims):
    return lax.dot_general(a, b, dims, preferred_element_type=f32)


def row_stats(x):
    average = jnp.mean(x, axis=1, keepdims=True)
    centered = x - average
    return centered, lax.rsqrt(jnp.mean(centered * centered, axis=1, keepdims=True) + NORM_EPS)


def norm_rows(x, scaling, offset):
    centered, inverse = row_stats(x)
    return (centered * inverse * scaling + offset).astype(bf16)


def norm_back(x, grad, scaling):
    centered, inverse = row_stats(x)
    unit = centered * inverse
    e = grad * scaling
    inner = e - jnp.mean(e, axis=1, keepdims=True) - unit * jnp.mean(e * unit, axis=1, keepdims=True)
    return inverse * inner, grad * unit


def col_sum(a):
    return jnp.sum(a, axis=0, keepdims=True)


def vmem(*shape, dtype=f32):
    return pltpu.VMEM(shape, dtype)


def params():
    return pltpu.CompilerParams(vmem_limit_bytes=60 << 20)


ROOT = math.sqrt(0.5)
DENS = 1.0 / math.sqrt(2.0 * math.pi)


def reorder(order_ref, source, target):
    size = source.shape[1] // order_ref.shape[0]
    for i in range(order_ref.shape[0]):
        at = pl.multiple_of(order_ref[i] * size, size)
        target[:, i * size:(i + 1) * size] = source[:, pl.ds(at, size)]


def mlp_kernel(order_ref, x_ref, c_ref, gain_ref, shift_ref, win_ref, bin_ref, wout_ref,
               out_ref, gin_ref, dwin_send, dwin_keep, dwout_send, dwout_keep, dbin_ref, dbout_ref, dgain_ref, dshift_ref,
               h_ref, turned_ref, act_ref, gp_ref, gh_ref):
    step = pl.program_id(0)
    rows = x_ref.shape[0]
    blocks = [slice(r, r + RB) for r in range(0, rows, RB)]

    @pl.when(step == 0)
    def _():
        for r in blocks:
            h_ref[r, :] = norm_rows(x_ref[r, :].astype(f32), gain_ref[...], shift_ref[...])
            out_ref[r, :] = jnp.zeros((RB, out_ref.shape[1]), f32)
            gh_ref[r, :] = jnp.zeros((RB, gh_ref.shape[1]), f32)
        reorder(order_ref, h_ref, turned_ref)

    dbin = jnp.zeros(dbin_ref.shape, f32)
    for r in blocks:
        pre = mm(h_ref[r, :], win_ref[...], NN) + bin_ref[...]
        phi = 0.5 + 0.5 * lax.erf(pre * ROOT)
        act_ref[r, :] = (pre * phi).astype(bf16)
        gp = phi + pre * (DENS * jnp.exp(-0.5 * (pre * pre)))
        gact = mm(c_ref[r, :], wout_ref[...], NT)
        gpre = (gact * gp).astype(bf16)
        gp_ref[r, :] = gpre
        dbin = dbin + col_sum(gpre.astype(f32))
    for r in blocks:
        out_ref[r, :] += mm(act_ref[r, :], wout_ref[...], NN)
        gh_ref[r, :] += mm(gp_ref[r, :], win_ref[...], NT)
    dwout = mm(act_ref[...], c_ref[...], TN).astype(bf16)
    middle = pl.num_programs(0) // 2

    @pl.when(step < middle)
    def _():
        dwout_send[...] = dwout

    @pl.when(step >= middle)
    def _():
        dwout_keep[...] = dwout

    dwin = mm(turned_ref[...], gp_ref[...], TN).astype(bf16)
    dwin_send[...] = dwin[:dwin_send.shape[0]]
    dwin_keep[...] = dwin[dwin_send.shape[0]:]
    dbin_ref[...] = dbin

    @pl.when(step == pl.num_programs(0) - 1)
    def _():
        dgain = jnp.zeros(dgain_ref.shape, f32)
        dshift = jnp.zeros(dshift_ref.shape, f32)
        dbout = jnp.zeros(dbout_ref.shape, f32)
        for r in blocks:
            grad = gh_ref[r, :]
            back, scaled = norm_back(x_ref[r, :].astype(f32), grad, gain_ref[...])
            c = c_ref[r, :].astype(f32)
            gin_ref[r, :] = back + c
            dgain += col_sum(scaled)
            dshift += col_sum(grad)
            dbout += col_sum(c)
        dgain_ref[...] = dgain
        dshift_ref[...] = dshift
        dbout_ref[...] = dbout


def mlp(order, x, c, gain, shift, weight_in, bias_in, weight_out):
    rows, width = x.shape
    ff = weight_in.shape[1]
    steps = order.shape[0]
    fc = ff // steps
    whole = pl.BlockSpec((rows, width), lambda j, o: (0, 0))
    line = pl.BlockSpec((1, width), lambda j, o: (0, 0))
    down = pl.BlockSpec((width // 2, fc), lambda j, o: (0, o[j]))
    s = jax.ShapeDtypeStruct
    return pl.pallas_call(
        mlp_kernel,
        grid_spec=pltpu.PrefetchScalarGridSpec(
            num_scalar_prefetch=1,
            grid=(steps,),
            in_specs=[whole, whole, line, line, pl.BlockSpec((width, fc), lambda j, o: (0, o[j])),
                      pl.BlockSpec((1, fc), lambda j, o: (0, o[j])), pl.BlockSpec((fc, width), lambda j, o: (o[j], 0))],
            out_specs=[whole, whole, down, down,
                       pl.BlockSpec((fc, width), lambda j, o: (jnp.minimum(j, steps // 2 - 1), 0)),
                       pl.BlockSpec((fc, width), lambda j, o: (jnp.maximum(j - steps // 2, 0), 0)),
                       pl.BlockSpec((1, fc), lambda j, o: (0, o[j])), line, line, line],
            scratch_shapes=[vmem(rows, width, dtype=bf16), vmem(rows, width, dtype=bf16), vmem(rows, fc, dtype=bf16),
                            vmem(rows, fc, dtype=bf16), vmem(rows, width)],
        ),
        out_shape=[s((rows, width), f32), s((rows, width), f32), s((width // 2, ff), bf16), s((width // 2, ff), bf16),
                   s((ff // 2, width), bf16), s((ff // 2, width), bf16), s((1, ff), f32), s((1, width), f32),
                   s((1, width), f32), s((1, width), f32)],
        compiler_params=params(),
        cost_estimate=pl.CostEstimate(flops=1 << 20, bytes_accessed=1 << 16, transcendentals=0),
        name="mlp",
    )(order, x, c, gain.reshape(1, -1), shift.reshape(1, -1), weight_in, bias_in.reshape(1, -1), weight_out)


def turn_lanes(u, cosine, low, high, sign):
    half = ROT // 2
    parts = []
    for at in range(0, u.shape[1], PAIR):
        g = u[:, at:at + PAIR]
        parts.append(g * cosine + sign * (pltpu.roll(g, half, 1) * high - pltpu.roll(g, PAIR - half, 1) * low))
    return jnp.concatenate(parts, axis=1)


def qkv_kernel(far, spot_ref, order_ref, gain_ref, shift_ref, w_ref, b_ref, cos_ref, low_ref, high_ref, *refs):
    with_q = far == 0
    if with_q:
        x_ref, outs = refs[0], refs[1:]
    else:
        x_refs, outs, x_ref = refs[:far], refs[far:-1], refs[-1]
        step = pl.program_id(0)
        per = pl.num_programs(0) // far
        for s in range(far):
            @pl.when(step // per == s)
            def _(s=s):
                x_ref[...] = x_refs[s][...]
    width = x_ref.shape[1]
    h = norm_rows(x_ref[...].astype(f32), gain_ref[...], shift_ref[...])
    tables = (cos_ref[...], low_ref[...], high_ref[...])
    if with_q:
        h_ref, q_ref, k_ref, v_ref, plain_ref = outs
        plain_ref[...] = h
        reorder(order_ref, plain_ref, h_ref)
        q = mm(h, w_ref[:, :width], NN) + b_ref[:, :width]
        q_ref[...] = (turn_lanes(q, *tables, 1.0) * (HD ** (-0.5) / math.log(2.0))).astype(bf16)
    else:
        k_ref, v_ref = outs
    k = mm(h, w_ref[:, width:2 * width], NN) + b_ref[:, width:2 * width]
    k_ref[...] = turn_lanes(k, *tables, 1.0).astype(bf16)
    v_ref[...] = (mm(h, w_ref[:, 2 * width:], NN) + b_ref[:, 2 * width:]).astype(bf16)


def qkv(spots, order, xs, gain, shift, weight, bias, tables):
    far = len(xs) if len(xs) > 1 else 0
    rows, width = xs[0].shape
    per = rows // RB
    total = len(xs) * rows
    s = jax.ShapeDtypeStruct((total, width), bf16)
    block = pl.BlockSpec((RB, width), lambda j, spot, o: (j, 0))
    line = pl.BlockSpec((1, width), lambda j, spot, o: (0, 0))
    table = pl.BlockSpec((RB, PAIR), lambda j, spot, o: (spot[j], 0))
    count = 2 if far else 4

    def window(i):
        return pl.BlockSpec((RB, width), lambda j, spot, o: (jnp.clip(j - i * per, 0, per - 1), 0))

    return pl.pallas_call(
        partial(qkv_kernel, far),
        grid_spec=pltpu.PrefetchScalarGridSpec(
            num_scalar_prefetch=2,
            grid=(total // RB,),
            in_specs=[line, line, pl.BlockSpec((width, 3 * width), lambda j, spot, o: (0, 0)),
                      pl.BlockSpec((1, 3 * width), lambda j, spot, o: (0, 0)), table, table, table]
            + [window(i) for i in range(len(xs))],
            out_specs=[block] * count,
            scratch_shapes=[vmem(RB, width, dtype=bf16)],
        ),
        out_shape=[s] * count,
        compiler_params=params(),
        cost_estimate=pl.CostEstimate(flops=1 << 20, bytes_accessed=1 << 16, transcendentals=0),
        name="kv_remote" if far else "qkv_own",
    )(spots, order, gain.reshape(1, -1), shift.reshape(1, -1), weight, bias.reshape(1, -1), *tables, *xs)


def gather_rows(step, spot, tables, own_refs, come_refs, p_ref, k_at, v_at):
    half = pl.num_programs(0) // 2
    columns = [(g, at) for g in range(len(own_refs)) for at in range(0, own_refs[g].shape[1], 2 * PAIR)]

    def put(refs):
        for to, (g, at) in enumerate(columns):
            turned = turn_lanes(refs[g][:, at:at + PAIR].astype(f32), *tables, -1.0).astype(bf16)
            p_ref[spot, k_at + to * PAIR:k_at + (to + 1) * PAIR] = turned
            p_ref[spot, v_at + to * PAIR:v_at + (to + 1) * PAIR] = refs[g][:, at + PAIR:at + 2 * PAIR]

    @pl.when(step < half)
    def _():
        put(come_refs)

    @pl.when(step >= half)
    def _():
        put(own_refs)


def half_windows(arrays, count):
    half = count // 2
    come = [pl.BlockSpec((RB, a.shape[1]), lambda j, *o: (jnp.clip(j, 0, half - 1), 0)) for a in arrays]
    own = [pl.BlockSpec((RB, a.shape[1]), lambda j, *o: (jnp.clip(j - half, 0, half - 1), 0)) for a in arrays]
    return own, come


def first_kernel(groups, spot_ref, order_ref, c_ref, h_ref, wq_ref, wk_ref, wv_ref, cos_ref, low_ref, high_ref, own_ref,
                 come_ref, *refs):
    att_refs, dq_refs = refs[:groups], refs[groups:2 * groups]
    send_ref, keep_ref, gh_ref, db_ref, p_ref, att_ref, turned_ref = refs[2 * groups:]
    step = pl.program_id(0)
    width = c_ref.shape[1]
    spot = pl.ds(pl.multiple_of(step * RB, RB), RB)
    at = 0
    for g in range(groups):
        size = att_refs[g].shape[1]
        att_ref[:, at:at + size] = att_refs[g][...]
        p_ref[spot, at:at + size] = dq_refs[g][...]
        at += size
    for i in range(order_ref.shape[0]):
        size = width // order_ref.shape[0]
        lanes = pl.ds(pl.multiple_of(order_ref[i] * size, size), size)
        turned_ref[spot, i * size:(i + 1) * size] = att_ref[:, lanes]
    count = wk_ref.shape[1]
    gather_rows(step, spot, (cos_ref[...], low_ref[...], high_ref[...]), [own_ref], [come_ref], p_ref, width, width + count)
    gh_ref[...] = (mm(p_ref[spot, :width], wq_ref[...], NT) + mm(p_ref[spot, width:width + count], wk_ref[...], NT)
                   + mm(p_ref[spot, width + count:], wv_ref[...], NT))
    db = col_sum(p_ref[spot, :].astype(f32))

    @pl.when(step == 0)
    def _():
        db_ref[...] = db

    @pl.when(step > 0)
    def _():
        db_ref[...] += db

    @pl.when(step == pl.num_programs(0) - 1)
    def _():
        half = send_ref.shape[0]
        for to in range(0, send_ref.shape[1], 512):
            if to < width:
                dw = mm(turned_ref[...], c_ref[:, to:to + 512], TN)
            else:
                dw = mm(h_ref[...], p_ref[:, to - width:to - width + 512], TN)
            dw = dw.astype(bf16)
            send_ref[:, to:to + 512] = dw[:half]
            keep_ref[:, to:to + 512] = dw[half:]


def first_tail(spots, order, c, h, weights, tables, attended, dqs, own, come):
    rows, width = c.shape
    cols = own.shape[1] // 2
    steps = rows // RB
    total = 2 * width + 2 * cols
    s = jax.ShapeDtypeStruct

    def full(shape):
        return pl.BlockSpec(shape, lambda j, spot, o: (0, 0), pipeline_mode=pl.Buffered(1))

    def weight(size, at):
        return pl.BlockSpec((width, size), lambda j, spot, o: (0, at // size), pipeline_mode=pl.Buffered(1))

    def window(a):
        return pl.BlockSpec((RB, a.shape[1]), lambda j, spot, o: (j, 0))

    table = pl.BlockSpec((RB, PAIR), lambda j, spot, o: (spot[j], 0))
    owns, comes = half_windows([own], steps)
    return pl.pallas_call(
        partial(first_kernel, len(dqs)),
        grid_spec=pltpu.PrefetchScalarGridSpec(
            num_scalar_prefetch=2,
            grid=(steps,),
            in_specs=[full(c.shape), full(h.shape), weight(width, 0), weight(cols, width), weight(cols, 2 * width)] + [table] * 3
            + owns + comes + [window(a) for a in (*attended, *dqs)],
            out_specs=[full((width // 2, total)), full((width // 2, total)), window(c), full((1, total - width))],
            scratch_shapes=[vmem(rows, total - width, dtype=bf16), vmem(RB, width, dtype=bf16), vmem(rows, width, dtype=bf16)],
        ),
        out_shape=[s((width // 2, total), bf16), s((width // 2, total), bf16), s((rows, width), f32), s((1, total - width), f32)],
        compiler_params=params(),
        cost_estimate=pl.CostEstimate(flops=24 << 30, bytes_accessed=1 << 20, transcendentals=0),
        name="first_tail",
    )(spots, order, c, h, weights, weights, weights, *tables, own, come, *attended, *dqs)


def last_kernel(groups, spot_ref, h_ref, gain_ref, wk_ref, wv_ref, x_ref, cos_ref, low_ref, high_ref, gin_ref, ghin_ref, *refs):
    own_refs, come_refs = refs[:groups], refs[groups:2 * groups]
    grad_ref, send_ref, keep_ref, db_ref, dgain_ref, dshift_ref, p_ref = refs[2 * groups:]
    step = pl.program_id(0)
    spot = pl.ds(pl.multiple_of(step * RB, RB), RB)
    count = wk_ref.shape[1]
    gather_rows(step, spot, (cos_ref[...], low_ref[...], high_ref[...]), own_refs, come_refs, p_ref, 0, count)
    grad = (ghin_ref[...] + mm(p_ref[spot, :count], wk_ref[...], NT) + mm(p_ref[spot, count:], wv_ref[...], NT))
    back, scaled = norm_back(x_ref[...].astype(f32), grad, gain_ref[...])
    grad_ref[...] = back + gin_ref[...]
    sums = col_sum(p_ref[spot, :].astype(f32)), col_sum(scaled), col_sum(grad)

    @pl.when(step == 0)
    def _():
        for ref, value in zip((db_ref, dgain_ref, dshift_ref), sums):
            ref[...] = value

    @pl.when(step > 0)
    def _():
        for ref, value in zip((db_ref, dgain_ref, dshift_ref), sums):
            ref[...] += value

    @pl.when(step == pl.num_programs(0) - 1)
    def _():
        half = send_ref.shape[0]
        for to in range(0, send_ref.shape[1], 512):
            dw = mm(h_ref[...], p_ref[:, to:to + 512], TN).astype(bf16)
            send_ref[:, to:to + 512] = dw[:half]
            keep_ref[:, to:to + 512] = dw[half:]


def last_tail(spots, x, h, gain, weights, tables, gin, gh, owns, comes):
    rows, width = x.shape
    cols = sum(a.shape[1] for a in owns) // 2
    steps = rows // RB
    s = jax.ShapeDtypeStruct

    def full(shape):
        return pl.BlockSpec(shape, lambda j, spot: (0, 0), pipeline_mode=pl.Buffered(1))

    def weight(at):
        return pl.BlockSpec((width, cols), lambda j, spot: (0, at // cols), pipeline_mode=pl.Buffered(1))

    block = pl.BlockSpec((RB, width), lambda j, spot: (j, 0))
    table = pl.BlockSpec((RB, PAIR), lambda j, spot: (spot[j], 0))
    own_windows, come_windows = half_windows(owns, steps)
    return pl.pallas_call(
        partial(last_kernel, len(owns)),
        grid_spec=pltpu.PrefetchScalarGridSpec(
            num_scalar_prefetch=1,
            grid=(steps,),
            in_specs=[full(h.shape), full((1, width)), weight(2 * width - cols), weight(3 * width - cols), block] + [table] * 3
            + [block, block] + own_windows + come_windows,
            out_specs=[block, full((width // 2, 2 * cols)), full((width // 2, 2 * cols)), full((1, 2 * cols)), full((1, width)),
                       full((1, width))],
            scratch_shapes=[vmem(rows, 2 * cols, dtype=bf16)],
        ),
        out_shape=[s((rows, width), f32), s((width // 2, 2 * cols), bf16), s((width // 2, 2 * cols), bf16), s((1, 2 * cols), f32),
                   s((1, width), f32), s((1, width), f32)],
        compiler_params=params(),
        cost_estimate=pl.CostEstimate(flops=12 << 30, bytes_accessed=1 << 20, transcendentals=0),
        name="last_tail",
    )(spots, h, gain.reshape(1, -1), weights, weights, x, *tables, gin, gh, *owns, *comes)


def join_kernel(groups, x_ref, w_ref, mlp_ref, b_ref, *refs):
    att_refs, (out_ref, att_ref) = refs[:groups], refs[groups:]
    at = 0
    for ref in att_refs:
        att_ref[:, at:at + ref.shape[1]] = ref[...]
        at += ref.shape[1]
    out = x_ref[...].astype(f32) + mm(att_ref[...], w_ref[...], NN) + mlp_ref[...] + b_ref[...]
    out_ref[...] = out.astype(bf16)


def join(x, attended, weights, mlp_out, bias):
    rows, width = x.shape
    s = jax.ShapeDtypeStruct
    block = pl.BlockSpec((RB, width), lambda j: (j, 0))
    return pl.pallas_call(
        partial(join_kernel, len(attended)),
        grid=(rows // RB,),
        in_specs=[block, pl.BlockSpec((width, width), lambda j: (0, 3)), block, pl.BlockSpec((1, width), lambda j: (0, 0))]
        + [pl.BlockSpec((RB, a.shape[1]), lambda j: (j, 0)) for a in attended],
        out_specs=block,
        out_shape=s((rows, width), bf16),
        scratch_shapes=[vmem(RB, width, dtype=bf16)],
        compiler_params=params(),
        cost_estimate=pl.CostEstimate(flops=12 << 30, bytes_accessed=1 << 20, transcendentals=0),
        name="join",
    )(x, weights, mlp_out, bias.reshape(1, -1), *attended)


def spread_kernel(c_ref, w_ref, out_ref):
    out_ref[...] = mm(c_ref[...], w_ref[...], NT).astype(bf16)


def spread(c, weights):
    rows, width = c.shape
    block = pl.BlockSpec((RB, width), lambda j: (j, 0))
    return pl.pallas_call(
        spread_kernel,
        grid=(rows // RB,),
        in_specs=[block, pl.BlockSpec((width, width), lambda j: (0, 3))],
        out_specs=block,
        out_shape=jax.ShapeDtypeStruct((rows, width), bf16),
        compiler_params=params(),
        cost_estimate=pl.CostEstimate(flops=1 << 20, bytes_accessed=1 << 16, transcendentals=0),
        name="spread",
    )(c, weights)


def fold(x, op):
    return op(x.reshape(x.shape[0] // 8, 8, x.shape[1]), axis=0)


def eye(size):
    return (lax.broadcasted_iota(jnp.int32, (size, size), 0) == lax.broadcasted_iota(jnp.int32, (size, size), 1)).astype(bf16)


def attention_kernel(half, n, kind_ref, owner_ref, cos_ref, sin_ref, q_ref, do_ref, *refs):
    k_refs, v_refs = refs[:2], refs[2:4]
    o_ref, dq_ref, all_ref, cont_ref, kt_ref, vt_ref, s_ref, p_ref, ds_ref, dka_ref, dva_ref = refs[4:]
    per = half // QB
    wide = n * half
    count = wide // QB
    spots = [(0, c * QB) for c in range(per)] + [(1, c * QB) for c in range((n - 1) * per)]

    ident = eye(PAIR)
    for refs_in, out in ((k_refs, kt_ref), (v_refs, vt_ref)):
        for c, (s, at) in enumerate(spots):
            out[:, c * QB:(c + 1) * QB] = refs_in[s][at:at + QB, :].T
        for c in range(per):
            out[:, wide + c * QB:wide + (c + 1) * QB] = refs_in[0][half + c * QB:half + (c + 1) * QB, :].T
    dka_ref[...] = jnp.zeros_like(dka_ref)
    dva_ref[...] = jnp.zeros_like(dva_ref)


    def block(qb, carry):
        own = pl.ds(pl.multiple_of(qb * QB, QB), QB)
        slot = pl.ds(pl.multiple_of(jnp.where(qb < per, qb * QB, wide + (qb - per) * QB), QB), QB)
        zero = jnp.zeros((), bf16)
        causal = lax.broadcasted_iota(jnp.int32, (QB, QB), 0) <= lax.broadcasted_iota(jnp.int32, (QB, QB), 1)
        left = lax.broadcasted_iota(jnp.int32, (QB, PAIR), 1) < HD

        def by_head(a):
            return jnp.where(left, a, zero), jnp.where(left, zero, a)

        def keys_of(some, c):
            if c == count:
                return some[0][own, :]
            s, at = spots[c]
            return some[s][at:at + QB, :]

        def cut(c):
            return slice(c * QB, (c + 1) * QB)

        ident = eye(QB)
        q_heads = by_head(q_ref[own, :])
        do_t = mm(eye(PAIR), do_ref[own, :], NT)
        upper = lax.broadcasted_iota(jnp.int32, (PAIR, QB), 0) < HD
        q_t = mm(eye(PAIR), q_ref[own, :], NT).astype(bf16)
        q_cols = jnp.where(upper, q_t, zero), jnp.where(upper, zero, q_t)
        peaks, norms, outs, deltas, scaled = [None, None], [None, None], [None, None], [None, None], [None, None]

        def scores(h):
            peak = jnp.full((8, QB), MASKED, f32)
            for c in range(count + 1):
                s = mm(keys_of(k_refs, c), q_cols[h], NN)
                if c == count:
                    s = jnp.where(causal, s, MASKED)
                    top = fold(s, jnp.max)
                else:
                    top = fold(s, jnp.max) + kind_ref[qb, c]
                s_ref[h, cut(c)] = s
                peak = jnp.maximum(peak, top)
            peaks[h] = jnp.max(peak, axis=0, keepdims=True)

        def weigh(h):
            total = jnp.zeros((8, QB), f32)
            for c in range(count + 1):
                bias = -peaks[h] if c == count else kind_ref[qb, c] - peaks[h]
                e = jnp.exp2(s_ref[h, cut(c)] + bias)
                total = total + fold(e, jnp.sum)
                p_ref[h, cut(c)] = e.astype(bf16)
            norms[h] = 1.0 / jnp.sum(total, axis=0, keepdims=True)

        def attend(h):
            lines = slice(h * HD, (h + 1) * HD)
            out = mm(vt_ref[lines, 0:wide], p_ref[h, 0:wide], NN) + mm(vt_ref[lines, slot], p_ref[h, wide:], NN)
            outs[h] = out * norms[h]
            deltas[h] = jnp.sum(outs[h] * do_t[lines], axis=0, keepdims=True) * norms[h]
            scaled[h] = do_t[lines] * norms[h]

        scores(0)
        scores(1)
        weigh(0)
        attend(0)
        weigh(1)
        attend(1)
        d_t = jnp.concatenate(scaled, axis=0).astype(bf16)
        d_cols = jnp.where(upper, d_t, zero), jnp.where(upper, zero, d_t)
        do_heads = by_head(mm(ident, d_t, NT).astype(bf16))
        grads = []
        for h in range(2):
            lines = slice(h * HD, (h + 1) * HD)
            for c in range(count + 1):
                dp = mm(keys_of(v_refs, c), d_cols[h], NN)
                ds_ref[h, cut(c)] = (p_ref[h, cut(c)].astype(f32) * (dp - deltas[h])).astype(bf16)
            dq = mm(kt_ref[lines, 0:wide], ds_ref[h, 0:wide], NN) + mm(kt_ref[lines, slot], ds_ref[h, wide:], NN)
            a, b = dq[:ROT // 2], dq[ROT // 2:ROT]
            cosine, sine = cos_ref[:, own], sin_ref[:, own]
            grads.append(jnp.concatenate([a * cosine + b * sine, b * cosine - a * sine, dq[ROT:]], axis=0))
        for c in range(count + 1):
            at = slot if c == count else cut(c)
            dva_ref[at, :] += mm(p_ref[0, cut(c)], do_heads[0], NN) + mm(p_ref[1, cut(c)], do_heads[1], NN)
            dka_ref[at, :] += mm(ds_ref[0, cut(c)], q_heads[0], NN) + mm(ds_ref[1, cut(c)], q_heads[1], NN)
        o_ref[own, :] = mm(ident, jnp.concatenate(outs, axis=0).astype(bf16), NT).astype(bf16)
        dq_ref[own, :] = mm(ident, (jnp.concatenate(grads, axis=0) * (HD ** (-0.5))).astype(bf16), NT).astype(bf16)

        return carry

    lax.fori_loop(0, 2 * per, block, 0)

    def flush(out, to, frm):
        rows = pl.ds(to, half)
        out[rows, :PAIR] = (dka_ref[frm:frm + half, :] * math.log(2.0)).astype(bf16)
        out[rows, PAIR:] = dva_ref[frm:frm + half, :].astype(bf16)

    flush(cont_ref, 0, wide)
    for s in range(n):
        flush(all_ref, pl.multiple_of(owner_ref[s] * half, half), s * half)


def attention(kind, owners, cos_t, sin_t, q, do, ks, vs, first, pairs):
    rows = q.shape[0]
    half = rows // 2
    n = 1 + ks[1].shape[0] // half
    wide = n * half
    keys = wide + half
    total = wide + QB
    qspec = pl.BlockSpec((rows, PAIR), lambda p: (0, p + first))
    ospec = pl.BlockSpec((rows, PAIR), lambda p: (0, p))
    table = pl.BlockSpec((ROT // 2, rows), lambda p: (0, 0))
    kspecs = [pl.BlockSpec((k.shape[0], PAIR), lambda p: (0, p + first)) for k in ks]
    gspecs = [pl.BlockSpec((size, 2 * PAIR), lambda p: (0, p)) for size in (wide, half)]
    s = jax.ShapeDtypeStruct
    pieces = pairs * rows // QB
    return pl.pallas_call(
        partial(attention_kernel, half, n),
        grid=(pairs,),
        in_specs=[pl.BlockSpec(memory_space=pltpu.SMEM), pl.BlockSpec(memory_space=pltpu.SMEM), table, table, qspec, qspec] + kspecs + kspecs,
        out_specs=[ospec, ospec] + gspecs,
        out_shape=[s((rows, pairs * PAIR), bf16), s((rows, pairs * PAIR), bf16)]
        + [s((size, 2 * pairs * PAIR), bf16) for size in (wide, half)],
        scratch_shapes=[pltpu.VMEM((PAIR, keys), bf16), pltpu.VMEM((PAIR, keys), bf16),
                        pltpu.VMEM((2, total, QB), f32), pltpu.VMEM((2, total, QB), bf16),
                        pltpu.VMEM((2, total, QB), bf16),
                        pltpu.VMEM((keys, PAIR), f32), pltpu.VMEM((keys, PAIR), f32)],
        compiler_params=pltpu.CompilerParams(vmem_limit_bytes=60 << 20),
        cost_estimate=pl.CostEstimate(flops=1 << 20, bytes_accessed=1 << 16, transcendentals=0),
        name="attention",
    )(kind, owners, cos_t, sin_t, q, do, *ks, *vs)


def pairs_of(bit, size):
    return [(a, a ^ bit) for a in range(size)]


def add_kernel(plan, *refs):
    for a, b, moves in plan:
        for source, to, target in moves:
            refs[to][target] = (refs[a][source].astype(f32) + refs[b][source].astype(f32)).astype(bf16)


def add_parts(arrays, plan, shapes, steps, load=0):
    def spec(shape):
        block = (*shape[:-1], shape[-1] // steps)
        return pl.BlockSpec(block, lambda j: (0,) * (len(shape) - 1) + (j,))

    return pl.pallas_call(
        partial(add_kernel, plan),
        grid=(steps,),
        in_specs=[spec(a.shape) for a in arrays],
        out_specs=[spec(shape) for shape in shapes],
        out_shape=[jax.ShapeDtypeStruct(shape, bf16) for shape in shapes],
        compiler_params=params(),
        cost_estimate=pl.CostEstimate(flops=(load << 30) + 1, bytes_accessed=1 << 16, transcendentals=0),
        name="add_parts",
    )(*arrays)


EVERY = slice(None)


def swap(a, bit):
    return lax.ppermute(a, "fsdp", pairs_of(bit, 8))


def steps_for(arrays):
    smallest = min(a.shape[-1] for a in arrays)
    return 4 if smallest % (4 * PAIR) == 0 else 1


def core_step(sends, keeps):
    count = len(sends)
    arrays, plan, shapes = [], [], []
    for send, keep in zip(sends, keeps):
        rows, cols = send.shape
        cut = (2, 2, 2, rows // 8, cols)
        to = 2 * count + len(shapes)
        moves = [((EVERY, 1, 0), to, (EVERY,)), ((EVERY, 0, 0), to + 1, (EVERY,)),
                 ((1, EVERY, 1), to + 2, (EVERY,)), ((0, EVERY, 1), to + 3, (EVERY,))]
        plan.append((len(arrays), len(arrays) + 1, moves))
        arrays += [keep.reshape(cut), swap(send, 1).reshape(cut)]
        shapes += [(2, rows // 8, cols)] * 4
    return add_parts(arrays, plan, shapes, steps_for(arrays))


def side_step(items):
    arrays, plan, shapes = [], [], []
    for i in range(0, len(items), 4):
        for send, keep, bit in ((items[i], items[i + 1], 2), (items[i + 2], items[i + 3], 4)):
            to = len(items) + len(shapes)
            plan.append((len(arrays), len(arrays) + 1, [((1,), to, (EVERY,)), ((0,), to + 1, (EVERY,))]))
            arrays += [keep, swap(send, bit)]
            shapes += [keep.shape[1:]] * 2
    return add_parts(arrays, plan, shapes, steps_for(arrays))


def last_step(items, load=0):
    arrays, plan, shapes = [], [], []
    for i in range(0, len(items), 4):
        to = len(items) + len(shapes)
        for at, (send, keep, bit) in enumerate(((items[i], items[i + 1], 4), (items[i + 2], items[i + 3], 2))):
            plan.append((len(arrays), len(arrays) + 1, [((EVERY,), to, (at,))]))
            arrays += [keep, swap(send, bit)]
        shapes.append((2, *keep.shape))
    parts = add_parts(arrays, plan, shapes, steps_for(arrays), load)
    return [part.reshape(-1, part.shape[-1]) for part in parts]


def along(part):
    return lax.psum_scatter(part, "ctx", scatter_dimension=0, tiled=True)


def after(value, *others):
    return lax.optimization_barrier((value, *others))[0]


def kept_after(items, *others):
    return [after(a, *others) if i % 2 else a for i, a in enumerate(items)]


def fast(inputs, cotangent, positions, segments, ln1_gain, ln1_bias, w_qkv, b_qkv, w_attn_out, b_out,
         ln2_gain, ln2_bias, w_in, b_in, w_out):
    x, grad_out, pos = inputs[0], cotangent[0], positions[0]
    rows, width = x.shape
    half = rows // 2
    n = lax.axis_size("ctx")
    ring = [(i, (i + 1) % n) for i in range(n)]
    back = [(i, (i - 1) % n) for i in range(n)]
    me, place = lax.axis_index("fsdp"), lax.axis_index("ctx")
    relative = [4 * dy + 2 * dx + 1 - keep for keep in (0, 1) for dy in (0, 1) for dx in (0, 1)]
    order = jnp.bitwise_xor(me, jnp.array(relative, jnp.int32))
    owners = lax.rem(place + n - jnp.arange(n), n)
    far = [None] * n
    far[0] = x[:half]
    for s in range(1, n):
        far[s] = lax.ppermute(far[s - 1], "ctx", ring)
    spots = [pos[::RB] // RB]
    for s in range(1, n):
        spots.append(lax.ppermute(spots[0][:half // RB], "ctx", [(i, (i + s) % n) for i in range(n)]))
    mine = (ln1_gain, ln1_bias, b_qkv, b_out, ln2_gain, ln2_bias, b_in)
    small = lax.all_gather(jnp.concatenate(mine).reshape(1, -1), "fsdp", axis=0, tiled=True)
    full, at = [], 0
    for a in mine:
        full.append(small[:, at:at + a.shape[0]].reshape(-1).astype(f32))
        at += a.shape[0]
    gain_attn, shift_attn, bias_qkv, bias_out, gain_mlp, shift_mlp, bias_in = full
    weights = lax.all_gather(jnp.concatenate([w_qkv, w_attn_out], axis=1), "fsdp", axis=0, tiled=True)

    lane = jnp.arange(PAIR) % HD
    inverse = jnp.exp(-math.log(10000.0) * (2.0 / ROT) * (lane % (ROT // 2)).astype(f32))
    angles = jnp.arange(n * half + CLEN).astype(f32)[:, None] * inverse[None, :]
    sine = jnp.sin(angles)
    tables = (jnp.where(lane < ROT, jnp.cos(angles), 1.0), jnp.where(lane < ROT // 2, sine, 0.0),
              jnp.where((lane >= ROT // 2) & (lane < ROT), sine, 0.0))
    angles_t = pos.astype(f32)[None, :] * inverse[:ROT // 2, None]
    cos_t, sin_t = jnp.cos(angles_t), jnp.sin(angles_t)

    normed, queries, own_keys, own_values = qkv(
        spots[0], order, [after(x, far[n - 2], *spots[1:])], gain_attn, shift_attn, weights, bias_qkv, tables)
    far_keys, far_values = qkv(
        jnp.concatenate(spots[1:]), order, far[1:], gain_attn, shift_attn, weights, bias_qkv, tables)
    keys, values = (own_keys, far_keys), (own_values, far_values)
    grad_att = spread(grad_out, weights)
    weight_in = lax.all_gather(after(w_in, far[1]), "fsdp", axis=0, tiled=True)
    weight_out = lax.all_gather(after(w_out, far[1]), "fsdp", axis=0, tiled=True)

    per = half // QB
    earlier = jnp.stack([spots[s][0] < spots[0][0] for s in range(1, n)])
    local_row = jnp.arange(2 * per)[:, None]
    seen_own = local_row > jnp.arange(per)[None, :]
    seen_far = jnp.repeat(earlier[None, :] | (local_row >= per), per, axis=1)
    kind = jnp.where(jnp.concatenate([seen_own, seen_far], axis=1), 0.0, MASKED).astype(f32)

    attended, grad_q, own_kv, come_kv = [], [], [], []

    def attend(first, count, wait):
        out = attention(kind, owners, cos_t, sin_t, after(queries, *wait), grad_att, keys, values, first, count)
        attended.append(out[0])
        grad_q.append(out[1])
        come_kv.append(lax.psum_scatter(out[2], "ctx", scatter_dimension=0, tiled=True))
        own_kv.append(out[3])

    attend(0, 4, ())
    mlp_out, grad_mlp, in_send, in_keep, out_send, out_keep, db_in, db_out, dgain_mlp, dshift_mlp = mlp(
        order, after(x, *attended), grad_out, gain_mlp, shift_mlp, weight_in, bias_in, weight_out)
    attend(4, 2, (mlp_out,))
    steps_mlp = core_step([out_send, in_send], [out_keep, in_keep])
    attend(6, 2, (*attended, *steps_mlp))
    steps_mlp = side_step(kept_after(steps_mlp, *attended))
    output = join(after(x, *steps_mlp), attended, weights, mlp_out, bias_out)
    first_send, first_keep, grad_heads, db_first = first_tail(
        spots[0], order, after(grad_out, output), normed, weights, tables, attended, grad_q, own_kv[0], come_kv[0])
    part_out, part_in = last_step(kept_after(steps_mlp, grad_heads), 48)
    steps_first = core_step([first_send], [first_keep])
    grad_inputs, last_send, last_keep, db_last, dgain_attn, dshift_attn = last_tail(
        spots[0], after(x, part_out, part_in, *steps_first), normed, gain_attn, weights, tables, grad_mlp, grad_heads,
        own_kv[1:], come_kv[1:])
    sum_out, sum_in = along(part_out), along(part_in)
    steps_first = side_step(kept_after(steps_first, last_send))
    cols = db_last.shape[1] // 2
    split = [width, width + (db_first.shape[1] - width) // 2]
    db_q, db_k, db_v = jnp.split(db_first, split, axis=1)
    db_qkv = jnp.concatenate([db_q, db_k, db_last[:, :cols], db_v, db_last[:, cols:]], axis=1)
    parts = 8 * n
    smalls = [a.reshape(parts, -1) for a in (dgain_attn, dshift_attn, db_qkv, db_out, dgain_mlp, dshift_mlp, db_in)]
    flat = jnp.concatenate(smalls, axis=1).astype(bf16).reshape(parts, -1, PAIR)
    lines = flat.shape[1]
    packed = jnp.pad(flat, ((0, 0), (0, width // parts - lines), (0, 0))).reshape(width, PAIR)
    packed = packed.reshape(8, width // 8, PAIR)[order].reshape(2, width // 2, PAIR)
    steps_last = core_step([after(last_send, *steps_first), packed[0]], [last_keep, packed[1]])
    part_first = last_step(steps_first)
    part_last = last_step(side_step(kept_after(steps_last, *part_first)))
    total = along(jnp.concatenate([*part_first, *part_last], axis=1))
    ends = [width, 2 * width, split[1] + width, db_first.shape[1] + width]
    ends += [ends[-1] + cols, ends[-1] + 2 * cols]
    sum_attn, sum_q, sum_k, sum_v, end_k, end_v, packed = jnp.split(total, ends, axis=1)
    sum_qkv = jnp.concatenate([sum_q, sum_k, end_k, sum_v, end_v], axis=1)
    packed = packed[:lines].astype(f32).reshape(-1)
    done, at = [], 0
    for a in smalls:
        done.append(packed[at:at + a.shape[1]])
        at += a.shape[1]
    return (output[None], grad_inputs[None], done[0], done[1], sum_qkv.astype(f32), done[2], sum_attn.astype(f32),
            done[3], done[4], done[5], sum_in.astype(f32), done[6], sum_out.astype(f32))


def local(*args):
    half = args[0].shape[1] // 2
    if args[0].shape[0] == 1 and half % CLEN == 0 and lax.axis_size("fsdp") == 8:
        return fast(*args)
    return generic(*args)


def generic(
    inputs,
    cotangent,
    positions,
    segments,
    ln1_gain,
    ln1_bias,
    w_qkv,
    b_qkv,
    w_attn_out,
    b_out,
    ln2_gain,
    ln2_bias,
    w_in,
    b_in,
    w_out,
):
    shards = (
        ln1_gain,
        ln1_bias,
        w_qkv,
        b_qkv,
        w_attn_out,
        b_out,
        ln2_gain,
        ln2_bias,
        w_in,
        b_in,
        w_out,
    )
    params = (
        lax.all_gather(shards[0], "fsdp", axis=0, tiled=True),
        lax.all_gather(shards[1], "fsdp", axis=0, tiled=True),
        lax.all_gather(shards[2], "fsdp", axis=0, tiled=True),
        lax.all_gather(shards[3], "fsdp", axis=0, tiled=True),
        lax.all_gather(shards[4], "fsdp", axis=0, tiled=True),
        lax.all_gather(shards[5], "fsdp", axis=0, tiled=True),
        lax.all_gather(shards[6], "fsdp", axis=0, tiled=True),
        lax.all_gather(shards[7], "fsdp", axis=0, tiled=True),
        lax.all_gather(shards[8], "fsdp", axis=0, tiled=True),
        lax.all_gather(shards[9], "fsdp", axis=0, tiled=True),
        lax.all_gather(shards[10], "fsdp", axis=0, tiled=True),
    )
    groups, local_len, width = inputs.shape
    rows_total = groups * local_len
    block = math.gcd(local_len, 256)
    label_pos, label_seg = (
        lax.all_gather(positions, "ctx", axis=1, tiled=True),
        lax.all_gather(segments, "ctx", axis=1, tiled=True),
    )
    count = label_pos.shape[1] // block
    f32 = jnp.float32
    bf16 = jnp.bfloat16
    (
        gain_attn,
        shift_attn,
        weight_qkv,
        bias_qkv,
        weight_attn,
        bias_out,
        gain_mlp,
        shift_mlp,
        weight_in,
        bias_in,
        weight_out,
    ) = params
    flat_in = inputs.reshape(rows_total, width).astype(f32)
    normed_attn = layer_norm(flat_in, gain_attn.astype(f32), shift_attn.astype(f32)).astype(bf16)
    normed_mlp = layer_norm(flat_in, gain_mlp.astype(f32), shift_mlp.astype(f32)).astype(bf16)
    projected = jnp.dot(normed_attn, weight_qkv, preferred_element_type=f32) + bias_qkv.astype(f32)
    cosine, sine = rotary_tables(positions)

    def split_heads(columns):
        return columns.reshape(groups, local_len, HEADS, HD)

    scale = HD ** (-0.5)
    queries = (rotate(split_heads(projected[:, :width]), cosine, sine) * scale).astype(bf16)
    keys_own = rotate(split_heads(projected[:, width : 2 * width]), cosine, sine).astype(bf16)
    values_own = split_heads(projected[:, 2 * width :]).astype(bf16)
    keys_all, values_all = (
        lax.all_gather(keys_own, "ctx", axis=1, tiled=True),
        lax.all_gather(values_own, "ctx", axis=1, tiled=True),
    )

    def key_block(index):
        start = index * block
        keys_blk = lax.dynamic_slice_in_dim(keys_all, start, block, 1)
        values_blk = lax.dynamic_slice_in_dim(values_all, start, block, 1)
        mask = allowed_mask(
            positions,
            segments,
            lax.dynamic_slice_in_dim(label_pos, start, block, 1),
            lax.dynamic_slice_in_dim(label_seg, start, block, 1),
        )
        return (keys_blk, values_blk, mask)

    def total_step(carry, index):
        peak, total = carry
        keys_blk, values_blk, mask = key_block(index)
        scores = jnp.where(mask, scores_of(queries, keys_blk), MASKED)
        fresh = jnp.maximum(peak, jnp.max(scores, axis=-1))
        added = jnp.sum(jnp.where(mask, jnp.exp(scores - fresh[..., None]), 0.0), axis=-1)
        return ((fresh, total * jnp.exp(peak - fresh) + added), None)

    stat_shape = (groups, HEADS, local_len)
    (peak, total), unused = lax.scan(
        total_step,
        (jnp.full(stat_shape, MASKED, f32), jnp.zeros(stat_shape, f32)),
        jnp.arange(count),
    )
    log_total = peak + jnp.log(total)

    def attend_step(rounded_sum, index):
        keys_blk, values_blk, mask = key_block(index)
        probs = jnp.where(mask, jnp.exp(scores_of(queries, keys_blk) - log_total[..., None]), 0.0)
        rounded_sum = rounded_sum + jnp.einsum(
            "ghqk,gkhd->gqhd", probs.astype(bf16), values_blk, preferred_element_type=f32
        )
        return (rounded_sum, None)

    head_shape = (groups, local_len, HEADS, HD)
    rounded_sum, unused = lax.scan(attend_step, jnp.zeros(head_shape, f32), jnp.arange(count))
    attended = rounded_sum.reshape(rows_total, width).astype(bf16)
    pre_act = jnp.dot(normed_mlp, weight_in, preferred_element_type=f32) + bias_in.astype(f32)
    activated = jax.nn.gelu(pre_act, approximate=False).astype(bf16)
    output = (
        flat_in
        + jnp.dot(attended, weight_attn, preferred_element_type=f32)
        + jnp.dot(activated, weight_out, preferred_element_type=f32)
        + bias_out.astype(f32)
    )
    (
        gain_attn,
        shift_attn,
        weight_qkv,
        bias_qkv,
        weight_attn,
        bias_out,
        gain_mlp,
        shift_mlp,
        weight_in,
        bias_in,
        weight_out,
    ) = params
    grad_out = cotangent.reshape(rows_total, width)
    grad_bias_out = jnp.sum(grad_out.astype(f32), axis=0)
    grad_weight_out = jnp.einsum("rf,rd->fd", activated, grad_out, preferred_element_type=f32)
    grad_act = jnp.einsum("rd,fd->rf", grad_out, weight_out, preferred_element_type=f32)
    unused, gelu_back = jax.vjp(partial(jax.nn.gelu, approximate=False), pre_act)
    grad_pre = gelu_back(grad_act)[0].astype(bf16)
    grad_weight_in = jnp.einsum("rd,rf->df", normed_mlp, grad_pre, preferred_element_type=f32)
    grad_bias_in = jnp.sum(grad_pre.astype(f32), axis=0)
    grad_normed_mlp = jnp.einsum("rf,df->rd", grad_pre, weight_in, preferred_element_type=f32)
    grad_weight_attn = jnp.einsum("ra,rd->ad", attended, grad_out, preferred_element_type=f32)
    grad_att = (
        jnp.einsum("rd,ad->ra", grad_out, weight_attn, preferred_element_type=f32)
        .astype(bf16)
        .reshape(head_shape)
    )
    delta = jnp.einsum(
        "gqhd,gqhd->ghq", grad_att.astype(f32), rounded_sum, precision=lax.Precision.HIGHEST
    )

    def back_step(carry, index):
        keys_blk, values_blk, mask = key_block(index)
        rounded, grad_scores = block_grads(
            queries, grad_att, log_total, delta, mask, keys_blk, values_blk
        )
        carry = carry + jnp.einsum(
            "ghqk,gkhd->gqhd", grad_scores, keys_blk, preferred_element_type=f32
        )
        key_term = jnp.einsum("ghqk,gqhd->gkhd", grad_scores, queries, preferred_element_type=f32)
        value_term = jnp.einsum("ghqk,gqhd->gkhd", rounded, grad_att, preferred_element_type=f32)
        return (carry, (key_term, value_term))

    grad_queries, (key_terms, value_terms) = lax.scan(
        back_step, jnp.zeros(head_shape, f32), jnp.arange(count)
    )
    key_sums, value_sums = (
        lax.psum_scatter(
            key_terms.astype(jnp.bfloat16), "ctx", scatter_dimension=0, tiled=True
        ).astype(jnp.float32),
        lax.psum_scatter(
            value_terms.astype(jnp.bfloat16), "ctx", scatter_dimension=0, tiled=True
        ).astype(jnp.float32),
    )
    grad_keys = jnp.transpose(key_sums, (1, 0, 2, 3, 4)).reshape(head_shape)
    grad_values = jnp.transpose(value_sums, (1, 0, 2, 3, 4)).reshape(head_shape)
    grad_q_pre = unrotate(grad_queries * scale, cosine, sine).reshape(rows_total, width)
    grad_k_pre = unrotate(grad_keys, cosine, sine).reshape(rows_total, width)
    grad_projected = jnp.concatenate(
        [grad_q_pre, grad_k_pre, grad_values.reshape(rows_total, width)], axis=1
    ).astype(bf16)
    grad_weight_qkv = jnp.einsum(
        "rd,re->de", normed_attn, grad_projected, preferred_element_type=f32
    )
    grad_bias_qkv = jnp.sum(grad_projected.astype(f32), axis=0)
    grad_normed_attn = jnp.einsum(
        "re,de->rd", grad_projected, weight_qkv, preferred_element_type=f32
    )
    unused, norm_back_attn = jax.vjp(
        layer_norm, flat_in, gain_attn.astype(f32), shift_attn.astype(f32)
    )
    grad_in_attn, grad_gain_attn, grad_shift_attn = norm_back_attn(grad_normed_attn)
    unused, norm_back_mlp = jax.vjp(
        layer_norm, flat_in, gain_mlp.astype(f32), shift_mlp.astype(f32)
    )
    grad_in_mlp, grad_gain_mlp, grad_shift_mlp = norm_back_mlp(grad_normed_mlp)
    grad_inputs = (grad_out.astype(f32) + grad_in_attn + grad_in_mlp).reshape(
        groups, local_len, width
    )
    sums = (
        lax.psum_scatter(grad_gain_attn, ("fsdp", "ctx"), scatter_dimension=0, tiled=True),
        lax.psum_scatter(grad_shift_attn, ("fsdp", "ctx"), scatter_dimension=0, tiled=True),
        lax.psum_scatter(grad_weight_qkv, ("fsdp", "ctx"), scatter_dimension=0, tiled=True),
        lax.psum_scatter(grad_bias_qkv, ("fsdp", "ctx"), scatter_dimension=0, tiled=True),
        lax.psum_scatter(grad_weight_attn, ("fsdp", "ctx"), scatter_dimension=0, tiled=True),
        lax.psum_scatter(grad_bias_out, ("fsdp", "ctx"), scatter_dimension=0, tiled=True),
        lax.psum_scatter(grad_gain_mlp, ("fsdp", "ctx"), scatter_dimension=0, tiled=True),
        lax.psum_scatter(grad_shift_mlp, ("fsdp", "ctx"), scatter_dimension=0, tiled=True),
        lax.psum_scatter(grad_weight_in, ("fsdp", "ctx"), scatter_dimension=0, tiled=True),
        lax.psum_scatter(grad_bias_in, ("fsdp", "ctx"), scatter_dimension=0, tiled=True),
        lax.psum_scatter(grad_weight_out, ("fsdp", "ctx"), scatter_dimension=0, tiled=True),
    )
    result = output.reshape(groups, local_len, width).astype(bf16)
    return (
        result,
        grad_inputs,
        sums[0],
        sums[1],
        sums[2],
        sums[3],
        sums[4],
        sums[5],
        sums[6],
        sums[7],
        sums[8],
        sums[9],
        sums[10],
    )


def solution(mesh):
    in_specs = (
        P("fsdp", "ctx", None),
        P("fsdp", "ctx", None),
        P("fsdp", "ctx"),
        P("fsdp", "ctx"),
        P("fsdp"),
        P("fsdp"),
        P("fsdp", None),
        P("fsdp"),
        P("fsdp", None),
        P("fsdp"),
        P("fsdp"),
        P("fsdp"),
        P("fsdp", None),
        P("fsdp"),
        P("fsdp", None),
    )
    out_specs = (
        P("fsdp", "ctx", None),
        P("fsdp", "ctx", None),
        P(("fsdp", "ctx")),
        P(("fsdp", "ctx")),
        P(("fsdp", "ctx"), None),
        P(("fsdp", "ctx")),
        P(("fsdp", "ctx"), None),
        P(("fsdp", "ctx")),
        P(("fsdp", "ctx")),
        P(("fsdp", "ctx")),
        P(("fsdp", "ctx"), None),
        P(("fsdp", "ctx")),
        P(("fsdp", "ctx"), None),
    )
    return jax.shard_map(local, mesh=mesh, in_specs=in_specs, out_specs=out_specs, check_vma=False)
```

```python
from functools import partial
import math

import jax
import jax.numpy as jnp
from jax import lax
from jax.experimental import pallas as pl
from jax.experimental.pallas import tpu as pltpu
from jax.sharding import PartitionSpec as P

HEADS = 16
HD = 64
ROT = 16
CLEN = 256
QB = 256
RB = 256
PAIR = 2 * HD
bf16 = jnp.bfloat16
f32 = jnp.float32
NN = (((1,), (0,)), ((), ()))
NT = (((1,), (1,)), ((), ()))
TN = (((0,), (0,)), ((), ()))


NORM_EPS = 1e-05
MASKED = -1e30


def layer_norm(values, scaling, offset):
    average = jnp.mean(values, axis=-1, keepdims=True)
    centered = values - average
    variance = jnp.mean(centered * centered, axis=-1, keepdims=True)
    return centered * lax.rsqrt(variance + NORM_EPS) * scaling + offset


def rotary_tables(positions):
    halfway = ROT // 2
    spacing = jnp.arange(halfway, dtype=jnp.float32) * (2.0 / ROT)
    inverse = jnp.exp(-math.log(10000.0) * spacing)
    angles = positions.astype(jnp.float32)[..., None] * inverse
    return (jnp.cos(angles), jnp.sin(angles))


def rotate(heads_in, cosine, sine):
    halfway = ROT // 2
    cosine = cosine[..., None, :]
    sine = sine[..., None, :]
    first = heads_in[..., :halfway]
    second = heads_in[..., halfway:ROT]
    return jnp.concatenate(
        [first * cosine - second * sine, second * cosine + first * sine, heads_in[..., ROT:]],
        axis=-1,
    )


def unrotate(grads_in, cosine, sine):
    halfway = ROT // 2
    cosine = cosine[..., None, :]
    sine = sine[..., None, :]
    first = grads_in[..., :halfway]
    second = grads_in[..., halfway:ROT]
    return jnp.concatenate(
        [first * cosine + second * sine, second * cosine - first * sine, grads_in[..., ROT:]],
        axis=-1,
    )


def allowed_mask(query_pos, query_seg, key_pos, key_seg):
    same_doc = (key_seg[:, None, :] == 0) | (key_seg[:, None, :] == query_seg[:, :, None])
    causal = key_pos[:, None, :] <= query_pos[:, :, None]
    return (same_doc & causal)[:, None]


def scores_of(queries, keys_blk):
    return jnp.einsum("gqhd,gkhd->ghqk", queries, keys_blk, preferred_element_type=jnp.float32)


def block_grads(queries, grad_att, log_total, delta, mask, keys_blk, values_blk):
    probs = jnp.where(mask, jnp.exp(scores_of(queries, keys_blk) - log_total[..., None]), 0.0)
    dprobs = jnp.einsum("gqhd,gkhd->ghqk", grad_att, values_blk, preferred_element_type=jnp.float32)
    grad_scores = (probs * (dprobs - delta[..., None])).astype(jnp.bfloat16)
    return (probs.astype(jnp.bfloat16), grad_scores)


def mm(a, b, dims):
    return lax.dot_general(a, b, dims, preferred_element_type=f32)


def row_stats(x):
    average = jnp.mean(x, axis=1, keepdims=True)
    centered = x - average
    return centered, lax.rsqrt(jnp.mean(centered * centered, axis=1, keepdims=True) + NORM_EPS)


def norm_rows(x, scaling, offset):
    centered, inverse = row_stats(x)
    return (centered * inverse * scaling + offset).astype(bf16)


def norm_back(x, grad, scaling):
    centered, inverse = row_stats(x)
    unit = centered * inverse
    e = grad * scaling
    inner = e - jnp.mean(e, axis=1, keepdims=True) - unit * jnp.mean(e * unit, axis=1, keepdims=True)
    return inverse * inner, grad * unit


def col_sum(a):
    return jnp.sum(a, axis=0, keepdims=True)


def vmem(*shape, dtype=f32):
    return pltpu.VMEM(shape, dtype)


def params():
    return pltpu.CompilerParams(vmem_limit_bytes=60 << 20)


ROOT = math.sqrt(0.5)
DENS = 1.0 / math.sqrt(2.0 * math.pi)


def reorder(order_ref, source, target):
    size = source.shape[1] // order_ref.shape[0]
    for i in range(order_ref.shape[0]):
        at = pl.multiple_of(order_ref[i] * size, size)
        target[:, i * size:(i + 1) * size] = source[:, pl.ds(at, size)]


def mlp_kernel(order_ref, x_ref, c_ref, gain_ref, shift_ref, win_ref, bin_ref, wout_ref,
               out_ref, gin_ref, dwin_send, dwin_keep, dwout_send, dwout_keep, dbin_ref, dbout_ref, dgain_ref, dshift_ref,
               h_ref, turned_ref, act_ref, gp_ref, gh_ref):
    step = pl.program_id(0)
    rows = x_ref.shape[0]
    blocks = [slice(r, r + RB) for r in range(0, rows, RB)]

    @pl.when(step == 0)
    def _():
        for r in blocks:
            h_ref[r, :] = norm_rows(x_ref[r, :].astype(f32), gain_ref[...], shift_ref[...])
            out_ref[r, :] = jnp.zeros((RB, out_ref.shape[1]), f32)
            gh_ref[r, :] = jnp.zeros((RB, gh_ref.shape[1]), f32)
        reorder(order_ref, h_ref, turned_ref)

    dbin = jnp.zeros(dbin_ref.shape, f32)
    for r in blocks:
        pre = mm(h_ref[r, :], win_ref[...], NN) + bin_ref[...]
        phi = 0.5 + 0.5 * lax.erf(pre * ROOT)
        act_ref[r, :] = (pre * phi).astype(bf16)
        gp = phi + pre * (DENS * jnp.exp(-0.5 * (pre * pre)))
        gact = mm(c_ref[r, :], wout_ref[...], NT)
        gpre = (gact * gp).astype(bf16)
        gp_ref[r, :] = gpre
        dbin = dbin + col_sum(gpre.astype(f32))
    for r in blocks:
        out_ref[r, :] += mm(act_ref[r, :], wout_ref[...], NN)
        gh_ref[r, :] += mm(gp_ref[r, :], win_ref[...], NT)
    dwout = mm(act_ref[...], c_ref[...], TN).astype(bf16)
    middle = pl.num_programs(0) // 2

    @pl.when(step < middle)
    def _():
        dwout_send[...] = dwout

    @pl.when(step >= middle)
    def _():
        dwout_keep[...] = dwout

    dwin = mm(turned_ref[...], gp_ref[...], TN).astype(bf16)
    dwin_send[...] = dwin[:dwin_send.shape[0]]
    dwin_keep[...] = dwin[dwin_send.shape[0]:]
    dbin_ref[...] = dbin

    @pl.when(step == pl.num_programs(0) - 1)
    def _():
        dgain = jnp.zeros(dgain_ref.shape, f32)
        dshift = jnp.zeros(dshift_ref.shape, f32)
        dbout = jnp.zeros(dbout_ref.shape, f32)
        for r in blocks:
            grad = gh_ref[r, :]
            back, scaled = norm_back(x_ref[r, :].astype(f32), grad, gain_ref[...])
            c = c_ref[r, :].astype(f32)
            gin_ref[r, :] = back + c
            dgain += col_sum(scaled)
            dshift += col_sum(grad)
            dbout += col_sum(c)
        dgain_ref[...] = dgain
        dshift_ref[...] = dshift
        dbout_ref[...] = dbout


def mlp(order, x, c, gain, shift, weight_in, bias_in, weight_out):
    rows, width = x.shape
    ff = weight_in.shape[1]
    steps = order.shape[0]
    fc = ff // steps
    whole = pl.BlockSpec((rows, width), lambda j, o: (0, 0))
    line = pl.BlockSpec((1, width), lambda j, o: (0, 0))
    down = pl.BlockSpec((width // 2, fc), lambda j, o: (0, o[j]))
    s = jax.ShapeDtypeStruct
    return pl.pallas_call(
        mlp_kernel,
        grid_spec=pltpu.PrefetchScalarGridSpec(
            num_scalar_prefetch=1,
            grid=(steps,),
            in_specs=[whole, whole, line, line, pl.BlockSpec((width, fc), lambda j, o: (0, o[j])),
                      pl.BlockSpec((1, fc), lambda j, o: (0, o[j])), pl.BlockSpec((fc, width), lambda j, o: (o[j], 0))],
            out_specs=[whole, whole, down, down,
                       pl.BlockSpec((fc, width), lambda j, o: (jnp.minimum(j, steps // 2 - 1), 0)),
                       pl.BlockSpec((fc, width), lambda j, o: (jnp.maximum(j - steps // 2, 0), 0)),
                       pl.BlockSpec((1, fc), lambda j, o: (0, o[j])), line, line, line],
            scratch_shapes=[vmem(rows, width, dtype=bf16), vmem(rows, width, dtype=bf16), vmem(rows, fc, dtype=bf16),
                            vmem(rows, fc, dtype=bf16), vmem(rows, width)],
        ),
        out_shape=[s((rows, width), f32), s((rows, width), f32), s((width // 2, ff), bf16), s((width // 2, ff), bf16),
                   s((ff // 2, width), bf16), s((ff // 2, width), bf16), s((1, ff), f32), s((1, width), f32),
                   s((1, width), f32), s((1, width), f32)],
        compiler_params=params(),
        cost_estimate=pl.CostEstimate(flops=1 << 20, bytes_accessed=1 << 16, transcendentals=0),
        name="mlp",
    )(order, x, c, gain.reshape(1, -1), shift.reshape(1, -1), weight_in, bias_in.reshape(1, -1), weight_out)


def turn_lanes(u, cosine, low, high, sign):
    half = ROT // 2
    parts = []
    for at in range(0, u.shape[1], PAIR):
        g = u[:, at:at + PAIR]
        parts.append(g * cosine + sign * (pltpu.roll(g, half, 1) * high - pltpu.roll(g, PAIR - half, 1) * low))
    return jnp.concatenate(parts, axis=1)


def qkv_kernel(far, spot_ref, order_ref, gain_ref, shift_ref, w_ref, b_ref, cos_ref, low_ref, high_ref, *refs):
    with_q = far == 0
    if with_q:
        x_ref, outs = refs[0], refs[1:]
    else:
        x_refs, outs, x_ref = refs[:far], refs[far:-1], refs[-1]
        step = pl.program_id(0)
        per = pl.num_programs(0) // far
        for s in range(far):
            @pl.when(step // per == s)
            def _(s=s):
                x_ref[...] = x_refs[s][...]
    width = x_ref.shape[1]
    h = norm_rows(x_ref[...].astype(f32), gain_ref[...], shift_ref[...])
    tables = (cos_ref[...], low_ref[...], high_ref[...])
    if with_q:
        h_ref, q_ref, k_ref, v_ref, plain_ref = outs
        plain_ref[...] = h
        reorder(order_ref, plain_ref, h_ref)
        q = mm(h, w_ref[:, :width], NN) + b_ref[:, :width]
        q_ref[...] = (turn_lanes(q, *tables, 1.0) * (HD ** (-0.5) / math.log(2.0))).astype(bf16)
    else:
        k_ref, v_ref = outs
    k = mm(h, w_ref[:, width:2 * width], NN) + b_ref[:, width:2 * width]
    k_ref[...] = turn_lanes(k, *tables, 1.0).astype(bf16)
    v_ref[...] = (mm(h, w_ref[:, 2 * width:], NN) + b_ref[:, 2 * width:]).astype(bf16)


def qkv(spots, order, xs, gain, shift, weight, bias, tables):
    far = len(xs) if len(xs) > 1 else 0
    rows, width = xs[0].shape
    per = rows // RB
    total = len(xs) * rows
    s = jax.ShapeDtypeStruct((total, width), bf16)
    block = pl.BlockSpec((RB, width), lambda j, spot, o: (j, 0))
    line = pl.BlockSpec((1, width), lambda j, spot, o: (0, 0))
    table = pl.BlockSpec((RB, PAIR), lambda j, spot, o: (spot[j], 0))
    count = 2 if far else 4

    def window(i):
        return pl.BlockSpec((RB, width), lambda j, spot, o: (jnp.clip(j - i * per, 0, per - 1), 0))

    return pl.pallas_call(
        partial(qkv_kernel, far),
        grid_spec=pltpu.PrefetchScalarGridSpec(
            num_scalar_prefetch=2,
            grid=(total // RB,),
            in_specs=[line, line, pl.BlockSpec((width, 3 * width), lambda j, spot, o: (0, 0)),
                      pl.BlockSpec((1, 3 * width), lambda j, spot, o: (0, 0)), table, table, table]
            + [window(i) for i in range(len(xs))],
            out_specs=[block] * count,
            scratch_shapes=[vmem(RB, width, dtype=bf16)],
        ),
        out_shape=[s] * count,
        compiler_params=params(),
        cost_estimate=pl.CostEstimate(flops=1 << 20, bytes_accessed=1 << 16, transcendentals=0),
        name="kv_remote" if far else "qkv_own",
    )(spots, order, gain.reshape(1, -1), shift.reshape(1, -1), weight, bias.reshape(1, -1), *tables, *xs)


def gather_rows(step, spot, tables, own_refs, come_refs, p_ref, k_at, v_at):
    half = pl.num_programs(0) // 2
    columns = [(g, at) for g in range(len(own_refs)) for at in range(0, own_refs[g].shape[1], 2 * PAIR)]

    def put(refs):
        for to, (g, at) in enumerate(columns):
            turned = turn_lanes(refs[g][:, at:at + PAIR].astype(f32), *tables, -1.0).astype(bf16)
            p_ref[spot, k_at + to * PAIR:k_at + (to + 1) * PAIR] = turned
            p_ref[spot, v_at + to * PAIR:v_at + (to + 1) * PAIR] = refs[g][:, at + PAIR:at + 2 * PAIR]

    @pl.when(step < half)
    def _():
        put(come_refs)

    @pl.when(step >= half)
    def _():
        put(own_refs)


def half_windows(arrays, count):
    half = count // 2
    come = [pl.BlockSpec((RB, a.shape[1]), lambda j, *o: (jnp.clip(j, 0, half - 1), 0)) for a in arrays]
    own = [pl.BlockSpec((RB, a.shape[1]), lambda j, *o: (jnp.clip(j - half, 0, half - 1), 0)) for a in arrays]
    return own, come


def first_kernel(groups, spot_ref, order_ref, c_ref, h_ref, wq_ref, wk_ref, wv_ref, cos_ref, low_ref, high_ref, own_ref,
                 come_ref, *refs):
    att_refs, dq_refs = refs[:groups], refs[groups:2 * groups]
    send_ref, keep_ref, gh_ref, db_ref, p_ref, att_ref, turned_ref = refs[2 * groups:]
    step = pl.program_id(0)
    width = c_ref.shape[1]
    spot = pl.ds(pl.multiple_of(step * RB, RB), RB)
    at = 0
    for g in range(groups):
        size = att_refs[g].shape[1]
        att_ref[:, at:at + size] = att_refs[g][...]
        p_ref[spot, at:at + size] = dq_refs[g][...]
        at += size
    for i in range(order_ref.shape[0]):
        size = width // order_ref.shape[0]
        lanes = pl.ds(pl.multiple_of(order_ref[i] * size, size), size)
        turned_ref[spot, i * size:(i + 1) * size] = att_ref[:, lanes]
    count = wk_ref.shape[1]
    gather_rows(step, spot, (cos_ref[...], low_ref[...], high_ref[...]), [own_ref], [come_ref], p_ref, width, width + count)
    gh_ref[...] = (mm(p_ref[spot, :width], wq_ref[...], NT) + mm(p_ref[spot, width:width + count], wk_ref[...], NT)
                   + mm(p_ref[spot, width + count:], wv_ref[...], NT))
    db = col_sum(p_ref[spot, :].astype(f32))

    @pl.when(step == 0)
    def _():
        db_ref[...] = db

    @pl.when(step > 0)
    def _():
        db_ref[...] += db

    @pl.when(step == pl.num_programs(0) - 1)
    def _():
        half = send_ref.shape[0]
        for to in range(0, send_ref.shape[1], 512):
            if to < width:
                dw = mm(turned_ref[...], c_ref[:, to:to + 512], TN)
            else:
                dw = mm(h_ref[...], p_ref[:, to - width:to - width + 512], TN)
            dw = dw.astype(bf16)
            send_ref[:, to:to + 512] = dw[:half]
            keep_ref[:, to:to + 512] = dw[half:]


def first_tail(spots, order, c, h, weights, tables, attended, dqs, own, come):
    rows, width = c.shape
    cols = own.shape[1] // 2
    steps = rows // RB
    total = 2 * width + 2 * cols
    s = jax.ShapeDtypeStruct

    def full(shape):
        return pl.BlockSpec(shape, lambda j, spot, o: (0, 0), pipeline_mode=pl.Buffered(1))

    def weight(size, at):
        return pl.BlockSpec((width, size), lambda j, spot, o: (0, at // size), pipeline_mode=pl.Buffered(1))

    def window(a):
        return pl.BlockSpec((RB, a.shape[1]), lambda j, spot, o: (j, 0))

    table = pl.BlockSpec((RB, PAIR), lambda j, spot, o: (spot[j], 0))
    owns, comes = half_windows([own], steps)
    return pl.pallas_call(
        partial(first_kernel, len(dqs)),
        grid_spec=pltpu.PrefetchScalarGridSpec(
            num_scalar_prefetch=2,
            grid=(steps,),
            in_specs=[full(c.shape), full(h.shape), weight(width, 0), weight(cols, width), weight(cols, 2 * width)] + [table] * 3
            + owns + comes + [window(a) for a in (*attended, *dqs)],
            out_specs=[full((width // 2, total)), full((width // 2, total)), window(c), full((1, total - width))],
            scratch_shapes=[vmem(rows, total - width, dtype=bf16), vmem(RB, width, dtype=bf16), vmem(rows, width, dtype=bf16)],
        ),
        out_shape=[s((width // 2, total), bf16), s((width // 2, total), bf16), s((rows, width), f32), s((1, total - width), f32)],
        compiler_params=params(),
        cost_estimate=pl.CostEstimate(flops=24 << 30, bytes_accessed=1 << 20, transcendentals=0),
        name="first_tail",
    )(spots, order, c, h, weights, weights, weights, *tables, own, come, *attended, *dqs)


def last_kernel(groups, spot_ref, h_ref, gain_ref, wk_ref, wv_ref, x_ref, cos_ref, low_ref, high_ref, gin_ref, ghin_ref, *refs):
    own_refs, come_refs = refs[:groups], refs[groups:2 * groups]
    grad_ref, send_ref, keep_ref, db_ref, dgain_ref, dshift_ref, p_ref = refs[2 * groups:]
    step = pl.program_id(0)
    spot = pl.ds(pl.multiple_of(step * RB, RB), RB)
    count = wk_ref.shape[1]
    gather_rows(step, spot, (cos_ref[...], low_ref[...], high_ref[...]), own_refs, come_refs, p_ref, 0, count)
    grad = (ghin_ref[...] + mm(p_ref[spot, :count], wk_ref[...], NT) + mm(p_ref[spot, count:], wv_ref[...], NT))
    back, scaled = norm_back(x_ref[...].astype(f32), grad, gain_ref[...])
    grad_ref[...] = back + gin_ref[...]
    sums = col_sum(p_ref[spot, :].astype(f32)), col_sum(scaled), col_sum(grad)

    @pl.when(step == 0)
    def _():
        for ref, value in zip((db_ref, dgain_ref, dshift_ref), sums):
            ref[...] = value

    @pl.when(step > 0)
    def _():
        for ref, value in zip((db_ref, dgain_ref, dshift_ref), sums):
            ref[...] += value

    @pl.when(step == pl.num_programs(0) - 1)
    def _():
        half = send_ref.shape[0]
        for to in range(0, send_ref.shape[1], 512):
            dw = mm(h_ref[...], p_ref[:, to:to + 512], TN).astype(bf16)
            send_ref[:, to:to + 512] = dw[:half]
            keep_ref[:, to:to + 512] = dw[half:]


def last_tail(spots, x, h, gain, weights, tables, gin, gh, owns, comes):
    rows, width = x.shape
    cols = sum(a.shape[1] for a in owns) // 2
    steps = rows // RB
    s = jax.ShapeDtypeStruct

    def full(shape):
        return pl.BlockSpec(shape, lambda j, spot: (0, 0), pipeline_mode=pl.Buffered(1))

    def weight(at):
        return pl.BlockSpec((width, cols), lambda j, spot: (0, at // cols), pipeline_mode=pl.Buffered(1))

    block = pl.BlockSpec((RB, width), lambda j, spot: (j, 0))
    table = pl.BlockSpec((RB, PAIR), lambda j, spot: (spot[j], 0))
    own_windows, come_windows = half_windows(owns, steps)
    return pl.pallas_call(
        partial(last_kernel, len(owns)),
        grid_spec=pltpu.PrefetchScalarGridSpec(
            num_scalar_prefetch=1,
            grid=(steps,),
            in_specs=[full(h.shape), full((1, width)), weight(2 * width - cols), weight(3 * width - cols), block] + [table] * 3
            + [block, block] + own_windows + come_windows,
            out_specs=[block, full((width // 2, 2 * cols)), full((width // 2, 2 * cols)), full((1, 2 * cols)), full((1, width)),
                       full((1, width))],
            scratch_shapes=[vmem(rows, 2 * cols, dtype=bf16)],
        ),
        out_shape=[s((rows, width), f32), s((width // 2, 2 * cols), bf16), s((width // 2, 2 * cols), bf16), s((1, 2 * cols), f32),
                   s((1, width), f32), s((1, width), f32)],
        compiler_params=params(),
        cost_estimate=pl.CostEstimate(flops=12 << 30, bytes_accessed=1 << 20, transcendentals=0),
        name="last_tail",
    )(spots, h, gain.reshape(1, -1), weights, weights, x, *tables, gin, gh, *owns, *comes)


def join_kernel(groups, x_ref, w_ref, mlp_ref, b_ref, *refs):
    att_refs, (out_ref, att_ref) = refs[:groups], refs[groups:]
    at = 0
    for ref in att_refs:
        att_ref[:, at:at + ref.shape[1]] = ref[...]
        at += ref.shape[1]
    out = x_ref[...].astype(f32) + mm(att_ref[...], w_ref[...], NN) + mlp_ref[...] + b_ref[...]
    out_ref[...] = out.astype(bf16)


def join(x, attended, weights, mlp_out, bias):
    rows, width = x.shape
    s = jax.ShapeDtypeStruct
    block = pl.BlockSpec((RB, width), lambda j: (j, 0))
    return pl.pallas_call(
        partial(join_kernel, len(attended)),
        grid=(rows // RB,),
        in_specs=[block, pl.BlockSpec((width, width), lambda j: (0, 3)), block, pl.BlockSpec((1, width), lambda j: (0, 0))]
        + [pl.BlockSpec((RB, a.shape[1]), lambda j: (j, 0)) for a in attended],
        out_specs=block,
        out_shape=s((rows, width), bf16),
        scratch_shapes=[vmem(RB, width, dtype=bf16)],
        compiler_params=params(),
        cost_estimate=pl.CostEstimate(flops=12 << 30, bytes_accessed=1 << 20, transcendentals=0),
        name="join",
    )(x, weights, mlp_out, bias.reshape(1, -1), *attended)


def spread_kernel(c_ref, w_ref, out_ref):
    out_ref[...] = mm(c_ref[...], w_ref[...], NT).astype(bf16)


def spread(c, weights):
    rows, width = c.shape
    block = pl.BlockSpec((RB, width), lambda j: (j, 0))
    return pl.pallas_call(
        spread_kernel,
        grid=(rows // RB,),
        in_specs=[block, pl.BlockSpec((width, width), lambda j: (0, 3))],
        out_specs=block,
        out_shape=jax.ShapeDtypeStruct((rows, width), bf16),
        compiler_params=params(),
        cost_estimate=pl.CostEstimate(flops=1 << 20, bytes_accessed=1 << 16, transcendentals=0),
        name="spread",
    )(c, weights)


def fold(x, op):
    return op(x.reshape(x.shape[0] // 8, 8, x.shape[1]), axis=0)


def eye(size):
    return (lax.broadcasted_iota(jnp.int32, (size, size), 0) == lax.broadcasted_iota(jnp.int32, (size, size), 1)).astype(bf16)


def attention_kernel(half, n, kind_ref, owner_ref, cos_ref, sin_ref, q_ref, do_ref, *refs):
    k_refs, v_refs = refs[:2], refs[2:4]
    o_ref, dq_ref, all_ref, cont_ref, kt_ref, vt_ref, s_ref, p_ref, ds_ref, dka_ref, dva_ref = refs[4:]
    per = half // QB
    wide = n * half
    count = wide // QB
    spots = [(0, c * QB) for c in range(per)] + [(1, c * QB) for c in range((n - 1) * per)]

    ident = eye(PAIR)
    for refs_in, out in ((k_refs, kt_ref), (v_refs, vt_ref)):
        for c, (s, at) in enumerate(spots):
            out[:, c * QB:(c + 1) * QB] = refs_in[s][at:at + QB, :].T
        for c in range(per):
            out[:, wide + c * QB:wide + (c + 1) * QB] = refs_in[0][half + c * QB:half + (c + 1) * QB, :].T
    cont = slice(wide, wide + half)
    dka_ref[cont, :] = jnp.zeros((half, PAIR), f32)
    dva_ref[cont, :] = jnp.zeros((half, PAIR), f32)


    def block(qb, carry):
        own = pl.ds(pl.multiple_of(qb * QB, QB), QB)
        slot = pl.ds(pl.multiple_of(jnp.where(qb < per, qb * QB, wide + (qb - per) * QB), QB), QB)
        zero = jnp.zeros((), bf16)
        causal = lax.broadcasted_iota(jnp.int32, (QB, QB), 0) <= lax.broadcasted_iota(jnp.int32, (QB, QB), 1)
        left = lax.broadcasted_iota(jnp.int32, (QB, PAIR), 1) < HD

        def by_head(a):
            return jnp.where(left, a, zero), jnp.where(left, zero, a)

        def keys_of(some, c):
            if c == count:
                return some[0][own, :]
            s, at = spots[c]
            return some[s][at:at + QB, :]

        def cut(c):
            return slice(c * QB, (c + 1) * QB)

        ident = eye(QB)
        q_heads = by_head(q_ref[own, :])
        do_t = mm(eye(PAIR), do_ref[own, :], NT)
        upper = lax.broadcasted_iota(jnp.int32, (PAIR, QB), 0) < HD
        q_t = mm(eye(PAIR), q_ref[own, :], NT).astype(bf16)
        q_cols = jnp.where(upper, q_t, zero), jnp.where(upper, zero, q_t)
        peaks, norms, outs, deltas, scaled = [None, None], [None, None], [None, None], [None, None], [None, None]

        def scores(h):
            peak = jnp.full((8, QB), MASKED, f32)
            for c in range(count + 1):
                s = mm(keys_of(k_refs, c), q_cols[h], NN)
                if c == count:
                    s = jnp.where(causal, s, MASKED)
                    top = fold(s, jnp.max)
                else:
                    top = fold(s, jnp.max) + kind_ref[qb, c]
                s_ref[h, cut(c)] = s
                peak = jnp.maximum(peak, top)
            peaks[h] = jnp.max(peak, axis=0, keepdims=True)

        def weigh(h):
            total = jnp.zeros((8, QB), f32)
            for c in range(count + 1):
                bias = -peaks[h] if c == count else kind_ref[qb, c] - peaks[h]
                e = jnp.exp2(s_ref[h, cut(c)] + bias)
                total = total + fold(e, jnp.sum)
                p_ref[h, cut(c)] = e.astype(bf16)
            norms[h] = 1.0 / jnp.sum(total, axis=0, keepdims=True)

        def attend(h):
            lines = slice(h * HD, (h + 1) * HD)
            out = mm(vt_ref[lines, 0:wide], p_ref[h, 0:wide], NN) + mm(vt_ref[lines, slot], p_ref[h, wide:], NN)
            outs[h] = out * norms[h]
            deltas[h] = jnp.sum(outs[h] * do_t[lines], axis=0, keepdims=True) * norms[h]
            scaled[h] = do_t[lines] * norms[h]

        scores(0)
        scores(1)
        weigh(0)
        attend(0)
        weigh(1)
        attend(1)
        d_t = jnp.concatenate(scaled, axis=0).astype(bf16)
        d_cols = jnp.where(upper, d_t, zero), jnp.where(upper, zero, d_t)
        do_heads = by_head(mm(ident, d_t, NT).astype(bf16))
        grads = []
        for h in range(2):
            lines = slice(h * HD, (h + 1) * HD)
            for c in range(count + 1):
                dp = mm(keys_of(v_refs, c), d_cols[h], NN)
                ds_ref[h, cut(c)] = p_ref[h, cut(c)] * (dp - deltas[h]).astype(bf16)
            dq = mm(kt_ref[lines, 0:wide], ds_ref[h, 0:wide], NN) + mm(kt_ref[lines, slot], ds_ref[h, wide:], NN)
            a, b = dq[:ROT // 2], dq[ROT // 2:ROT]
            cosine, sine = cos_ref[:, own], sin_ref[:, own]
            grads.append(jnp.concatenate([a * cosine + b * sine, b * cosine - a * sine, dq[ROT:]], axis=0))
        for c in range(count + 1):
            at = slot if c == count else cut(c)
            dv = mm(p_ref[0, cut(c)], do_heads[0], NN) + mm(p_ref[1, cut(c)], do_heads[1], NN)
            dk = mm(ds_ref[0, cut(c)], q_heads[0], NN) + mm(ds_ref[1, cut(c)], q_heads[1], NN)
            if c == count:
                dva_ref[at, :] += dv
                dka_ref[at, :] += dk
            else:
                dva_ref[at, :] = jnp.where(qb == 0, dv, dva_ref[at, :] + dv)
                dka_ref[at, :] = jnp.where(qb == 0, dk, dka_ref[at, :] + dk)
        o_ref[own, :] = mm(ident, jnp.concatenate(outs, axis=0).astype(bf16), NT).astype(bf16)
        dq_ref[own, :] = mm(ident, (jnp.concatenate(grads, axis=0) * (HD ** (-0.5))).astype(bf16), NT).astype(bf16)

        return carry

    lax.fori_loop(0, 2 * per, block, 0)

    def flush(out, to, frm):
        rows = pl.ds(to, half)
        out[rows, :PAIR] = (dka_ref[frm:frm + half, :] * math.log(2.0)).astype(bf16)
        out[rows, PAIR:] = dva_ref[frm:frm + half, :].astype(bf16)

    flush(cont_ref, 0, wide)
    for s in range(n):
        flush(all_ref, pl.multiple_of(owner_ref[s] * half, half), s * half)


def attention(kind, owners, cos_t, sin_t, q, do, ks, vs, first, pairs):
    rows = q.shape[0]
    half = rows // 2
    n = 1 + ks[1].shape[0] // half
    wide = n * half
    keys = wide + half
    total = wide + QB
    qspec = pl.BlockSpec((rows, PAIR), lambda p: (0, p + first))
    ospec = pl.BlockSpec((rows, PAIR), lambda p: (0, p))
    table = pl.BlockSpec((ROT // 2, rows), lambda p: (0, 0))
    kspecs = [pl.BlockSpec((k.shape[0], PAIR), lambda p: (0, p + first)) for k in ks]
    gspecs = [pl.BlockSpec((size, 2 * PAIR), lambda p: (0, p)) for size in (wide, half)]
    s = jax.ShapeDtypeStruct
    pieces = pairs * rows // QB
    return pl.pallas_call(
        partial(attention_kernel, half, n),
        grid=(pairs,),
        in_specs=[pl.BlockSpec(memory_space=pltpu.SMEM), pl.BlockSpec(memory_space=pltpu.SMEM), table, table, qspec, qspec] + kspecs + kspecs,
        out_specs=[ospec, ospec] + gspecs,
        out_shape=[s((rows, pairs * PAIR), bf16), s((rows, pairs * PAIR), bf16)]
        + [s((size, 2 * pairs * PAIR), bf16) for size in (wide, half)],
        scratch_shapes=[pltpu.VMEM((PAIR, keys), bf16), pltpu.VMEM((PAIR, keys), bf16),
                        pltpu.VMEM((2, total, QB), f32), pltpu.VMEM((2, total, QB), bf16),
                        pltpu.VMEM((2, total, QB), bf16),
                        pltpu.VMEM((keys, PAIR), f32), pltpu.VMEM((keys, PAIR), f32)],
        compiler_params=pltpu.CompilerParams(vmem_limit_bytes=60 << 20),
        cost_estimate=pl.CostEstimate(flops=1 << 20, bytes_accessed=1 << 16, transcendentals=0),
        name="attention",
    )(kind, owners, cos_t, sin_t, q, do, *ks, *vs)


def pairs_of(bit, size):
    return [(a, a ^ bit) for a in range(size)]


def add_kernel(plan, *refs):
    for a, b, moves in plan:
        for source, to, target in moves:
            refs[to][target] = (refs[a][source].astype(f32) + refs[b][source].astype(f32)).astype(bf16)


def add_parts(arrays, plan, shapes, steps, load=0):
    def spec(shape):
        block = (*shape[:-1], shape[-1] // steps)
        return pl.BlockSpec(block, lambda j: (0,) * (len(shape) - 1) + (j,))

    return pl.pallas_call(
        partial(add_kernel, plan),
        grid=(steps,),
        in_specs=[spec(a.shape) for a in arrays],
        out_specs=[spec(shape) for shape in shapes],
        out_shape=[jax.ShapeDtypeStruct(shape, bf16) for shape in shapes],
        compiler_params=params(),
        cost_estimate=pl.CostEstimate(flops=(load << 30) + 1, bytes_accessed=1 << 16, transcendentals=0),
        name="add_parts",
    )(*arrays)


EVERY = slice(None)


def swap(a, bit):
    return lax.ppermute(a, "fsdp", pairs_of(bit, 8))


def steps_for(arrays):
    smallest = min(a.shape[-1] for a in arrays)
    return 4 if smallest % (4 * PAIR) == 0 else 1


def core_step(sends, keeps):
    count = len(sends)
    arrays, plan, shapes = [], [], []
    for send, keep in zip(sends, keeps):
        rows, cols = send.shape
        cut = (2, 2, 2, rows // 8, cols)
        to = 2 * count + len(shapes)
        moves = [((EVERY, 1, 0), to, (EVERY,)), ((EVERY, 0, 0), to + 1, (EVERY,)),
                 ((1, EVERY, 1), to + 2, (EVERY,)), ((0, EVERY, 1), to + 3, (EVERY,))]
        plan.append((len(arrays), len(arrays) + 1, moves))
        arrays += [keep.reshape(cut), swap(send, 1).reshape(cut)]
        shapes += [(2, rows // 8, cols)] * 4
    return add_parts(arrays, plan, shapes, steps_for(arrays))


def side_step(items):
    arrays, plan, shapes = [], [], []
    for i in range(0, len(items), 4):
        for send, keep, bit in ((items[i], items[i + 1], 2), (items[i + 2], items[i + 3], 4)):
            to = len(items) + len(shapes)
            plan.append((len(arrays), len(arrays) + 1, [((1,), to, (EVERY,)), ((0,), to + 1, (EVERY,))]))
            arrays += [keep, swap(send, bit)]
            shapes += [keep.shape[1:]] * 2
    return add_parts(arrays, plan, shapes, steps_for(arrays))


def last_step(items, load=0):
    arrays, plan, shapes = [], [], []
    for i in range(0, len(items), 4):
        to = len(items) + len(shapes)
        for at, (send, keep, bit) in enumerate(((items[i], items[i + 1], 4), (items[i + 2], items[i + 3], 2))):
            plan.append((len(arrays), len(arrays) + 1, [((EVERY,), to, (at,))]))
            arrays += [keep, swap(send, bit)]
        shapes.append((2, *keep.shape))
    parts = add_parts(arrays, plan, shapes, steps_for(arrays), load)
    return [part.reshape(-1, part.shape[-1]) for part in parts]


def along(part):
    return lax.psum_scatter(part, "ctx", scatter_dimension=0, tiled=True)


def after(value, *others):
    return lax.optimization_barrier((value, *others))[0]


def kept_after(items, *others):
    return [after(a, *others) if i % 2 else a for i, a in enumerate(items)]


def fast(inputs, cotangent, positions, segments, ln1_gain, ln1_bias, w_qkv, b_qkv, w_attn_out, b_out,
         ln2_gain, ln2_bias, w_in, b_in, w_out):
    x, grad_out, pos = inputs[0], cotangent[0], positions[0]
    rows, width = x.shape
    half = rows // 2
    n = lax.axis_size("ctx")
    ring = [(i, (i + 1) % n) for i in range(n)]
    back = [(i, (i - 1) % n) for i in range(n)]
    me, place = lax.axis_index("fsdp"), lax.axis_index("ctx")
    relative = [4 * dy + 2 * dx + 1 - keep for keep in (0, 1) for dy in (0, 1) for dx in (0, 1)]
    order = jnp.bitwise_xor(me, jnp.array(relative, jnp.int32))
    owners = lax.rem(place + n - jnp.arange(n), n)
    far = [None] * n
    far[0] = x[:half]
    for s in range(1, n):
        far[s] = lax.ppermute(far[s - 1], "ctx", ring)
    spots = [pos[::RB] // RB]
    for s in range(1, n):
        spots.append(lax.ppermute(spots[0][:half // RB], "ctx", [(i, (i + s) % n) for i in range(n)]))
    mine = (ln1_gain, ln1_bias, b_qkv, b_out, ln2_gain, ln2_bias, b_in)
    small = lax.all_gather(jnp.concatenate(mine).reshape(1, -1), "fsdp", axis=0, tiled=True)
    full, at = [], 0
    for a in mine:
        full.append(small[:, at:at + a.shape[0]].reshape(-1).astype(f32))
        at += a.shape[0]
    gain_attn, shift_attn, bias_qkv, bias_out, gain_mlp, shift_mlp, bias_in = full
    weights = lax.all_gather(jnp.concatenate([w_qkv, w_attn_out], axis=1), "fsdp", axis=0, tiled=True)

    lane = jnp.arange(PAIR) % HD
    inverse = jnp.exp(-math.log(10000.0) * (2.0 / ROT) * (lane % (ROT // 2)).astype(f32))
    angles = jnp.arange(n * half + CLEN).astype(f32)[:, None] * inverse[None, :]
    sine = jnp.sin(angles)
    tables = (jnp.where(lane < ROT, jnp.cos(angles), 1.0), jnp.where(lane < ROT // 2, sine, 0.0),
              jnp.where((lane >= ROT // 2) & (lane < ROT), sine, 0.0))
    angles_t = pos.astype(f32)[None, :] * inverse[:ROT // 2, None]
    cos_t, sin_t = jnp.cos(angles_t), jnp.sin(angles_t)

    normed, queries, own_keys, own_values = qkv(
        spots[0], order, [after(x, far[n - 2], *spots[1:])], gain_attn, shift_attn, weights, bias_qkv, tables)
    far_keys, far_values = qkv(
        jnp.concatenate(spots[1:]), order, far[1:], gain_attn, shift_attn, weights, bias_qkv, tables)
    keys, values = (own_keys, far_keys), (own_values, far_values)
    grad_att = spread(grad_out, weights)
    weight_in = lax.all_gather(after(w_in, far[1], *full, *tables, cos_t, sin_t), "fsdp", axis=0, tiled=True)
    weight_out = lax.all_gather(after(w_out, far[1], *full, *tables, cos_t, sin_t), "fsdp", axis=0, tiled=True)

    per = half // QB
    earlier = jnp.stack([spots[s][0] < spots[0][0] for s in range(1, n)])
    local_row = jnp.arange(2 * per)[:, None]
    seen_own = local_row > jnp.arange(per)[None, :]
    seen_far = jnp.repeat(earlier[None, :] | (local_row >= per), per, axis=1)
    kind = jnp.where(jnp.concatenate([seen_own, seen_far], axis=1), 0.0, MASKED).astype(f32)

    attended, grad_q, own_kv, come_kv = [], [], [], []

    def attend(first, count, wait):
        out = attention(kind, owners, cos_t, sin_t, after(queries, *wait), grad_att, keys, values, first, count)
        attended.append(out[0])
        grad_q.append(out[1])
        come_kv.append(lax.psum_scatter(out[2], "ctx", scatter_dimension=0, tiled=True))
        own_kv.append(out[3])

    attend(0, 4, ())
    mlp_out, grad_mlp, in_send, in_keep, out_send, out_keep, db_in, db_out, dgain_mlp, dshift_mlp = mlp(
        order, after(x, *attended), grad_out, gain_mlp, shift_mlp, weight_in, bias_in, weight_out)
    attend(4, 2, (mlp_out,))
    steps_mlp = core_step([out_send, in_send], [out_keep, in_keep])
    attend(6, 2, (*attended, *steps_mlp))
    steps_mlp = side_step(kept_after(steps_mlp, *attended))
    output = join(after(x, *steps_mlp), attended, weights, mlp_out, bias_out)
    first_send, first_keep, grad_heads, db_first = first_tail(
        spots[0], order, after(grad_out, output), normed, weights, tables, attended, grad_q, own_kv[0], come_kv[0])
    part_out, part_in = last_step(kept_after(steps_mlp, grad_heads), 48)
    steps_first = core_step([first_send], [first_keep])
    grad_inputs, last_send, last_keep, db_last, dgain_attn, dshift_attn = last_tail(
        spots[0], after(x, part_out, part_in, *steps_first), normed, gain_attn, weights, tables, grad_mlp, grad_heads,
        own_kv[1:], come_kv[1:])
    sum_out, sum_in = along(part_out), along(part_in)
    steps_first = side_step(kept_after(steps_first, last_send))
    cols = db_last.shape[1] // 2
    split = [width, width + (db_first.shape[1] - width) // 2]
    db_q, db_k, db_v = jnp.split(db_first, split, axis=1)
    db_qkv = jnp.concatenate([db_q, db_k, db_last[:, :cols], db_v, db_last[:, cols:]], axis=1)
    parts = 8 * n
    smalls = [a.reshape(parts, -1) for a in (dgain_attn, dshift_attn, db_qkv, db_out, dgain_mlp, dshift_mlp, db_in)]
    flat = jnp.concatenate(smalls, axis=1).astype(bf16).reshape(parts, -1, PAIR)
    lines = flat.shape[1]
    packed = jnp.pad(flat, ((0, 0), (0, width // parts - lines), (0, 0))).reshape(width, PAIR)
    packed = packed.reshape(8, width // 8, PAIR)[order].reshape(2, width // 2, PAIR)
    steps_last = core_step([last_send, packed[0]], [after(last_keep, *steps_first), packed[1]])
    part_first = last_step(steps_first)
    part_last = last_step(side_step(kept_after(steps_last, *part_first)))
    total = along(jnp.concatenate([*part_first, *part_last], axis=1))
    ends = [width, 2 * width, split[1] + width, db_first.shape[1] + width]
    ends += [ends[-1] + cols, ends[-1] + 2 * cols]
    sum_attn, sum_q, sum_k, sum_v, end_k, end_v, packed = jnp.split(total, ends, axis=1)
    sum_qkv = jnp.concatenate([sum_q, sum_k, end_k, sum_v, end_v], axis=1)
    packed = packed[:lines].astype(f32).reshape(-1)
    done, at = [], 0
    for a in smalls:
        done.append(packed[at:at + a.shape[1]])
        at += a.shape[1]
    return (output[None], grad_inputs[None], done[0], done[1], sum_qkv.astype(f32), done[2], sum_attn.astype(f32),
            done[3], done[4], done[5], sum_in.astype(f32), done[6], sum_out.astype(f32))


def local(*args):
    half = args[0].shape[1] // 2
    if args[0].shape[0] == 1 and half % CLEN == 0 and lax.axis_size("fsdp") == 8:
        return fast(*args)
    return generic(*args)


def generic(
    inputs,
    cotangent,
    positions,
    segments,
    ln1_gain,
    ln1_bias,
    w_qkv,
    b_qkv,
    w_attn_out,
    b_out,
    ln2_gain,
    ln2_bias,
    w_in,
    b_in,
    w_out,
):
    shards = (
        ln1_gain,
        ln1_bias,
        w_qkv,
        b_qkv,
        w_attn_out,
        b_out,
        ln2_gain,
        ln2_bias,
        w_in,
        b_in,
        w_out,
    )
    params = (
        lax.all_gather(shards[0], "fsdp", axis=0, tiled=True),
        lax.all_gather(shards[1], "fsdp", axis=0, tiled=True),
        lax.all_gather(shards[2], "fsdp", axis=0, tiled=True),
        lax.all_gather(shards[3], "fsdp", axis=0, tiled=True),
        lax.all_gather(shards[4], "fsdp", axis=0, tiled=True),
        lax.all_gather(shards[5], "fsdp", axis=0, tiled=True),
        lax.all_gather(shards[6], "fsdp", axis=0, tiled=True),
        lax.all_gather(shards[7], "fsdp", axis=0, tiled=True),
        lax.all_gather(shards[8], "fsdp", axis=0, tiled=True),
        lax.all_gather(shards[9], "fsdp", axis=0, tiled=True),
        lax.all_gather(shards[10], "fsdp", axis=0, tiled=True),
    )
    groups, local_len, width = inputs.shape
    rows_total = groups * local_len
    block = math.gcd(local_len, 256)
    label_pos, label_seg = (
        lax.all_gather(positions, "ctx", axis=1, tiled=True),
        lax.all_gather(segments, "ctx", axis=1, tiled=True),
    )
    count = label_pos.shape[1] // block
    f32 = jnp.float32
    bf16 = jnp.bfloat16
    (
        gain_attn,
        shift_attn,
        weight_qkv,
        bias_qkv,
        weight_attn,
        bias_out,
        gain_mlp,
        shift_mlp,
        weight_in,
        bias_in,
        weight_out,
    ) = params
    flat_in = inputs.reshape(rows_total, width).astype(f32)
    normed_attn = layer_norm(flat_in, gain_attn.astype(f32), shift_attn.astype(f32)).astype(bf16)
    normed_mlp = layer_norm(flat_in, gain_mlp.astype(f32), shift_mlp.astype(f32)).astype(bf16)
    projected = jnp.dot(normed_attn, weight_qkv, preferred_element_type=f32) + bias_qkv.astype(f32)
    cosine, sine = rotary_tables(positions)

    def split_heads(columns):
        return columns.reshape(groups, local_len, HEADS, HD)

    scale = HD ** (-0.5)
    queries = (rotate(split_heads(projected[:, :width]), cosine, sine) * scale).astype(bf16)
    keys_own = rotate(split_heads(projected[:, width : 2 * width]), cosine, sine).astype(bf16)
    values_own = split_heads(projected[:, 2 * width :]).astype(bf16)
    keys_all, values_all = (
        lax.all_gather(keys_own, "ctx", axis=1, tiled=True),
        lax.all_gather(values_own, "ctx", axis=1, tiled=True),
    )

    def key_block(index):
        start = index * block
        keys_blk = lax.dynamic_slice_in_dim(keys_all, start, block, 1)
        values_blk = lax.dynamic_slice_in_dim(values_all, start, block, 1)
        mask = allowed_mask(
            positions,
            segments,
            lax.dynamic_slice_in_dim(label_pos, start, block, 1),
            lax.dynamic_slice_in_dim(label_seg, start, block, 1),
        )
        return (keys_blk, values_blk, mask)

    def total_step(carry, index):
        peak, total = carry
        keys_blk, values_blk, mask = key_block(index)
        scores = jnp.where(mask, scores_of(queries, keys_blk), MASKED)
        fresh = jnp.maximum(peak, jnp.max(scores, axis=-1))
        added = jnp.sum(jnp.where(mask, jnp.exp(scores - fresh[..., None]), 0.0), axis=-1)
        return ((fresh, total * jnp.exp(peak - fresh) + added), None)

    stat_shape = (groups, HEADS, local_len)
    (peak, total), unused = lax.scan(
        total_step,
        (jnp.full(stat_shape, MASKED, f32), jnp.zeros(stat_shape, f32)),
        jnp.arange(count),
    )
    log_total = peak + jnp.log(total)

    def attend_step(rounded_sum, index):
        keys_blk, values_blk, mask = key_block(index)
        probs = jnp.where(mask, jnp.exp(scores_of(queries, keys_blk) - log_total[..., None]), 0.0)
        rounded_sum = rounded_sum + jnp.einsum(
            "ghqk,gkhd->gqhd", probs.astype(bf16), values_blk, preferred_element_type=f32
        )
        return (rounded_sum, None)

    head_shape = (groups, local_len, HEADS, HD)
    rounded_sum, unused = lax.scan(attend_step, jnp.zeros(head_shape, f32), jnp.arange(count))
    attended = rounded_sum.reshape(rows_total, width).astype(bf16)
    pre_act = jnp.dot(normed_mlp, weight_in, preferred_element_type=f32) + bias_in.astype(f32)
    activated = jax.nn.gelu(pre_act, approximate=False).astype(bf16)
    output = (
        flat_in
        + jnp.dot(attended, weight_attn, preferred_element_type=f32)
        + jnp.dot(activated, weight_out, preferred_element_type=f32)
        + bias_out.astype(f32)
    )
    (
        gain_attn,
        shift_attn,
        weight_qkv,
        bias_qkv,
        weight_attn,
        bias_out,
        gain_mlp,
        shift_mlp,
        weight_in,
        bias_in,
        weight_out,
    ) = params
    grad_out = cotangent.reshape(rows_total, width)
    grad_bias_out = jnp.sum(grad_out.astype(f32), axis=0)
    grad_weight_out = jnp.einsum("rf,rd->fd", activated, grad_out, preferred_element_type=f32)
    grad_act = jnp.einsum("rd,fd->rf", grad_out, weight_out, preferred_element_type=f32)
    unused, gelu_back = jax.vjp(partial(jax.nn.gelu, approximate=False), pre_act)
    grad_pre = gelu_back(grad_act)[0].astype(bf16)
    grad_weight_in = jnp.einsum("rd,rf->df", normed_mlp, grad_pre, preferred_element_type=f32)
    grad_bias_in = jnp.sum(grad_pre.astype(f32), axis=0)
    grad_normed_mlp = jnp.einsum("rf,df->rd", grad_pre, weight_in, preferred_element_type=f32)
    grad_weight_attn = jnp.einsum("ra,rd->ad", attended, grad_out, preferred_element_type=f32)
    grad_att = (
        jnp.einsum("rd,ad->ra", grad_out, weight_attn, preferred_element_type=f32)
        .astype(bf16)
        .reshape(head_shape)
    )
    delta = jnp.einsum(
        "gqhd,gqhd->ghq", grad_att.astype(f32), rounded_sum, precision=lax.Precision.HIGHEST
    )

    def back_step(carry, index):
        keys_blk, values_blk, mask = key_block(index)
        rounded, grad_scores = block_grads(
            queries, grad_att, log_total, delta, mask, keys_blk, values_blk
        )
        carry = carry + jnp.einsum(
            "ghqk,gkhd->gqhd", grad_scores, keys_blk, preferred_element_type=f32
        )
        key_term = jnp.einsum("ghqk,gqhd->gkhd", grad_scores, queries, preferred_element_type=f32)
        value_term = jnp.einsum("ghqk,gqhd->gkhd", rounded, grad_att, preferred_element_type=f32)
        return (carry, (key_term, value_term))

    grad_queries, (key_terms, value_terms) = lax.scan(
        back_step, jnp.zeros(head_shape, f32), jnp.arange(count)
    )
    key_sums, value_sums = (
        lax.psum_scatter(
            key_terms.astype(jnp.bfloat16), "ctx", scatter_dimension=0, tiled=True
        ).astype(jnp.float32),
        lax.psum_scatter(
            value_terms.astype(jnp.bfloat16), "ctx", scatter_dimension=0, tiled=True
        ).astype(jnp.float32),
    )
    grad_keys = jnp.transpose(key_sums, (1, 0, 2, 3, 4)).reshape(head_shape)
    grad_values = jnp.transpose(value_sums, (1, 0, 2, 3, 4)).reshape(head_shape)
    grad_q_pre = unrotate(grad_queries * scale, cosine, sine).reshape(rows_total, width)
    grad_k_pre = unrotate(grad_keys, cosine, sine).reshape(rows_total, width)
    grad_projected = jnp.concatenate(
        [grad_q_pre, grad_k_pre, grad_values.reshape(rows_total, width)], axis=1
    ).astype(bf16)
    grad_weight_qkv = jnp.einsum(
        "rd,re->de", normed_attn, grad_projected, preferred_element_type=f32
    )
    grad_bias_qkv = jnp.sum(grad_projected.astype(f32), axis=0)
    grad_normed_attn = jnp.einsum(
        "re,de->rd", grad_projected, weight_qkv, preferred_element_type=f32
    )
    unused, norm_back_attn = jax.vjp(
        layer_norm, flat_in, gain_attn.astype(f32), shift_attn.astype(f32)
    )
    grad_in_attn, grad_gain_attn, grad_shift_attn = norm_back_attn(grad_normed_attn)
    unused, norm_back_mlp = jax.vjp(
        layer_norm, flat_in, gain_mlp.astype(f32), shift_mlp.astype(f32)
    )
    grad_in_mlp, grad_gain_mlp, grad_shift_mlp = norm_back_mlp(grad_normed_mlp)
    grad_inputs = (grad_out.astype(f32) + grad_in_attn + grad_in_mlp).reshape(
        groups, local_len, width
    )
    sums = (
        lax.psum_scatter(grad_gain_attn, ("fsdp", "ctx"), scatter_dimension=0, tiled=True),
        lax.psum_scatter(grad_shift_attn, ("fsdp", "ctx"), scatter_dimension=0, tiled=True),
        lax.psum_scatter(grad_weight_qkv, ("fsdp", "ctx"), scatter_dimension=0, tiled=True),
        lax.psum_scatter(grad_bias_qkv, ("fsdp", "ctx"), scatter_dimension=0, tiled=True),
        lax.psum_scatter(grad_weight_attn, ("fsdp", "ctx"), scatter_dimension=0, tiled=True),
        lax.psum_scatter(grad_bias_out, ("fsdp", "ctx"), scatter_dimension=0, tiled=True),
        lax.psum_scatter(grad_gain_mlp, ("fsdp", "ctx"), scatter_dimension=0, tiled=True),
        lax.psum_scatter(grad_shift_mlp, ("fsdp", "ctx"), scatter_dimension=0, tiled=True),
        lax.psum_scatter(grad_weight_in, ("fsdp", "ctx"), scatter_dimension=0, tiled=True),
        lax.psum_scatter(grad_bias_in, ("fsdp", "ctx"), scatter_dimension=0, tiled=True),
        lax.psum_scatter(grad_weight_out, ("fsdp", "ctx"), scatter_dimension=0, tiled=True),
    )
    result = output.reshape(groups, local_len, width).astype(bf16)
    return (
        result,
        grad_inputs,
        sums[0],
        sums[1],
        sums[2],
        sums[3],
        sums[4],
        sums[5],
        sums[6],
        sums[7],
        sums[8],
        sums[9],
        sums[10],
    )


def solution(mesh):
    in_specs = (
        P("fsdp", "ctx", None),
        P("fsdp", "ctx", None),
        P("fsdp", "ctx"),
        P("fsdp", "ctx"),
        P("fsdp"),
        P("fsdp"),
        P("fsdp", None),
        P("fsdp"),
        P("fsdp", None),
        P("fsdp"),
        P("fsdp"),
        P("fsdp"),
        P("fsdp", None),
        P("fsdp"),
        P("fsdp", None),
    )
    out_specs = (
        P("fsdp", "ctx", None),
        P("fsdp", "ctx", None),
        P(("fsdp", "ctx")),
        P(("fsdp", "ctx")),
        P(("fsdp", "ctx"), None),
        P(("fsdp", "ctx")),
        P(("fsdp", "ctx"), None),
        P(("fsdp", "ctx")),
        P(("fsdp", "ctx")),
        P(("fsdp", "ctx")),
        P(("fsdp", "ctx"), None),
        P(("fsdp", "ctx")),
        P(("fsdp", "ctx"), None),
    )
    return jax.shard_map(local, mesh=mesh, in_specs=in_specs, out_specs=out_specs, check_vma=False)
```

```python
from functools import partial
import math

import jax
import jax.numpy as jnp
from jax import lax
from jax.experimental import pallas as pl
from jax.experimental.pallas import tpu as pltpu
from jax.sharding import PartitionSpec as P

HEADS = 16
HD = 64
ROT = 16
CLEN = 256
QB = 256
RB = 256
PAIR = 2 * HD
bf16 = jnp.bfloat16
f32 = jnp.float32
NN = (((1,), (0,)), ((), ()))
NT = (((1,), (1,)), ((), ()))
TN = (((0,), (0,)), ((), ()))


NORM_EPS = 1e-05
MASKED = -1e30


def layer_norm(values, scaling, offset):
    average = jnp.mean(values, axis=-1, keepdims=True)
    centered = values - average
    variance = jnp.mean(centered * centered, axis=-1, keepdims=True)
    return centered * lax.rsqrt(variance + NORM_EPS) * scaling + offset


def rotary_tables(positions):
    halfway = ROT // 2
    spacing = jnp.arange(halfway, dtype=jnp.float32) * (2.0 / ROT)
    inverse = jnp.exp(-math.log(10000.0) * spacing)
    angles = positions.astype(jnp.float32)[..., None] * inverse
    return (jnp.cos(angles), jnp.sin(angles))


def rotate(heads_in, cosine, sine):
    halfway = ROT // 2
    cosine = cosine[..., None, :]
    sine = sine[..., None, :]
    first = heads_in[..., :halfway]
    second = heads_in[..., halfway:ROT]
    return jnp.concatenate(
        [first * cosine - second * sine, second * cosine + first * sine, heads_in[..., ROT:]],
        axis=-1,
    )


def unrotate(grads_in, cosine, sine):
    halfway = ROT // 2
    cosine = cosine[..., None, :]
    sine = sine[..., None, :]
    first = grads_in[..., :halfway]
    second = grads_in[..., halfway:ROT]
    return jnp.concatenate(
        [first * cosine + second * sine, second * cosine - first * sine, grads_in[..., ROT:]],
        axis=-1,
    )


def allowed_mask(query_pos, query_seg, key_pos, key_seg):
    same_doc = (key_seg[:, None, :] == 0) | (key_seg[:, None, :] == query_seg[:, :, None])
    causal = key_pos[:, None, :] <= query_pos[:, :, None]
    return (same_doc & causal)[:, None]


def scores_of(queries, keys_blk):
    return jnp.einsum("gqhd,gkhd->ghqk", queries, keys_blk, preferred_element_type=jnp.float32)


def block_grads(queries, grad_att, log_total, delta, mask, keys_blk, values_blk):
    probs = jnp.where(mask, jnp.exp(scores_of(queries, keys_blk) - log_total[..., None]), 0.0)
    dprobs = jnp.einsum("gqhd,gkhd->ghqk", grad_att, values_blk, preferred_element_type=jnp.float32)
    grad_scores = (probs * (dprobs - delta[..., None])).astype(jnp.bfloat16)
    return (probs.astype(jnp.bfloat16), grad_scores)


def mm(a, b, dims):
    return lax.dot_general(a, b, dims, preferred_element_type=f32)


def row_stats(x):
    average = jnp.mean(x, axis=1, keepdims=True)
    centered = x - average
    return centered, lax.rsqrt(jnp.mean(centered * centered, axis=1, keepdims=True) + NORM_EPS)


def norm_rows(x, scaling, offset):
    centered, inverse = row_stats(x)
    return (centered * inverse * scaling + offset).astype(bf16)


def norm_back(x, grad, scaling):
    centered, inverse = row_stats(x)
    unit = centered * inverse
    e = grad * scaling
    inner = e - jnp.mean(e, axis=1, keepdims=True) - unit * jnp.mean(e * unit, axis=1, keepdims=True)
    return inverse * inner, grad * unit


def col_sum(a):
    return jnp.sum(a, axis=0, keepdims=True)


def vmem(*shape, dtype=f32):
    return pltpu.VMEM(shape, dtype)


def params():
    return pltpu.CompilerParams(vmem_limit_bytes=60 << 20)


ROOT = math.sqrt(0.5)
DENS = 1.0 / math.sqrt(2.0 * math.pi)


def reorder(order_ref, source, target):
    size = source.shape[1] // order_ref.shape[0]
    for i in range(order_ref.shape[0]):
        at = pl.multiple_of(order_ref[i] * size, size)
        target[:, i * size:(i + 1) * size] = source[:, pl.ds(at, size)]


def mlp_kernel(order_ref, x_ref, c_ref, gain_ref, shift_ref, win_ref, bin_ref, wout_ref,
               out_ref, gin_ref, dwin_send, dwin_keep, dwout_send, dwout_keep, dbin_ref, dbout_ref, dgain_ref, dshift_ref,
               h_ref, turned_ref, act_ref, gp_ref, gh_ref):
    step = pl.program_id(0)
    rows = x_ref.shape[0]
    blocks = [slice(r, r + RB) for r in range(0, rows, RB)]

    @pl.when(step == 0)
    def _():
        for r in blocks:
            h_ref[r, :] = norm_rows(x_ref[r, :].astype(f32), gain_ref[...], shift_ref[...])
            out_ref[r, :] = jnp.zeros((RB, out_ref.shape[1]), f32)
            gh_ref[r, :] = jnp.zeros((RB, gh_ref.shape[1]), f32)
        reorder(order_ref, h_ref, turned_ref)

    dbin = jnp.zeros(dbin_ref.shape, f32)
    for r in blocks:
        pre = mm(h_ref[r, :], win_ref[...], NN) + bin_ref[...]
        phi = 0.5 + 0.5 * lax.erf(pre * ROOT)
        act_ref[r, :] = (pre * phi).astype(bf16)
        gp = phi + pre * (DENS * jnp.exp(-0.5 * (pre * pre)))
        gact = mm(c_ref[r, :], wout_ref[...], NT)
        gpre = (gact * gp).astype(bf16)
        gp_ref[r, :] = gpre
        dbin = dbin + col_sum(gpre.astype(f32))
    for r in blocks:
        out_ref[r, :] += mm(act_ref[r, :], wout_ref[...], NN)
        gh_ref[r, :] += mm(gp_ref[r, :], win_ref[...], NT)
    dwout = mm(act_ref[...], c_ref[...], TN).astype(bf16)
    middle = pl.num_programs(0) // 2

    @pl.when(step < middle)
    def _():
        dwout_send[...] = dwout

    @pl.when(step >= middle)
    def _():
        dwout_keep[...] = dwout

    dwin = mm(turned_ref[...], gp_ref[...], TN).astype(bf16)
    dwin_send[...] = dwin[:dwin_send.shape[0]]
    dwin_keep[...] = dwin[dwin_send.shape[0]:]
    dbin_ref[...] = dbin

    @pl.when(step == pl.num_programs(0) - 1)
    def _():
        dgain = jnp.zeros(dgain_ref.shape, f32)
        dshift = jnp.zeros(dshift_ref.shape, f32)
        dbout = jnp.zeros(dbout_ref.shape, f32)
        for r in blocks:
            grad = gh_ref[r, :]
            back, scaled = norm_back(x_ref[r, :].astype(f32), grad, gain_ref[...])
            c = c_ref[r, :].astype(f32)
            gin_ref[r, :] = back + c
            dgain += col_sum(scaled)
            dshift += col_sum(grad)
            dbout += col_sum(c)
        dgain_ref[...] = dgain
        dshift_ref[...] = dshift
        dbout_ref[...] = dbout


def mlp(order, x, c, gain, shift, weight_in, bias_in, weight_out):
    rows, width = x.shape
    ff = weight_in.shape[1]
    steps = order.shape[0]
    fc = ff // steps
    whole = pl.BlockSpec((rows, width), lambda j, o: (0, 0))
    line = pl.BlockSpec((1, width), lambda j, o: (0, 0))
    down = pl.BlockSpec((width // 2, fc), lambda j, o: (0, o[j]))
    s = jax.ShapeDtypeStruct
    return pl.pallas_call(
        mlp_kernel,
        grid_spec=pltpu.PrefetchScalarGridSpec(
            num_scalar_prefetch=1,
            grid=(steps,),
            in_specs=[whole, whole, line, line, pl.BlockSpec((width, fc), lambda j, o: (0, o[j])),
                      pl.BlockSpec((1, fc), lambda j, o: (0, o[j])), pl.BlockSpec((fc, width), lambda j, o: (o[j], 0))],
            out_specs=[whole, whole, down, down,
                       pl.BlockSpec((fc, width), lambda j, o: (jnp.minimum(j, steps // 2 - 1), 0)),
                       pl.BlockSpec((fc, width), lambda j, o: (jnp.maximum(j - steps // 2, 0), 0)),
                       pl.BlockSpec((1, fc), lambda j, o: (0, o[j])), line, line, line],
            scratch_shapes=[vmem(rows, width, dtype=bf16), vmem(rows, width, dtype=bf16), vmem(rows, fc, dtype=bf16),
                            vmem(rows, fc, dtype=bf16), vmem(rows, width)],
        ),
        out_shape=[s((rows, width), f32), s((rows, width), f32), s((width // 2, ff), bf16), s((width // 2, ff), bf16),
                   s((ff // 2, width), bf16), s((ff // 2, width), bf16), s((1, ff), f32), s((1, width), f32),
                   s((1, width), f32), s((1, width), f32)],
        compiler_params=params(),
        cost_estimate=pl.CostEstimate(flops=1 << 20, bytes_accessed=1 << 16, transcendentals=0),
        name="mlp",
    )(order, x, c, gain.reshape(1, -1), shift.reshape(1, -1), weight_in, bias_in.reshape(1, -1), weight_out)


def turn_lanes(u, cosine, low, high, sign):
    half = ROT // 2
    parts = []
    for at in range(0, u.shape[1], PAIR):
        g = u[:, at:at + PAIR]
        parts.append(g * cosine + sign * (pltpu.roll(g, half, 1) * high - pltpu.roll(g, PAIR - half, 1) * low))
    return jnp.concatenate(parts, axis=1)


def qkv_kernel(far, spot_ref, order_ref, gain_ref, shift_ref, w_ref, b_ref, cos_ref, low_ref, high_ref, *refs):
    with_q = far == 0
    if with_q:
        x_ref, outs = refs[0], refs[1:]
    else:
        x_refs, outs, x_ref = refs[:far], refs[far:-1], refs[-1]
        step = pl.program_id(0)
        per = pl.num_programs(0) // far
        for s in range(far):
            @pl.when(step // per == s)
            def _(s=s):
                x_ref[...] = x_refs[s][...]
    width = x_ref.shape[1]
    h = norm_rows(x_ref[...].astype(f32), gain_ref[...], shift_ref[...])
    tables = (cos_ref[...], low_ref[...], high_ref[...])
    if with_q:
        h_ref, q_ref, k_ref, v_ref, plain_ref = outs
        plain_ref[...] = h
        reorder(order_ref, plain_ref, h_ref)
        q = mm(h, w_ref[:, :width], NN) + b_ref[:, :width]
        q_ref[...] = (turn_lanes(q, *tables, 1.0) * (HD ** (-0.5) / math.log(2.0))).astype(bf16)
    else:
        k_ref, v_ref = outs
    k = mm(h, w_ref[:, width:2 * width], NN) + b_ref[:, width:2 * width]
    k_ref[...] = turn_lanes(k, *tables, 1.0).astype(bf16)
    v_ref[...] = (mm(h, w_ref[:, 2 * width:], NN) + b_ref[:, 2 * width:]).astype(bf16)


def qkv(spots, order, xs, gain, shift, weight, bias, tables):
    far = len(xs) if len(xs) > 1 else 0
    rows, width = xs[0].shape
    per = rows // RB
    total = len(xs) * rows
    s = jax.ShapeDtypeStruct((total, width), bf16)
    block = pl.BlockSpec((RB, width), lambda j, spot, o: (j, 0))
    line = pl.BlockSpec((1, width), lambda j, spot, o: (0, 0))
    table = pl.BlockSpec((RB, PAIR), lambda j, spot, o: (spot[j], 0))
    count = 2 if far else 4

    def window(i):
        return pl.BlockSpec((RB, width), lambda j, spot, o: (jnp.clip(j - i * per, 0, per - 1), 0))

    return pl.pallas_call(
        partial(qkv_kernel, far),
        grid_spec=pltpu.PrefetchScalarGridSpec(
            num_scalar_prefetch=2,
            grid=(total // RB,),
            in_specs=[line, line, pl.BlockSpec((width, 3 * width), lambda j, spot, o: (0, 0)),
                      pl.BlockSpec((1, 3 * width), lambda j, spot, o: (0, 0)), table, table, table]
            + [window(i) for i in range(len(xs))],
            out_specs=[block] * count,
            scratch_shapes=[vmem(RB, width, dtype=bf16)],
        ),
        out_shape=[s] * count,
        compiler_params=params(),
        cost_estimate=pl.CostEstimate(flops=1 << 20, bytes_accessed=1 << 16, transcendentals=0),
        name="kv_remote" if far else "qkv_own",
    )(spots, order, gain.reshape(1, -1), shift.reshape(1, -1), weight, bias.reshape(1, -1), *tables, *xs)


def gather_rows(step, spot, tables, own_refs, come_refs, p_ref, k_at, v_at):
    half = pl.num_programs(0) // 2
    columns = [(g, at) for g in range(len(own_refs)) for at in range(0, own_refs[g].shape[1], 2 * PAIR)]

    def put(refs):
        for to, (g, at) in enumerate(columns):
            turned = turn_lanes(refs[g][:, at:at + PAIR].astype(f32), *tables, -1.0).astype(bf16)
            p_ref[spot, k_at + to * PAIR:k_at + (to + 1) * PAIR] = turned
            p_ref[spot, v_at + to * PAIR:v_at + (to + 1) * PAIR] = refs[g][:, at + PAIR:at + 2 * PAIR]

    @pl.when(step < half)
    def _():
        put(come_refs)

    @pl.when(step >= half)
    def _():
        put(own_refs)


def half_windows(arrays, count):
    half = count // 2
    come = [pl.BlockSpec((RB, a.shape[1]), lambda j, *o: (jnp.clip(j, 0, half - 1), 0)) for a in arrays]
    own = [pl.BlockSpec((RB, a.shape[1]), lambda j, *o: (jnp.clip(j - half, 0, half - 1), 0)) for a in arrays]
    return own, come


def first_kernel(groups, spot_ref, order_ref, c_ref, h_ref, wq_ref, wk_ref, wv_ref, cos_ref, low_ref, high_ref, own_ref,
                 come_ref, *refs):
    att_refs, dq_refs = refs[:groups], refs[groups:2 * groups]
    send_ref, keep_ref, gh_ref, db_ref, p_ref, att_ref, turned_ref = refs[2 * groups:]
    step = pl.program_id(0)
    width = c_ref.shape[1]
    spot = pl.ds(pl.multiple_of(step * RB, RB), RB)
    at = 0
    for g in range(groups):
        size = att_refs[g].shape[1]
        att_ref[:, at:at + size] = att_refs[g][...]
        p_ref[spot, at:at + size] = dq_refs[g][...]
        at += size
    for i in range(order_ref.shape[0]):
        size = width // order_ref.shape[0]
        lanes = pl.ds(pl.multiple_of(order_ref[i] * size, size), size)
        turned_ref[spot, i * size:(i + 1) * size] = att_ref[:, lanes]
    count = wk_ref.shape[1]
    gather_rows(step, spot, (cos_ref[...], low_ref[...], high_ref[...]), [own_ref], [come_ref], p_ref, width, width + count)
    gh_ref[...] = (mm(p_ref[spot, :width], wq_ref[...], NT) + mm(p_ref[spot, width:width + count], wk_ref[...], NT)
                   + mm(p_ref[spot, width + count:], wv_ref[...], NT))
    db = col_sum(p_ref[spot, :].astype(f32))

    @pl.when(step == 0)
    def _():
        db_ref[...] = db

    @pl.when(step > 0)
    def _():
        db_ref[...] += db

    @pl.when(step == pl.num_programs(0) - 1)
    def _():
        half = send_ref.shape[0]
        for to in range(0, send_ref.shape[1], 512):
            if to < width:
                dw = mm(turned_ref[...], c_ref[:, to:to + 512], TN)
            else:
                dw = mm(h_ref[...], p_ref[:, to - width:to - width + 512], TN)
            dw = dw.astype(bf16)
            send_ref[:, to:to + 512] = dw[:half]
            keep_ref[:, to:to + 512] = dw[half:]


def first_tail(spots, order, c, h, weights, tables, attended, dqs, own, come):
    rows, width = c.shape
    cols = own.shape[1] // 2
    steps = rows // RB
    total = 2 * width + 2 * cols
    s = jax.ShapeDtypeStruct

    def full(shape):
        return pl.BlockSpec(shape, lambda j, spot, o: (0, 0), pipeline_mode=pl.Buffered(1))

    def weight(size, at):
        return pl.BlockSpec((width, size), lambda j, spot, o: (0, at // size), pipeline_mode=pl.Buffered(1))

    def window(a):
        return pl.BlockSpec((RB, a.shape[1]), lambda j, spot, o: (j, 0))

    table = pl.BlockSpec((RB, PAIR), lambda j, spot, o: (spot[j], 0))
    owns, comes = half_windows([own], steps)
    return pl.pallas_call(
        partial(first_kernel, len(dqs)),
        grid_spec=pltpu.PrefetchScalarGridSpec(
            num_scalar_prefetch=2,
            grid=(steps,),
            in_specs=[full(c.shape), full(h.shape), weight(width, 0), weight(cols, width), weight(cols, 2 * width)] + [table] * 3
            + owns + comes + [window(a) for a in (*attended, *dqs)],
            out_specs=[full((width // 2, total)), full((width // 2, total)), window(c), full((1, total - width))],
            scratch_shapes=[vmem(rows, total - width, dtype=bf16), vmem(RB, width, dtype=bf16), vmem(rows, width, dtype=bf16)],
        ),
        out_shape=[s((width // 2, total), bf16), s((width // 2, total), bf16), s((rows, width), f32), s((1, total - width), f32)],
        compiler_params=params(),
        cost_estimate=pl.CostEstimate(flops=24 << 30, bytes_accessed=1 << 20, transcendentals=0),
        name="first_tail",
    )(spots, order, c, h, weights, weights, weights, *tables, own, come, *attended, *dqs)


def last_kernel(groups, spot_ref, h_ref, gain_ref, wk_ref, wv_ref, x_ref, cos_ref, low_ref, high_ref, gin_ref, ghin_ref, *refs):
    own_refs, come_refs = refs[:groups], refs[groups:2 * groups]
    grad_ref, send_ref, keep_ref, db_ref, dgain_ref, dshift_ref, p_ref = refs[2 * groups:]
    step = pl.program_id(0)
    spot = pl.ds(pl.multiple_of(step * RB, RB), RB)
    count = wk_ref.shape[1]
    gather_rows(step, spot, (cos_ref[...], low_ref[...], high_ref[...]), own_refs, come_refs, p_ref, 0, count)
    grad = (ghin_ref[...] + mm(p_ref[spot, :count], wk_ref[...], NT) + mm(p_ref[spot, count:], wv_ref[...], NT))
    back, scaled = norm_back(x_ref[...].astype(f32), grad, gain_ref[...])
    grad_ref[...] = back + gin_ref[...]
    sums = col_sum(p_ref[spot, :].astype(f32)), col_sum(scaled), col_sum(grad)

    @pl.when(step == 0)
    def _():
        for ref, value in zip((db_ref, dgain_ref, dshift_ref), sums):
            ref[...] = value

    @pl.when(step > 0)
    def _():
        for ref, value in zip((db_ref, dgain_ref, dshift_ref), sums):
            ref[...] += value

    @pl.when(step == pl.num_programs(0) - 1)
    def _():
        half = send_ref.shape[0]
        for to in range(0, send_ref.shape[1], 512):
            dw = mm(h_ref[...], p_ref[:, to:to + 512], TN).astype(bf16)
            send_ref[:, to:to + 512] = dw[:half]
            keep_ref[:, to:to + 512] = dw[half:]


def last_tail(spots, x, h, gain, weights, tables, gin, gh, owns, comes):
    rows, width = x.shape
    cols = sum(a.shape[1] for a in owns) // 2
    steps = rows // RB
    s = jax.ShapeDtypeStruct

    def full(shape):
        return pl.BlockSpec(shape, lambda j, spot: (0, 0), pipeline_mode=pl.Buffered(1))

    def weight(at):
        return pl.BlockSpec((width, cols), lambda j, spot: (0, at // cols), pipeline_mode=pl.Buffered(1))

    block = pl.BlockSpec((RB, width), lambda j, spot: (j, 0))
    table = pl.BlockSpec((RB, PAIR), lambda j, spot: (spot[j], 0))
    own_windows, come_windows = half_windows(owns, steps)
    return pl.pallas_call(
        partial(last_kernel, len(owns)),
        grid_spec=pltpu.PrefetchScalarGridSpec(
            num_scalar_prefetch=1,
            grid=(steps,),
            in_specs=[full(h.shape), full((1, width)), weight(2 * width - cols), weight(3 * width - cols), block] + [table] * 3
            + [block, block] + own_windows + come_windows,
            out_specs=[block, full((width // 2, 2 * cols)), full((width // 2, 2 * cols)), full((1, 2 * cols)), full((1, width)),
                       full((1, width))],
            scratch_shapes=[vmem(rows, 2 * cols, dtype=bf16)],
        ),
        out_shape=[s((rows, width), f32), s((width // 2, 2 * cols), bf16), s((width // 2, 2 * cols), bf16), s((1, 2 * cols), f32),
                   s((1, width), f32), s((1, width), f32)],
        compiler_params=params(),
        cost_estimate=pl.CostEstimate(flops=12 << 30, bytes_accessed=1 << 20, transcendentals=0),
        name="last_tail",
    )(spots, h, gain.reshape(1, -1), weights, weights, x, *tables, gin, gh, *owns, *comes)


def join_kernel(groups, x_ref, w_ref, mlp_ref, b_ref, *refs):
    att_refs, (out_ref, att_ref) = refs[:groups], refs[groups:]
    at = 0
    for ref in att_refs:
        att_ref[:, at:at + ref.shape[1]] = ref[...]
        at += ref.shape[1]
    out = x_ref[...].astype(f32) + mm(att_ref[...], w_ref[...], NN) + mlp_ref[...] + b_ref[...]
    out_ref[...] = out.astype(bf16)


def join(x, attended, weights, mlp_out, bias):
    rows, width = x.shape
    s = jax.ShapeDtypeStruct
    block = pl.BlockSpec((RB, width), lambda j: (j, 0))
    return pl.pallas_call(
        partial(join_kernel, len(attended)),
        grid=(rows // RB,),
        in_specs=[block, pl.BlockSpec((width, width), lambda j: (0, 3)), block, pl.BlockSpec((1, width), lambda j: (0, 0))]
        + [pl.BlockSpec((RB, a.shape[1]), lambda j: (j, 0)) for a in attended],
        out_specs=block,
        out_shape=s((rows, width), bf16),
        scratch_shapes=[vmem(RB, width, dtype=bf16)],
        compiler_params=params(),
        cost_estimate=pl.CostEstimate(flops=12 << 30, bytes_accessed=1 << 20, transcendentals=0),
        name="join",
    )(x, weights, mlp_out, bias.reshape(1, -1), *attended)


def spread_kernel(c_ref, w_ref, out_ref):
    out_ref[...] = mm(c_ref[...], w_ref[...], NT).astype(bf16)


def spread(c, weights):
    rows, width = c.shape
    block = pl.BlockSpec((RB, width), lambda j: (j, 0))
    return pl.pallas_call(
        spread_kernel,
        grid=(rows // RB,),
        in_specs=[block, pl.BlockSpec((width, width), lambda j: (0, 3))],
        out_specs=block,
        out_shape=jax.ShapeDtypeStruct((rows, width), bf16),
        compiler_params=params(),
        cost_estimate=pl.CostEstimate(flops=1 << 20, bytes_accessed=1 << 16, transcendentals=0),
        name="spread",
    )(c, weights)


def fold(x, op):
    return op(x.reshape(x.shape[0] // 8, 8, x.shape[1]), axis=0)


def eye(size):
    return (lax.broadcasted_iota(jnp.int32, (size, size), 0) == lax.broadcasted_iota(jnp.int32, (size, size), 1)).astype(bf16)


def attention_kernel(half, n, kind_ref, owner_ref, cos_ref, sin_ref, q_ref, do_ref, *refs):
    k_refs, v_refs = refs[:2], refs[2:4]
    o_ref, dq_ref, all_ref, cont_ref, kt_ref, vt_ref, s_ref, p_ref, ds_ref, dka_ref, dva_ref = refs[4:]
    per = half // QB
    wide = n * half
    count = wide // QB
    spots = [(0, c * QB) for c in range(per)] + [(1, c * QB) for c in range((n - 1) * per)]

    ident = eye(PAIR)
    for refs_in, out in ((k_refs, kt_ref), (v_refs, vt_ref)):
        for c, (s, at) in enumerate(spots):
            out[:, c * QB:(c + 1) * QB] = refs_in[s][at:at + QB, :].T
        for c in range(per):
            out[:, wide + c * QB:wide + (c + 1) * QB] = refs_in[0][half + c * QB:half + (c + 1) * QB, :].T
    cont = slice(wide, wide + half)
    dka_ref[cont, :] = jnp.zeros((half, PAIR), f32)
    dva_ref[cont, :] = jnp.zeros((half, PAIR), f32)


    def block(qb, carry):
        own = pl.ds(pl.multiple_of(qb * QB, QB), QB)
        slot = pl.ds(pl.multiple_of(jnp.where(qb < per, qb * QB, wide + (qb - per) * QB), QB), QB)
        zero = jnp.zeros((), bf16)
        causal = lax.broadcasted_iota(jnp.int32, (QB, QB), 0) <= lax.broadcasted_iota(jnp.int32, (QB, QB), 1)
        left = lax.broadcasted_iota(jnp.int32, (QB, PAIR), 1) < HD

        def by_head(a):
            return jnp.where(left, a, zero), jnp.where(left, zero, a)

        def keys_of(some, c):
            if c == count:
                return some[0][own, :]
            s, at = spots[c]
            return some[s][at:at + QB, :]

        def cut(c):
            return slice(c * QB, (c + 1) * QB)

        ident = eye(QB)
        q_heads = by_head(q_ref[own, :])
        do_t = mm(eye(PAIR), do_ref[own, :], NT)
        upper = lax.broadcasted_iota(jnp.int32, (PAIR, QB), 0) < HD
        q_t = mm(eye(PAIR), q_ref[own, :], NT).astype(bf16)
        q_cols = jnp.where(upper, q_t, zero), jnp.where(upper, zero, q_t)
        peaks, norms, outs, deltas, scaled = [None, None], [None, None], [None, None], [None, None], [None, None]

        def scores(h):
            peak = jnp.full((8, QB), MASKED, f32)
            for c in range(count + 1):
                s = mm(keys_of(k_refs, c), q_cols[h], NN)
                if c == count:
                    s = jnp.where(causal, s, MASKED)
                    top = fold(s, jnp.max)
                else:
                    top = fold(s, jnp.max) + kind_ref[qb, c]
                s_ref[h, cut(c)] = s
                peak = jnp.maximum(peak, top)
            peaks[h] = jnp.max(peak, axis=0, keepdims=True)

        def weigh(h):
            total = jnp.zeros((8, QB), f32)
            for c in range(count + 1):
                bias = -peaks[h] if c == count else kind_ref[qb, c] - peaks[h]
                e = jnp.exp2(s_ref[h, cut(c)] + bias)
                total = total + fold(e, jnp.sum)
                p_ref[h, cut(c)] = e.astype(bf16)
            norms[h] = 1.0 / jnp.sum(total, axis=0, keepdims=True)

        def attend(h):
            lines = slice(h * HD, (h + 1) * HD)
            out = mm(vt_ref[lines, 0:wide], p_ref[h, 0:wide], NN) + mm(vt_ref[lines, slot], p_ref[h, wide:], NN)
            outs[h] = out * norms[h]
            deltas[h] = jnp.sum(outs[h] * do_t[lines], axis=0, keepdims=True) * norms[h]
            scaled[h] = do_t[lines] * norms[h]

        scores(0)
        scores(1)
        weigh(0)
        attend(0)
        weigh(1)
        attend(1)
        d_t = jnp.concatenate(scaled, axis=0).astype(bf16)
        d_cols = jnp.where(upper, d_t, zero), jnp.where(upper, zero, d_t)
        do_heads = by_head(mm(ident, d_t, NT).astype(bf16))
        grads = []
        for h in range(2):
            lines = slice(h * HD, (h + 1) * HD)
            for c in range(count + 1):
                dp = mm(keys_of(v_refs, c), d_cols[h], NN)
                ds_ref[h, cut(c)] = p_ref[h, cut(c)] * (dp - deltas[h]).astype(bf16)
            dq = mm(kt_ref[lines, 0:wide], ds_ref[h, 0:wide], NN) + mm(kt_ref[lines, slot], ds_ref[h, wide:], NN)
            a, b = dq[:ROT // 2], dq[ROT // 2:ROT]
            cosine, sine = cos_ref[:, own], sin_ref[:, own]
            grads.append(jnp.concatenate([a * cosine + b * sine, b * cosine - a * sine, dq[ROT:]], axis=0))
        for c in range(count + 1):
            at = slot if c == count else cut(c)
            dv = mm(p_ref[0, cut(c)], do_heads[0], NN) + mm(p_ref[1, cut(c)], do_heads[1], NN)
            dk = mm(ds_ref[0, cut(c)], q_heads[0], NN) + mm(ds_ref[1, cut(c)], q_heads[1], NN)
            if c == count:
                dva_ref[at, :] += dv
                dka_ref[at, :] += dk
            else:
                dva_ref[at, :] = jnp.where(qb == 0, dv, dva_ref[at, :] + dv)
                dka_ref[at, :] = jnp.where(qb == 0, dk, dka_ref[at, :] + dk)
        o_ref[own, :] = mm(ident, jnp.concatenate(outs, axis=0).astype(bf16), NT).astype(bf16)
        dq_ref[own, :] = mm(ident, (jnp.concatenate(grads, axis=0) * (HD ** (-0.5))).astype(bf16), NT).astype(bf16)

        return carry

    lax.fori_loop(0, 2 * per, block, 0)

    def flush(out, to, frm):
        rows = pl.ds(to, half)
        out[rows, :PAIR] = (dka_ref[frm:frm + half, :] * math.log(2.0)).astype(bf16)
        out[rows, PAIR:] = dva_ref[frm:frm + half, :].astype(bf16)

    flush(cont_ref, 0, wide)
    for s in range(n):
        flush(all_ref, pl.multiple_of(owner_ref[s] * half, half), s * half)


def attention(kind, owners, cos_t, sin_t, q, do, ks, vs, first, pairs):
    rows = q.shape[0]
    half = rows // 2
    n = 1 + ks[1].shape[0] // half
    wide = n * half
    keys = wide + half
    total = wide + QB
    qspec = pl.BlockSpec((rows, PAIR), lambda p: (0, p + first))
    ospec = pl.BlockSpec((rows, PAIR), lambda p: (0, p))
    table = pl.BlockSpec((ROT // 2, rows), lambda p: (0, 0))
    kspecs = [pl.BlockSpec((k.shape[0], PAIR), lambda p: (0, p + first)) for k in ks]
    gspecs = [pl.BlockSpec((size, 2 * PAIR), lambda p: (0, p)) for size in (wide, half)]
    s = jax.ShapeDtypeStruct
    pieces = pairs * rows // QB
    return pl.pallas_call(
        partial(attention_kernel, half, n),
        grid=(pairs,),
        in_specs=[pl.BlockSpec(memory_space=pltpu.SMEM), pl.BlockSpec(memory_space=pltpu.SMEM), table, table, qspec, qspec] + kspecs + kspecs,
        out_specs=[ospec, ospec] + gspecs,
        out_shape=[s((rows, pairs * PAIR), bf16), s((rows, pairs * PAIR), bf16)]
        + [s((size, 2 * pairs * PAIR), bf16) for size in (wide, half)],
        scratch_shapes=[pltpu.VMEM((PAIR, keys), bf16), pltpu.VMEM((PAIR, keys), bf16),
                        pltpu.VMEM((2, total, QB), f32), pltpu.VMEM((2, total, QB), bf16),
                        pltpu.VMEM((2, total, QB), bf16),
                        pltpu.VMEM((keys, PAIR), f32), pltpu.VMEM((keys, PAIR), f32)],
        compiler_params=pltpu.CompilerParams(vmem_limit_bytes=60 << 20),
        cost_estimate=pl.CostEstimate(flops=1 << 20, bytes_accessed=1 << 16, transcendentals=0),
        name="attention",
    )(kind, owners, cos_t, sin_t, q, do, *ks, *vs)


def pairs_of(bit, size):
    return [(a, a ^ bit) for a in range(size)]


def add_kernel(plan, *refs):
    for a, b, moves in plan:
        for source, to, target in moves:
            refs[to][target] = (refs[a][source].astype(f32) + refs[b][source].astype(f32)).astype(bf16)


def add_parts(arrays, plan, shapes, steps, load=0):
    def spec(shape):
        block = (*shape[:-1], shape[-1] // steps)
        return pl.BlockSpec(block, lambda j: (0,) * (len(shape) - 1) + (j,))

    return pl.pallas_call(
        partial(add_kernel, plan),
        grid=(steps,),
        in_specs=[spec(a.shape) for a in arrays],
        out_specs=[spec(shape) for shape in shapes],
        out_shape=[jax.ShapeDtypeStruct(shape, bf16) for shape in shapes],
        compiler_params=params(),
        cost_estimate=pl.CostEstimate(flops=(load << 30) + 1, bytes_accessed=1 << 16, transcendentals=0),
        name="add_parts",
    )(*arrays)


EVERY = slice(None)


def swap(a, bit):
    return lax.ppermute(a, "fsdp", pairs_of(bit, 8))


def steps_for(arrays):
    smallest = min(a.shape[-1] for a in arrays)
    return 4 if smallest % (4 * PAIR) == 0 else 1


def core_step(sends, keeps):
    count = len(sends)
    arrays, plan, shapes = [], [], []
    for send, keep in zip(sends, keeps):
        rows, cols = send.shape
        cut = (2, 2, 2, rows // 8, cols)
        to = 2 * count + len(shapes)
        moves = [((EVERY, 1, 0), to, (EVERY,)), ((EVERY, 0, 0), to + 1, (EVERY,)),
                 ((1, EVERY, 1), to + 2, (EVERY,)), ((0, EVERY, 1), to + 3, (EVERY,))]
        plan.append((len(arrays), len(arrays) + 1, moves))
        arrays += [keep.reshape(cut), swap(send, 1).reshape(cut)]
        shapes += [(2, rows // 8, cols)] * 4
    return add_parts(arrays, plan, shapes, steps_for(arrays))


def side_step(items):
    arrays, plan, shapes = [], [], []
    for i in range(0, len(items), 4):
        for send, keep, bit in ((items[i], items[i + 1], 2), (items[i + 2], items[i + 3], 4)):
            to = len(items) + len(shapes)
            plan.append((len(arrays), len(arrays) + 1, [((1,), to, (EVERY,)), ((0,), to + 1, (EVERY,))]))
            arrays += [keep, swap(send, bit)]
            shapes += [keep.shape[1:]] * 2
    return add_parts(arrays, plan, shapes, steps_for(arrays))


def last_step(items, load=0):
    arrays, plan, shapes = [], [], []
    for i in range(0, len(items), 4):
        to = len(items) + len(shapes)
        for at, (send, keep, bit) in enumerate(((items[i], items[i + 1], 4), (items[i + 2], items[i + 3], 2))):
            plan.append((len(arrays), len(arrays) + 1, [((EVERY,), to, (at,))]))
            arrays += [keep, swap(send, bit)]
        shapes.append((2, *keep.shape))
    parts = add_parts(arrays, plan, shapes, steps_for(arrays), load)
    return [part.reshape(-1, part.shape[-1]) for part in parts]


def along(part):
    return lax.psum_scatter(part, "ctx", scatter_dimension=0, tiled=True)


def after(value, *others):
    return lax.optimization_barrier((value, *others))[0]


def kept_after(items, *others):
    return [after(a, *others) if i % 2 else a for i, a in enumerate(items)]


def fast(inputs, cotangent, positions, segments, ln1_gain, ln1_bias, w_qkv, b_qkv, w_attn_out, b_out,
         ln2_gain, ln2_bias, w_in, b_in, w_out):
    x, grad_out, pos = inputs[0], cotangent[0], positions[0]
    rows, width = x.shape
    half = rows // 2
    n = lax.axis_size("ctx")
    ring = [(i, (i + 1) % n) for i in range(n)]
    back = [(i, (i - 1) % n) for i in range(n)]
    me, place = lax.axis_index("fsdp"), lax.axis_index("ctx")
    relative = [4 * dy + 2 * dx + 1 - keep for keep in (0, 1) for dy in (0, 1) for dx in (0, 1)]
    order = jnp.bitwise_xor(me, jnp.array(relative, jnp.int32))
    owners = lax.rem(place + n - jnp.arange(n), n)
    far = [None] * n
    far[0] = x[:half]
    for s in range(1, n):
        far[s] = lax.ppermute(far[s - 1], "ctx", ring)
    spots = [pos[::RB] // RB]
    for s in range(1, n):
        spots.append(lax.ppermute(spots[0][:half // RB], "ctx", [(i, (i + s) % n) for i in range(n)]))
    mine = (ln1_gain, ln1_bias, b_qkv, b_out, ln2_gain, ln2_bias, b_in)
    small = lax.all_gather(jnp.concatenate(mine).reshape(1, -1), "fsdp", axis=0, tiled=True)
    full, at = [], 0
    for a in mine:
        full.append(small[:, at:at + a.shape[0]].reshape(-1).astype(f32))
        at += a.shape[0]
    gain_attn, shift_attn, bias_qkv, bias_out, gain_mlp, shift_mlp, bias_in = full
    weights = lax.all_gather(jnp.concatenate([w_qkv, w_attn_out], axis=1), "fsdp", axis=0, tiled=True)

    lane = jnp.arange(PAIR) % HD
    inverse = jnp.exp(-math.log(10000.0) * (2.0 / ROT) * (lane % (ROT // 2)).astype(f32))
    angles = jnp.arange(n * half + CLEN).astype(f32)[:, None] * inverse[None, :]
    sine = jnp.sin(angles)
    tables = (jnp.where(lane < ROT, jnp.cos(angles), 1.0), jnp.where(lane < ROT // 2, sine, 0.0),
              jnp.where((lane >= ROT // 2) & (lane < ROT), sine, 0.0))
    angles_t = pos.astype(f32)[None, :] * inverse[:ROT // 2, None]
    cos_t, sin_t = jnp.cos(angles_t), jnp.sin(angles_t)

    normed, queries, own_keys, own_values = qkv(
        spots[0], order, [after(x, far[n - 2], *spots[1:])], gain_attn, shift_attn, weights, bias_qkv, tables)
    far_keys, far_values = qkv(
        jnp.concatenate(spots[1:]), order, far[1:], gain_attn, shift_attn, weights, bias_qkv, tables)
    keys, values = (own_keys, far_keys), (own_values, far_values)
    grad_att = spread(grad_out, weights)
    weight_in = lax.all_gather(after(w_in, far[1], *full, *tables, cos_t, sin_t), "fsdp", axis=0, tiled=True)
    weight_out = lax.all_gather(after(w_out, far[1], *full, *tables, cos_t, sin_t), "fsdp", axis=0, tiled=True)

    per = half // QB
    earlier = jnp.stack([spots[s][0] < spots[0][0] for s in range(1, n)])
    local_row = jnp.arange(2 * per)[:, None]
    seen_own = local_row > jnp.arange(per)[None, :]
    seen_far = jnp.repeat(earlier[None, :] | (local_row >= per), per, axis=1)
    kind = jnp.where(jnp.concatenate([seen_own, seen_far], axis=1), 0.0, MASKED).astype(f32)

    attended, grad_q, own_kv, come_kv = [], [], [], []

    def attend(first, count, wait):
        out = attention(kind, owners, cos_t, sin_t, after(queries, *wait), grad_att, keys, values, first, count)
        attended.append(out[0])
        grad_q.append(out[1])
        come_kv.append(lax.psum_scatter(out[2], "ctx", scatter_dimension=0, tiled=True))
        own_kv.append(out[3])

    attend(0, 4, ())
    mlp_out, grad_mlp, in_send, in_keep, out_send, out_keep, db_in, db_out, dgain_mlp, dshift_mlp = mlp(
        order, after(x, *attended), grad_out, gain_mlp, shift_mlp, weight_in, bias_in, weight_out)
    attend(4, 1, (mlp_out,))
    steps_mlp = core_step([out_send, in_send], [out_keep, in_keep])
    attend(5, 3, (*attended, *steps_mlp))
    steps_mlp = side_step(kept_after(steps_mlp, *attended))
    output = join(after(x, *steps_mlp), attended, weights, mlp_out, bias_out)
    first_send, first_keep, grad_heads, db_first = first_tail(
        spots[0], order, after(grad_out, output), normed, weights, tables, attended, grad_q, own_kv[0], come_kv[0])
    part_out, part_in = last_step(kept_after(steps_mlp, grad_heads), 48)
    steps_first = core_step([first_send], [first_keep])
    grad_inputs, last_send, last_keep, db_last, dgain_attn, dshift_attn = last_tail(
        spots[0], after(x, part_out, part_in, *steps_first), normed, gain_attn, weights, tables, grad_mlp, grad_heads,
        own_kv[1:], come_kv[1:])
    sum_out, sum_in = along(part_out), along(part_in)
    steps_first = side_step(kept_after(steps_first, last_send))
    cols = db_last.shape[1] // 2
    split = [width, width + (db_first.shape[1] - width) // 2]
    db_q, db_k, db_v = jnp.split(db_first, split, axis=1)
    db_qkv = jnp.concatenate([db_q, db_k, db_last[:, :cols], db_v, db_last[:, cols:]], axis=1)
    parts = 8 * n
    smalls = [a.reshape(parts, -1) for a in (dgain_attn, dshift_attn, db_qkv, db_out, dgain_mlp, dshift_mlp, db_in)]
    flat = jnp.concatenate(smalls, axis=1).astype(bf16).reshape(parts, -1, PAIR)
    lines = flat.shape[1]
    packed = jnp.pad(flat, ((0, 0), (0, width // parts - lines), (0, 0))).reshape(width, PAIR)
    packed = packed.reshape(8, width // 8, PAIR)[order].reshape(2, width // 2, PAIR)
    steps_last = core_step([last_send, packed[0]], [after(last_keep, *steps_first), packed[1]])
    part_first = last_step(steps_first)
    part_last = last_step(side_step(kept_after(steps_last, *part_first)))
    total = along(jnp.concatenate([*part_first, *part_last], axis=1))
    ends = [width, 2 * width, split[1] + width, db_first.shape[1] + width]
    ends += [ends[-1] + cols, ends[-1] + 2 * cols]
    sum_attn, sum_q, sum_k, sum_v, end_k, end_v, packed = jnp.split(total, ends, axis=1)
    sum_qkv = jnp.concatenate([sum_q, sum_k, end_k, sum_v, end_v], axis=1)
    packed = packed[:lines].astype(f32).reshape(-1)
    done, at = [], 0
    for a in smalls:
        done.append(packed[at:at + a.shape[1]])
        at += a.shape[1]
    return (output[None], grad_inputs[None], done[0], done[1], sum_qkv.astype(f32), done[2], sum_attn.astype(f32),
            done[3], done[4], done[5], sum_in.astype(f32), done[6], sum_out.astype(f32))


def local(*args):
    half = args[0].shape[1] // 2
    if args[0].shape[0] == 1 and half % CLEN == 0 and lax.axis_size("fsdp") == 8:
        return fast(*args)
    return generic(*args)


def generic(
    inputs,
    cotangent,
    positions,
    segments,
    ln1_gain,
    ln1_bias,
    w_qkv,
    b_qkv,
    w_attn_out,
    b_out,
    ln2_gain,
    ln2_bias,
    w_in,
    b_in,
    w_out,
):
    shards = (
        ln1_gain,
        ln1_bias,
        w_qkv,
        b_qkv,
        w_attn_out,
        b_out,
        ln2_gain,
        ln2_bias,
        w_in,
        b_in,
        w_out,
    )
    params = (
        lax.all_gather(shards[0], "fsdp", axis=0, tiled=True),
        lax.all_gather(shards[1], "fsdp", axis=0, tiled=True),
        lax.all_gather(shards[2], "fsdp", axis=0, tiled=True),
        lax.all_gather(shards[3], "fsdp", axis=0, tiled=True),
        lax.all_gather(shards[4], "fsdp", axis=0, tiled=True),
        lax.all_gather(shards[5], "fsdp", axis=0, tiled=True),
        lax.all_gather(shards[6], "fsdp", axis=0, tiled=True),
        lax.all_gather(shards[7], "fsdp", axis=0, tiled=True),
        lax.all_gather(shards[8], "fsdp", axis=0, tiled=True),
        lax.all_gather(shards[9], "fsdp", axis=0, tiled=True),
        lax.all_gather(shards[10], "fsdp", axis=0, tiled=True),
    )
    groups, local_len, width = inputs.shape
    rows_total = groups * local_len
    block = math.gcd(local_len, 256)
    label_pos, label_seg = (
        lax.all_gather(positions, "ctx", axis=1, tiled=True),
        lax.all_gather(segments, "ctx", axis=1, tiled=True),
    )
    count = label_pos.shape[1] // block
    f32 = jnp.float32
    bf16 = jnp.bfloat16
    (
        gain_attn,
        shift_attn,
        weight_qkv,
        bias_qkv,
        weight_attn,
        bias_out,
        gain_mlp,
        shift_mlp,
        weight_in,
        bias_in,
        weight_out,
    ) = params
    flat_in = inputs.reshape(rows_total, width).astype(f32)
    normed_attn = layer_norm(flat_in, gain_attn.astype(f32), shift_attn.astype(f32)).astype(bf16)
    normed_mlp = layer_norm(flat_in, gain_mlp.astype(f32), shift_mlp.astype(f32)).astype(bf16)
    projected = jnp.dot(normed_attn, weight_qkv, preferred_element_type=f32) + bias_qkv.astype(f32)
    cosine, sine = rotary_tables(positions)

    def split_heads(columns):
        return columns.reshape(groups, local_len, HEADS, HD)

    scale = HD ** (-0.5)
    queries = (rotate(split_heads(projected[:, :width]), cosine, sine) * scale).astype(bf16)
    keys_own = rotate(split_heads(projected[:, width : 2 * width]), cosine, sine).astype(bf16)
    values_own = split_heads(projected[:, 2 * width :]).astype(bf16)
    keys_all, values_all = (
        lax.all_gather(keys_own, "ctx", axis=1, tiled=True),
        lax.all_gather(values_own, "ctx", axis=1, tiled=True),
    )

    def key_block(index):
        start = index * block
        keys_blk = lax.dynamic_slice_in_dim(keys_all, start, block, 1)
        values_blk = lax.dynamic_slice_in_dim(values_all, start, block, 1)
        mask = allowed_mask(
            positions,
            segments,
            lax.dynamic_slice_in_dim(label_pos, start, block, 1),
            lax.dynamic_slice_in_dim(label_seg, start, block, 1),
        )
        return (keys_blk, values_blk, mask)

    def total_step(carry, index):
        peak, total = carry
        keys_blk, values_blk, mask = key_block(index)
        scores = jnp.where(mask, scores_of(queries, keys_blk), MASKED)
        fresh = jnp.maximum(peak, jnp.max(scores, axis=-1))
        added = jnp.sum(jnp.where(mask, jnp.exp(scores - fresh[..., None]), 0.0), axis=-1)
        return ((fresh, total * jnp.exp(peak - fresh) + added), None)

    stat_shape = (groups, HEADS, local_len)
    (peak, total), unused = lax.scan(
        total_step,
        (jnp.full(stat_shape, MASKED, f32), jnp.zeros(stat_shape, f32)),
        jnp.arange(count),
    )
    log_total = peak + jnp.log(total)

    def attend_step(rounded_sum, index):
        keys_blk, values_blk, mask = key_block(index)
        probs = jnp.where(mask, jnp.exp(scores_of(queries, keys_blk) - log_total[..., None]), 0.0)
        rounded_sum = rounded_sum + jnp.einsum(
            "ghqk,gkhd->gqhd", probs.astype(bf16), values_blk, preferred_element_type=f32
        )
        return (rounded_sum, None)

    head_shape = (groups, local_len, HEADS, HD)
    rounded_sum, unused = lax.scan(attend_step, jnp.zeros(head_shape, f32), jnp.arange(count))
    attended = rounded_sum.reshape(rows_total, width).astype(bf16)
    pre_act = jnp.dot(normed_mlp, weight_in, preferred_element_type=f32) + bias_in.astype(f32)
    activated = jax.nn.gelu(pre_act, approximate=False).astype(bf16)
    output = (
        flat_in
        + jnp.dot(attended, weight_attn, preferred_element_type=f32)
        + jnp.dot(activated, weight_out, preferred_element_type=f32)
        + bias_out.astype(f32)
    )
    (
        gain_attn,
        shift_attn,
        weight_qkv,
        bias_qkv,
        weight_attn,
        bias_out,
        gain_mlp,
        shift_mlp,
        weight_in,
        bias_in,
        weight_out,
    ) = params
    grad_out = cotangent.reshape(rows_total, width)
    grad_bias_out = jnp.sum(grad_out.astype(f32), axis=0)
    grad_weight_out = jnp.einsum("rf,rd->fd", activated, grad_out, preferred_element_type=f32)
    grad_act = jnp.einsum("rd,fd->rf", grad_out, weight_out, preferred_element_type=f32)
    unused, gelu_back = jax.vjp(partial(jax.nn.gelu, approximate=False), pre_act)
    grad_pre = gelu_back(grad_act)[0].astype(bf16)
    grad_weight_in = jnp.einsum("rd,rf->df", normed_mlp, grad_pre, preferred_element_type=f32)
    grad_bias_in = jnp.sum(grad_pre.astype(f32), axis=0)
    grad_normed_mlp = jnp.einsum("rf,df->rd", grad_pre, weight_in, preferred_element_type=f32)
    grad_weight_attn = jnp.einsum("ra,rd->ad", attended, grad_out, preferred_element_type=f32)
    grad_att = (
        jnp.einsum("rd,ad->ra", grad_out, weight_attn, preferred_element_type=f32)
        .astype(bf16)
        .reshape(head_shape)
    )
    delta = jnp.einsum(
        "gqhd,gqhd->ghq", grad_att.astype(f32), rounded_sum, precision=lax.Precision.HIGHEST
    )

    def back_step(carry, index):
        keys_blk, values_blk, mask = key_block(index)
        rounded, grad_scores = block_grads(
            queries, grad_att, log_total, delta, mask, keys_blk, values_blk
        )
        carry = carry + jnp.einsum(
            "ghqk,gkhd->gqhd", grad_scores, keys_blk, preferred_element_type=f32
        )
        key_term = jnp.einsum("ghqk,gqhd->gkhd", grad_scores, queries, preferred_element_type=f32)
        value_term = jnp.einsum("ghqk,gqhd->gkhd", rounded, grad_att, preferred_element_type=f32)
        return (carry, (key_term, value_term))

    grad_queries, (key_terms, value_terms) = lax.scan(
        back_step, jnp.zeros(head_shape, f32), jnp.arange(count)
    )
    key_sums, value_sums = (
        lax.psum_scatter(
            key_terms.astype(jnp.bfloat16), "ctx", scatter_dimension=0, tiled=True
        ).astype(jnp.float32),
        lax.psum_scatter(
            value_terms.astype(jnp.bfloat16), "ctx", scatter_dimension=0, tiled=True
        ).astype(jnp.float32),
    )
    grad_keys = jnp.transpose(key_sums, (1, 0, 2, 3, 4)).reshape(head_shape)
    grad_values = jnp.transpose(value_sums, (1, 0, 2, 3, 4)).reshape(head_shape)
    grad_q_pre = unrotate(grad_queries * scale, cosine, sine).reshape(rows_total, width)
    grad_k_pre = unrotate(grad_keys, cosine, sine).reshape(rows_total, width)
    grad_projected = jnp.concatenate(
        [grad_q_pre, grad_k_pre, grad_values.reshape(rows_total, width)], axis=1
    ).astype(bf16)
    grad_weight_qkv = jnp.einsum(
        "rd,re->de", normed_attn, grad_projected, preferred_element_type=f32
    )
    grad_bias_qkv = jnp.sum(grad_projected.astype(f32), axis=0)
    grad_normed_attn = jnp.einsum(
        "re,de->rd", grad_projected, weight_qkv, preferred_element_type=f32
    )
    unused, norm_back_attn = jax.vjp(
        layer_norm, flat_in, gain_attn.astype(f32), shift_attn.astype(f32)
    )
    grad_in_attn, grad_gain_attn, grad_shift_attn = norm_back_attn(grad_normed_attn)
    unused, norm_back_mlp = jax.vjp(
        layer_norm, flat_in, gain_mlp.astype(f32), shift_mlp.astype(f32)
    )
    grad_in_mlp, grad_gain_mlp, grad_shift_mlp = norm_back_mlp(grad_normed_mlp)
    grad_inputs = (grad_out.astype(f32) + grad_in_attn + grad_in_mlp).reshape(
        groups, local_len, width
    )
    sums = (
        lax.psum_scatter(grad_gain_attn, ("fsdp", "ctx"), scatter_dimension=0, tiled=True),
        lax.psum_scatter(grad_shift_attn, ("fsdp", "ctx"), scatter_dimension=0, tiled=True),
        lax.psum_scatter(grad_weight_qkv, ("fsdp", "ctx"), scatter_dimension=0, tiled=True),
        lax.psum_scatter(grad_bias_qkv, ("fsdp", "ctx"), scatter_dimension=0, tiled=True),
        lax.psum_scatter(grad_weight_attn, ("fsdp", "ctx"), scatter_dimension=0, tiled=True),
        lax.psum_scatter(grad_bias_out, ("fsdp", "ctx"), scatter_dimension=0, tiled=True),
        lax.psum_scatter(grad_gain_mlp, ("fsdp", "ctx"), scatter_dimension=0, tiled=True),
        lax.psum_scatter(grad_shift_mlp, ("fsdp", "ctx"), scatter_dimension=0, tiled=True),
        lax.psum_scatter(grad_weight_in, ("fsdp", "ctx"), scatter_dimension=0, tiled=True),
        lax.psum_scatter(grad_bias_in, ("fsdp", "ctx"), scatter_dimension=0, tiled=True),
        lax.psum_scatter(grad_weight_out, ("fsdp", "ctx"), scatter_dimension=0, tiled=True),
    )
    result = output.reshape(groups, local_len, width).astype(bf16)
    return (
        result,
        grad_inputs,
        sums[0],
        sums[1],
        sums[2],
        sums[3],
        sums[4],
        sums[5],
        sums[6],
        sums[7],
        sums[8],
        sums[9],
        sums[10],
    )


def solution(mesh):
    in_specs = (
        P("fsdp", "ctx", None),
        P("fsdp", "ctx", None),
        P("fsdp", "ctx"),
        P("fsdp", "ctx"),
        P("fsdp"),
        P("fsdp"),
        P("fsdp", None),
        P("fsdp"),
        P("fsdp", None),
        P("fsdp"),
        P("fsdp"),
        P("fsdp"),
        P("fsdp", None),
        P("fsdp"),
        P("fsdp", None),
    )
    out_specs = (
        P("fsdp", "ctx", None),
        P("fsdp", "ctx", None),
        P(("fsdp", "ctx")),
        P(("fsdp", "ctx")),
        P(("fsdp", "ctx"), None),
        P(("fsdp", "ctx")),
        P(("fsdp", "ctx"), None),
        P(("fsdp", "ctx")),
        P(("fsdp", "ctx")),
        P(("fsdp", "ctx")),
        P(("fsdp", "ctx"), None),
        P(("fsdp", "ctx")),
        P(("fsdp", "ctx"), None),
    )
    return jax.shard_map(local, mesh=mesh, in_specs=in_specs, out_specs=out_specs, check_vma=False)
```

```python
from functools import partial
import math

import jax
import jax.numpy as jnp
from jax import lax
from jax.experimental import pallas as pl
from jax.experimental.pallas import tpu as pltpu
from jax.sharding import PartitionSpec as P

HEADS = 16
HD = 64
ROT = 16
CLEN = 256
QB = 256
RB = 256
PAIR = 2 * HD
bf16 = jnp.bfloat16
f32 = jnp.float32
NN = (((1,), (0,)), ((), ()))
NT = (((1,), (1,)), ((), ()))
TN = (((0,), (0,)), ((), ()))


NORM_EPS = 1e-05
MASKED = -1e30


def layer_norm(values, scaling, offset):
    average = jnp.mean(values, axis=-1, keepdims=True)
    centered = values - average
    variance = jnp.mean(centered * centered, axis=-1, keepdims=True)
    return centered * lax.rsqrt(variance + NORM_EPS) * scaling + offset


def rotary_tables(positions):
    halfway = ROT // 2
    spacing = jnp.arange(halfway, dtype=jnp.float32) * (2.0 / ROT)
    inverse = jnp.exp(-math.log(10000.0) * spacing)
    angles = positions.astype(jnp.float32)[..., None] * inverse
    return (jnp.cos(angles), jnp.sin(angles))


def rotate(heads_in, cosine, sine):
    halfway = ROT // 2
    cosine = cosine[..., None, :]
    sine = sine[..., None, :]
    first = heads_in[..., :halfway]
    second = heads_in[..., halfway:ROT]
    return jnp.concatenate(
        [first * cosine - second * sine, second * cosine + first * sine, heads_in[..., ROT:]],
        axis=-1,
    )


def unrotate(grads_in, cosine, sine):
    halfway = ROT // 2
    cosine = cosine[..., None, :]
    sine = sine[..., None, :]
    first = grads_in[..., :halfway]
    second = grads_in[..., halfway:ROT]
    return jnp.concatenate(
        [first * cosine + second * sine, second * cosine - first * sine, grads_in[..., ROT:]],
        axis=-1,
    )


def allowed_mask(query_pos, query_seg, key_pos, key_seg):
    same_doc = (key_seg[:, None, :] == 0) | (key_seg[:, None, :] == query_seg[:, :, None])
    causal = key_pos[:, None, :] <= query_pos[:, :, None]
    return (same_doc & causal)[:, None]


def scores_of(queries, keys_blk):
    return jnp.einsum("gqhd,gkhd->ghqk", queries, keys_blk, preferred_element_type=jnp.float32)


def block_grads(queries, grad_att, log_total, delta, mask, keys_blk, values_blk):
    probs = jnp.where(mask, jnp.exp(scores_of(queries, keys_blk) - log_total[..., None]), 0.0)
    dprobs = jnp.einsum("gqhd,gkhd->ghqk", grad_att, values_blk, preferred_element_type=jnp.float32)
    grad_scores = (probs * (dprobs - delta[..., None])).astype(jnp.bfloat16)
    return (probs.astype(jnp.bfloat16), grad_scores)


def mm(a, b, dims):
    return lax.dot_general(a, b, dims, preferred_element_type=f32)


def row_stats(x):
    average = jnp.mean(x, axis=1, keepdims=True)
    centered = x - average
    return centered, lax.rsqrt(jnp.mean(centered * centered, axis=1, keepdims=True) + NORM_EPS)


def norm_rows(x, scaling, offset):
    centered, inverse = row_stats(x)
    return (centered * inverse * scaling + offset).astype(bf16)


def norm_back(x, grad, scaling):
    centered, inverse = row_stats(x)
    unit = centered * inverse
    e = grad * scaling
    inner = e - jnp.mean(e, axis=1, keepdims=True) - unit * jnp.mean(e * unit, axis=1, keepdims=True)
    return inverse * inner, grad * unit


def col_sum(a):
    return jnp.sum(a, axis=0, keepdims=True)


def vmem(*shape, dtype=f32):
    return pltpu.VMEM(shape, dtype)


def params():
    return pltpu.CompilerParams(vmem_limit_bytes=60 << 20)


ROOT = math.sqrt(0.5)
DENS = 1.0 / math.sqrt(2.0 * math.pi)


def reorder(order_ref, source, target):
    size = source.shape[1] // order_ref.shape[0]
    for i in range(order_ref.shape[0]):
        at = pl.multiple_of(order_ref[i] * size, size)
        target[:, i * size:(i + 1) * size] = source[:, pl.ds(at, size)]


def mlp_kernel(order_ref, x_ref, c_ref, gain_ref, shift_ref, win_ref, bin_ref, wout_ref,
               out_ref, gin_ref, dwin_send, dwin_keep, dwout_send, dwout_keep, dbin_ref, dbout_ref, dgain_ref, dshift_ref,
               h_ref, turned_ref, act_ref, gp_ref, gh_ref):
    step = pl.program_id(0)
    rows = x_ref.shape[0]
    blocks = [slice(r, r + RB) for r in range(0, rows, RB)]

    @pl.when(step == 0)
    def _():
        for r in blocks:
            h_ref[r, :] = norm_rows(x_ref[r, :].astype(f32), gain_ref[...], shift_ref[...])
            out_ref[r, :] = jnp.zeros((RB, out_ref.shape[1]), f32)
            gh_ref[r, :] = jnp.zeros((RB, gh_ref.shape[1]), f32)
        reorder(order_ref, h_ref, turned_ref)

    dbin = jnp.zeros(dbin_ref.shape, f32)
    for r in blocks:
        pre = mm(h_ref[r, :], win_ref[...], NN) + bin_ref[...]
        phi = 0.5 + 0.5 * lax.erf(pre * ROOT)
        act_ref[r, :] = (pre * phi).astype(bf16)
        gp = phi + pre * (DENS * jnp.exp(-0.5 * (pre * pre)))
        gact = mm(c_ref[r, :], wout_ref[...], NT)
        gpre = (gact * gp).astype(bf16)
        gp_ref[r, :] = gpre
        dbin = dbin + col_sum(gpre.astype(f32))
    for r in blocks:
        out_ref[r, :] += mm(act_ref[r, :], wout_ref[...], NN)
        gh_ref[r, :] += mm(gp_ref[r, :], win_ref[...], NT)
    dwout = mm(act_ref[...], c_ref[...], TN).astype(bf16)
    middle = pl.num_programs(0) // 2

    @pl.when(step < middle)
    def _():
        dwout_send[...] = dwout

    @pl.when(step >= middle)
    def _():
        dwout_keep[...] = dwout

    dwin = mm(turned_ref[...], gp_ref[...], TN).astype(bf16)
    dwin_send[...] = dwin[:dwin_send.shape[0]]
    dwin_keep[...] = dwin[dwin_send.shape[0]:]
    dbin_ref[...] = dbin

    @pl.when(step == pl.num_programs(0) - 1)
    def _():
        dgain = jnp.zeros(dgain_ref.shape, f32)
        dshift = jnp.zeros(dshift_ref.shape, f32)
        dbout = jnp.zeros(dbout_ref.shape, f32)
        for r in blocks:
            grad = gh_ref[r, :]
            back, scaled = norm_back(x_ref[r, :].astype(f32), grad, gain_ref[...])
            c = c_ref[r, :].astype(f32)
            gin_ref[r, :] = back + c
            dgain += col_sum(scaled)
            dshift += col_sum(grad)
            dbout += col_sum(c)
        dgain_ref[...] = dgain
        dshift_ref[...] = dshift
        dbout_ref[...] = dbout


def mlp(order, x, c, gain, shift, weight_in, bias_in, weight_out):
    rows, width = x.shape
    ff = weight_in.shape[1]
    steps = order.shape[0]
    fc = ff // steps
    whole = pl.BlockSpec((rows, width), lambda j, o: (0, 0))
    line = pl.BlockSpec((1, width), lambda j, o: (0, 0))
    down = pl.BlockSpec((width // 2, fc), lambda j, o: (0, o[j]))
    s = jax.ShapeDtypeStruct
    return pl.pallas_call(
        mlp_kernel,
        grid_spec=pltpu.PrefetchScalarGridSpec(
            num_scalar_prefetch=1,
            grid=(steps,),
            in_specs=[whole, whole, line, line, pl.BlockSpec((width, fc), lambda j, o: (0, o[j])),
                      pl.BlockSpec((1, fc), lambda j, o: (0, o[j])), pl.BlockSpec((fc, width), lambda j, o: (o[j], 0))],
            out_specs=[whole, whole, down, down,
                       pl.BlockSpec((fc, width), lambda j, o: (jnp.minimum(j, steps // 2 - 1), 0)),
                       pl.BlockSpec((fc, width), lambda j, o: (jnp.maximum(j - steps // 2, 0), 0)),
                       pl.BlockSpec((1, fc), lambda j, o: (0, o[j])), line, line, line],
            scratch_shapes=[vmem(rows, width, dtype=bf16), vmem(rows, width, dtype=bf16), vmem(rows, fc, dtype=bf16),
                            vmem(rows, fc, dtype=bf16), vmem(rows, width)],
        ),
        out_shape=[s((rows, width), f32), s((rows, width), f32), s((width // 2, ff), bf16), s((width // 2, ff), bf16),
                   s((ff // 2, width), bf16), s((ff // 2, width), bf16), s((1, ff), f32), s((1, width), f32),
                   s((1, width), f32), s((1, width), f32)],
        compiler_params=params(),
        cost_estimate=pl.CostEstimate(flops=1 << 20, bytes_accessed=1 << 16, transcendentals=0),
        name="mlp",
    )(order, x, c, gain.reshape(1, -1), shift.reshape(1, -1), weight_in, bias_in.reshape(1, -1), weight_out)


def turn_lanes(u, cosine, low, high, sign):
    half = ROT // 2
    parts = []
    for at in range(0, u.shape[1], PAIR):
        g = u[:, at:at + PAIR]
        parts.append(g * cosine + sign * (pltpu.roll(g, half, 1) * high - pltpu.roll(g, PAIR - half, 1) * low))
    return jnp.concatenate(parts, axis=1)


def qkv_kernel(far, spot_ref, order_ref, gain_ref, shift_ref, w_ref, b_ref, cos_ref, low_ref, high_ref, *refs):
    with_q = far == 0
    if with_q:
        x_ref, outs = refs[0], refs[1:]
    else:
        x_refs, outs, x_ref = refs[:far], refs[far:-1], refs[-1]
        step = pl.program_id(0)
        per = pl.num_programs(0) // far
        for s in range(far):
            @pl.when(step // per == s)
            def _(s=s):
                x_ref[...] = x_refs[s][...]
    width = x_ref.shape[1]
    h = norm_rows(x_ref[...].astype(f32), gain_ref[...], shift_ref[...])
    tables = (cos_ref[...], low_ref[...], high_ref[...])
    if with_q:
        h_ref, q_ref, k_ref, v_ref, plain_ref = outs
        plain_ref[...] = h
        reorder(order_ref, plain_ref, h_ref)
        q = mm(h, w_ref[:, :width], NN) + b_ref[:, :width]
        q_ref[...] = (turn_lanes(q, *tables, 1.0) * (HD ** (-0.5) / math.log(2.0))).astype(bf16)
    else:
        k_ref, v_ref = outs
    k = mm(h, w_ref[:, width:2 * width], NN) + b_ref[:, width:2 * width]
    k_ref[...] = turn_lanes(k, *tables, 1.0).astype(bf16)
    v_ref[...] = (mm(h, w_ref[:, 2 * width:], NN) + b_ref[:, 2 * width:]).astype(bf16)


def qkv(spots, order, xs, gain, shift, weight, bias, tables):
    far = len(xs) if len(xs) > 1 else 0
    rows, width = xs[0].shape
    per = rows // RB
    total = len(xs) * rows
    s = jax.ShapeDtypeStruct((total, width), bf16)
    block = pl.BlockSpec((RB, width), lambda j, spot, o: (j, 0))
    line = pl.BlockSpec((1, width), lambda j, spot, o: (0, 0))
    table = pl.BlockSpec((RB, PAIR), lambda j, spot, o: (spot[j], 0))
    count = 2 if far else 4

    def window(i):
        return pl.BlockSpec((RB, width), lambda j, spot, o: (jnp.clip(j - i * per, 0, per - 1), 0))

    return pl.pallas_call(
        partial(qkv_kernel, far),
        grid_spec=pltpu.PrefetchScalarGridSpec(
            num_scalar_prefetch=2,
            grid=(total // RB,),
            in_specs=[line, line, pl.BlockSpec((width, 3 * width), lambda j, spot, o: (0, 0)),
                      pl.BlockSpec((1, 3 * width), lambda j, spot, o: (0, 0)), table, table, table]
            + [window(i) for i in range(len(xs))],
            out_specs=[block] * count,
            scratch_shapes=[vmem(RB, width, dtype=bf16)],
        ),
        out_shape=[s] * count,
        compiler_params=params(),
        cost_estimate=pl.CostEstimate(flops=1 << 20, bytes_accessed=1 << 16, transcendentals=0),
        name="kv_remote" if far else "qkv_own",
    )(spots, order, gain.reshape(1, -1), shift.reshape(1, -1), weight, bias.reshape(1, -1), *tables, *xs)


def gather_rows(step, spot, tables, own_refs, come_refs, p_ref, k_at, v_at):
    half = pl.num_programs(0) // 2
    columns = [(g, at) for g in range(len(own_refs)) for at in range(0, own_refs[g].shape[1], 2 * PAIR)]

    def put(refs):
        for to, (g, at) in enumerate(columns):
            turned = turn_lanes(refs[g][:, at:at + PAIR].astype(f32), *tables, -1.0).astype(bf16)
            p_ref[spot, k_at + to * PAIR:k_at + (to + 1) * PAIR] = turned
            p_ref[spot, v_at + to * PAIR:v_at + (to + 1) * PAIR] = refs[g][:, at + PAIR:at + 2 * PAIR]

    @pl.when(step < half)
    def _():
        put(come_refs)

    @pl.when(step >= half)
    def _():
        put(own_refs)


def half_windows(arrays, count):
    half = count // 2
    come = [pl.BlockSpec((RB, a.shape[1]), lambda j, *o: (jnp.clip(j, 0, half - 1), 0)) for a in arrays]
    own = [pl.BlockSpec((RB, a.shape[1]), lambda j, *o: (jnp.clip(j - half, 0, half - 1), 0)) for a in arrays]
    return own, come


def first_kernel(groups, spot_ref, order_ref, c_ref, h_ref, wq_ref, wk_ref, wv_ref, cos_ref, low_ref, high_ref, own_ref,
                 come_ref, *refs):
    att_refs, dq_refs = refs[:groups], refs[groups:2 * groups]
    send_ref, keep_ref, gh_ref, db_ref, p_ref, att_ref, turned_ref = refs[2 * groups:]
    step = pl.program_id(0)
    width = c_ref.shape[1]
    spot = pl.ds(pl.multiple_of(step * RB, RB), RB)
    at = 0
    for g in range(groups):
        size = att_refs[g].shape[1]
        att_ref[:, at:at + size] = att_refs[g][...]
        p_ref[spot, at:at + size] = dq_refs[g][...]
        at += size
    for i in range(order_ref.shape[0]):
        size = width // order_ref.shape[0]
        lanes = pl.ds(pl.multiple_of(order_ref[i] * size, size), size)
        turned_ref[spot, i * size:(i + 1) * size] = att_ref[:, lanes]
    count = wk_ref.shape[1]
    gather_rows(step, spot, (cos_ref[...], low_ref[...], high_ref[...]), [own_ref], [come_ref], p_ref, width, width + count)
    gh_ref[...] = (mm(p_ref[spot, :width], wq_ref[...], NT) + mm(p_ref[spot, width:width + count], wk_ref[...], NT)
                   + mm(p_ref[spot, width + count:], wv_ref[...], NT))
    db = col_sum(p_ref[spot, :].astype(f32))

    @pl.when(step == 0)
    def _():
        db_ref[...] = db

    @pl.when(step > 0)
    def _():
        db_ref[...] += db

    @pl.when(step == pl.num_programs(0) - 1)
    def _():
        half = send_ref.shape[0]
        for to in range(0, send_ref.shape[1], 512):
            if to < width:
                dw = mm(turned_ref[...], c_ref[:, to:to + 512], TN)
            else:
                dw = mm(h_ref[...], p_ref[:, to - width:to - width + 512], TN)
            dw = dw.astype(bf16)
            send_ref[:, to:to + 512] = dw[:half]
            keep_ref[:, to:to + 512] = dw[half:]


def first_tail(spots, order, c, h, weights, tables, attended, dqs, own, come):
    rows, width = c.shape
    cols = own.shape[1] // 2
    steps = rows // RB
    total = 2 * width + 2 * cols
    s = jax.ShapeDtypeStruct

    def full(shape):
        return pl.BlockSpec(shape, lambda j, spot, o: (0, 0), pipeline_mode=pl.Buffered(1))

    def weight(size, at):
        return pl.BlockSpec((width, size), lambda j, spot, o: (0, at // size), pipeline_mode=pl.Buffered(1))

    def window(a):
        return pl.BlockSpec((RB, a.shape[1]), lambda j, spot, o: (j, 0))

    table = pl.BlockSpec((RB, PAIR), lambda j, spot, o: (spot[j], 0))
    owns, comes = half_windows([own], steps)
    return pl.pallas_call(
        partial(first_kernel, len(dqs)),
        grid_spec=pltpu.PrefetchScalarGridSpec(
            num_scalar_prefetch=2,
            grid=(steps,),
            in_specs=[full(c.shape), full(h.shape), weight(width, 0), weight(cols, width), weight(cols, 2 * width)] + [table] * 3
            + owns + comes + [window(a) for a in (*attended, *dqs)],
            out_specs=[full((width // 2, total)), full((width // 2, total)), window(c), full((1, total - width))],
            scratch_shapes=[vmem(rows, total - width, dtype=bf16), vmem(RB, width, dtype=bf16), vmem(rows, width, dtype=bf16)],
        ),
        out_shape=[s((width // 2, total), bf16), s((width // 2, total), bf16), s((rows, width), f32), s((1, total - width), f32)],
        compiler_params=params(),
        cost_estimate=pl.CostEstimate(flops=24 << 30, bytes_accessed=1 << 20, transcendentals=0),
        name="first_tail",
    )(spots, order, c, h, weights, weights, weights, *tables, own, come, *attended, *dqs)


def last_kernel(groups, spot_ref, h_ref, gain_ref, wk_ref, wv_ref, x_ref, cos_ref, low_ref, high_ref, gin_ref, ghin_ref, *refs):
    own_refs, come_refs = refs[:groups], refs[groups:2 * groups]
    grad_ref, send_ref, keep_ref, db_ref, dgain_ref, dshift_ref, p_ref = refs[2 * groups:]
    step = pl.program_id(0)
    spot = pl.ds(pl.multiple_of(step * RB, RB), RB)
    count = wk_ref.shape[1]
    gather_rows(step, spot, (cos_ref[...], low_ref[...], high_ref[...]), own_refs, come_refs, p_ref, 0, count)
    grad = (ghin_ref[...] + mm(p_ref[spot, :count], wk_ref[...], NT) + mm(p_ref[spot, count:], wv_ref[...], NT))
    back, scaled = norm_back(x_ref[...].astype(f32), grad, gain_ref[...])
    grad_ref[...] = back + gin_ref[...]
    sums = col_sum(p_ref[spot, :].astype(f32)), col_sum(scaled), col_sum(grad)

    @pl.when(step == 0)
    def _():
        for ref, value in zip((db_ref, dgain_ref, dshift_ref), sums):
            ref[...] = value

    @pl.when(step > 0)
    def _():
        for ref, value in zip((db_ref, dgain_ref, dshift_ref), sums):
            ref[...] += value

    @pl.when(step == pl.num_programs(0) - 1)
    def _():
        half = send_ref.shape[0]
        for to in range(0, send_ref.shape[1], 512):
            dw = mm(h_ref[...], p_ref[:, to:to + 512], TN).astype(bf16)
            send_ref[:, to:to + 512] = dw[:half]
            keep_ref[:, to:to + 512] = dw[half:]


def last_tail(spots, x, h, gain, weights, tables, gin, gh, owns, comes):
    rows, width = x.shape
    cols = sum(a.shape[1] for a in owns) // 2
    steps = rows // RB
    s = jax.ShapeDtypeStruct

    def full(shape):
        return pl.BlockSpec(shape, lambda j, spot: (0, 0), pipeline_mode=pl.Buffered(1))

    def weight(at):
        return pl.BlockSpec((width, cols), lambda j, spot: (0, at // cols), pipeline_mode=pl.Buffered(1))

    block = pl.BlockSpec((RB, width), lambda j, spot: (j, 0))
    table = pl.BlockSpec((RB, PAIR), lambda j, spot: (spot[j], 0))
    own_windows, come_windows = half_windows(owns, steps)
    return pl.pallas_call(
        partial(last_kernel, len(owns)),
        grid_spec=pltpu.PrefetchScalarGridSpec(
            num_scalar_prefetch=1,
            grid=(steps,),
            in_specs=[full(h.shape), full((1, width)), weight(2 * width - cols), weight(3 * width - cols), block] + [table] * 3
            + [block, block] + own_windows + come_windows,
            out_specs=[block, full((width // 2, 2 * cols)), full((width // 2, 2 * cols)), full((1, 2 * cols)), full((1, width)),
                       full((1, width))],
            scratch_shapes=[vmem(rows, 2 * cols, dtype=bf16)],
        ),
        out_shape=[s((rows, width), f32), s((width // 2, 2 * cols), bf16), s((width // 2, 2 * cols), bf16), s((1, 2 * cols), f32),
                   s((1, width), f32), s((1, width), f32)],
        compiler_params=params(),
        cost_estimate=pl.CostEstimate(flops=12 << 30, bytes_accessed=1 << 20, transcendentals=0),
        name="last_tail",
    )(spots, h, gain.reshape(1, -1), weights, weights, x, *tables, gin, gh, *owns, *comes)


def join_kernel(groups, x_ref, w_ref, mlp_ref, b_ref, *refs):
    att_refs, (out_ref, att_ref) = refs[:groups], refs[groups:]
    at = 0
    for ref in att_refs:
        att_ref[:, at:at + ref.shape[1]] = ref[...]
        at += ref.shape[1]
    out = x_ref[...].astype(f32) + mm(att_ref[...], w_ref[...], NN) + mlp_ref[...] + b_ref[...]
    out_ref[...] = out.astype(bf16)


def join(x, attended, weights, mlp_out, bias):
    rows, width = x.shape
    s = jax.ShapeDtypeStruct
    block = pl.BlockSpec((RB, width), lambda j: (j, 0))
    return pl.pallas_call(
        partial(join_kernel, len(attended)),
        grid=(rows // RB,),
        in_specs=[block, pl.BlockSpec((width, width), lambda j: (0, 3)), block, pl.BlockSpec((1, width), lambda j: (0, 0))]
        + [pl.BlockSpec((RB, a.shape[1]), lambda j: (j, 0)) for a in attended],
        out_specs=block,
        out_shape=s((rows, width), bf16),
        scratch_shapes=[vmem(RB, width, dtype=bf16)],
        compiler_params=params(),
        cost_estimate=pl.CostEstimate(flops=12 << 30, bytes_accessed=1 << 20, transcendentals=0),
        name="join",
    )(x, weights, mlp_out, bias.reshape(1, -1), *attended)


def spread_kernel(c_ref, w_ref, out_ref):
    out_ref[...] = mm(c_ref[...], w_ref[...], NT).astype(bf16)


def spread(c, weights):
    rows, width = c.shape
    block = pl.BlockSpec((RB, width), lambda j: (j, 0))
    return pl.pallas_call(
        spread_kernel,
        grid=(rows // RB,),
        in_specs=[block, pl.BlockSpec((width, width), lambda j: (0, 3))],
        out_specs=block,
        out_shape=jax.ShapeDtypeStruct((rows, width), bf16),
        compiler_params=params(),
        cost_estimate=pl.CostEstimate(flops=1 << 20, bytes_accessed=1 << 16, transcendentals=0),
        name="spread",
    )(c, weights)


def fold(x, op):
    return op(x.reshape(x.shape[0] // 8, 8, x.shape[1]), axis=0)


def eye(size):
    return (lax.broadcasted_iota(jnp.int32, (size, size), 0) == lax.broadcasted_iota(jnp.int32, (size, size), 1)).astype(bf16)


def attention_kernel(half, n, kind_ref, owner_ref, cos_ref, sin_ref, q_ref, do_ref, *refs):
    k_refs, v_refs = refs[:2], refs[2:4]
    o_ref, dq_ref, all_ref, cont_ref, kt_ref, vt_ref, s_ref, p_ref, ds_ref, dka_ref, dva_ref = refs[4:]
    per = half // QB
    wide = n * half
    count = wide // QB
    spots = [(0, c * QB) for c in range(per)] + [(1, c * QB) for c in range((n - 1) * per)]

    ident = eye(PAIR)
    for refs_in, out in ((k_refs, kt_ref), (v_refs, vt_ref)):
        for c, (s, at) in enumerate(spots):
            out[:, c * QB:(c + 1) * QB] = refs_in[s][at:at + QB, :].T
        for c in range(per):
            out[:, wide + c * QB:wide + (c + 1) * QB] = refs_in[0][half + c * QB:half + (c + 1) * QB, :].T
    cont = slice(wide, wide + half)
    dka_ref[cont, :] = jnp.zeros((half, PAIR), f32)
    dva_ref[cont, :] = jnp.zeros((half, PAIR), f32)


    def block(qb, carry):
        own = pl.ds(pl.multiple_of(qb * QB, QB), QB)
        slot = pl.ds(pl.multiple_of(jnp.where(qb < per, qb * QB, wide + (qb - per) * QB), QB), QB)
        zero = jnp.zeros((), bf16)
        causal = lax.broadcasted_iota(jnp.int32, (QB, QB), 0) <= lax.broadcasted_iota(jnp.int32, (QB, QB), 1)
        left = lax.broadcasted_iota(jnp.int32, (QB, PAIR), 1) < HD

        def by_head(a):
            return jnp.where(left, a, zero), jnp.where(left, zero, a)

        def keys_of(some, c):
            if c == count:
                return some[0][own, :]
            s, at = spots[c]
            return some[s][at:at + QB, :]

        def cut(c):
            return slice(c * QB, (c + 1) * QB)

        ident = eye(QB)
        q_heads = by_head(q_ref[own, :])
        do_t = mm(eye(PAIR), do_ref[own, :], NT)
        upper = lax.broadcasted_iota(jnp.int32, (PAIR, QB), 0) < HD
        q_t = mm(eye(PAIR), q_ref[own, :], NT).astype(bf16)
        q_cols = jnp.where(upper, q_t, zero), jnp.where(upper, zero, q_t)
        peaks, norms, outs, deltas, scaled = [None, None], [None, None], [None, None], [None, None], [None, None]

        def scores(h):
            peak = jnp.full((8, QB), MASKED, f32)
            for c in range(count + 1):
                s = mm(keys_of(k_refs, c), q_cols[h], NN)
                if c == count:
                    s = jnp.where(causal, s, MASKED)
                    top = fold(s, jnp.max)
                else:
                    top = fold(s, jnp.max) + kind_ref[qb, c]
                s_ref[h, cut(c)] = s
                peak = jnp.maximum(peak, top)
            peaks[h] = jnp.max(peak, axis=0, keepdims=True)

        def weigh(h):
            total = jnp.zeros((8, QB), f32)
            for c in range(count + 1):
                bias = -peaks[h] if c == count else kind_ref[qb, c] - peaks[h]
                e = jnp.exp2(s_ref[h, cut(c)] + bias)
                total = total + fold(e, jnp.sum)
                p_ref[h, cut(c)] = e.astype(bf16)
            norms[h] = 1.0 / jnp.sum(total, axis=0, keepdims=True)

        def attend(h):
            lines = slice(h * HD, (h + 1) * HD)
            out = mm(vt_ref[lines, 0:wide], p_ref[h, 0:wide], NN) + mm(vt_ref[lines, slot], p_ref[h, wide:], NN)
            outs[h] = out * norms[h]
            deltas[h] = jnp.sum(outs[h] * do_t[lines], axis=0, keepdims=True) * norms[h]
            scaled[h] = do_t[lines] * norms[h]

        scores(0)
        scores(1)
        weigh(0)
        attend(0)
        weigh(1)
        attend(1)
        d_t = jnp.concatenate(scaled, axis=0).astype(bf16)
        d_cols = jnp.where(upper, d_t, zero), jnp.where(upper, zero, d_t)
        do_heads = by_head(mm(ident, d_t, NT).astype(bf16))
        grads = []
        for h in range(2):
            lines = slice(h * HD, (h + 1) * HD)
            for c in range(count + 1):
                dp = mm(keys_of(v_refs, c), d_cols[h], NN)
                ds_ref[h, cut(c)] = p_ref[h, cut(c)] * (dp - deltas[h]).astype(bf16)
            dq = mm(kt_ref[lines, 0:wide], ds_ref[h, 0:wide], NN) + mm(kt_ref[lines, slot], ds_ref[h, wide:], NN)
            a, b = dq[:ROT // 2], dq[ROT // 2:ROT]
            cosine, sine = cos_ref[:, own], sin_ref[:, own]
            grads.append(jnp.concatenate([a * cosine + b * sine, b * cosine - a * sine, dq[ROT:]], axis=0))
        for c in range(count + 1):
            at = slot if c == count else cut(c)
            dv = mm(p_ref[0, cut(c)], do_heads[0], NN) + mm(p_ref[1, cut(c)], do_heads[1], NN)
            dk = mm(ds_ref[0, cut(c)], q_heads[0], NN) + mm(ds_ref[1, cut(c)], q_heads[1], NN)
            if c == count:
                dva_ref[at, :] += dv
                dka_ref[at, :] += dk
            else:
                dva_ref[at, :] = jnp.where(qb == 0, dv, dva_ref[at, :] + dv)
                dka_ref[at, :] = jnp.where(qb == 0, dk, dka_ref[at, :] + dk)
        o_ref[own, :] = mm(ident, jnp.concatenate(outs, axis=0).astype(bf16), NT).astype(bf16)
        dq_ref[own, :] = mm(ident, (jnp.concatenate(grads, axis=0) * (HD ** (-0.5))).astype(bf16), NT).astype(bf16)

        return carry

    lax.fori_loop(0, 2 * per, block, 0)

    def flush(out, to, frm):
        rows = pl.ds(to, half)
        out[rows, :PAIR] = (dka_ref[frm:frm + half, :] * math.log(2.0)).astype(bf16)
        out[rows, PAIR:] = dva_ref[frm:frm + half, :].astype(bf16)

    flush(cont_ref, 0, wide)
    for s in range(n):
        flush(all_ref, pl.multiple_of(owner_ref[s] * half, half), s * half)


def attention(kind, owners, cos_t, sin_t, q, do, ks, vs, first, pairs):
    rows = q.shape[0]
    half = rows // 2
    n = 1 + ks[1].shape[0] // half
    wide = n * half
    keys = wide + half
    total = wide + QB
    qspec = pl.BlockSpec((rows, PAIR), lambda p: (0, p + first))
    ospec = pl.BlockSpec((rows, PAIR), lambda p: (0, p))
    table = pl.BlockSpec((ROT // 2, rows), lambda p: (0, 0))
    kspecs = [pl.BlockSpec((k.shape[0], PAIR), lambda p: (0, p + first)) for k in ks]
    gspecs = [pl.BlockSpec((size, 2 * PAIR), lambda p: (0, p)) for size in (wide, half)]
    s = jax.ShapeDtypeStruct
    pieces = pairs * rows // QB
    return pl.pallas_call(
        partial(attention_kernel, half, n),
        grid=(pairs,),
        in_specs=[pl.BlockSpec(memory_space=pltpu.SMEM), pl.BlockSpec(memory_space=pltpu.SMEM), table, table, qspec, qspec] + kspecs + kspecs,
        out_specs=[ospec, ospec] + gspecs,
        out_shape=[s((rows, pairs * PAIR), bf16), s((rows, pairs * PAIR), bf16)]
        + [s((size, 2 * pairs * PAIR), bf16) for size in (wide, half)],
        scratch_shapes=[pltpu.VMEM((PAIR, keys), bf16), pltpu.VMEM((PAIR, keys), bf16),
                        pltpu.VMEM((2, total, QB), f32), pltpu.VMEM((2, total, QB), bf16),
                        pltpu.VMEM((2, total, QB), bf16),
                        pltpu.VMEM((keys, PAIR), f32), pltpu.VMEM((keys, PAIR), f32)],
        compiler_params=pltpu.CompilerParams(vmem_limit_bytes=60 << 20),
        cost_estimate=pl.CostEstimate(flops=1 << 20, bytes_accessed=1 << 16, transcendentals=0),
        name="attention",
    )(kind, owners, cos_t, sin_t, q, do, *ks, *vs)


def pairs_of(bit, size):
    return [(a, a ^ bit) for a in range(size)]


def add_kernel(plan, *refs):
    for a, b, moves in plan:
        for source, to, target in moves:
            refs[to][target] = (refs[a][source].astype(f32) + refs[b][source].astype(f32)).astype(bf16)


def add_parts(arrays, plan, shapes, steps, load=0):
    def spec(shape):
        block = (*shape[:-1], shape[-1] // steps)
        return pl.BlockSpec(block, lambda j: (0,) * (len(shape) - 1) + (j,))

    return pl.pallas_call(
        partial(add_kernel, plan),
        grid=(steps,),
        in_specs=[spec(a.shape) for a in arrays],
        out_specs=[spec(shape) for shape in shapes],
        out_shape=[jax.ShapeDtypeStruct(shape, bf16) for shape in shapes],
        compiler_params=params(),
        cost_estimate=pl.CostEstimate(flops=(load << 30) + 1, bytes_accessed=1 << 16, transcendentals=0),
        name="add_parts",
    )(*arrays)


EVERY = slice(None)


def swap(a, bit):
    return lax.ppermute(a, "fsdp", pairs_of(bit, 8))


def steps_for(arrays):
    smallest = min(a.shape[-1] for a in arrays)
    return 4 if smallest % (4 * PAIR) == 0 else 1


def core_step(sends, keeps):
    count = len(sends)
    arrays, plan, shapes = [], [], []
    for send, keep in zip(sends, keeps):
        rows, cols = send.shape
        cut = (2, 2, 2, rows // 8, cols)
        to = 2 * count + len(shapes)
        moves = [((EVERY, 1, 0), to, (EVERY,)), ((EVERY, 0, 0), to + 1, (EVERY,)),
                 ((1, EVERY, 1), to + 2, (EVERY,)), ((0, EVERY, 1), to + 3, (EVERY,))]
        plan.append((len(arrays), len(arrays) + 1, moves))
        arrays += [keep.reshape(cut), swap(send, 1).reshape(cut)]
        shapes += [(2, rows // 8, cols)] * 4
    return add_parts(arrays, plan, shapes, steps_for(arrays))


def side_step(items):
    arrays, plan, shapes = [], [], []
    for i in range(0, len(items), 4):
        for send, keep, bit in ((items[i], items[i + 1], 2), (items[i + 2], items[i + 3], 4)):
            to = len(items) + len(shapes)
            plan.append((len(arrays), len(arrays) + 1, [((1,), to, (EVERY,)), ((0,), to + 1, (EVERY,))]))
            arrays += [keep, swap(send, bit)]
            shapes += [keep.shape[1:]] * 2
    return add_parts(arrays, plan, shapes, steps_for(arrays))


def last_step(items, load=0):
    arrays, plan, shapes = [], [], []
    for i in range(0, len(items), 4):
        to = len(items) + len(shapes)
        for at, (send, keep, bit) in enumerate(((items[i], items[i + 1], 4), (items[i + 2], items[i + 3], 2))):
            plan.append((len(arrays), len(arrays) + 1, [((EVERY,), to, (at,))]))
            arrays += [keep, swap(send, bit)]
        shapes.append((2, *keep.shape))
    parts = add_parts(arrays, plan, shapes, steps_for(arrays), load)
    return [part.reshape(-1, part.shape[-1]) for part in parts]


def along(part):
    return lax.psum_scatter(part, "ctx", scatter_dimension=0, tiled=True)


def after(value, *others):
    return lax.optimization_barrier((value, *others))[0]


def kept_after(items, *others):
    return [after(a, *others) if i % 2 else a for i, a in enumerate(items)]


def fast(inputs, cotangent, positions, segments, ln1_gain, ln1_bias, w_qkv, b_qkv, w_attn_out, b_out,
         ln2_gain, ln2_bias, w_in, b_in, w_out):
    x, grad_out, pos = inputs[0], cotangent[0], positions[0]
    rows, width = x.shape
    half = rows // 2
    n = lax.axis_size("ctx")
    ring = [(i, (i + 1) % n) for i in range(n)]
    back = [(i, (i - 1) % n) for i in range(n)]
    me, place = lax.axis_index("fsdp"), lax.axis_index("ctx")
    relative = [4 * dy + 2 * dx + 1 - keep for keep in (0, 1) for dy in (0, 1) for dx in (0, 1)]
    order = jnp.bitwise_xor(me, jnp.array(relative, jnp.int32))
    owners = lax.rem(place + n - jnp.arange(n), n)
    far = [None] * n
    far[0] = x[:half]
    for s in range(1, n):
        far[s] = lax.ppermute(far[s - 1], "ctx", ring)
    spots = [pos[::RB] // RB]
    for s in range(1, n):
        spots.append(lax.ppermute(spots[0][:half // RB], "ctx", [(i, (i + s) % n) for i in range(n)]))
    mine = (ln1_gain, ln1_bias, b_qkv, b_out, ln2_gain, ln2_bias, b_in)
    small = lax.all_gather(jnp.concatenate(mine).reshape(1, -1), "fsdp", axis=0, tiled=True)
    full, at = [], 0
    for a in mine:
        full.append(small[:, at:at + a.shape[0]].reshape(-1).astype(f32))
        at += a.shape[0]
    gain_attn, shift_attn, bias_qkv, bias_out, gain_mlp, shift_mlp, bias_in = full
    weights = lax.all_gather(jnp.concatenate([w_qkv, w_attn_out], axis=1), "fsdp", axis=0, tiled=True)

    lane = jnp.arange(PAIR) % HD
    inverse = jnp.exp(-math.log(10000.0) * (2.0 / ROT) * (lane % (ROT // 2)).astype(f32))
    angles = jnp.arange(n * half + CLEN).astype(f32)[:, None] * inverse[None, :]
    sine = jnp.sin(angles)
    tables = (jnp.where(lane < ROT, jnp.cos(angles), 1.0), jnp.where(lane < ROT // 2, sine, 0.0),
              jnp.where((lane >= ROT // 2) & (lane < ROT), sine, 0.0))
    angles_t = pos.astype(f32)[None, :] * inverse[:ROT // 2, None]
    cos_t, sin_t = jnp.cos(angles_t), jnp.sin(angles_t)

    normed, queries, own_keys, own_values = qkv(
        spots[0], order, [after(x, far[n - 2], *spots[1:])], gain_attn, shift_attn, weights, bias_qkv, tables)
    far_keys, far_values = qkv(
        jnp.concatenate(spots[1:]), order, far[1:], gain_attn, shift_attn, weights, bias_qkv, tables)
    keys, values = (own_keys, far_keys), (own_values, far_values)
    grad_att = spread(grad_out, weights)
    weight_in = lax.all_gather(after(w_in, far[1], *full, *tables, cos_t, sin_t), "fsdp", axis=0, tiled=True)
    weight_out = lax.all_gather(after(w_out, far[1], *full, *tables, cos_t, sin_t), "fsdp", axis=0, tiled=True)

    per = half // QB
    earlier = jnp.stack([spots[s][0] < spots[0][0] for s in range(1, n)])
    local_row = jnp.arange(2 * per)[:, None]
    seen_own = local_row > jnp.arange(per)[None, :]
    seen_far = jnp.repeat(earlier[None, :] | (local_row >= per), per, axis=1)
    kind = jnp.where(jnp.concatenate([seen_own, seen_far], axis=1), 0.0, MASKED).astype(f32)

    attended, grad_q, own_kv, come_kv = [], [], [], []

    def attend(first, count, wait):
        out = attention(kind, owners, cos_t, sin_t, after(queries, *wait), grad_att, keys, values, first, count)
        attended.append(out[0])
        grad_q.append(out[1])
        come_kv.append(lax.psum_scatter(out[2], "ctx", scatter_dimension=0, tiled=True))
        own_kv.append(out[3])

    attend(0, 4, ())
    mlp_out, grad_mlp, in_send, in_keep, out_send, out_keep, db_in, db_out, dgain_mlp, dshift_mlp = mlp(
        order, after(x, *attended), grad_out, gain_mlp, shift_mlp, weight_in, bias_in, weight_out)
    attend(4, 1, (mlp_out,))
    steps_mlp = core_step([out_send, in_send], [out_keep, in_keep])
    attend(5, 3, (*attended, *steps_mlp))
    steps_mlp = side_step(kept_after(steps_mlp, *attended))
    output = join(after(x, *steps_mlp), attended, weights, mlp_out, bias_out)
    first_send, first_keep, grad_heads, db_first = first_tail(
        spots[0], order, after(grad_out, output), normed, weights, tables, attended, grad_q, own_kv[0], come_kv[0])
    part_out, part_in = last_step(kept_after(steps_mlp, grad_heads), 48)
    steps_first = core_step([first_send], [first_keep])
    grad_inputs, last_send, last_keep, db_last, dgain_attn, dshift_attn = last_tail(
        spots[0], after(x, part_out, part_in, *steps_first), normed, gain_attn, weights, tables, grad_mlp, grad_heads,
        own_kv[1:], come_kv[1:])
    sum_out, sum_in = along(part_out), along(part_in)
    steps_first = side_step(kept_after(steps_first, last_send))
    cols = db_last.shape[1] // 2
    split = [width, width + (db_first.shape[1] - width) // 2]
    db_q, db_k, db_v = jnp.split(db_first, split, axis=1)
    db_qkv = jnp.concatenate([db_q, db_k, db_last[:, :cols], db_v, db_last[:, cols:]], axis=1)
    parts = 8 * n
    smalls = [a.reshape(parts, -1) for a in (dgain_attn, dshift_attn, db_qkv, db_out, dgain_mlp, dshift_mlp, db_in)]
    flat = jnp.concatenate(smalls, axis=1).astype(bf16).reshape(parts, -1, PAIR)
    lines = flat.shape[1]
    packed = jnp.pad(flat, ((0, 0), (0, width // parts - lines), (0, 0))).reshape(width, PAIR)
    packed = packed.reshape(8, width // 8, PAIR)[order].reshape(2, width // 2, PAIR)
    steps_last = core_step([jnp.concatenate([last_send, packed[0]], axis=1)],
                           [jnp.concatenate([after(last_keep, *steps_first), packed[1]], axis=1)])
    part_first = last_step(steps_first)
    part_last = last_step(side_step(kept_after(steps_last, *part_first)))
    total = along(jnp.concatenate([*part_first, *part_last], axis=1))
    ends = [width, 2 * width, split[1] + width, db_first.shape[1] + width]
    ends += [ends[-1] + cols, ends[-1] + 2 * cols]
    sum_attn, sum_q, sum_k, sum_v, end_k, end_v, packed = jnp.split(total, ends, axis=1)
    sum_qkv = jnp.concatenate([sum_q, sum_k, end_k, sum_v, end_v], axis=1)
    packed = packed[:lines].astype(f32).reshape(-1)
    done, at = [], 0
    for a in smalls:
        done.append(packed[at:at + a.shape[1]])
        at += a.shape[1]
    return (output[None], grad_inputs[None], done[0], done[1], sum_qkv.astype(f32), done[2], sum_attn.astype(f32),
            done[3], done[4], done[5], sum_in.astype(f32), done[6], sum_out.astype(f32))


def local(*args):
    half = args[0].shape[1] // 2
    if args[0].shape[0] == 1 and half % CLEN == 0 and lax.axis_size("fsdp") == 8:
        return fast(*args)
    return generic(*args)


def generic(
    inputs,
    cotangent,
    positions,
    segments,
    ln1_gain,
    ln1_bias,
    w_qkv,
    b_qkv,
    w_attn_out,
    b_out,
    ln2_gain,
    ln2_bias,
    w_in,
    b_in,
    w_out,
):
    shards = (
        ln1_gain,
        ln1_bias,
        w_qkv,
        b_qkv,
        w_attn_out,
        b_out,
        ln2_gain,
        ln2_bias,
        w_in,
        b_in,
        w_out,
    )
    params = (
        lax.all_gather(shards[0], "fsdp", axis=0, tiled=True),
        lax.all_gather(shards[1], "fsdp", axis=0, tiled=True),
        lax.all_gather(shards[2], "fsdp", axis=0, tiled=True),
        lax.all_gather(shards[3], "fsdp", axis=0, tiled=True),
        lax.all_gather(shards[4], "fsdp", axis=0, tiled=True),
        lax.all_gather(shards[5], "fsdp", axis=0, tiled=True),
        lax.all_gather(shards[6], "fsdp", axis=0, tiled=True),
        lax.all_gather(shards[7], "fsdp", axis=0, tiled=True),
        lax.all_gather(shards[8], "fsdp", axis=0, tiled=True),
        lax.all_gather(shards[9], "fsdp", axis=0, tiled=True),
        lax.all_gather(shards[10], "fsdp", axis=0, tiled=True),
    )
    groups, local_len, width = inputs.shape
    rows_total = groups * local_len
    block = math.gcd(local_len, 256)
    label_pos, label_seg = (
        lax.all_gather(positions, "ctx", axis=1, tiled=True),
        lax.all_gather(segments, "ctx", axis=1, tiled=True),
    )
    count = label_pos.shape[1] // block
    f32 = jnp.float32
    bf16 = jnp.bfloat16
    (
        gain_attn,
        shift_attn,
        weight_qkv,
        bias_qkv,
        weight_attn,
        bias_out,
        gain_mlp,
        shift_mlp,
        weight_in,
        bias_in,
        weight_out,
    ) = params
    flat_in = inputs.reshape(rows_total, width).astype(f32)
    normed_attn = layer_norm(flat_in, gain_attn.astype(f32), shift_attn.astype(f32)).astype(bf16)
    normed_mlp = layer_norm(flat_in, gain_mlp.astype(f32), shift_mlp.astype(f32)).astype(bf16)
    projected = jnp.dot(normed_attn, weight_qkv, preferred_element_type=f32) + bias_qkv.astype(f32)
    cosine, sine = rotary_tables(positions)

    def split_heads(columns):
        return columns.reshape(groups, local_len, HEADS, HD)

    scale = HD ** (-0.5)
    queries = (rotate(split_heads(projected[:, :width]), cosine, sine) * scale).astype(bf16)
    keys_own = rotate(split_heads(projected[:, width : 2 * width]), cosine, sine).astype(bf16)
    values_own = split_heads(projected[:, 2 * width :]).astype(bf16)
    keys_all, values_all = (
        lax.all_gather(keys_own, "ctx", axis=1, tiled=True),
        lax.all_gather(values_own, "ctx", axis=1, tiled=True),
    )

    def key_block(index):
        start = index * block
        keys_blk = lax.dynamic_slice_in_dim(keys_all, start, block, 1)
        values_blk = lax.dynamic_slice_in_dim(values_all, start, block, 1)
        mask = allowed_mask(
            positions,
            segments,
            lax.dynamic_slice_in_dim(label_pos, start, block, 1),
            lax.dynamic_slice_in_dim(label_seg, start, block, 1),
        )
        return (keys_blk, values_blk, mask)

    def total_step(carry, index):
        peak, total = carry
        keys_blk, values_blk, mask = key_block(index)
        scores = jnp.where(mask, scores_of(queries, keys_blk), MASKED)
        fresh = jnp.maximum(peak, jnp.max(scores, axis=-1))
        added = jnp.sum(jnp.where(mask, jnp.exp(scores - fresh[..., None]), 0.0), axis=-1)
        return ((fresh, total * jnp.exp(peak - fresh) + added), None)

    stat_shape = (groups, HEADS, local_len)
    (peak, total), unused = lax.scan(
        total_step,
        (jnp.full(stat_shape, MASKED, f32), jnp.zeros(stat_shape, f32)),
        jnp.arange(count),
    )
    log_total = peak + jnp.log(total)

    def attend_step(rounded_sum, index):
        keys_blk, values_blk, mask = key_block(index)
        probs = jnp.where(mask, jnp.exp(scores_of(queries, keys_blk) - log_total[..., None]), 0.0)
        rounded_sum = rounded_sum + jnp.einsum(
            "ghqk,gkhd->gqhd", probs.astype(bf16), values_blk, preferred_element_type=f32
        )
        return (rounded_sum, None)

    head_shape = (groups, local_len, HEADS, HD)
    rounded_sum, unused = lax.scan(attend_step, jnp.zeros(head_shape, f32), jnp.arange(count))
    attended = rounded_sum.reshape(rows_total, width).astype(bf16)
    pre_act = jnp.dot(normed_mlp, weight_in, preferred_element_type=f32) + bias_in.astype(f32)
    activated = jax.nn.gelu(pre_act, approximate=False).astype(bf16)
    output = (
        flat_in
        + jnp.dot(attended, weight_attn, preferred_element_type=f32)
        + jnp.dot(activated, weight_out, preferred_element_type=f32)
        + bias_out.astype(f32)
    )
    (
        gain_attn,
        shift_attn,
        weight_qkv,
        bias_qkv,
        weight_attn,
        bias_out,
        gain_mlp,
        shift_mlp,
        weight_in,
        bias_in,
        weight_out,
    ) = params
    grad_out = cotangent.reshape(rows_total, width)
    grad_bias_out = jnp.sum(grad_out.astype(f32), axis=0)
    grad_weight_out = jnp.einsum("rf,rd->fd", activated, grad_out, preferred_element_type=f32)
    grad_act = jnp.einsum("rd,fd->rf", grad_out, weight_out, preferred_element_type=f32)
    unused, gelu_back = jax.vjp(partial(jax.nn.gelu, approximate=False), pre_act)
    grad_pre = gelu_back(grad_act)[0].astype(bf16)
    grad_weight_in = jnp.einsum("rd,rf->df", normed_mlp, grad_pre, preferred_element_type=f32)
    grad_bias_in = jnp.sum(grad_pre.astype(f32), axis=0)
    grad_normed_mlp = jnp.einsum("rf,df->rd", grad_pre, weight_in, preferred_element_type=f32)
    grad_weight_attn = jnp.einsum("ra,rd->ad", attended, grad_out, preferred_element_type=f32)
    grad_att = (
        jnp.einsum("rd,ad->ra", grad_out, weight_attn, preferred_element_type=f32)
        .astype(bf16)
        .reshape(head_shape)
    )
    delta = jnp.einsum(
        "gqhd,gqhd->ghq", grad_att.astype(f32), rounded_sum, precision=lax.Precision.HIGHEST
    )

    def back_step(carry, index):
        keys_blk, values_blk, mask = key_block(index)
        rounded, grad_scores = block_grads(
            queries, grad_att, log_total, delta, mask, keys_blk, values_blk
        )
        carry = carry + jnp.einsum(
            "ghqk,gkhd->gqhd", grad_scores, keys_blk, preferred_element_type=f32
        )
        key_term = jnp.einsum("ghqk,gqhd->gkhd", grad_scores, queries, preferred_element_type=f32)
        value_term = jnp.einsum("ghqk,gqhd->gkhd", rounded, grad_att, preferred_element_type=f32)
        return (carry, (key_term, value_term))

    grad_queries, (key_terms, value_terms) = lax.scan(
        back_step, jnp.zeros(head_shape, f32), jnp.arange(count)
    )
    key_sums, value_sums = (
        lax.psum_scatter(
            key_terms.astype(jnp.bfloat16), "ctx", scatter_dimension=0, tiled=True
        ).astype(jnp.float32),
        lax.psum_scatter(
            value_terms.astype(jnp.bfloat16), "ctx", scatter_dimension=0, tiled=True
        ).astype(jnp.float32),
    )
    grad_keys = jnp.transpose(key_sums, (1, 0, 2, 3, 4)).reshape(head_shape)
    grad_values = jnp.transpose(value_sums, (1, 0, 2, 3, 4)).reshape(head_shape)
    grad_q_pre = unrotate(grad_queries * scale, cosine, sine).reshape(rows_total, width)
    grad_k_pre = unrotate(grad_keys, cosine, sine).reshape(rows_total, width)
    grad_projected = jnp.concatenate(
        [grad_q_pre, grad_k_pre, grad_values.reshape(rows_total, width)], axis=1
    ).astype(bf16)
    grad_weight_qkv = jnp.einsum(
        "rd,re->de", normed_attn, grad_projected, preferred_element_type=f32
    )
    grad_bias_qkv = jnp.sum(grad_projected.astype(f32), axis=0)
    grad_normed_attn = jnp.einsum(
        "re,de->rd", grad_projected, weight_qkv, preferred_element_type=f32
    )
    unused, norm_back_attn = jax.vjp(
        layer_norm, flat_in, gain_attn.astype(f32), shift_attn.astype(f32)
    )
    grad_in_attn, grad_gain_attn, grad_shift_attn = norm_back_attn(grad_normed_attn)
    unused, norm_back_mlp = jax.vjp(
        layer_norm, flat_in, gain_mlp.astype(f32), shift_mlp.astype(f32)
    )
    grad_in_mlp, grad_gain_mlp, grad_shift_mlp = norm_back_mlp(grad_normed_mlp)
    grad_inputs = (grad_out.astype(f32) + grad_in_attn + grad_in_mlp).reshape(
        groups, local_len, width
    )
    sums = (
        lax.psum_scatter(grad_gain_attn, ("fsdp", "ctx"), scatter_dimension=0, tiled=True),
        lax.psum_scatter(grad_shift_attn, ("fsdp", "ctx"), scatter_dimension=0, tiled=True),
        lax.psum_scatter(grad_weight_qkv, ("fsdp", "ctx"), scatter_dimension=0, tiled=True),
        lax.psum_scatter(grad_bias_qkv, ("fsdp", "ctx"), scatter_dimension=0, tiled=True),
        lax.psum_scatter(grad_weight_attn, ("fsdp", "ctx"), scatter_dimension=0, tiled=True),
        lax.psum_scatter(grad_bias_out, ("fsdp", "ctx"), scatter_dimension=0, tiled=True),
        lax.psum_scatter(grad_gain_mlp, ("fsdp", "ctx"), scatter_dimension=0, tiled=True),
        lax.psum_scatter(grad_shift_mlp, ("fsdp", "ctx"), scatter_dimension=0, tiled=True),
        lax.psum_scatter(grad_weight_in, ("fsdp", "ctx"), scatter_dimension=0, tiled=True),
        lax.psum_scatter(grad_bias_in, ("fsdp", "ctx"), scatter_dimension=0, tiled=True),
        lax.psum_scatter(grad_weight_out, ("fsdp", "ctx"), scatter_dimension=0, tiled=True),
    )
    result = output.reshape(groups, local_len, width).astype(bf16)
    return (
        result,
        grad_inputs,
        sums[0],
        sums[1],
        sums[2],
        sums[3],
        sums[4],
        sums[5],
        sums[6],
        sums[7],
        sums[8],
        sums[9],
        sums[10],
    )


def solution(mesh):
    in_specs = (
        P("fsdp", "ctx", None),
        P("fsdp", "ctx", None),
        P("fsdp", "ctx"),
        P("fsdp", "ctx"),
        P("fsdp"),
        P("fsdp"),
        P("fsdp", None),
        P("fsdp"),
        P("fsdp", None),
        P("fsdp"),
        P("fsdp"),
        P("fsdp"),
        P("fsdp", None),
        P("fsdp"),
        P("fsdp", None),
    )
    out_specs = (
        P("fsdp", "ctx", None),
        P("fsdp", "ctx", None),
        P(("fsdp", "ctx")),
        P(("fsdp", "ctx")),
        P(("fsdp", "ctx"), None),
        P(("fsdp", "ctx")),
        P(("fsdp", "ctx"), None),
        P(("fsdp", "ctx")),
        P(("fsdp", "ctx")),
        P(("fsdp", "ctx")),
        P(("fsdp", "ctx"), None),
        P(("fsdp", "ctx")),
        P(("fsdp", "ctx"), None),
    )
    return jax.shard_map(local, mesh=mesh, in_specs=in_specs, out_specs=out_specs, check_vma=False)
```

```python
from functools import partial
import math

import jax
import jax.numpy as jnp
from jax import lax
from jax.experimental import pallas as pl
from jax.experimental.pallas import tpu as pltpu
from jax.sharding import PartitionSpec as P

HEADS = 16
HD = 64
ROT = 16
CLEN = 256
QB = 256
RB = 256
PAIR = 2 * HD
bf16 = jnp.bfloat16
f32 = jnp.float32
NN = (((1,), (0,)), ((), ()))
NT = (((1,), (1,)), ((), ()))
TN = (((0,), (0,)), ((), ()))


NORM_EPS = 1e-05
MASKED = -1e30


def layer_norm(values, scaling, offset):
    average = jnp.mean(values, axis=-1, keepdims=True)
    centered = values - average
    variance = jnp.mean(centered * centered, axis=-1, keepdims=True)
    return centered * lax.rsqrt(variance + NORM_EPS) * scaling + offset


def rotary_tables(positions):
    halfway = ROT // 2
    spacing = jnp.arange(halfway, dtype=jnp.float32) * (2.0 / ROT)
    inverse = jnp.exp(-math.log(10000.0) * spacing)
    angles = positions.astype(jnp.float32)[..., None] * inverse
    return (jnp.cos(angles), jnp.sin(angles))


def rotate(heads_in, cosine, sine):
    halfway = ROT // 2
    cosine = cosine[..., None, :]
    sine = sine[..., None, :]
    first = heads_in[..., :halfway]
    second = heads_in[..., halfway:ROT]
    return jnp.concatenate(
        [first * cosine - second * sine, second * cosine + first * sine, heads_in[..., ROT:]],
        axis=-1,
    )


def unrotate(grads_in, cosine, sine):
    halfway = ROT // 2
    cosine = cosine[..., None, :]
    sine = sine[..., None, :]
    first = grads_in[..., :halfway]
    second = grads_in[..., halfway:ROT]
    return jnp.concatenate(
        [first * cosine + second * sine, second * cosine - first * sine, grads_in[..., ROT:]],
        axis=-1,
    )


def allowed_mask(query_pos, query_seg, key_pos, key_seg):
    same_doc = (key_seg[:, None, :] == 0) | (key_seg[:, None, :] == query_seg[:, :, None])
    causal = key_pos[:, None, :] <= query_pos[:, :, None]
    return (same_doc & causal)[:, None]


def scores_of(queries, keys_blk):
    return jnp.einsum("gqhd,gkhd->ghqk", queries, keys_blk, preferred_element_type=jnp.float32)


def block_grads(queries, grad_att, log_total, delta, mask, keys_blk, values_blk):
    probs = jnp.where(mask, jnp.exp(scores_of(queries, keys_blk) - log_total[..., None]), 0.0)
    dprobs = jnp.einsum("gqhd,gkhd->ghqk", grad_att, values_blk, preferred_element_type=jnp.float32)
    grad_scores = (probs * (dprobs - delta[..., None])).astype(jnp.bfloat16)
    return (probs.astype(jnp.bfloat16), grad_scores)


def mm(a, b, dims):
    return lax.dot_general(a, b, dims, preferred_element_type=f32)


def row_stats(x):
    average = jnp.mean(x, axis=1, keepdims=True)
    centered = x - average
    return centered, lax.rsqrt(jnp.mean(centered * centered, axis=1, keepdims=True) + NORM_EPS)


def norm_rows(x, scaling, offset):
    centered, inverse = row_stats(x)
    return (centered * inverse * scaling + offset).astype(bf16)


def norm_back(x, grad, scaling):
    centered, inverse = row_stats(x)
    unit = centered * inverse
    e = grad * scaling
    inner = e - jnp.mean(e, axis=1, keepdims=True) - unit * jnp.mean(e * unit, axis=1, keepdims=True)
    return inverse * inner, grad * unit


def col_sum(a):
    return jnp.sum(a, axis=0, keepdims=True)


def vmem(*shape, dtype=f32):
    return pltpu.VMEM(shape, dtype)


def params():
    return pltpu.CompilerParams(vmem_limit_bytes=60 << 20)


ROOT = math.sqrt(0.5)
DENS = 1.0 / math.sqrt(2.0 * math.pi)


def reorder(order_ref, source, target):
    size = source.shape[1] // order_ref.shape[0]
    for i in range(order_ref.shape[0]):
        at = pl.multiple_of(order_ref[i] * size, size)
        target[:, i * size:(i + 1) * size] = source[:, pl.ds(at, size)]


def mlp_kernel(order_ref, x_ref, c_ref, gain_ref, shift_ref, win_ref, bin_ref, wout_ref,
               out_ref, gin_ref, dwin_send, dwin_keep, dwout_send, dwout_keep, dbin_ref, dbout_ref, dgain_ref, dshift_ref,
               h_ref, turned_ref, act_ref, gp_ref, gh_ref):
    step = pl.program_id(0)
    rows = x_ref.shape[0]
    blocks = [slice(r, r + RB) for r in range(0, rows, RB)]

    @pl.when(step == 0)
    def _():
        for r in blocks:
            h_ref[r, :] = norm_rows(x_ref[r, :].astype(f32), gain_ref[...], shift_ref[...])
            out_ref[r, :] = jnp.zeros((RB, out_ref.shape[1]), f32)
            gh_ref[r, :] = jnp.zeros((RB, gh_ref.shape[1]), f32)
        reorder(order_ref, h_ref, turned_ref)

    dbin = jnp.zeros(dbin_ref.shape, f32)
    for r in blocks:
        pre = mm(h_ref[r, :], win_ref[...], NN) + bin_ref[...]
        phi = 0.5 + 0.5 * lax.erf(pre * ROOT)
        act_ref[r, :] = (pre * phi).astype(bf16)
        gp = phi + pre * (DENS * jnp.exp(-0.5 * (pre * pre)))
        gact = mm(c_ref[r, :], wout_ref[...], NT)
        gpre = (gact * gp).astype(bf16)
        gp_ref[r, :] = gpre
        dbin = dbin + col_sum(gpre.astype(f32))
    for r in blocks:
        out_ref[r, :] += mm(act_ref[r, :], wout_ref[...], NN)
        gh_ref[r, :] += mm(gp_ref[r, :], win_ref[...], NT)
    dwout = mm(act_ref[...], c_ref[...], TN).astype(bf16)
    middle = pl.num_programs(0) // 2

    @pl.when(step < middle)
    def _():
        dwout_send[...] = dwout

    @pl.when(step >= middle)
    def _():
        dwout_keep[...] = dwout

    dwin = mm(turned_ref[...], gp_ref[...], TN).astype(bf16)
    dwin_send[...] = dwin[:dwin_send.shape[0]]
    dwin_keep[...] = dwin[dwin_send.shape[0]:]
    dbin_ref[...] = dbin

    @pl.when(step == pl.num_programs(0) - 1)
    def _():
        dgain = jnp.zeros(dgain_ref.shape, f32)
        dshift = jnp.zeros(dshift_ref.shape, f32)
        dbout = jnp.zeros(dbout_ref.shape, f32)
        for r in blocks:
            grad = gh_ref[r, :]
            back, scaled = norm_back(x_ref[r, :].astype(f32), grad, gain_ref[...])
            c = c_ref[r, :].astype(f32)
            gin_ref[r, :] = back + c
            dgain += col_sum(scaled)
            dshift += col_sum(grad)
            dbout += col_sum(c)
        dgain_ref[...] = dgain
        dshift_ref[...] = dshift
        dbout_ref[...] = dbout


def mlp(order, x, c, gain, shift, weight_in, bias_in, weight_out):
    rows, width = x.shape
    ff = weight_in.shape[1]
    steps = order.shape[0]
    fc = ff // steps
    whole = pl.BlockSpec((rows, width), lambda j, o: (0, 0))
    line = pl.BlockSpec((1, width), lambda j, o: (0, 0))
    down = pl.BlockSpec((width // 2, fc), lambda j, o: (0, o[j]))
    s = jax.ShapeDtypeStruct
    return pl.pallas_call(
        mlp_kernel,
        grid_spec=pltpu.PrefetchScalarGridSpec(
            num_scalar_prefetch=1,
            grid=(steps,),
            in_specs=[whole, whole, line, line, pl.BlockSpec((width, fc), lambda j, o: (0, o[j])),
                      pl.BlockSpec((1, fc), lambda j, o: (0, o[j])), pl.BlockSpec((fc, width), lambda j, o: (o[j], 0))],
            out_specs=[whole, whole, down, down,
                       pl.BlockSpec((fc, width), lambda j, o: (jnp.minimum(j, steps // 2 - 1), 0)),
                       pl.BlockSpec((fc, width), lambda j, o: (jnp.maximum(j - steps // 2, 0), 0)),
                       pl.BlockSpec((1, fc), lambda j, o: (0, o[j])), line, line, line],
            scratch_shapes=[vmem(rows, width, dtype=bf16), vmem(rows, width, dtype=bf16), vmem(rows, fc, dtype=bf16),
                            vmem(rows, fc, dtype=bf16), vmem(rows, width)],
        ),
        out_shape=[s((rows, width), f32), s((rows, width), f32), s((width // 2, ff), bf16), s((width // 2, ff), bf16),
                   s((ff // 2, width), bf16), s((ff // 2, width), bf16), s((1, ff), f32), s((1, width), f32),
                   s((1, width), f32), s((1, width), f32)],
        compiler_params=params(),
        cost_estimate=pl.CostEstimate(flops=1 << 20, bytes_accessed=1 << 16, transcendentals=0),
        name="mlp",
    )(order, x, c, gain.reshape(1, -1), shift.reshape(1, -1), weight_in, bias_in.reshape(1, -1), weight_out)


def turn_lanes(u, cosine, low, high, sign):
    half = ROT // 2
    parts = []
    for at in range(0, u.shape[1], PAIR):
        g = u[:, at:at + PAIR]
        parts.append(g * cosine + sign * (pltpu.roll(g, half, 1) * high - pltpu.roll(g, PAIR - half, 1) * low))
    return jnp.concatenate(parts, axis=1)


def qkv_kernel(far, spot_ref, order_ref, gain_ref, shift_ref, w_ref, b_ref, cos_ref, low_ref, high_ref, *refs):
    with_q = far == 0
    if with_q:
        x_ref, outs = refs[0], refs[1:]
    else:
        x_refs, outs, x_ref = refs[:far], refs[far:-1], refs[-1]
        step = pl.program_id(0)
        per = pl.num_programs(0) // far
        for s in range(far):
            @pl.when(step // per == s)
            def _(s=s):
                x_ref[...] = x_refs[s][...]
    width = x_ref.shape[1]
    h = norm_rows(x_ref[...].astype(f32), gain_ref[...], shift_ref[...])
    tables = (cos_ref[...], low_ref[...], high_ref[...])
    if with_q:
        h_ref, q_ref, k_ref, v_ref, plain_ref = outs
        plain_ref[...] = h
        reorder(order_ref, plain_ref, h_ref)
        q = mm(h, w_ref[:, :width], NN) + b_ref[:, :width]
        q_ref[...] = (turn_lanes(q, *tables, 1.0) * (HD ** (-0.5) / math.log(2.0))).astype(bf16)
    else:
        k_ref, v_ref = outs
    k = mm(h, w_ref[:, width:2 * width], NN) + b_ref[:, width:2 * width]
    k_ref[...] = turn_lanes(k, *tables, 1.0).astype(bf16)
    v_ref[...] = (mm(h, w_ref[:, 2 * width:], NN) + b_ref[:, 2 * width:]).astype(bf16)


def qkv(spots, order, xs, gain, shift, weight, bias, tables):
    far = len(xs) if len(xs) > 1 else 0
    rows, width = xs[0].shape
    per = rows // RB
    total = len(xs) * rows
    s = jax.ShapeDtypeStruct((total, width), bf16)
    block = pl.BlockSpec((RB, width), lambda j, spot, o: (j, 0))
    line = pl.BlockSpec((1, width), lambda j, spot, o: (0, 0))
    table = pl.BlockSpec((RB, PAIR), lambda j, spot, o: (spot[j], 0))
    count = 2 if far else 4

    def window(i):
        return pl.BlockSpec((RB, width), lambda j, spot, o: (jnp.clip(j - i * per, 0, per - 1), 0))

    return pl.pallas_call(
        partial(qkv_kernel, far),
        grid_spec=pltpu.PrefetchScalarGridSpec(
            num_scalar_prefetch=2,
            grid=(total // RB,),
            in_specs=[line, line, pl.BlockSpec((width, 3 * width), lambda j, spot, o: (0, 0)),
                      pl.BlockSpec((1, 3 * width), lambda j, spot, o: (0, 0)), table, table, table]
            + [window(i) for i in range(len(xs))],
            out_specs=[block] * count,
            scratch_shapes=[vmem(RB, width, dtype=bf16)],
        ),
        out_shape=[s] * count,
        compiler_params=params(),
        cost_estimate=pl.CostEstimate(flops=1 << 20, bytes_accessed=1 << 16, transcendentals=0),
        name="kv_remote" if far else "qkv_own",
    )(spots, order, gain.reshape(1, -1), shift.reshape(1, -1), weight, bias.reshape(1, -1), *tables, *xs)


def gather_rows(step, spot, tables, own_refs, come_refs, p_ref, k_at, v_at):
    half = pl.num_programs(0) // 2
    columns = [(g, at) for g in range(len(own_refs)) for at in range(0, own_refs[g].shape[1], 2 * PAIR)]

    def put(refs):
        for to, (g, at) in enumerate(columns):
            turned = turn_lanes(refs[g][:, at:at + PAIR].astype(f32), *tables, -1.0).astype(bf16)
            p_ref[spot, k_at + to * PAIR:k_at + (to + 1) * PAIR] = turned
            p_ref[spot, v_at + to * PAIR:v_at + (to + 1) * PAIR] = refs[g][:, at + PAIR:at + 2 * PAIR]

    @pl.when(step < half)
    def _():
        put(come_refs)

    @pl.when(step >= half)
    def _():
        put(own_refs)


def half_windows(arrays, count):
    half = count // 2
    come = [pl.BlockSpec((RB, a.shape[1]), lambda j, *o: (jnp.clip(j, 0, half - 1), 0)) for a in arrays]
    own = [pl.BlockSpec((RB, a.shape[1]), lambda j, *o: (jnp.clip(j - half, 0, half - 1), 0)) for a in arrays]
    return own, come


def first_kernel(groups, spot_ref, order_ref, c_ref, h_ref, wq_ref, wk_ref, wv_ref, cos_ref, low_ref, high_ref, own_ref,
                 come_ref, *refs):
    att_refs, dq_refs = refs[:groups], refs[groups:2 * groups]
    send_ref, keep_ref, gh_ref, db_ref, p_ref, att_ref, turned_ref = refs[2 * groups:]
    step = pl.program_id(0)
    width = c_ref.shape[1]
    spot = pl.ds(pl.multiple_of(step * RB, RB), RB)
    at = 0
    for g in range(groups):
        size = att_refs[g].shape[1]
        att_ref[:, at:at + size] = att_refs[g][...]
        p_ref[spot, at:at + size] = dq_refs[g][...]
        at += size
    for i in range(order_ref.shape[0]):
        size = width // order_ref.shape[0]
        lanes = pl.ds(pl.multiple_of(order_ref[i] * size, size), size)
        turned_ref[spot, i * size:(i + 1) * size] = att_ref[:, lanes]
    count = wk_ref.shape[1]
    gather_rows(step, spot, (cos_ref[...], low_ref[...], high_ref[...]), [own_ref], [come_ref], p_ref, width, width + count)
    gh_ref[...] = (mm(p_ref[spot, :width], wq_ref[...], NT) + mm(p_ref[spot, width:width + count], wk_ref[...], NT)
                   + mm(p_ref[spot, width + count:], wv_ref[...], NT))
    db = col_sum(p_ref[spot, :].astype(f32))

    @pl.when(step == 0)
    def _():
        db_ref[...] = db

    @pl.when(step > 0)
    def _():
        db_ref[...] += db

    @pl.when(step == pl.num_programs(0) - 1)
    def _():
        half = send_ref.shape[0]
        for to in range(0, send_ref.shape[1], 512):
            if to < width:
                dw = mm(turned_ref[...], c_ref[:, to:to + 512], TN)
            else:
                dw = mm(h_ref[...], p_ref[:, to - width:to - width + 512], TN)
            dw = dw.astype(bf16)
            send_ref[:, to:to + 512] = dw[:half]
            keep_ref[:, to:to + 512] = dw[half:]


def first_tail(spots, order, c, h, weights, tables, attended, dqs, own, come):
    rows, width = c.shape
    cols = own.shape[1] // 2
    steps = rows // RB
    total = 2 * width + 2 * cols
    s = jax.ShapeDtypeStruct

    def full(shape):
        return pl.BlockSpec(shape, lambda j, spot, o: (0, 0), pipeline_mode=pl.Buffered(1))

    def weight(size, at):
        return pl.BlockSpec((width, size), lambda j, spot, o: (0, at // size), pipeline_mode=pl.Buffered(1))

    def window(a):
        return pl.BlockSpec((RB, a.shape[1]), lambda j, spot, o: (j, 0))

    table = pl.BlockSpec((RB, PAIR), lambda j, spot, o: (spot[j], 0))
    owns, comes = half_windows([own], steps)
    return pl.pallas_call(
        partial(first_kernel, len(dqs)),
        grid_spec=pltpu.PrefetchScalarGridSpec(
            num_scalar_prefetch=2,
            grid=(steps,),
            in_specs=[full(c.shape), full(h.shape), weight(width, 0), weight(cols, width), weight(cols, 2 * width)] + [table] * 3
            + owns + comes + [window(a) for a in (*attended, *dqs)],
            out_specs=[full((width // 2, total)), full((width // 2, total)), window(c), full((1, total - width))],
            scratch_shapes=[vmem(rows, total - width, dtype=bf16), vmem(RB, width, dtype=bf16), vmem(rows, width, dtype=bf16)],
        ),
        out_shape=[s((width // 2, total), bf16), s((width // 2, total), bf16), s((rows, width), f32), s((1, total - width), f32)],
        compiler_params=params(),
        cost_estimate=pl.CostEstimate(flops=24 << 30, bytes_accessed=1 << 20, transcendentals=0),
        name="first_tail",
    )(spots, order, c, h, weights, weights, weights, *tables, own, come, *attended, *dqs)


def last_kernel(groups, spot_ref, h_ref, gain_ref, wk_ref, wv_ref, x_ref, cos_ref, low_ref, high_ref, gin_ref, ghin_ref, *refs):
    own_refs, come_refs = refs[:groups], refs[groups:2 * groups]
    grad_ref, send_ref, keep_ref, db_ref, dgain_ref, dshift_ref, p_ref = refs[2 * groups:]
    step = pl.program_id(0)
    spot = pl.ds(pl.multiple_of(step * RB, RB), RB)
    count = wk_ref.shape[1]
    gather_rows(step, spot, (cos_ref[...], low_ref[...], high_ref[...]), own_refs, come_refs, p_ref, 0, count)
    grad = (ghin_ref[...] + mm(p_ref[spot, :count], wk_ref[...], NT) + mm(p_ref[spot, count:], wv_ref[...], NT))
    back, scaled = norm_back(x_ref[...].astype(f32), grad, gain_ref[...])
    grad_ref[...] = back + gin_ref[...]
    sums = col_sum(p_ref[spot, :].astype(f32)), col_sum(scaled), col_sum(grad)

    @pl.when(step == 0)
    def _():
        for ref, value in zip((db_ref, dgain_ref, dshift_ref), sums):
            ref[...] = value

    @pl.when(step > 0)
    def _():
        for ref, value in zip((db_ref, dgain_ref, dshift_ref), sums):
            ref[...] += value

    @pl.when(step == pl.num_programs(0) - 1)
    def _():
        half = send_ref.shape[0]
        for to in range(0, send_ref.shape[1], 512):
            dw = mm(h_ref[...], p_ref[:, to:to + 512], TN).astype(bf16)
            send_ref[:, to:to + 512] = dw[:half]
            keep_ref[:, to:to + 512] = dw[half:]


def last_tail(spots, x, h, gain, weights, tables, gin, gh, owns, comes):
    rows, width = x.shape
    cols = sum(a.shape[1] for a in owns) // 2
    steps = rows // RB
    s = jax.ShapeDtypeStruct

    def full(shape):
        return pl.BlockSpec(shape, lambda j, spot: (0, 0), pipeline_mode=pl.Buffered(1))

    def weight(at):
        return pl.BlockSpec((width, cols), lambda j, spot: (0, at // cols), pipeline_mode=pl.Buffered(1))

    block = pl.BlockSpec((RB, width), lambda j, spot: (j, 0))
    table = pl.BlockSpec((RB, PAIR), lambda j, spot: (spot[j], 0))
    own_windows, come_windows = half_windows(owns, steps)
    return pl.pallas_call(
        partial(last_kernel, len(owns)),
        grid_spec=pltpu.PrefetchScalarGridSpec(
            num_scalar_prefetch=1,
            grid=(steps,),
            in_specs=[full(h.shape), full((1, width)), weight(2 * width - cols), weight(3 * width - cols), block] + [table] * 3
            + [block, block] + own_windows + come_windows,
            out_specs=[block, full((width // 2, 2 * cols)), full((width // 2, 2 * cols)), full((1, 2 * cols)), full((1, width)),
                       full((1, width))],
            scratch_shapes=[vmem(rows, 2 * cols, dtype=bf16)],
        ),
        out_shape=[s((rows, width), f32), s((width // 2, 2 * cols), bf16), s((width // 2, 2 * cols), bf16), s((1, 2 * cols), f32),
                   s((1, width), f32), s((1, width), f32)],
        compiler_params=params(),
        cost_estimate=pl.CostEstimate(flops=12 << 30, bytes_accessed=1 << 20, transcendentals=0),
        name="last_tail",
    )(spots, h, gain.reshape(1, -1), weights, weights, x, *tables, gin, gh, *owns, *comes)


def join_kernel(groups, x_ref, w_ref, mlp_ref, b_ref, *refs):
    att_refs, (out_ref, att_ref) = refs[:groups], refs[groups:]
    at = 0
    for ref in att_refs:
        att_ref[:, at:at + ref.shape[1]] = ref[...]
        at += ref.shape[1]
    out = x_ref[...].astype(f32) + mm(att_ref[...], w_ref[...], NN) + mlp_ref[...] + b_ref[...]
    out_ref[...] = out.astype(bf16)


def join(x, attended, weights, mlp_out, bias):
    rows, width = x.shape
    s = jax.ShapeDtypeStruct
    block = pl.BlockSpec((RB, width), lambda j: (j, 0))
    return pl.pallas_call(
        partial(join_kernel, len(attended)),
        grid=(rows // RB,),
        in_specs=[block, pl.BlockSpec((width, width), lambda j: (0, 3)), block, pl.BlockSpec((1, width), lambda j: (0, 0))]
        + [pl.BlockSpec((RB, a.shape[1]), lambda j: (j, 0)) for a in attended],
        out_specs=block,
        out_shape=s((rows, width), bf16),
        scratch_shapes=[vmem(RB, width, dtype=bf16)],
        compiler_params=params(),
        cost_estimate=pl.CostEstimate(flops=12 << 30, bytes_accessed=1 << 20, transcendentals=0),
        name="join",
    )(x, weights, mlp_out, bias.reshape(1, -1), *attended)


def spread_kernel(c_ref, w_ref, out_ref):
    out_ref[...] = mm(c_ref[...], w_ref[...], NT).astype(bf16)


def spread(c, weights):
    rows, width = c.shape
    block = pl.BlockSpec((RB, width), lambda j: (j, 0))
    return pl.pallas_call(
        spread_kernel,
        grid=(rows // RB,),
        in_specs=[block, pl.BlockSpec((width, width), lambda j: (0, 3))],
        out_specs=block,
        out_shape=jax.ShapeDtypeStruct((rows, width), bf16),
        compiler_params=params(),
        cost_estimate=pl.CostEstimate(flops=1 << 20, bytes_accessed=1 << 16, transcendentals=0),
        name="spread",
    )(c, weights)


def fold(x, op):
    return op(x.reshape(x.shape[0] // 8, 8, x.shape[1]), axis=0)


def eye(size):
    return (lax.broadcasted_iota(jnp.int32, (size, size), 0) == lax.broadcasted_iota(jnp.int32, (size, size), 1)).astype(bf16)


def attention_kernel(half, n, kind_ref, owner_ref, cos_ref, sin_ref, q_ref, do_ref, *refs):
    k_refs, v_refs = refs[:2], refs[2:4]
    o_ref, dq_ref, all_ref, cont_ref, kt_ref, vt_ref, s_ref, p_ref, ds_ref, dka_ref, dva_ref = refs[4:]
    per = half // QB
    wide = n * half
    count = wide // QB
    spots = [(0, c * QB) for c in range(per)] + [(1, c * QB) for c in range((n - 1) * per)]

    ident = eye(PAIR)
    for refs_in, out in ((k_refs, kt_ref), (v_refs, vt_ref)):
        for c, (s, at) in enumerate(spots):
            out[:, c * QB:(c + 1) * QB] = refs_in[s][at:at + QB, :].T
        for c in range(per):
            out[:, wide + c * QB:wide + (c + 1) * QB] = refs_in[0][half + c * QB:half + (c + 1) * QB, :].T
    cont = slice(wide, wide + half)
    dka_ref[cont, :] = jnp.zeros((half, PAIR), f32)
    dva_ref[cont, :] = jnp.zeros((half, PAIR), f32)


    def block(qb, carry):
        own = pl.ds(pl.multiple_of(qb * QB, QB), QB)
        slot = pl.ds(pl.multiple_of(jnp.where(qb < per, qb * QB, wide + (qb - per) * QB), QB), QB)
        zero = jnp.zeros((), bf16)
        causal = lax.broadcasted_iota(jnp.int32, (QB, QB), 0) <= lax.broadcasted_iota(jnp.int32, (QB, QB), 1)
        left = lax.broadcasted_iota(jnp.int32, (QB, PAIR), 1) < HD

        def by_head(a):
            return jnp.where(left, a, zero), jnp.where(left, zero, a)

        def keys_of(some, c):
            if c == count:
                return some[0][own, :]
            s, at = spots[c]
            return some[s][at:at + QB, :]

        def cut(c):
            return slice(c * QB, (c + 1) * QB)

        ident = eye(QB)
        q_heads = by_head(q_ref[own, :])
        do_t = mm(eye(PAIR), do_ref[own, :], NT)
        upper = lax.broadcasted_iota(jnp.int32, (PAIR, QB), 0) < HD
        q_t = mm(eye(PAIR), q_ref[own, :], NT).astype(bf16)
        q_cols = jnp.where(upper, q_t, zero), jnp.where(upper, zero, q_t)
        peaks, norms, outs, deltas, scaled = [None, None], [None, None], [None, None], [None, None], [None, None]

        def scores(h):
            peak = jnp.full((8, QB), MASKED, f32)
            for c in range(count + 1):
                s = mm(keys_of(k_refs, c), q_cols[h], NN)
                if c == count:
                    s = jnp.where(causal, s, MASKED)
                    top = fold(s, jnp.max)
                else:
                    top = fold(s, jnp.max) + kind_ref[qb, c]
                s_ref[h, cut(c)] = s
                peak = jnp.maximum(peak, top)
            peaks[h] = jnp.max(peak, axis=0, keepdims=True)

        def weigh(h):
            total = jnp.zeros((8, QB), f32)
            for c in range(count + 1):
                bias = -peaks[h] if c == count else kind_ref[qb, c] - peaks[h]
                e = jnp.exp2(s_ref[h, cut(c)] + bias)
                total = total + fold(e, jnp.sum)
                p_ref[h, cut(c)] = e.astype(bf16)
            norms[h] = 1.0 / jnp.sum(total, axis=0, keepdims=True)

        def attend(h):
            lines = slice(h * HD, (h + 1) * HD)
            out = mm(vt_ref[lines, 0:wide], p_ref[h, 0:wide], NN) + mm(vt_ref[lines, slot], p_ref[h, wide:], NN)
            outs[h] = out * norms[h]
            deltas[h] = jnp.sum(outs[h] * do_t[lines], axis=0, keepdims=True) * norms[h]
            scaled[h] = do_t[lines] * norms[h]

        scores(0)
        scores(1)
        weigh(0)
        attend(0)
        weigh(1)
        attend(1)
        d_t = jnp.concatenate(scaled, axis=0).astype(bf16)
        d_cols = jnp.where(upper, d_t, zero), jnp.where(upper, zero, d_t)
        do_heads = by_head(mm(ident, d_t, NT).astype(bf16))
        grads = []
        for h in range(2):
            lines = slice(h * HD, (h + 1) * HD)
            for c in range(count + 1):
                dp = mm(keys_of(v_refs, c), d_cols[h], NN)
                ds_ref[h, cut(c)] = p_ref[h, cut(c)] * (dp - deltas[h]).astype(bf16)
            dq = mm(kt_ref[lines, 0:wide], ds_ref[h, 0:wide], NN) + mm(kt_ref[lines, slot], ds_ref[h, wide:], NN)
            a, b = dq[:ROT // 2], dq[ROT // 2:ROT]
            cosine, sine = cos_ref[:, own], sin_ref[:, own]
            grads.append(jnp.concatenate([a * cosine + b * sine, b * cosine - a * sine, dq[ROT:]], axis=0))
        for c in range(count + 1):
            at = slot if c == count else cut(c)
            dv = mm(p_ref[0, cut(c)], do_heads[0], NN) + mm(p_ref[1, cut(c)], do_heads[1], NN)
            dk = mm(ds_ref[0, cut(c)], q_heads[0], NN) + mm(ds_ref[1, cut(c)], q_heads[1], NN)
            if c == count:
                dva_ref[at, :] += dv
                dka_ref[at, :] += dk
            else:
                dva_ref[at, :] = jnp.where(qb == 0, dv, dva_ref[at, :] + dv)
                dka_ref[at, :] = jnp.where(qb == 0, dk, dka_ref[at, :] + dk)
        o_ref[own, :] = mm(ident, jnp.concatenate(outs, axis=0).astype(bf16), NT).astype(bf16)
        dq_ref[own, :] = mm(ident, (jnp.concatenate(grads, axis=0) * (HD ** (-0.5))).astype(bf16), NT).astype(bf16)

        return carry

    lax.fori_loop(0, 2 * per, block, 0)

    def flush(out, to, frm):
        rows = pl.ds(to, half)
        out[rows, :PAIR] = (dka_ref[frm:frm + half, :] * math.log(2.0)).astype(bf16)
        out[rows, PAIR:] = dva_ref[frm:frm + half, :].astype(bf16)

    flush(cont_ref, 0, wide)
    for s in range(n):
        flush(all_ref, pl.multiple_of(owner_ref[s] * half, half), s * half)


def attention(kind, owners, cos_t, sin_t, q, do, ks, vs, first, pairs):
    rows = q.shape[0]
    half = rows // 2
    n = 1 + ks[1].shape[0] // half
    wide = n * half
    keys = wide + half
    total = wide + QB
    qspec = pl.BlockSpec((rows, PAIR), lambda p: (0, p + first))
    ospec = pl.BlockSpec((rows, PAIR), lambda p: (0, p))
    table = pl.BlockSpec((ROT // 2, rows), lambda p: (0, 0))
    kspecs = [pl.BlockSpec((k.shape[0], PAIR), lambda p: (0, p + first)) for k in ks]
    gspecs = [pl.BlockSpec((size, 2 * PAIR), lambda p: (0, p)) for size in (wide, half)]
    s = jax.ShapeDtypeStruct
    pieces = pairs * rows // QB
    return pl.pallas_call(
        partial(attention_kernel, half, n),
        grid=(pairs,),
        in_specs=[pl.BlockSpec(memory_space=pltpu.SMEM), pl.BlockSpec(memory_space=pltpu.SMEM), table, table, qspec, qspec] + kspecs + kspecs,
        out_specs=[ospec, ospec] + gspecs,
        out_shape=[s((rows, pairs * PAIR), bf16), s((rows, pairs * PAIR), bf16)]
        + [s((size, 2 * pairs * PAIR), bf16) for size in (wide, half)],
        scratch_shapes=[pltpu.VMEM((PAIR, keys), bf16), pltpu.VMEM((PAIR, keys), bf16),
                        pltpu.VMEM((2, total, QB), f32), pltpu.VMEM((2, total, QB), bf16),
                        pltpu.VMEM((2, total, QB), bf16),
                        pltpu.VMEM((keys, PAIR), f32), pltpu.VMEM((keys, PAIR), f32)],
        compiler_params=pltpu.CompilerParams(vmem_limit_bytes=60 << 20),
        cost_estimate=pl.CostEstimate(flops=1 << 20, bytes_accessed=1 << 16, transcendentals=0),
        name="attention",
    )(kind, owners, cos_t, sin_t, q, do, *ks, *vs)


def pairs_of(bit, size):
    return [(a, a ^ bit) for a in range(size)]


def add_kernel(plan, *refs):
    for a, b, moves in plan:
        for source, to, target in moves:
            refs[to][target] = (refs[a][source].astype(f32) + refs[b][source].astype(f32)).astype(bf16)


def add_parts(arrays, plan, shapes, steps, load=0):
    def spec(shape):
        block = (*shape[:-1], shape[-1] // steps)
        return pl.BlockSpec(block, lambda j: (0,) * (len(shape) - 1) + (j,))

    return pl.pallas_call(
        partial(add_kernel, plan),
        grid=(steps,),
        in_specs=[spec(a.shape) for a in arrays],
        out_specs=[spec(shape) for shape in shapes],
        out_shape=[jax.ShapeDtypeStruct(shape, bf16) for shape in shapes],
        compiler_params=params(),
        cost_estimate=pl.CostEstimate(flops=(load << 30) + 1, bytes_accessed=1 << 16, transcendentals=0),
        name="add_parts",
    )(*arrays)


EVERY = slice(None)


def swap(a, bit):
    return lax.ppermute(a, "fsdp", pairs_of(bit, 8))


def steps_for(arrays):
    smallest = min(a.shape[-1] for a in arrays)
    return 4 if smallest % (4 * PAIR) == 0 else 1


def core_step(sends, keeps):
    count = len(sends)
    arrays, plan, shapes = [], [], []
    for send, keep in zip(sends, keeps):
        rows, cols = send.shape
        cut = (2, 2, 2, rows // 8, cols)
        to = 2 * count + len(shapes)
        moves = [((EVERY, 1, 0), to, (EVERY,)), ((EVERY, 0, 0), to + 1, (EVERY,)),
                 ((1, EVERY, 1), to + 2, (EVERY,)), ((0, EVERY, 1), to + 3, (EVERY,))]
        plan.append((len(arrays), len(arrays) + 1, moves))
        arrays += [keep.reshape(cut), swap(send, 1).reshape(cut)]
        shapes += [(2, rows // 8, cols)] * 4
    return add_parts(arrays, plan, shapes, steps_for(arrays))


def side_step(items, load=0):
    arrays, plan, shapes = [], [], []
    for i in range(0, len(items), 4):
        for send, keep, bit in ((items[i], items[i + 1], 2), (items[i + 2], items[i + 3], 4)):
            to = len(items) + len(shapes)
            plan.append((len(arrays), len(arrays) + 1, [((1,), to, (EVERY,)), ((0,), to + 1, (EVERY,))]))
            arrays += [keep, swap(send, bit)]
            shapes += [keep.shape[1:]] * 2
    return add_parts(arrays, plan, shapes, steps_for(arrays), load)


def last_step(items, load=0):
    arrays, plan, shapes = [], [], []
    for i in range(0, len(items), 4):
        to = len(items) + len(shapes)
        for at, (send, keep, bit) in enumerate(((items[i], items[i + 1], 4), (items[i + 2], items[i + 3], 2))):
            plan.append((len(arrays), len(arrays) + 1, [((EVERY,), to, (at,))]))
            arrays += [keep, swap(send, bit)]
        shapes.append((2, *keep.shape))
    parts = add_parts(arrays, plan, shapes, steps_for(arrays), load)
    return [part.reshape(-1, part.shape[-1]) for part in parts]


def along(part):
    return lax.psum_scatter(part, "ctx", scatter_dimension=0, tiled=True)


def after(value, *others):
    return lax.optimization_barrier((value, *others))[0]


def kept_after(items, *others):
    return [after(a, *others) if i % 2 else a for i, a in enumerate(items)]


def fast(inputs, cotangent, positions, segments, ln1_gain, ln1_bias, w_qkv, b_qkv, w_attn_out, b_out,
         ln2_gain, ln2_bias, w_in, b_in, w_out):
    x, grad_out, pos = inputs[0], cotangent[0], positions[0]
    rows, width = x.shape
    half = rows // 2
    n = lax.axis_size("ctx")
    ring = [(i, (i + 1) % n) for i in range(n)]
    back = [(i, (i - 1) % n) for i in range(n)]
    me, place = lax.axis_index("fsdp"), lax.axis_index("ctx")
    relative = [4 * dy + 2 * dx + 1 - keep for keep in (0, 1) for dy in (0, 1) for dx in (0, 1)]
    order = jnp.bitwise_xor(me, jnp.array(relative, jnp.int32))
    owners = lax.rem(place + n - jnp.arange(n), n)
    far = [None] * n
    far[0] = x[:half]
    for s in range(1, n):
        far[s] = lax.ppermute(far[s - 1], "ctx", ring)
    spots = [pos[::RB] // RB]
    for s in range(1, n):
        spots.append(lax.ppermute(spots[0][:half // RB], "ctx", [(i, (i + s) % n) for i in range(n)]))
    mine = (ln1_gain, ln1_bias, b_qkv, b_out, ln2_gain, ln2_bias, b_in)
    small = lax.all_gather(jnp.concatenate(mine).reshape(1, -1), "fsdp", axis=0, tiled=True)
    full, at = [], 0
    for a in mine:
        full.append(small[:, at:at + a.shape[0]].reshape(-1).astype(f32))
        at += a.shape[0]
    gain_attn, shift_attn, bias_qkv, bias_out, gain_mlp, shift_mlp, bias_in = full
    weights = lax.all_gather(jnp.concatenate([w_qkv, w_attn_out], axis=1), "fsdp", axis=0, tiled=True)

    lane = jnp.arange(PAIR) % HD
    inverse = jnp.exp(-math.log(10000.0) * (2.0 / ROT) * (lane % (ROT // 2)).astype(f32))
    angles = jnp.arange(n * half + CLEN).astype(f32)[:, None] * inverse[None, :]
    sine = jnp.sin(angles)
    tables = (jnp.where(lane < ROT, jnp.cos(angles), 1.0), jnp.where(lane < ROT // 2, sine, 0.0),
              jnp.where((lane >= ROT // 2) & (lane < ROT), sine, 0.0))
    angles_t = pos.astype(f32)[None, :] * inverse[:ROT // 2, None]
    cos_t, sin_t = jnp.cos(angles_t), jnp.sin(angles_t)

    normed, queries, own_keys, own_values = qkv(
        spots[0], order, [after(x, far[n - 2], *spots[1:])], gain_attn, shift_attn, weights, bias_qkv, tables)
    far_keys, far_values = qkv(
        jnp.concatenate(spots[1:]), order, far[1:], gain_attn, shift_attn, weights, bias_qkv, tables)
    keys, values = (own_keys, far_keys), (own_values, far_values)
    grad_att = spread(grad_out, weights)
    weight_in = lax.all_gather(after(w_in, far[1], *full, *tables, cos_t, sin_t), "fsdp", axis=0, tiled=True)
    weight_out = lax.all_gather(after(w_out, far[1], *full, *tables, cos_t, sin_t), "fsdp", axis=0, tiled=True)

    per = half // QB
    earlier = jnp.stack([spots[s][0] < spots[0][0] for s in range(1, n)])
    local_row = jnp.arange(2 * per)[:, None]
    seen_own = local_row > jnp.arange(per)[None, :]
    seen_far = jnp.repeat(earlier[None, :] | (local_row >= per), per, axis=1)
    kind = jnp.where(jnp.concatenate([seen_own, seen_far], axis=1), 0.0, MASKED).astype(f32)

    attended, grad_q, own_kv, come_kv = [], [], [], []

    def attend(first, count, wait):
        out = attention(kind, owners, cos_t, sin_t, after(queries, *wait), grad_att, keys, values, first, count)
        attended.append(out[0])
        grad_q.append(out[1])
        come_kv.append(lax.psum_scatter(out[2], "ctx", scatter_dimension=0, tiled=True))
        own_kv.append(out[3])

    attend(0, 4, ())
    mlp_out, grad_mlp, in_send, in_keep, out_send, out_keep, db_in, db_out, dgain_mlp, dshift_mlp = mlp(
        order, after(x, *attended), grad_out, gain_mlp, shift_mlp, weight_in, bias_in, weight_out)
    attend(4, 1, (mlp_out,))
    steps_mlp = core_step([out_send, in_send], [out_keep, in_keep])
    attend(5, 3, (*attended, *steps_mlp))
    steps_mlp = side_step(kept_after(steps_mlp, *attended))
    output = join(after(x, *steps_mlp), attended, weights, mlp_out, bias_out)
    first_send, first_keep, grad_heads, db_first = first_tail(
        spots[0], order, after(grad_out, output), normed, weights, tables, attended, grad_q, own_kv[0], come_kv[0])
    part_out, part_in = last_step(kept_after(steps_mlp, grad_heads), 48)
    steps_first = core_step([first_send], [first_keep])
    grad_inputs, last_send, last_keep, db_last, dgain_attn, dshift_attn = last_tail(
        spots[0], after(x, part_out, part_in, *steps_first), normed, gain_attn, weights, tables, grad_mlp, grad_heads,
        own_kv[1:], come_kv[1:])
    sum_out, sum_in = along(part_out), along(part_in)
    steps_first = side_step(kept_after(steps_first, last_send), 48)
    cols = db_last.shape[1] // 2
    split = [width, width + (db_first.shape[1] - width) // 2]
    db_q, db_k, db_v = jnp.split(db_first, split, axis=1)
    db_qkv = jnp.concatenate([db_q, db_k, db_last[:, :cols], db_v, db_last[:, cols:]], axis=1)
    parts = 8 * n
    smalls = [a.reshape(parts, -1) for a in (dgain_attn, dshift_attn, db_qkv, db_out, dgain_mlp, dshift_mlp, db_in)]
    flat = jnp.concatenate(smalls, axis=1).astype(bf16).reshape(parts, -1, PAIR)
    lines = flat.shape[1]
    packed = jnp.pad(flat, ((0, 0), (0, width // parts - lines), (0, 0))).reshape(width, PAIR)
    packed = packed.reshape(8, width // 8, PAIR)[order].reshape(2, width // 2, PAIR)
    steps_last = core_step([last_send, packed[0]], [after(last_keep, *steps_first), packed[1]])
    part_first = last_step(steps_first)
    part_last = last_step(side_step(steps_last))
    total = along(jnp.concatenate([*part_first, *part_last], axis=1))
    ends = [width, 2 * width, split[1] + width, db_first.shape[1] + width]
    ends += [ends[-1] + cols, ends[-1] + 2 * cols]
    sum_attn, sum_q, sum_k, sum_v, end_k, end_v, packed = jnp.split(total, ends, axis=1)
    sum_qkv = jnp.concatenate([sum_q, sum_k, end_k, sum_v, end_v], axis=1)
    packed = packed[:lines].astype(f32).reshape(-1)
    done, at = [], 0
    for a in smalls:
        done.append(packed[at:at + a.shape[1]])
        at += a.shape[1]
    return (output[None], grad_inputs[None], done[0], done[1], sum_qkv.astype(f32), done[2], sum_attn.astype(f32),
            done[3], done[4], done[5], sum_in.astype(f32), done[6], sum_out.astype(f32))


def local(*args):
    half = args[0].shape[1] // 2
    if args[0].shape[0] == 1 and half % CLEN == 0 and lax.axis_size("fsdp") == 8:
        return fast(*args)
    return generic(*args)


def generic(
    inputs,
    cotangent,
    positions,
    segments,
    ln1_gain,
    ln1_bias,
    w_qkv,
    b_qkv,
    w_attn_out,
    b_out,
    ln2_gain,
    ln2_bias,
    w_in,
    b_in,
    w_out,
):
    shards = (
        ln1_gain,
        ln1_bias,
        w_qkv,
        b_qkv,
        w_attn_out,
        b_out,
        ln2_gain,
        ln2_bias,
        w_in,
        b_in,
        w_out,
    )
    params = (
        lax.all_gather(shards[0], "fsdp", axis=0, tiled=True),
        lax.all_gather(shards[1], "fsdp", axis=0, tiled=True),
        lax.all_gather(shards[2], "fsdp", axis=0, tiled=True),
        lax.all_gather(shards[3], "fsdp", axis=0, tiled=True),
        lax.all_gather(shards[4], "fsdp", axis=0, tiled=True),
        lax.all_gather(shards[5], "fsdp", axis=0, tiled=True),
        lax.all_gather(shards[6], "fsdp", axis=0, tiled=True),
        lax.all_gather(shards[7], "fsdp", axis=0, tiled=True),
        lax.all_gather(shards[8], "fsdp", axis=0, tiled=True),
        lax.all_gather(shards[9], "fsdp", axis=0, tiled=True),
        lax.all_gather(shards[10], "fsdp", axis=0, tiled=True),
    )
    groups, local_len, width = inputs.shape
    rows_total = groups * local_len
    block = math.gcd(local_len, 256)
    label_pos, label_seg = (
        lax.all_gather(positions, "ctx", axis=1, tiled=True),
        lax.all_gather(segments, "ctx", axis=1, tiled=True),
    )
    count = label_pos.shape[1] // block
    f32 = jnp.float32
    bf16 = jnp.bfloat16
    (
        gain_attn,
        shift_attn,
        weight_qkv,
        bias_qkv,
        weight_attn,
        bias_out,
        gain_mlp,
        shift_mlp,
        weight_in,
        bias_in,
        weight_out,
    ) = params
    flat_in = inputs.reshape(rows_total, width).astype(f32)
    normed_attn = layer_norm(flat_in, gain_attn.astype(f32), shift_attn.astype(f32)).astype(bf16)
    normed_mlp = layer_norm(flat_in, gain_mlp.astype(f32), shift_mlp.astype(f32)).astype(bf16)
    projected = jnp.dot(normed_attn, weight_qkv, preferred_element_type=f32) + bias_qkv.astype(f32)
    cosine, sine = rotary_tables(positions)

    def split_heads(columns):
        return columns.reshape(groups, local_len, HEADS, HD)

    scale = HD ** (-0.5)
    queries = (rotate(split_heads(projected[:, :width]), cosine, sine) * scale).astype(bf16)
    keys_own = rotate(split_heads(projected[:, width : 2 * width]), cosine, sine).astype(bf16)
    values_own = split_heads(projected[:, 2 * width :]).astype(bf16)
    keys_all, values_all = (
        lax.all_gather(keys_own, "ctx", axis=1, tiled=True),
        lax.all_gather(values_own, "ctx", axis=1, tiled=True),
    )

    def key_block(index):
        start = index * block
        keys_blk = lax.dynamic_slice_in_dim(keys_all, start, block, 1)
        values_blk = lax.dynamic_slice_in_dim(values_all, start, block, 1)
        mask = allowed_mask(
            positions,
            segments,
            lax.dynamic_slice_in_dim(label_pos, start, block, 1),
            lax.dynamic_slice_in_dim(label_seg, start, block, 1),
        )
        return (keys_blk, values_blk, mask)

    def total_step(carry, index):
        peak, total = carry
        keys_blk, values_blk, mask = key_block(index)
        scores = jnp.where(mask, scores_of(queries, keys_blk), MASKED)
        fresh = jnp.maximum(peak, jnp.max(scores, axis=-1))
        added = jnp.sum(jnp.where(mask, jnp.exp(scores - fresh[..., None]), 0.0), axis=-1)
        return ((fresh, total * jnp.exp(peak - fresh) + added), None)

    stat_shape = (groups, HEADS, local_len)
    (peak, total), unused = lax.scan(
        total_step,
        (jnp.full(stat_shape, MASKED, f32), jnp.zeros(stat_shape, f32)),
        jnp.arange(count),
    )
    log_total = peak + jnp.log(total)

    def attend_step(rounded_sum, index):
        keys_blk, values_blk, mask = key_block(index)
        probs = jnp.where(mask, jnp.exp(scores_of(queries, keys_blk) - log_total[..., None]), 0.0)
        rounded_sum = rounded_sum + jnp.einsum(
            "ghqk,gkhd->gqhd", probs.astype(bf16), values_blk, preferred_element_type=f32
        )
        return (rounded_sum, None)

    head_shape = (groups, local_len, HEADS, HD)
    rounded_sum, unused = lax.scan(attend_step, jnp.zeros(head_shape, f32), jnp.arange(count))
    attended = rounded_sum.reshape(rows_total, width).astype(bf16)
    pre_act = jnp.dot(normed_mlp, weight_in, preferred_element_type=f32) + bias_in.astype(f32)
    activated = jax.nn.gelu(pre_act, approximate=False).astype(bf16)
    output = (
        flat_in
        + jnp.dot(attended, weight_attn, preferred_element_type=f32)
        + jnp.dot(activated, weight_out, preferred_element_type=f32)
        + bias_out.astype(f32)
    )
    (
        gain_attn,
        shift_attn,
        weight_qkv,
        bias_qkv,
        weight_attn,
        bias_out,
        gain_mlp,
        shift_mlp,
        weight_in,
        bias_in,
        weight_out,
    ) = params
    grad_out = cotangent.reshape(rows_total, width)
    grad_bias_out = jnp.sum(grad_out.astype(f32), axis=0)
    grad_weight_out = jnp.einsum("rf,rd->fd", activated, grad_out, preferred_element_type=f32)
    grad_act = jnp.einsum("rd,fd->rf", grad_out, weight_out, preferred_element_type=f32)
    unused, gelu_back = jax.vjp(partial(jax.nn.gelu, approximate=False), pre_act)
    grad_pre = gelu_back(grad_act)[0].astype(bf16)
    grad_weight_in = jnp.einsum("rd,rf->df", normed_mlp, grad_pre, preferred_element_type=f32)
    grad_bias_in = jnp.sum(grad_pre.astype(f32), axis=0)
    grad_normed_mlp = jnp.einsum("rf,df->rd", grad_pre, weight_in, preferred_element_type=f32)
    grad_weight_attn = jnp.einsum("ra,rd->ad", attended, grad_out, preferred_element_type=f32)
    grad_att = (
        jnp.einsum("rd,ad->ra", grad_out, weight_attn, preferred_element_type=f32)
        .astype(bf16)
        .reshape(head_shape)
    )
    delta = jnp.einsum(
        "gqhd,gqhd->ghq", grad_att.astype(f32), rounded_sum, precision=lax.Precision.HIGHEST
    )

    def back_step(carry, index):
        keys_blk, values_blk, mask = key_block(index)
        rounded, grad_scores = block_grads(
            queries, grad_att, log_total, delta, mask, keys_blk, values_blk
        )
        carry = carry + jnp.einsum(
            "ghqk,gkhd->gqhd", grad_scores, keys_blk, preferred_element_type=f32
        )
        key_term = jnp.einsum("ghqk,gqhd->gkhd", grad_scores, queries, preferred_element_type=f32)
        value_term = jnp.einsum("ghqk,gqhd->gkhd", rounded, grad_att, preferred_element_type=f32)
        return (carry, (key_term, value_term))

    grad_queries, (key_terms, value_terms) = lax.scan(
        back_step, jnp.zeros(head_shape, f32), jnp.arange(count)
    )
    key_sums, value_sums = (
        lax.psum_scatter(
            key_terms.astype(jnp.bfloat16), "ctx", scatter_dimension=0, tiled=True
        ).astype(jnp.float32),
        lax.psum_scatter(
            value_terms.astype(jnp.bfloat16), "ctx", scatter_dimension=0, tiled=True
        ).astype(jnp.float32),
    )
    grad_keys = jnp.transpose(key_sums, (1, 0, 2, 3, 4)).reshape(head_shape)
    grad_values = jnp.transpose(value_sums, (1, 0, 2, 3, 4)).reshape(head_shape)
    grad_q_pre = unrotate(grad_queries * scale, cosine, sine).reshape(rows_total, width)
    grad_k_pre = unrotate(grad_keys, cosine, sine).reshape(rows_total, width)
    grad_projected = jnp.concatenate(
        [grad_q_pre, grad_k_pre, grad_values.reshape(rows_total, width)], axis=1
    ).astype(bf16)
    grad_weight_qkv = jnp.einsum(
        "rd,re->de", normed_attn, grad_projected, preferred_element_type=f32
    )
    grad_bias_qkv = jnp.sum(grad_projected.astype(f32), axis=0)
    grad_normed_attn = jnp.einsum(
        "re,de->rd", grad_projected, weight_qkv, preferred_element_type=f32
    )
    unused, norm_back_attn = jax.vjp(
        layer_norm, flat_in, gain_attn.astype(f32), shift_attn.astype(f32)
    )
    grad_in_attn, grad_gain_attn, grad_shift_attn = norm_back_attn(grad_normed_attn)
    unused, norm_back_mlp = jax.vjp(
        layer_norm, flat_in, gain_mlp.astype(f32), shift_mlp.astype(f32)
    )
    grad_in_mlp, grad_gain_mlp, grad_shift_mlp = norm_back_mlp(grad_normed_mlp)
    grad_inputs = (grad_out.astype(f32) + grad_in_attn + grad_in_mlp).reshape(
        groups, local_len, width
    )
    sums = (
        lax.psum_scatter(grad_gain_attn, ("fsdp", "ctx"), scatter_dimension=0, tiled=True),
        lax.psum_scatter(grad_shift_attn, ("fsdp", "ctx"), scatter_dimension=0, tiled=True),
        lax.psum_scatter(grad_weight_qkv, ("fsdp", "ctx"), scatter_dimension=0, tiled=True),
        lax.psum_scatter(grad_bias_qkv, ("fsdp", "ctx"), scatter_dimension=0, tiled=True),
        lax.psum_scatter(grad_weight_attn, ("fsdp", "ctx"), scatter_dimension=0, tiled=True),
        lax.psum_scatter(grad_bias_out, ("fsdp", "ctx"), scatter_dimension=0, tiled=True),
        lax.psum_scatter(grad_gain_mlp, ("fsdp", "ctx"), scatter_dimension=0, tiled=True),
        lax.psum_scatter(grad_shift_mlp, ("fsdp", "ctx"), scatter_dimension=0, tiled=True),
        lax.psum_scatter(grad_weight_in, ("fsdp", "ctx"), scatter_dimension=0, tiled=True),
        lax.psum_scatter(grad_bias_in, ("fsdp", "ctx"), scatter_dimension=0, tiled=True),
        lax.psum_scatter(grad_weight_out, ("fsdp", "ctx"), scatter_dimension=0, tiled=True),
    )
    result = output.reshape(groups, local_len, width).astype(bf16)
    return (
        result,
        grad_inputs,
        sums[0],
        sums[1],
        sums[2],
        sums[3],
        sums[4],
        sums[5],
        sums[6],
        sums[7],
        sums[8],
        sums[9],
        sums[10],
    )


def solution(mesh):
    in_specs = (
        P("fsdp", "ctx", None),
        P("fsdp", "ctx", None),
        P("fsdp", "ctx"),
        P("fsdp", "ctx"),
        P("fsdp"),
        P("fsdp"),
        P("fsdp", None),
        P("fsdp"),
        P("fsdp", None),
        P("fsdp"),
        P("fsdp"),
        P("fsdp"),
        P("fsdp", None),
        P("fsdp"),
        P("fsdp", None),
    )
    out_specs = (
        P("fsdp", "ctx", None),
        P("fsdp", "ctx", None),
        P(("fsdp", "ctx")),
        P(("fsdp", "ctx")),
        P(("fsdp", "ctx"), None),
        P(("fsdp", "ctx")),
        P(("fsdp", "ctx"), None),
        P(("fsdp", "ctx")),
        P(("fsdp", "ctx")),
        P(("fsdp", "ctx")),
        P(("fsdp", "ctx"), None),
        P(("fsdp", "ctx")),
        P(("fsdp", "ctx"), None),
    )
    return jax.shard_map(local, mesh=mesh, in_specs=in_specs, out_specs=out_specs, check_vma=False)
```
